256 devices in a mesh: slab: 64 (over y, z, x_lo), ffn: 4 (over x_hi, core).
Axes of the slice: x: 4 (x_hi: 2, x_lo: 2; x = x_hi * 2 + x_lo), y: 4, z: 8, core: 2. Of those that a mesh axis runs over, the one named last changes fastest.
Arguments:
- tokens: bfloat16 [32768, 512], P('slab'), may hold values from -6 to 6
- gain_attn: float32 [512], replicated, may hold values from 0.1 to 1.9
- w_reduce: bfloat16 [4096, 512], replicated, may hold values from -0.09375 to 0.09375
- gain_keys: float32 [512], replicated, may hold values from 0.1 to 1.9
- w_query: bfloat16 [512, 512], P(None, 'ffn'), may hold values from -1.5 to 1.5
- w_key: bfloat16 [512, 512], P(None, 'ffn'), may hold values from -1.5 to 1.5
- w_value: bfloat16 [512, 512], P(None, 'ffn'), may hold values from -0.25 to 0.25
- w_out: bfloat16 [512, 512], P('ffn'), may hold values from -1.796875 to 1.796875
- gain_ffn: float32 [512], replicated, may hold values from 0.1 to 1.9
- w_up: bfloat16 [512, 2048], P(None, 'ffn'), may hold values from -0.25 to 0.25
- w_depth: float32 [27, 2048], P(None, 'ffn'), may hold values from -1.25 to 1.25
- w_down: bfloat16 [2048, 512], P('ffn'), may hold values from -0.125 to 0.125
- grad_out: bfloat16 [32768, 512], P('slab'), may hold values from -0.0625 to 0.0625
Outputs:
- attended: bfloat16 [32768, 512], P('slab')
- grad_up: float32 [512, 2048], P('slab', 'ffn')
- grad_down: float32 [512, 2048], P('slab', 'ffn')
The draws below stay inside these ranges and needn't reach their ends.
All inputs are finite; a program needn't handle non-finite values.
Results may differ from the reference program's by a relative error of at most 0.024.
The reference program's roundings to bfloat16 on the way count: a program that leaves them out, or rounds other values in their place, can miss the bound.
Values may be sent and summed in bfloat16 or wider, within the bound.
A program may use at most 64 MiB of HBM per device.

```python
import jax
import jax.numpy as jnp
from jax import lax

D = 512
HEADS = 8
FF = 2048
HEAD = 64
GX = 16
GY = 16
NZ = 128
TOK_DEV = 512
TOKENS = 32768
RED = 4096
N_SLAB = 64


def own_part(key, salt):
    return jax.random.normal(jax.random.fold_in(key, salt), (D, D), jnp.float32) * (1.4 / D ** 0.5)


def draw_w_query(key, part):
    values = own_part(key, 11)
    return jnp.clip(values, -1.5, 1.5).astype(jnp.bfloat16)


def draw_w_key(key, part):
    values = own_part(key, 23)
    return jnp.clip(values, -1.5, 1.5).astype(jnp.bfloat16)


def raised(entries, rng, source, target, parts, factor):
    owner, partner = [(jnp.arange(entries.shape[dim]) // (entries.shape[dim] // parts)).reshape([-1 if axis == dim else 1 for axis in range(entries.ndim)]) for dim in (source, target)]
    chosen = jax.random.permutation(rng, parts)[partner]
    strong = (owner == chosen) | (owner == (partner + parts // 2) % parts)
    return jnp.where(strong, factor * entries, entries)


def block_levels(stream_key, dims, shards, least, top_value):
    gain = 1.0
    for dim, parts in shards:
        heights = jax.random.uniform(jax.random.fold_in(jax.random.fold_in(stream_key, 6), dim), (parts,), jnp.float32, least / len(shards), top_value / len(shards))
        gain = gain * jnp.repeat(jnp.exp(heights), dims[dim] // parts).reshape((-1,) + (1,) * (len(dims) - 1 - dim))
    return gain


def gaussian(stream_key, dims, spread, bound, cuts=(), kind=jnp.bfloat16):
    array = jax.random.normal(stream_key, dims, jnp.float32) * spread
    if len(cuts) > 0:
        array = block_levels(stream_key, dims, cuts, -0.22, 0.18) * array
    return jnp.clip(array, min=-bound, max=bound).astype(kind)


def heavy_noise(stream_key, dims, scale, most, shards, heavy, held_as=jnp.bfloat16):
    entries = scale * jax.random.normal(stream_key, dims, jnp.float32)
    if shards:
        entries = entries * block_levels(stream_key, dims, shards, -0.22, 0.18)
    return jnp.clip(raised(entries, jax.random.fold_in(stream_key, 3), *heavy), -most, most).astype(held_as)


def setup_inputs(seed: int = 0) -> dict:
    seeds = jax.random.split(jax.random.key(seed), 14)
    tokens = gaussian(seeds[0], (TOKENS, D), 1.0, 6.0, ((0, 64),))
    gain_attn = jnp.clip(1.0 + 0.18 * jax.random.normal(seeds[1], (D,), jnp.float32), 0.1, 1.9)
    w_reduce = gaussian(seeds[2], (8 * D, D), (8 * D) ** -0.5, 0.09375)
    gain_keys = jnp.clip(1.0 + 0.18 * jax.random.normal(seeds[3], (D,), jnp.float32), 0.1, 1.9)
    w_query = draw_w_query(jax.random.fold_in(seeds[13], 71), 0)
    w_key = draw_w_key(jax.random.fold_in(seeds[13], 71), 0)
    w_value = gaussian(seeds[6], (D, D), D ** -0.5, 0.25, ((1, 4),))
    w_out = gaussian(seeds[7], (D, D), 0.3, 1.796875, ((0, 4),))
    gain_ffn = jnp.clip(1.0 + 0.18 * jax.random.normal(seeds[8], (D,), jnp.float32), 0.1, 1.9)
    w_up = gaussian(seeds[9], (D, FF), D ** -0.5, 0.25, ((1, 4),))
    w_depth = gaussian(seeds[10], (27, FF), 27 ** -0.5, 1.25, ((1, 4),), jnp.float32)
    w_down = gaussian(seeds[11], (FF, D), FF ** -0.5, 0.125, ((0, 4),))
    grad_out = heavy_noise(seeds[12], (TOKENS, D), 0.004, 0.0625, ((0, 64),), (0, 1, 64, 4.0))
    return {"tokens": tokens, "gain_attn": gain_attn, "w_reduce": w_reduce, "gain_keys": gain_keys, "w_query": w_query, "w_key": w_key, "w_value": w_value, "w_out": w_out, "gain_ffn": gain_ffn, "w_up": w_up, "w_depth": w_depth, "w_down": w_down, "grad_out": grad_out}


EPSILON = 1e-05
ROPE_BASE = 100.0
ROOT_HALF = 0.7071067811865476
NORMAL_SCALE = 0.3989422804014327

def layer_norm(values, scale_gain):
    values = values.astype(jnp.float32)
    centered = values - lax.optimization_barrier(jnp.mean(values, axis=-1, keepdims=True))
    variance = lax.optimization_barrier(jnp.mean(centered * centered, axis=-1, keepdims=True))
    return centered * lax.rsqrt(variance + EPSILON) * scale_gain.astype(jnp.float32)

def rope_tables(coord_x, coord_y, coord_z, head_size):
    pair_count = head_size // 2
    position = jnp.arange(pair_count, dtype=jnp.int32)
    axis_pick = position % 3
    per_axis = (pair_count + 2) // 3
    frequency = ROPE_BASE ** (-(position // 3).astype(jnp.float32) / per_axis)
    angles = (coord_x[:, None] * (axis_pick == 0) + coord_y[:, None] * (axis_pick == 1) + coord_z[:, None] * (axis_pick == 2)) * frequency
    return (jnp.cos(angles)[:, None, :], jnp.sin(angles)[:, None, :])

def token_tables(first_plane, planes, head_size):
    position = jnp.arange(planes * GY * GX, dtype=jnp.int32)
    coord_x = (position % GX).astype(jnp.float32)
    coord_y = (position // GX % GY).astype(jnp.float32)
    coord_z = (first_plane + position // (GX * GY)).astype(jnp.float32)
    return rope_tables(coord_x, coord_y, coord_z, head_size)

def key_tables(first_row, row_count, head_size):
    position = first_row + jnp.arange(row_count, dtype=jnp.int32)
    half_x = GX // 2
    half_y = GY // 2
    coord_x = (position % half_x).astype(jnp.float32) * 2.0 + 0.5
    coord_y = (position // half_x % half_y).astype(jnp.float32) * 2.0 + 0.5
    coord_z = (position // (half_x * half_y)).astype(jnp.float32) * 2.0 + 0.5
    return rope_tables(coord_x, coord_y, coord_z, head_size)

def rotate(values, cosine, sine_table):
    half_size = values.shape[-1] // 2
    front_half = values[..., :half_size]
    back_half = values[..., half_size:]
    return jnp.concatenate([front_half * cosine - back_half * sine_table, back_half * cosine + front_half * sine_table], axis=-1)

def make_patches(normed, planes):
    width = normed.shape[-1]
    cell_grid = normed.reshape(planes // 2, 2, GY // 2, 2, GX // 2, 2, width)
    return cell_grid.transpose(0, 2, 4, 1, 3, 5, 6).reshape(-1, 8 * width)

def depth_conv(padded, weights, planes):
    height = padded.shape[1] - 2
    width_x = padded.shape[2] - 2
    result = jnp.zeros((planes, height, width_x, padded.shape[3]), jnp.float32)
    for offset in range(27):
        shift_z = offset // 9
        shift_y = offset // 3 % 3
        shift_x = offset % 3
        window = padded[shift_z:shift_z + planes, shift_y:shift_y + height, shift_x:shift_x + width_x]
        result = result + window.astype(jnp.float32) * weights[offset].astype(jnp.float32)
    return result

def reference(tokens, gain_attn, w_reduce, gain_keys, w_query, w_key, w_value, w_out, gain_ffn, w_up, w_depth, w_down, grad_out):
    normed = layer_norm(tokens, gain_attn).astype(jnp.bfloat16)
    patches = make_patches(normed, NZ)
    reduced = jnp.dot(patches, w_reduce, preferred_element_type=jnp.float32)
    key_input = layer_norm(reduced, gain_keys).astype(jnp.bfloat16)
    tok_cos, tok_sin = token_tables(0, NZ, HEAD)
    key_cos, key_sin = key_tables(0, RED, HEAD)
    queries = jnp.dot(normed, w_query, preferred_element_type=jnp.float32).reshape(TOKENS, HEADS, HEAD)
    queries = rotate(queries, tok_cos, tok_sin).astype(jnp.bfloat16)
    key_rows = jnp.dot(key_input, w_key, preferred_element_type=jnp.float32).reshape(RED, HEADS, HEAD)
    key_rows = rotate(key_rows, key_cos, key_sin).astype(jnp.bfloat16)
    value_rows = jnp.dot(key_input, w_value, preferred_element_type=jnp.float32).astype(jnp.bfloat16).reshape(RED, HEADS, HEAD)
    score_scale = HEAD ** (-0.5)

    def attend_rows(query_block):
        scores = jnp.einsum('qhd,khd->hqk', query_block.astype(jnp.float32), key_rows.astype(jnp.float32)) * score_scale
        row_max = lax.optimization_barrier(jnp.max(scores, axis=2, keepdims=True))
        expo = jnp.exp(scores - row_max)
        row_sum = lax.optimization_barrier(jnp.sum(expo, axis=2))
        weights = lax.optimization_barrier(expo.astype(jnp.bfloat16)).astype(jnp.float32)
        weighted = jnp.einsum('hqk,khd->hqd', weights, value_rows.astype(jnp.float32))
        result = weighted / row_sum[:, :, None]
        return result.transpose(1, 0, 2).reshape(query_block.shape[0], D).astype(jnp.bfloat16)
    heads_out = lax.map(attend_rows, queries.reshape(N_SLAB, TOK_DEV, HEADS, HEAD)).reshape(TOKENS, D)
    head_total = jnp.dot(heads_out, w_out, preferred_element_type=jnp.float32)
    attended = head_total.astype(jnp.bfloat16)
    residual = tokens.astype(jnp.float32) + head_total
    normed_ffn = layer_norm(residual, gain_ffn).astype(jnp.bfloat16)
    pre = jnp.dot(normed_ffn, w_up, preferred_element_type=jnp.float32).astype(jnp.bfloat16).reshape(NZ, GY, GX, FF)
    pre_pad = jnp.pad(pre, ((1, 1), (1, 1), (1, 1), (0, 0)))
    mixed = depth_conv(pre_pad, w_depth, NZ).reshape(TOKENS, FF)
    normal_cdf = 0.5 * (1.0 + lax.erf(mixed * ROOT_HALF))
    normal_pdf = jnp.exp(-0.5 * mixed * mixed) * NORMAL_SCALE
    activated = (mixed * normal_cdf).astype(jnp.bfloat16)
    grad_act = jnp.dot(grad_out, w_down.T, preferred_element_type=jnp.float32)
    grad_mixed = (grad_act * (normal_cdf + mixed * normal_pdf)).astype(jnp.bfloat16).reshape(NZ, GY, GX, FF)
    grad_pad = jnp.pad(grad_mixed, ((1, 1), (1, 1), (1, 1), (0, 0)))
    grad_pre = depth_conv(grad_pad, w_depth[::-1], NZ).astype(jnp.bfloat16).reshape(TOKENS, FF)
    grad_up = jnp.dot(normed_ffn.T, grad_pre, preferred_element_type=jnp.float32)
    grad_down = jnp.dot(grad_out.T, activated, preferred_element_type=jnp.float32)
    return (attended, grad_up, grad_down)
```

```python
import math

import jax
import jax.numpy as jnp
from jax import lax
from jax.sharding import Mesh
from jax.sharding import PartitionSpec as P

HEAD = 64
GX = 16
GY = 16
CZ = 2
SLAB = ("y", "z", "xl")
FFN = ("xh", "core")


EPSILON = 1e-05
ROPE_BASE = 100.0
ROOT_HALF = 0.7071067811865476
NORMAL_SCALE = 0.3989422804014327


def padded_2(cells, sides, width):
    for axis, dim in sides:
        count = lax.psum(1, axis)
        ends = count - 1
        head = lax.slice_in_dim(cells, 0, width, axis=dim)
        tail = lax.slice_in_dim(cells, cells.shape[dim] - width, cells.shape[dim], axis=dim)
        cells = jnp.concatenate(
            [
                lax.ppermute(tail, axis, [(i, (i + 1) % count) for i in range(ends)]),
                cells,
                lax.ppermute(head, axis, [((i + 1) % count, i) for i in range(ends)]),
            ],
            axis=dim,
        )
    return cells


def layer_norm(values, scale_gain):
    values = values.astype(jnp.float32)
    centered = values - jnp.mean(values, axis=-1, keepdims=True)
    variance = jnp.mean(centered * centered, axis=-1, keepdims=True)
    return centered * lax.rsqrt(variance + EPSILON) * scale_gain


def rope_tables(coord_x, coord_y, coord_z, head_size):
    pair_count = head_size // 2
    position = jnp.arange(pair_count, dtype=jnp.int32)
    axis_pick = position % 3
    per_axis = (pair_count + 2) // 3
    frequency = ROPE_BASE ** (-(position // 3).astype(jnp.float32) / per_axis)
    angles = (
        coord_x[:, None] * (axis_pick == 0)
        + coord_y[:, None] * (axis_pick == 1)
        + coord_z[:, None] * (axis_pick == 2)
    ) * frequency
    return (jnp.cos(angles)[:, None, :], jnp.sin(angles)[:, None, :])


def token_tables(first_plane, planes, head_size):
    position = jnp.arange(planes * GY * GX, dtype=jnp.int32)
    coord_x = (position % GX).astype(jnp.float32)
    coord_y = (position // GX % GY).astype(jnp.float32)
    coord_z = (first_plane + position // (GX * GY)).astype(jnp.float32)
    return rope_tables(coord_x, coord_y, coord_z, head_size)


def key_tables(first_row, row_count, head_size):
    position = first_row + jnp.arange(row_count, dtype=jnp.int32)
    half_x = GX // 2
    half_y = GY // 2
    coord_x = (position % half_x).astype(jnp.float32) * 2.0 + 0.5
    coord_y = (position // half_x % half_y).astype(jnp.float32) * 2.0 + 0.5
    coord_z = (position // (half_x * half_y)).astype(jnp.float32) * 2.0 + 0.5
    return rope_tables(coord_x, coord_y, coord_z, head_size)


def rotate(values, cosine, sine_table):
    half_size = values.shape[-1] // 2
    front_half = values[..., :half_size]
    back_half = values[..., half_size:]
    return jnp.concatenate(
        [
            front_half * cosine - back_half * sine_table,
            back_half * cosine + front_half * sine_table,
        ],
        axis=-1,
    )


def make_patches(normed, planes):
    width = normed.shape[-1]
    cell_grid = normed.reshape(planes // 2, 2, GY // 2, 2, GX // 2, 2, width)
    return cell_grid.transpose(0, 2, 4, 1, 3, 5, 6).reshape(-1, 8 * width)


def depth_conv(padded, weights, planes):
    height = padded.shape[1] - 2
    width_x = padded.shape[2] - 2
    result = jnp.zeros((planes, height, width_x, padded.shape[3]), jnp.float32)
    for offset in range(27):
        shift_z = offset // 9
        shift_y = offset // 3 % 3
        shift_x = offset % 3
        window = padded[
            shift_z : shift_z + planes, shift_y : shift_y + height, shift_x : shift_x + width_x
        ]
        result = result + window.astype(jnp.float32) * weights[offset]
    return result


def attend_piece(state_tuple, queries, key_rows, value_rows):
    row_max, row_sum, weighted = state_tuple
    score_scale = key_rows.shape[-1] ** (-0.5)
    scores = (
        jnp.einsum("qhd,khd->hqk", queries, key_rows, preferred_element_type=jnp.float32)
        * score_scale
    )
    new_max = jnp.maximum(row_max, jnp.max(scores, axis=2))
    rescale = jnp.exp(row_max - new_max)
    expo = jnp.exp(scores - new_max[:, :, None])
    row_sum = row_sum * rescale + jnp.sum(expo, axis=2)
    weighted = weighted * rescale[:, :, None] + jnp.einsum(
        "hqk,khd->hqd", expo.astype(jnp.bfloat16), value_rows, preferred_element_type=jnp.float32
    )
    return (new_max, row_sum, weighted)


def per_device(
    tokens,
    gain_attn,
    w_reduce,
    gain_keys,
    w_query,
    w_key,
    w_value,
    w_out,
    gain_ffn,
    w_up,
    w_depth,
    w_down,
    grad_out,
):
    slab_index = lax.axis_index(SLAB)
    tok_rows = tokens.shape[0]
    heads_dev = w_query.shape[1] // HEAD
    normed = layer_norm(tokens, gain_attn).astype(jnp.bfloat16)
    patches = make_patches(normed, CZ)
    reduced = jnp.dot(patches, w_reduce, preferred_element_type=jnp.float32)
    key_input = layer_norm(reduced, gain_keys).astype(jnp.bfloat16)
    tok_cos, tok_sin = token_tables(slab_index * CZ, CZ, HEAD)
    queries = jnp.dot(normed, w_query, preferred_element_type=jnp.float32).reshape(
        tok_rows, heads_dev, HEAD
    )
    queries = rotate(queries, tok_cos, tok_sin).astype(jnp.bfloat16)
    initial = (
        jnp.full((heads_dev, tok_rows), -1e30, jnp.float32),
        jnp.zeros((heads_dev, tok_rows), jnp.float32),
        jnp.zeros((heads_dev, tok_rows, HEAD), jnp.float32),
    )
    state_tuple = initial
    local_rows = key_input.shape[0]
    own_cos, own_sin = key_tables(slab_index * local_rows, local_rows, HEAD)
    own_keys = jnp.dot(key_input, w_key, preferred_element_type=jnp.float32).reshape(
        local_rows, heads_dev, HEAD
    )
    own_keys = rotate(own_keys, own_cos, own_sin).astype(jnp.bfloat16)
    own_values = jnp.dot(key_input, w_value, preferred_element_type=jnp.float32).astype(
        jnp.bfloat16
    )
    key_width = heads_dev * HEAD
    pieces = jnp.concatenate([own_keys.reshape(local_rows, key_width), own_values], axis=1)
    for axis in ("xl", "z", "y"):
        pieces = lax.all_gather(pieces, axis, axis=0, tiled=True)
    row_count = pieces.shape[0]
    block_rows = math.gcd(row_count, 1024)
    block_count = row_count // block_rows
    blocks = pieces.reshape(block_count, block_rows, pieces.shape[1])

    def one_block(state_inner, rows_in):
        key_block = rows_in[:, :key_width].reshape(block_rows, heads_dev, HEAD)
        value_block = rows_in[:, key_width:].reshape(block_rows, heads_dev, HEAD)
        return (attend_piece(state_inner, queries, key_block, value_block), None)

    state_tuple, _ = lax.scan(one_block, state_tuple, blocks)
    row_max, row_sum, weighted = state_tuple
    heads_out = (
        (weighted / row_sum[:, :, None])
        .transpose(1, 0, 2)
        .reshape(tok_rows, heads_dev * HEAD)
        .astype(jnp.bfloat16)
    )
    partial_value = jnp.dot(heads_out, w_out, preferred_element_type=jnp.float32)
    head_total = lax.psum(partial_value.astype(jnp.bfloat16), FFN).astype(jnp.float32)
    attended = head_total.astype(jnp.bfloat16)
    residual = tokens.astype(jnp.float32) + head_total
    normed_ffn = layer_norm(residual, gain_ffn).astype(jnp.bfloat16)
    channels = w_up.shape[1]
    pre = (
        jnp.dot(normed_ffn, w_up, preferred_element_type=jnp.float32)
        .astype(jnp.bfloat16)
        .reshape(CZ, GY, GX, channels)
    )
    pre_wide = padded_2(pre, ((SLAB, 0),), 1)
    pre_pad = jnp.pad(pre_wide, ((0, 0), (1, 1), (1, 1), (0, 0)))
    mixed = depth_conv(pre_pad, w_depth, CZ).reshape(tok_rows, channels)
    normal_cdf = 0.5 * (1.0 + lax.erf(mixed * ROOT_HALF))
    normal_pdf = jnp.exp(-0.5 * mixed * mixed) * NORMAL_SCALE
    activated = (mixed * normal_cdf).astype(jnp.bfloat16)
    grad_act = jnp.einsum("td,cd->tc", grad_out, w_down, preferred_element_type=jnp.float32)
    grad_mixed = (
        (grad_act * (normal_cdf + mixed * normal_pdf))
        .astype(jnp.bfloat16)
        .reshape(CZ, GY, GX, channels)
    )
    grad_wide = padded_2(grad_mixed, ((SLAB, 0),), 1)
    grad_pad = jnp.pad(grad_wide, ((0, 0), (1, 1), (1, 1), (0, 0)))
    grad_pre = (
        depth_conv(grad_pad, w_depth[::-1], CZ).astype(jnp.bfloat16).reshape(tok_rows, channels)
    )
    up_full = jnp.einsum("td,tc->dc", normed_ffn, grad_pre, preferred_element_type=jnp.float32)
    down_full = jnp.einsum("td,tc->dc", grad_out, activated, preferred_element_type=jnp.float32)
    grads = jnp.concatenate([up_full, down_full], axis=1)
    sizes = [lax.psum(1, axis) for axis in SLAB]
    grads = grads.reshape(sizes + [-1, grads.shape[1]])
    grads = grads.transpose(1, 0, 2, 3, 4).reshape(-1, grads.shape[-1])
    for axis in ("z", "y", "xl"):
        grads = lax.psum_scatter(grads, axis, scatter_dimension=0, tiled=True)
    return (attended, grads[:, :channels], grads[:, channels:])


def solution(mesh):
    mesh = Mesh(mesh.devices.reshape(4, 8, 2, 2, 2), SLAB + FFN)
    in_specs = (
        P(SLAB, None),
        P(),
        P(),
        P(),
        P(None, FFN),
        P(None, FFN),
        P(None, FFN),
        P(FFN, None),
        P(),
        P(None, FFN),
        P(None, FFN),
        P(FFN, None),
        P(SLAB, None),
    )
    out_specs = (P(SLAB, None), P(SLAB, FFN), P(SLAB, FFN))
    return jax.shard_map(
        per_device, mesh=mesh, in_specs=in_specs, out_specs=out_specs, check_vma=False
    )
```

```python
import functools
import math

import jax
import jax.numpy as jnp
from jax import lax
from jax.experimental import pallas as pl
from jax.experimental.pallas import tpu as pltpu
from jax.sharding import Mesh
from jax.sharding import PartitionSpec as P

HEAD = 64
GX = 16
GY = 16
CZ = 2
SLAB = ("y", "z", "xl")
FFN = ("xh", "core")


EPSILON = 1e-05
ROPE_BASE = 100.0
ROOT_HALF = 0.7071067811865476
NORMAL_SCALE = 0.3989422804014327


MESH = pl.DeviceIdType.MESH


def peer_id(p):
    return (p // 16, p // 2 % 8, p % 2, lax.axis_index("xh"), lax.axis_index("core"))


def greet_all(count, me):
    barrier = pltpu.get_barrier_semaphore()

    def body(k, carry):
        peer = lax.rem(me + k, count)
        pl.semaphore_signal(barrier, inc=1, device_id=peer_id(peer), device_id_type=MESH)
        return carry

    lax.fori_loop(1, count, body, 0)
    pl.semaphore_wait(barrier, count - 1)


def scatter_kernel(count, g_ref, out_ref, slots, send_sem, recv_sem):
    me = lax.axis_index(SLAB)
    rows = out_ref.shape[0]
    greet_all(count, me)

    def copy_to(peer, source):
        return pltpu.make_async_remote_copy(
            src_ref=g_ref.at[pl.ds(peer * rows, rows)],
            dst_ref=slots.at[source],
            send_sem=send_sem.at[peer],
            recv_sem=recv_sem.at[source],
            device_id=peer_id(peer),
            device_id_type=MESH,
        )

    def start(k, carry):
        copy_to(lax.rem(me + k, count), me).start()
        return carry

    lax.fori_loop(1, count, start, 0)
    out_ref[...] = g_ref[pl.ds(me * rows, rows)]

    def finish(k, carry):
        peer = lax.rem(me + k, count)
        copy_to(peer, me).wait_send()
        copy_to(peer, peer).wait_recv()
        out_ref[...] += slots[peer]
        return carry

    lax.fori_loop(1, count, finish, 0)


def slab_scatter(g, count):
    total_rows, width = g.shape
    rows = total_rows // count
    return pl.pallas_call(
        functools.partial(scatter_kernel, count),
        out_shape=jax.ShapeDtypeStruct((rows, width), g.dtype),
        in_specs=[pl.BlockSpec(memory_space=pltpu.VMEM)],
        out_specs=pl.BlockSpec(memory_space=pltpu.VMEM),
        scratch_shapes=[
            pltpu.VMEM((count, rows, width), g.dtype),
            pltpu.SemaphoreType.DMA((count,)),
            pltpu.SemaphoreType.DMA((count,)),
        ],
        compiler_params=pltpu.CompilerParams(collective_id=1, has_side_effects=True),
    )(g)


def padded_2(cells, sides, width):
    for axis, dim in sides:
        count = lax.psum(1, axis)
        ends = count - 1
        head = lax.slice_in_dim(cells, 0, width, axis=dim)
        tail = lax.slice_in_dim(cells, cells.shape[dim] - width, cells.shape[dim], axis=dim)
        cells = jnp.concatenate(
            [
                lax.ppermute(tail, axis, [(i, (i + 1) % count) for i in range(ends)]),
                cells,
                lax.ppermute(head, axis, [((i + 1) % count, i) for i in range(ends)]),
            ],
            axis=dim,
        )
    return cells


def layer_norm(values, scale_gain):
    values = values.astype(jnp.float32)
    centered = values - jnp.mean(values, axis=-1, keepdims=True)
    variance = jnp.mean(centered * centered, axis=-1, keepdims=True)
    return centered * lax.rsqrt(variance + EPSILON) * scale_gain


def rope_tables(coord_x, coord_y, coord_z, head_size):
    pair_count = head_size // 2
    position = jnp.arange(pair_count, dtype=jnp.int32)
    axis_pick = position % 3
    per_axis = (pair_count + 2) // 3
    frequency = ROPE_BASE ** (-(position // 3).astype(jnp.float32) / per_axis)
    angles = (
        coord_x[:, None] * (axis_pick == 0)
        + coord_y[:, None] * (axis_pick == 1)
        + coord_z[:, None] * (axis_pick == 2)
    ) * frequency
    return (jnp.cos(angles)[:, None, :], jnp.sin(angles)[:, None, :])


def token_tables(first_plane, planes, head_size):
    position = jnp.arange(planes * GY * GX, dtype=jnp.int32)
    coord_x = (position % GX).astype(jnp.float32)
    coord_y = (position // GX % GY).astype(jnp.float32)
    coord_z = (first_plane + position // (GX * GY)).astype(jnp.float32)
    return rope_tables(coord_x, coord_y, coord_z, head_size)


def key_tables(first_row, row_count, head_size):
    position = first_row + jnp.arange(row_count, dtype=jnp.int32)
    half_x = GX // 2
    half_y = GY // 2
    coord_x = (position % half_x).astype(jnp.float32) * 2.0 + 0.5
    coord_y = (position // half_x % half_y).astype(jnp.float32) * 2.0 + 0.5
    coord_z = (position // (half_x * half_y)).astype(jnp.float32) * 2.0 + 0.5
    return rope_tables(coord_x, coord_y, coord_z, head_size)


def rotate(values, cosine, sine_table):
    half_size = values.shape[-1] // 2
    front_half = values[..., :half_size]
    back_half = values[..., half_size:]
    return jnp.concatenate(
        [
            front_half * cosine - back_half * sine_table,
            back_half * cosine + front_half * sine_table,
        ],
        axis=-1,
    )


def make_patches(normed, planes):
    width = normed.shape[-1]
    cell_grid = normed.reshape(planes // 2, 2, GY // 2, 2, GX // 2, 2, width)
    return cell_grid.transpose(0, 2, 4, 1, 3, 5, 6).reshape(-1, 8 * width)


def depth_conv(padded, weights, planes):
    height = padded.shape[1] - 2
    width_x = padded.shape[2] - 2
    result = jnp.zeros((planes, height, width_x, padded.shape[3]), jnp.float32)
    for offset in range(27):
        shift_z = offset // 9
        shift_y = offset // 3 % 3
        shift_x = offset % 3
        window = padded[
            shift_z : shift_z + planes, shift_y : shift_y + height, shift_x : shift_x + width_x
        ]
        result = result + window.astype(jnp.float32) * weights[offset]
    return result


def attend_piece(state_tuple, queries, key_rows, value_rows):
    row_max, row_sum, weighted = state_tuple
    score_scale = key_rows.shape[-1] ** (-0.5)
    scores = (
        jnp.einsum("qhd,khd->hqk", queries, key_rows, preferred_element_type=jnp.float32)
        * score_scale
    )
    new_max = jnp.maximum(row_max, jnp.max(scores, axis=2))
    rescale = jnp.exp(row_max - new_max)
    expo = jnp.exp(scores - new_max[:, :, None])
    row_sum = row_sum * rescale + jnp.sum(expo, axis=2)
    weighted = weighted * rescale[:, :, None] + jnp.einsum(
        "hqk,khd->hqd", expo.astype(jnp.bfloat16), value_rows, preferred_element_type=jnp.float32
    )
    return (new_max, row_sum, weighted)


def per_device(
    tokens,
    gain_attn,
    w_reduce,
    gain_keys,
    w_query,
    w_key,
    w_value,
    w_out,
    gain_ffn,
    w_up,
    w_depth,
    w_down,
    grad_out,
):
    slab_index = lax.axis_index(SLAB)
    tok_rows = tokens.shape[0]
    heads_dev = w_query.shape[1] // HEAD
    normed = layer_norm(tokens, gain_attn).astype(jnp.bfloat16)
    patches = make_patches(normed, CZ)
    reduced = jnp.dot(patches, w_reduce, preferred_element_type=jnp.float32)
    key_input = layer_norm(reduced, gain_keys).astype(jnp.bfloat16)
    tok_cos, tok_sin = token_tables(slab_index * CZ, CZ, HEAD)
    queries = jnp.dot(normed, w_query, preferred_element_type=jnp.float32).reshape(
        tok_rows, heads_dev, HEAD
    )
    queries = rotate(queries, tok_cos, tok_sin).astype(jnp.bfloat16)
    initial = (
        jnp.full((heads_dev, tok_rows), -1e30, jnp.float32),
        jnp.zeros((heads_dev, tok_rows), jnp.float32),
        jnp.zeros((heads_dev, tok_rows, HEAD), jnp.float32),
    )
    state_tuple = initial
    local_rows = key_input.shape[0]
    own_cos, own_sin = key_tables(slab_index * local_rows, local_rows, HEAD)
    own_keys = jnp.dot(key_input, w_key, preferred_element_type=jnp.float32).reshape(
        local_rows, heads_dev, HEAD
    )
    own_keys = rotate(own_keys, own_cos, own_sin).astype(jnp.bfloat16)
    own_values = jnp.dot(key_input, w_value, preferred_element_type=jnp.float32).astype(
        jnp.bfloat16
    )
    key_width = heads_dev * HEAD
    pieces = jnp.concatenate([own_keys.reshape(local_rows, key_width), own_values], axis=1)
    for axis in ("xl", "z", "y"):
        pieces = lax.all_gather(pieces, axis, axis=0, tiled=True)
    row_count = pieces.shape[0]
    block_rows = math.gcd(row_count, 1024)
    block_count = row_count // block_rows
    blocks = pieces.reshape(block_count, block_rows, pieces.shape[1])

    def one_block(state_inner, rows_in):
        key_block = rows_in[:, :key_width].reshape(block_rows, heads_dev, HEAD)
        value_block = rows_in[:, key_width:].reshape(block_rows, heads_dev, HEAD)
        return (attend_piece(state_inner, queries, key_block, value_block), None)

    state_tuple, _ = lax.scan(one_block, state_tuple, blocks)
    row_max, row_sum, weighted = state_tuple
    heads_out = (
        (weighted / row_sum[:, :, None])
        .transpose(1, 0, 2)
        .reshape(tok_rows, heads_dev * HEAD)
        .astype(jnp.bfloat16)
    )
    partial_value = jnp.dot(heads_out, w_out, preferred_element_type=jnp.float32)
    head_total = lax.psum_scatter(
        partial_value.astype(jnp.bfloat16), FFN, scatter_dimension=0, tiled=True
    )
    head_total = lax.all_gather(head_total, FFN, axis=0, tiled=True).astype(jnp.float32)
    attended = head_total.astype(jnp.bfloat16)
    residual = tokens.astype(jnp.float32) + head_total
    normed_ffn = layer_norm(residual, gain_ffn).astype(jnp.bfloat16)
    channels = w_up.shape[1]
    pre = (
        jnp.dot(normed_ffn, w_up, preferred_element_type=jnp.float32)
        .astype(jnp.bfloat16)
        .reshape(CZ, GY, GX, channels)
    )
    pre_wide = padded_2(pre, ((SLAB, 0),), 1)
    pre_pad = jnp.pad(pre_wide, ((0, 0), (1, 1), (1, 1), (0, 0)))
    mixed = depth_conv(pre_pad, w_depth, CZ).reshape(tok_rows, channels)
    normal_cdf = 0.5 * (1.0 + lax.erf(mixed * ROOT_HALF))
    normal_pdf = jnp.exp(-0.5 * mixed * mixed) * NORMAL_SCALE
    activated = (mixed * normal_cdf).astype(jnp.bfloat16)
    grad_act = jnp.einsum("td,cd->tc", grad_out, w_down, preferred_element_type=jnp.float32)
    grad_mixed = (
        (grad_act * (normal_cdf + mixed * normal_pdf))
        .astype(jnp.bfloat16)
        .reshape(CZ, GY, GX, channels)
    )
    grad_wide = padded_2(grad_mixed, ((SLAB, 0),), 1)
    grad_pad = jnp.pad(grad_wide, ((0, 0), (1, 1), (1, 1), (0, 0)))
    grad_pre = (
        depth_conv(grad_pad, w_depth[::-1], CZ).astype(jnp.bfloat16).reshape(tok_rows, channels)
    )
    up_full = jnp.einsum("td,tc->dc", normed_ffn, grad_pre, preferred_element_type=jnp.float32)
    down_full = jnp.einsum("td,tc->dc", grad_out, activated, preferred_element_type=jnp.float32)
    grads = slab_scatter(jnp.concatenate([up_full, down_full], axis=1), lax.psum(1, SLAB))
    return (attended, grads[:, :channels], grads[:, channels:])


def solution(mesh):
    mesh = Mesh(mesh.devices.reshape(4, 8, 2, 2, 2), SLAB + FFN)
    in_specs = (
        P(SLAB, None),
        P(),
        P(),
        P(),
        P(None, FFN),
        P(None, FFN),
        P(None, FFN),
        P(FFN, None),
        P(),
        P(None, FFN),
        P(None, FFN),
        P(FFN, None),
        P(SLAB, None),
    )
    out_specs = (P(SLAB, None), P(SLAB, FFN), P(SLAB, FFN))
    return jax.shard_map(
        per_device, mesh=mesh, in_specs=in_specs, out_specs=out_specs, check_vma=False
    )
```

```python
import functools
import math

import jax
import jax.numpy as jnp
from jax import lax
from jax.experimental import pallas as pl
from jax.experimental.pallas import tpu as pltpu
from jax.sharding import Mesh
from jax.sharding import PartitionSpec as P

HEAD = 64
GX = 16
GY = 16
CZ = 2
SLAB = ("y", "z", "xl")
FFN = ("xh", "core")


EPSILON = 1e-05
ROPE_BASE = 100.0
ROOT_HALF = 0.7071067811865476
NORMAL_SCALE = 0.3989422804014327


MESH = pl.DeviceIdType.MESH


def peer_id(p):
    return (p // 16, p // 2 % 8, p % 2, lax.axis_index("xh"), lax.axis_index("core"))


def greet_all(count, me):
    barrier = pltpu.get_barrier_semaphore()

    def body(k, carry):
        peer = lax.rem(me + k, count)
        pl.semaphore_signal(barrier, inc=1, device_id=peer_id(peer), device_id_type=MESH)
        return carry

    lax.fori_loop(1, count, body, 0)
    pl.semaphore_wait(barrier, count - 1)


def scatter_kernel(count, g_ref, out_ref, slots, send_sem, recv_sem):
    me = lax.axis_index(SLAB)
    greet_all(count, me)

    def copy_to(peer, source):
        return pltpu.make_async_remote_copy(
            src_ref=g_ref.at[peer],
            dst_ref=slots.at[source],
            send_sem=send_sem.at[peer],
            recv_sem=recv_sem.at[source],
            device_id=peer_id(peer),
            device_id_type=MESH,
        )

    def start(k, carry):
        copy_to(lax.rem(me + k, count), me).start()
        return carry

    lax.fori_loop(1, count, start, 0)
    out_ref[...] = g_ref[me].astype(jnp.float32)

    def finish(k, carry):
        peer = lax.rem(me + k, count)
        copy_to(peer, me).wait_send()
        copy_to(peer, peer).wait_recv()
        out_ref[...] += slots[peer].astype(jnp.float32)
        return carry

    lax.fori_loop(1, count, finish, 0)


def slab_scatter(g, count):
    total_rows, width = g.shape
    rows = total_rows // count
    tile_rows = 16
    g = g.astype(jnp.bfloat16).reshape(count, tile_rows, rows * width // tile_rows)
    summed = pl.pallas_call(
        functools.partial(scatter_kernel, count),
        out_shape=jax.ShapeDtypeStruct(g.shape[1:], jnp.float32),
        in_specs=[pl.BlockSpec(memory_space=pltpu.VMEM)],
        out_specs=pl.BlockSpec(memory_space=pltpu.VMEM),
        scratch_shapes=[
            pltpu.VMEM(g.shape, g.dtype),
            pltpu.SemaphoreType.DMA((count,)),
            pltpu.SemaphoreType.DMA((count,)),
        ],
        compiler_params=pltpu.CompilerParams(collective_id=1, has_side_effects=True),
    )(g)
    return summed.reshape(rows, width)


def padded_2(cells, sides, width):
    for axis, dim in sides:
        count = lax.psum(1, axis)
        ends = count - 1
        head = lax.slice_in_dim(cells, 0, width, axis=dim)
        tail = lax.slice_in_dim(cells, cells.shape[dim] - width, cells.shape[dim], axis=dim)
        cells = jnp.concatenate(
            [
                lax.ppermute(tail, axis, [(i, (i + 1) % count) for i in range(ends)]),
                cells,
                lax.ppermute(head, axis, [((i + 1) % count, i) for i in range(ends)]),
            ],
            axis=dim,
        )
    return cells


def layer_norm(values, scale_gain):
    values = values.astype(jnp.float32)
    centered = values - jnp.mean(values, axis=-1, keepdims=True)
    variance = jnp.mean(centered * centered, axis=-1, keepdims=True)
    return centered * lax.rsqrt(variance + EPSILON) * scale_gain


def rope_tables(coord_x, coord_y, coord_z, head_size):
    pair_count = head_size // 2
    position = jnp.arange(pair_count, dtype=jnp.int32)
    axis_pick = position % 3
    per_axis = (pair_count + 2) // 3
    frequency = ROPE_BASE ** (-(position // 3).astype(jnp.float32) / per_axis)
    angles = (
        coord_x[:, None] * (axis_pick == 0)
        + coord_y[:, None] * (axis_pick == 1)
        + coord_z[:, None] * (axis_pick == 2)
    ) * frequency
    return (jnp.cos(angles)[:, None, :], jnp.sin(angles)[:, None, :])


def token_tables(first_plane, planes, head_size):
    position = jnp.arange(planes * GY * GX, dtype=jnp.int32)
    coord_x = (position % GX).astype(jnp.float32)
    coord_y = (position // GX % GY).astype(jnp.float32)
    coord_z = (first_plane + position // (GX * GY)).astype(jnp.float32)
    return rope_tables(coord_x, coord_y, coord_z, head_size)


def key_tables(first_row, row_count, head_size):
    position = first_row + jnp.arange(row_count, dtype=jnp.int32)
    half_x = GX // 2
    half_y = GY // 2
    coord_x = (position % half_x).astype(jnp.float32) * 2.0 + 0.5
    coord_y = (position // half_x % half_y).astype(jnp.float32) * 2.0 + 0.5
    coord_z = (position // (half_x * half_y)).astype(jnp.float32) * 2.0 + 0.5
    return rope_tables(coord_x, coord_y, coord_z, head_size)


def rotate(values, cosine, sine_table):
    half_size = values.shape[-1] // 2
    front_half = values[..., :half_size]
    back_half = values[..., half_size:]
    return jnp.concatenate(
        [
            front_half * cosine - back_half * sine_table,
            back_half * cosine + front_half * sine_table,
        ],
        axis=-1,
    )


def make_patches(normed, planes):
    width = normed.shape[-1]
    cell_grid = normed.reshape(planes // 2, 2, GY // 2, 2, GX // 2, 2, width)
    return cell_grid.transpose(0, 2, 4, 1, 3, 5, 6).reshape(-1, 8 * width)


def depth_conv(padded, weights, planes):
    height = padded.shape[1] - 2
    width_x = padded.shape[2] - 2
    result = jnp.zeros((planes, height, width_x, padded.shape[3]), jnp.float32)
    for offset in range(27):
        shift_z = offset // 9
        shift_y = offset // 3 % 3
        shift_x = offset % 3
        window = padded[
            shift_z : shift_z + planes, shift_y : shift_y + height, shift_x : shift_x + width_x
        ]
        result = result + window.astype(jnp.float32) * weights[offset]
    return result


def attend_piece(state_tuple, queries, key_rows, value_rows):
    row_max, row_sum, weighted = state_tuple
    score_scale = key_rows.shape[-1] ** (-0.5)
    scores = (
        jnp.einsum("qhd,khd->hqk", queries, key_rows, preferred_element_type=jnp.float32)
        * score_scale
    )
    new_max = jnp.maximum(row_max, jnp.max(scores, axis=2))
    rescale = jnp.exp(row_max - new_max)
    expo = jnp.exp(scores - new_max[:, :, None])
    row_sum = row_sum * rescale + jnp.sum(expo, axis=2)
    weighted = weighted * rescale[:, :, None] + jnp.einsum(
        "hqk,khd->hqd", expo.astype(jnp.bfloat16), value_rows, preferred_element_type=jnp.float32
    )
    return (new_max, row_sum, weighted)


def per_device(
    tokens,
    gain_attn,
    w_reduce,
    gain_keys,
    w_query,
    w_key,
    w_value,
    w_out,
    gain_ffn,
    w_up,
    w_depth,
    w_down,
    grad_out,
):
    slab_index = lax.axis_index(SLAB)
    tok_rows = tokens.shape[0]
    heads_dev = w_query.shape[1] // HEAD
    normed = layer_norm(tokens, gain_attn).astype(jnp.bfloat16)
    patches = make_patches(normed, CZ)
    reduced = jnp.dot(patches, w_reduce, preferred_element_type=jnp.float32)
    key_input = layer_norm(reduced, gain_keys).astype(jnp.bfloat16)
    tok_cos, tok_sin = token_tables(slab_index * CZ, CZ, HEAD)
    queries = jnp.dot(normed, w_query, preferred_element_type=jnp.float32).reshape(
        tok_rows, heads_dev, HEAD
    )
    queries = rotate(queries, tok_cos, tok_sin).astype(jnp.bfloat16)
    initial = (
        jnp.full((heads_dev, tok_rows), -1e30, jnp.float32),
        jnp.zeros((heads_dev, tok_rows), jnp.float32),
        jnp.zeros((heads_dev, tok_rows, HEAD), jnp.float32),
    )
    state_tuple = initial
    local_rows = key_input.shape[0]
    own_cos, own_sin = key_tables(slab_index * local_rows, local_rows, HEAD)
    own_keys = jnp.dot(key_input, w_key, preferred_element_type=jnp.float32).reshape(
        local_rows, heads_dev, HEAD
    )
    own_keys = rotate(own_keys, own_cos, own_sin).astype(jnp.bfloat16)
    own_values = jnp.dot(key_input, w_value, preferred_element_type=jnp.float32).astype(
        jnp.bfloat16
    )
    key_width = heads_dev * HEAD
    pieces = jnp.concatenate([own_keys.reshape(local_rows, key_width), own_values], axis=1)
    for axis in ("xl", "z", "y"):
        pieces = lax.all_gather(pieces, axis, axis=0, tiled=True)
    row_count = pieces.shape[0]
    block_rows = math.gcd(row_count, 1024)
    block_count = row_count // block_rows
    blocks = pieces.reshape(block_count, block_rows, pieces.shape[1])

    def one_block(state_inner, rows_in):
        key_block = rows_in[:, :key_width].reshape(block_rows, heads_dev, HEAD)
        value_block = rows_in[:, key_width:].reshape(block_rows, heads_dev, HEAD)
        return (attend_piece(state_inner, queries, key_block, value_block), None)

    state_tuple, _ = lax.scan(one_block, state_tuple, blocks)
    row_max, row_sum, weighted = state_tuple
    heads_out = (
        (weighted / row_sum[:, :, None])
        .transpose(1, 0, 2)
        .reshape(tok_rows, heads_dev * HEAD)
        .astype(jnp.bfloat16)
    )
    partial_value = jnp.dot(heads_out, w_out, preferred_element_type=jnp.float32)
    head_total = lax.psum_scatter(
        partial_value.astype(jnp.bfloat16), FFN, scatter_dimension=0, tiled=True
    )
    head_total = lax.all_gather(head_total, FFN, axis=0, tiled=True).astype(jnp.float32)
    attended = head_total.astype(jnp.bfloat16)
    residual = tokens.astype(jnp.float32) + head_total
    normed_ffn = layer_norm(residual, gain_ffn).astype(jnp.bfloat16)
    channels = w_up.shape[1]
    pre = (
        jnp.dot(normed_ffn, w_up, preferred_element_type=jnp.float32)
        .astype(jnp.bfloat16)
        .reshape(CZ, GY, GX, channels)
    )
    pre_wide = padded_2(pre, ((SLAB, 0),), 1)
    pre_pad = jnp.pad(pre_wide, ((0, 0), (1, 1), (1, 1), (0, 0)))
    mixed = depth_conv(pre_pad, w_depth, CZ).reshape(tok_rows, channels)
    normal_cdf = 0.5 * (1.0 + lax.erf(mixed * ROOT_HALF))
    normal_pdf = jnp.exp(-0.5 * mixed * mixed) * NORMAL_SCALE
    activated = (mixed * normal_cdf).astype(jnp.bfloat16)
    grad_act = jnp.einsum("td,cd->tc", grad_out, w_down, preferred_element_type=jnp.float32)
    grad_mixed = (
        (grad_act * (normal_cdf + mixed * normal_pdf))
        .astype(jnp.bfloat16)
        .reshape(CZ, GY, GX, channels)
    )
    grad_wide = padded_2(grad_mixed, ((SLAB, 0),), 1)
    grad_pad = jnp.pad(grad_wide, ((0, 0), (1, 1), (1, 1), (0, 0)))
    grad_pre = (
        depth_conv(grad_pad, w_depth[::-1], CZ).astype(jnp.bfloat16).reshape(tok_rows, channels)
    )
    up_full = jnp.einsum("td,tc->dc", normed_ffn, grad_pre, preferred_element_type=jnp.float32)
    down_full = jnp.einsum("td,tc->dc", grad_out, activated, preferred_element_type=jnp.float32)
    grads = slab_scatter(jnp.concatenate([up_full, down_full], axis=1), lax.psum(1, SLAB))
    return (attended, grads[:, :channels], grads[:, channels:])


def solution(mesh):
    mesh = Mesh(mesh.devices.reshape(4, 8, 2, 2, 2), SLAB + FFN)
    in_specs = (
        P(SLAB, None),
        P(),
        P(),
        P(),
        P(None, FFN),
        P(None, FFN),
        P(None, FFN),
        P(FFN, None),
        P(),
        P(None, FFN),
        P(None, FFN),
        P(FFN, None),
        P(SLAB, None),
    )
    out_specs = (P(SLAB, None), P(SLAB, FFN), P(SLAB, FFN))
    return jax.shard_map(
        per_device, mesh=mesh, in_specs=in_specs, out_specs=out_specs, check_vma=False
    )
```

```python
import functools
import math

import jax
import jax.numpy as jnp
from jax import lax
from jax.experimental import pallas as pl
from jax.experimental.pallas import tpu as pltpu
from jax.sharding import Mesh
from jax.sharding import PartitionSpec as P

HEAD = 64
GX = 16
GY = 16
CZ = 2
SLAB = ("y", "z", "xl")
FFN = ("xh", "core")


EPSILON = 1e-05
ROPE_BASE = 100.0
ROOT_HALF = 0.7071067811865476
NORMAL_SCALE = 0.3989422804014327


MESH = pl.DeviceIdType.MESH


def peer_id(p):
    return (p // 16, p // 2 % 8, p % 2, lax.axis_index("xh"), lax.axis_index("core"))


def greet_all(count, me):
    barrier = pltpu.get_barrier_semaphore()

    def body(k, carry):
        peer = lax.rem(me + k, count)
        pl.semaphore_signal(barrier, inc=1, device_id=peer_id(peer), device_id_type=MESH)
        return carry

    lax.fori_loop(1, count, body, 0)
    pl.semaphore_wait(barrier, count - 1)


def head_peer(q):
    return (lax.axis_index("y"), lax.axis_index("z"), lax.axis_index("xl"), q // 2, q % 2)


def head_sum_kernel(count, part_ref, out_ref, slots, send_sem, recv_sem, send_back, recv_back):
    me = lax.axis_index(FFN)
    barrier = pltpu.get_barrier_semaphore()
    for k in range(1, count):
        pl.semaphore_signal(
            barrier, inc=1, device_id=head_peer(lax.rem(me + k, count)), device_id_type=MESH
        )
    pl.semaphore_wait(barrier, count - 1)

    def share(peer, source):
        return pltpu.make_async_remote_copy(
            src_ref=part_ref.at[peer],
            dst_ref=slots.at[source],
            send_sem=send_sem.at[peer],
            recv_sem=recv_sem.at[source],
            device_id=head_peer(peer),
            device_id_type=MESH,
        )

    def spread(peer, source):
        return pltpu.make_async_remote_copy(
            src_ref=out_ref.at[source],
            dst_ref=out_ref.at[source],
            send_sem=send_back.at[peer],
            recv_sem=recv_back.at[source],
            device_id=head_peer(peer),
            device_id_type=MESH,
        )

    peers = [lax.rem(me + k, count) for k in range(1, count)]
    for peer in peers:
        share(peer, me).start()
    total = part_ref[me].astype(jnp.float32)
    for peer in peers:
        share(peer, me).wait_send()
        share(peer, peer).wait_recv()
        total = total + slots[peer].astype(jnp.float32)
    out_ref[me] = total.astype(out_ref.dtype)
    for peer in peers:
        spread(peer, me).start()
    for peer in peers:
        spread(peer, me).wait_send()
        spread(peer, peer).wait_recv()


def head_sum(partial_value, count):
    rows, width = partial_value.shape
    parts = partial_value.astype(jnp.bfloat16).reshape(count, rows // count, width)
    summed = pl.pallas_call(
        functools.partial(head_sum_kernel, count),
        out_shape=jax.ShapeDtypeStruct(parts.shape, parts.dtype),
        in_specs=[pl.BlockSpec(memory_space=pltpu.VMEM)],
        out_specs=pl.BlockSpec(memory_space=pltpu.VMEM),
        scratch_shapes=[
            pltpu.VMEM(parts.shape, parts.dtype),
            pltpu.SemaphoreType.DMA((count,)),
            pltpu.SemaphoreType.DMA((count,)),
            pltpu.SemaphoreType.DMA((count,)),
            pltpu.SemaphoreType.DMA((count,)),
        ],
        compiler_params=pltpu.CompilerParams(collective_id=2, has_side_effects=True),
    )(parts)
    return summed.reshape(rows, width)


def scatter_kernel(count, g_ref, out_ref, slots, send_sem, recv_sem):
    me = lax.axis_index(SLAB)
    greet_all(count, me)

    def copy_to(peer, source):
        return pltpu.make_async_remote_copy(
            src_ref=g_ref.at[peer],
            dst_ref=slots.at[source],
            send_sem=send_sem.at[peer],
            recv_sem=recv_sem.at[source],
            device_id=peer_id(peer),
            device_id_type=MESH,
        )

    def start(k, carry):
        copy_to(lax.rem(me + k, count), me).start()
        return carry

    lax.fori_loop(1, count, start, 0)
    out_ref[...] = g_ref[me].astype(jnp.float32)

    def finish(k, carry):
        peer = lax.rem(me + k, count)
        copy_to(peer, me).wait_send()
        copy_to(peer, peer).wait_recv()
        out_ref[...] += slots[peer].astype(jnp.float32)
        return carry

    lax.fori_loop(1, count, finish, 0)


def slab_scatter(g, count):
    total_rows, width = g.shape
    rows = total_rows // count
    tile_rows = 16
    g = g.astype(jnp.bfloat16).reshape(count, tile_rows, rows * width // tile_rows)
    summed = pl.pallas_call(
        functools.partial(scatter_kernel, count),
        out_shape=jax.ShapeDtypeStruct(g.shape[1:], jnp.float32),
        in_specs=[pl.BlockSpec(memory_space=pltpu.VMEM)],
        out_specs=pl.BlockSpec(memory_space=pltpu.VMEM),
        scratch_shapes=[
            pltpu.VMEM(g.shape, g.dtype),
            pltpu.SemaphoreType.DMA((count,)),
            pltpu.SemaphoreType.DMA((count,)),
        ],
        compiler_params=pltpu.CompilerParams(collective_id=1, has_side_effects=True),
    )(g)
    return summed.reshape(rows, width)


def padded_2(cells, sides, width):
    for axis, dim in sides:
        count = lax.psum(1, axis)
        ends = count - 1
        head = lax.slice_in_dim(cells, 0, width, axis=dim)
        tail = lax.slice_in_dim(cells, cells.shape[dim] - width, cells.shape[dim], axis=dim)
        cells = jnp.concatenate(
            [
                lax.ppermute(tail, axis, [(i, (i + 1) % count) for i in range(ends)]),
                cells,
                lax.ppermute(head, axis, [((i + 1) % count, i) for i in range(ends)]),
            ],
            axis=dim,
        )
    return cells


def layer_norm(values, scale_gain):
    values = values.astype(jnp.float32)
    centered = values - jnp.mean(values, axis=-1, keepdims=True)
    variance = jnp.mean(centered * centered, axis=-1, keepdims=True)
    return centered * lax.rsqrt(variance + EPSILON) * scale_gain


def rope_tables(coord_x, coord_y, coord_z, head_size):
    pair_count = head_size // 2
    position = jnp.arange(pair_count, dtype=jnp.int32)
    axis_pick = position % 3
    per_axis = (pair_count + 2) // 3
    frequency = ROPE_BASE ** (-(position // 3).astype(jnp.float32) / per_axis)
    angles = (
        coord_x[:, None] * (axis_pick == 0)
        + coord_y[:, None] * (axis_pick == 1)
        + coord_z[:, None] * (axis_pick == 2)
    ) * frequency
    return (jnp.cos(angles)[:, None, :], jnp.sin(angles)[:, None, :])


def token_tables(first_plane, planes, head_size):
    position = jnp.arange(planes * GY * GX, dtype=jnp.int32)
    coord_x = (position % GX).astype(jnp.float32)
    coord_y = (position // GX % GY).astype(jnp.float32)
    coord_z = (first_plane + position // (GX * GY)).astype(jnp.float32)
    return rope_tables(coord_x, coord_y, coord_z, head_size)


def key_tables(first_row, row_count, head_size):
    position = first_row + jnp.arange(row_count, dtype=jnp.int32)
    half_x = GX // 2
    half_y = GY // 2
    coord_x = (position % half_x).astype(jnp.float32) * 2.0 + 0.5
    coord_y = (position // half_x % half_y).astype(jnp.float32) * 2.0 + 0.5
    coord_z = (position // (half_x * half_y)).astype(jnp.float32) * 2.0 + 0.5
    return rope_tables(coord_x, coord_y, coord_z, head_size)


def rotate(values, cosine, sine_table):
    half_size = values.shape[-1] // 2
    front_half = values[..., :half_size]
    back_half = values[..., half_size:]
    return jnp.concatenate(
        [
            front_half * cosine - back_half * sine_table,
            back_half * cosine + front_half * sine_table,
        ],
        axis=-1,
    )


def make_patches(normed, planes):
    width = normed.shape[-1]
    cell_grid = normed.reshape(planes // 2, 2, GY // 2, 2, GX // 2, 2, width)
    return cell_grid.transpose(0, 2, 4, 1, 3, 5, 6).reshape(-1, 8 * width)


def depth_conv(padded, weights, planes):
    height = padded.shape[1] - 2
    width_x = padded.shape[2] - 2
    result = jnp.zeros((planes, height, width_x, padded.shape[3]), jnp.float32)
    for offset in range(27):
        shift_z = offset // 9
        shift_y = offset // 3 % 3
        shift_x = offset % 3
        window = padded[
            shift_z : shift_z + planes, shift_y : shift_y + height, shift_x : shift_x + width_x
        ]
        result = result + window.astype(jnp.float32) * weights[offset]
    return result


def attend_piece(state_tuple, queries, key_rows, value_rows):
    row_max, row_sum, weighted = state_tuple
    score_scale = key_rows.shape[-1] ** (-0.5)
    scores = (
        jnp.einsum("qhd,khd->hqk", queries, key_rows, preferred_element_type=jnp.float32)
        * score_scale
    )
    new_max = jnp.maximum(row_max, jnp.max(scores, axis=2))
    rescale = jnp.exp(row_max - new_max)
    expo = jnp.exp(scores - new_max[:, :, None])
    row_sum = row_sum * rescale + jnp.sum(expo, axis=2)
    weighted = weighted * rescale[:, :, None] + jnp.einsum(
        "hqk,khd->hqd", expo.astype(jnp.bfloat16), value_rows, preferred_element_type=jnp.float32
    )
    return (new_max, row_sum, weighted)


def per_device(
    tokens,
    gain_attn,
    w_reduce,
    gain_keys,
    w_query,
    w_key,
    w_value,
    w_out,
    gain_ffn,
    w_up,
    w_depth,
    w_down,
    grad_out,
):
    slab_index = lax.axis_index(SLAB)
    tok_rows = tokens.shape[0]
    heads_dev = w_query.shape[1] // HEAD
    normed = layer_norm(tokens, gain_attn).astype(jnp.bfloat16)
    patches = make_patches(normed, CZ)
    reduced = jnp.dot(patches, w_reduce, preferred_element_type=jnp.float32)
    key_input = layer_norm(reduced, gain_keys).astype(jnp.bfloat16)
    tok_cos, tok_sin = token_tables(slab_index * CZ, CZ, HEAD)
    queries = jnp.dot(normed, w_query, preferred_element_type=jnp.float32).reshape(
        tok_rows, heads_dev, HEAD
    )
    queries = rotate(queries, tok_cos, tok_sin).astype(jnp.bfloat16)
    initial = (
        jnp.full((heads_dev, tok_rows), -1e30, jnp.float32),
        jnp.zeros((heads_dev, tok_rows), jnp.float32),
        jnp.zeros((heads_dev, tok_rows, HEAD), jnp.float32),
    )
    state_tuple = initial
    local_rows = key_input.shape[0]
    own_cos, own_sin = key_tables(slab_index * local_rows, local_rows, HEAD)
    own_keys = jnp.dot(key_input, w_key, preferred_element_type=jnp.float32).reshape(
        local_rows, heads_dev, HEAD
    )
    own_keys = rotate(own_keys, own_cos, own_sin).astype(jnp.bfloat16)
    own_values = jnp.dot(key_input, w_value, preferred_element_type=jnp.float32).astype(
        jnp.bfloat16
    )
    key_width = heads_dev * HEAD
    pieces = jnp.concatenate([own_keys.reshape(local_rows, key_width), own_values], axis=1)
    for axis in ("xl", "z", "y"):
        pieces = lax.all_gather(pieces, axis, axis=0, tiled=True)
    row_count = pieces.shape[0]
    block_rows = math.gcd(row_count, 1024)
    block_count = row_count // block_rows
    blocks = pieces.reshape(block_count, block_rows, pieces.shape[1])

    def one_block(state_inner, rows_in):
        key_block = rows_in[:, :key_width].reshape(block_rows, heads_dev, HEAD)
        value_block = rows_in[:, key_width:].reshape(block_rows, heads_dev, HEAD)
        return (attend_piece(state_inner, queries, key_block, value_block), None)

    state_tuple, _ = lax.scan(one_block, state_tuple, blocks)
    row_max, row_sum, weighted = state_tuple
    heads_out = (
        (weighted / row_sum[:, :, None])
        .transpose(1, 0, 2)
        .reshape(tok_rows, heads_dev * HEAD)
        .astype(jnp.bfloat16)
    )
    partial_value = jnp.dot(heads_out, w_out, preferred_element_type=jnp.float32)
    head_total = head_sum(partial_value, lax.psum(1, FFN)).astype(jnp.float32)
    attended = head_total.astype(jnp.bfloat16)
    residual = tokens.astype(jnp.float32) + head_total
    normed_ffn = layer_norm(residual, gain_ffn).astype(jnp.bfloat16)
    channels = w_up.shape[1]
    pre = (
        jnp.dot(normed_ffn, w_up, preferred_element_type=jnp.float32)
        .astype(jnp.bfloat16)
        .reshape(CZ, GY, GX, channels)
    )
    pre_wide = padded_2(pre, ((SLAB, 0),), 1)
    pre_pad = jnp.pad(pre_wide, ((0, 0), (1, 1), (1, 1), (0, 0)))
    mixed = depth_conv(pre_pad, w_depth, CZ).reshape(tok_rows, channels)
    normal_cdf = 0.5 * (1.0 + lax.erf(mixed * ROOT_HALF))
    normal_pdf = jnp.exp(-0.5 * mixed * mixed) * NORMAL_SCALE
    activated = (mixed * normal_cdf).astype(jnp.bfloat16)
    grad_act = jnp.einsum("td,cd->tc", grad_out, w_down, preferred_element_type=jnp.float32)
    grad_mixed = (
        (grad_act * (normal_cdf + mixed * normal_pdf))
        .astype(jnp.bfloat16)
        .reshape(CZ, GY, GX, channels)
    )
    grad_wide = padded_2(grad_mixed, ((SLAB, 0),), 1)
    grad_pad = jnp.pad(grad_wide, ((0, 0), (1, 1), (1, 1), (0, 0)))
    grad_pre = (
        depth_conv(grad_pad, w_depth[::-1], CZ).astype(jnp.bfloat16).reshape(tok_rows, channels)
    )
    up_full = jnp.einsum("td,tc->dc", normed_ffn, grad_pre, preferred_element_type=jnp.float32)
    down_full = jnp.einsum("td,tc->dc", grad_out, activated, preferred_element_type=jnp.float32)
    grads = slab_scatter(jnp.concatenate([up_full, down_full], axis=1), lax.psum(1, SLAB))
    return (attended, grads[:, :channels], grads[:, channels:])


def solution(mesh):
    mesh = Mesh(mesh.devices.reshape(4, 8, 2, 2, 2), SLAB + FFN)
    in_specs = (
        P(SLAB, None),
        P(),
        P(),
        P(),
        P(None, FFN),
        P(None, FFN),
        P(None, FFN),
        P(FFN, None),
        P(),
        P(None, FFN),
        P(None, FFN),
        P(FFN, None),
        P(SLAB, None),
    )
    out_specs = (P(SLAB, None), P(SLAB, FFN), P(SLAB, FFN))
    return jax.shard_map(
        per_device, mesh=mesh, in_specs=in_specs, out_specs=out_specs, check_vma=False
    )
```

```python
import functools
import math

import jax
import jax.numpy as jnp
from jax import lax
from jax.experimental import pallas as pl
from jax.experimental.pallas import tpu as pltpu
from jax.sharding import Mesh
from jax.sharding import PartitionSpec as P

HEAD = 64
GX = 16
GY = 16
CZ = 2
SLAB = ("y", "z", "xl")
FFN = ("xh", "core")


EPSILON = 1e-05
ROPE_BASE = 100.0
ROOT_HALF = 0.7071067811865476
NORMAL_SCALE = 0.3989422804014327


MESH = pl.DeviceIdType.MESH


def peer_id(p):
    return (p // 16, p // 2 % 8, p % 2, lax.axis_index("xh"), lax.axis_index("core"))


def greet_all(count, me):
    barrier = pltpu.get_barrier_semaphore()

    def body(k, carry):
        peer = lax.rem(me + k, count)
        pl.semaphore_signal(barrier, inc=1, device_id=peer_id(peer), device_id_type=MESH)
        return carry

    lax.fori_loop(1, count, body, 0)
    pl.semaphore_wait(barrier, count - 1)


def gather_kernel(row_size, x_ref, out_ref, send_a, recv_a, send_b, recv_b, local_sem):
    me = lax.axis_index(SLAB)
    block = x_ref.shape[0]
    own_y, spot = me // row_size, me % row_size
    y_count = lax.psum(1, "y")
    barrier = pltpu.get_barrier_semaphore()

    def greet(k, carry):
        peer = own_y * row_size + lax.rem(spot + k, row_size)
        pl.semaphore_signal(barrier, inc=1, device_id=peer_id(peer), device_id_type=MESH)
        return carry

    lax.fori_loop(1, row_size, greet, 0)
    for j in range(1, y_count):
        peer = lax.rem(own_y + j, y_count) * row_size + spot
        pl.semaphore_signal(barrier, inc=1, device_id=peer_id(peer), device_id_type=MESH)
    pl.semaphore_wait(barrier, row_size + y_count - 2)

    def along_row(target, source):
        return pltpu.make_async_remote_copy(
            src_ref=x_ref,
            dst_ref=out_ref.at[pl.ds((own_y * row_size + source) * block, block)],
            send_sem=send_a.at[target],
            recv_sem=recv_a.at[source],
            device_id=peer_id(own_y * row_size + target),
            device_id_type=MESH,
        )

    def start_row(k, carry):
        along_row(lax.rem(spot + k, row_size), spot).start()
        return carry

    lax.fori_loop(1, row_size, start_row, 0)
    local = pltpu.make_async_copy(x_ref, out_ref.at[pl.ds(me * block, block)], local_sem)
    local.start()
    local.wait()

    def finish_row(k, carry):
        other = lax.rem(spot + k, row_size)
        along_row(other, spot).wait_send()
        along_row(other, other).wait_recv()
        return carry

    lax.fori_loop(1, row_size, finish_row, 0)
    row_rows = row_size * block

    def across(target_y, source_y):
        return pltpu.make_async_remote_copy(
            src_ref=out_ref.at[pl.ds(source_y * row_rows, row_rows)],
            dst_ref=out_ref.at[pl.ds(source_y * row_rows, row_rows)],
            send_sem=send_b.at[target_y],
            recv_sem=recv_b.at[source_y],
            device_id=peer_id(target_y * row_size + spot),
            device_id_type=MESH,
        )

    others = [lax.rem(own_y + j, y_count) for j in range(1, y_count)]
    for other in others:
        across(other, own_y).start()
    for other in others:
        across(other, own_y).wait_send()
        across(other, other).wait_recv()


def slab_gather(x, count, row_size):
    rows, width = x.shape
    y_count = count // row_size
    return pl.pallas_call(
        functools.partial(gather_kernel, row_size),
        out_shape=jax.ShapeDtypeStruct((count * rows, width), x.dtype),
        in_specs=[pl.BlockSpec(memory_space=pltpu.VMEM)],
        out_specs=pl.BlockSpec(memory_space=pltpu.VMEM),
        scratch_shapes=[
            pltpu.SemaphoreType.DMA((row_size,)),
            pltpu.SemaphoreType.DMA((row_size,)),
            pltpu.SemaphoreType.DMA((y_count,)),
            pltpu.SemaphoreType.DMA((y_count,)),
            pltpu.SemaphoreType.DMA(()),
        ],
        compiler_params=pltpu.CompilerParams(collective_id=0, has_side_effects=True),
    )(x)


def head_peer(q):
    return (lax.axis_index("y"), lax.axis_index("z"), lax.axis_index("xl"), q // 2, q % 2)


def head_sum_kernel(count, part_ref, out_ref, slots, send_sem, recv_sem, send_back, recv_back):
    me = lax.axis_index(FFN)
    barrier = pltpu.get_barrier_semaphore()
    for k in range(1, count):
        pl.semaphore_signal(
            barrier, inc=1, device_id=head_peer(lax.rem(me + k, count)), device_id_type=MESH
        )
    pl.semaphore_wait(barrier, count - 1)

    def share(peer, source):
        return pltpu.make_async_remote_copy(
            src_ref=part_ref.at[peer],
            dst_ref=slots.at[source],
            send_sem=send_sem.at[peer],
            recv_sem=recv_sem.at[source],
            device_id=head_peer(peer),
            device_id_type=MESH,
        )

    def spread(peer, source):
        return pltpu.make_async_remote_copy(
            src_ref=out_ref.at[source],
            dst_ref=out_ref.at[source],
            send_sem=send_back.at[peer],
            recv_sem=recv_back.at[source],
            device_id=head_peer(peer),
            device_id_type=MESH,
        )

    peers = [lax.rem(me + k, count) for k in range(1, count)]
    for peer in peers:
        share(peer, me).start()
    total = part_ref[me].astype(jnp.float32)
    for peer in peers:
        share(peer, me).wait_send()
        share(peer, peer).wait_recv()
        total = total + slots[peer].astype(jnp.float32)
    out_ref[me] = total.astype(out_ref.dtype)
    for peer in peers:
        spread(peer, me).start()
    for peer in peers:
        spread(peer, me).wait_send()
        spread(peer, peer).wait_recv()


def head_sum(partial_value, count):
    rows, width = partial_value.shape
    parts = partial_value.astype(jnp.bfloat16).reshape(count, rows // count, width)
    summed = pl.pallas_call(
        functools.partial(head_sum_kernel, count),
        out_shape=jax.ShapeDtypeStruct(parts.shape, parts.dtype),
        in_specs=[pl.BlockSpec(memory_space=pltpu.VMEM)],
        out_specs=pl.BlockSpec(memory_space=pltpu.VMEM),
        scratch_shapes=[
            pltpu.VMEM(parts.shape, parts.dtype),
            pltpu.SemaphoreType.DMA((count,)),
            pltpu.SemaphoreType.DMA((count,)),
            pltpu.SemaphoreType.DMA((count,)),
            pltpu.SemaphoreType.DMA((count,)),
        ],
        compiler_params=pltpu.CompilerParams(collective_id=2, has_side_effects=True),
    )(parts)
    return summed.reshape(rows, width)


def scatter_kernel(count, g_ref, out_ref, slots, send_sem, recv_sem):
    me = lax.axis_index(SLAB)
    greet_all(count, me)

    def copy_to(peer, source):
        return pltpu.make_async_remote_copy(
            src_ref=g_ref.at[peer],
            dst_ref=slots.at[source],
            send_sem=send_sem.at[peer],
            recv_sem=recv_sem.at[source],
            device_id=peer_id(peer),
            device_id_type=MESH,
        )

    def start(k, carry):
        copy_to(lax.rem(me + k, count), me).start()
        return carry

    lax.fori_loop(1, count, start, 0)
    out_ref[...] = g_ref[me].astype(jnp.float32)

    def finish(k, carry):
        peer = lax.rem(me + k, count)
        copy_to(peer, me).wait_send()
        copy_to(peer, peer).wait_recv()
        out_ref[...] += slots[peer].astype(jnp.float32)
        return carry

    lax.fori_loop(1, count, finish, 0)


def slab_scatter(g, count):
    total_rows, width = g.shape
    rows = total_rows // count
    tile_rows = 16
    g = g.astype(jnp.bfloat16).reshape(count, tile_rows, rows * width // tile_rows)
    summed = pl.pallas_call(
        functools.partial(scatter_kernel, count),
        out_shape=jax.ShapeDtypeStruct(g.shape[1:], jnp.float32),
        in_specs=[pl.BlockSpec(memory_space=pltpu.VMEM)],
        out_specs=pl.BlockSpec(memory_space=pltpu.VMEM),
        scratch_shapes=[
            pltpu.VMEM(g.shape, g.dtype),
            pltpu.SemaphoreType.DMA((count,)),
            pltpu.SemaphoreType.DMA((count,)),
        ],
        compiler_params=pltpu.CompilerParams(collective_id=1, has_side_effects=True),
    )(g)
    return summed.reshape(rows, width)


def padded_2(cells, sides, width):
    for axis, dim in sides:
        count = lax.psum(1, axis)
        ends = count - 1
        head = lax.slice_in_dim(cells, 0, width, axis=dim)
        tail = lax.slice_in_dim(cells, cells.shape[dim] - width, cells.shape[dim], axis=dim)
        cells = jnp.concatenate(
            [
                lax.ppermute(tail, axis, [(i, (i + 1) % count) for i in range(ends)]),
                cells,
                lax.ppermute(head, axis, [((i + 1) % count, i) for i in range(ends)]),
            ],
            axis=dim,
        )
    return cells


def layer_norm(values, scale_gain):
    values = values.astype(jnp.float32)
    centered = values - jnp.mean(values, axis=-1, keepdims=True)
    variance = jnp.mean(centered * centered, axis=-1, keepdims=True)
    return centered * lax.rsqrt(variance + EPSILON) * scale_gain


def rope_tables(coord_x, coord_y, coord_z, head_size):
    pair_count = head_size // 2
    position = jnp.arange(pair_count, dtype=jnp.int32)
    axis_pick = position % 3
    per_axis = (pair_count + 2) // 3
    frequency = ROPE_BASE ** (-(position // 3).astype(jnp.float32) / per_axis)
    angles = (
        coord_x[:, None] * (axis_pick == 0)
        + coord_y[:, None] * (axis_pick == 1)
        + coord_z[:, None] * (axis_pick == 2)
    ) * frequency
    return (jnp.cos(angles)[:, None, :], jnp.sin(angles)[:, None, :])


def token_tables(first_plane, planes, head_size):
    position = jnp.arange(planes * GY * GX, dtype=jnp.int32)
    coord_x = (position % GX).astype(jnp.float32)
    coord_y = (position // GX % GY).astype(jnp.float32)
    coord_z = (first_plane + position // (GX * GY)).astype(jnp.float32)
    return rope_tables(coord_x, coord_y, coord_z, head_size)


def key_tables(first_row, row_count, head_size):
    position = first_row + jnp.arange(row_count, dtype=jnp.int32)
    half_x = GX // 2
    half_y = GY // 2
    coord_x = (position % half_x).astype(jnp.float32) * 2.0 + 0.5
    coord_y = (position // half_x % half_y).astype(jnp.float32) * 2.0 + 0.5
    coord_z = (position // (half_x * half_y)).astype(jnp.float32) * 2.0 + 0.5
    return rope_tables(coord_x, coord_y, coord_z, head_size)


def rotate(values, cosine, sine_table):
    half_size = values.shape[-1] // 2
    front_half = values[..., :half_size]
    back_half = values[..., half_size:]
    return jnp.concatenate(
        [
            front_half * cosine - back_half * sine_table,
            back_half * cosine + front_half * sine_table,
        ],
        axis=-1,
    )


def make_patches(normed, planes):
    width = normed.shape[-1]
    cell_grid = normed.reshape(planes // 2, 2, GY // 2, 2, GX // 2, 2, width)
    return cell_grid.transpose(0, 2, 4, 1, 3, 5, 6).reshape(-1, 8 * width)


def depth_conv(padded, weights, planes):
    height = padded.shape[1] - 2
    width_x = padded.shape[2] - 2
    result = jnp.zeros((planes, height, width_x, padded.shape[3]), jnp.float32)
    for offset in range(27):
        shift_z = offset // 9
        shift_y = offset // 3 % 3
        shift_x = offset % 3
        window = padded[
            shift_z : shift_z + planes, shift_y : shift_y + height, shift_x : shift_x + width_x
        ]
        result = result + window.astype(jnp.float32) * weights[offset]
    return result


def attend_piece(state_tuple, queries, key_rows, value_rows):
    row_max, row_sum, weighted = state_tuple
    score_scale = key_rows.shape[-1] ** (-0.5)
    scores = (
        jnp.einsum("qhd,khd->hqk", queries, key_rows, preferred_element_type=jnp.float32)
        * score_scale
    )
    new_max = jnp.maximum(row_max, jnp.max(scores, axis=2))
    rescale = jnp.exp(row_max - new_max)
    expo = jnp.exp(scores - new_max[:, :, None])
    row_sum = row_sum * rescale + jnp.sum(expo, axis=2)
    weighted = weighted * rescale[:, :, None] + jnp.einsum(
        "hqk,khd->hqd", expo.astype(jnp.bfloat16), value_rows, preferred_element_type=jnp.float32
    )
    return (new_max, row_sum, weighted)


def per_device(
    tokens,
    gain_attn,
    w_reduce,
    gain_keys,
    w_query,
    w_key,
    w_value,
    w_out,
    gain_ffn,
    w_up,
    w_depth,
    w_down,
    grad_out,
):
    slab_index = lax.axis_index(SLAB)
    tok_rows = tokens.shape[0]
    heads_dev = w_query.shape[1] // HEAD
    normed = layer_norm(tokens, gain_attn).astype(jnp.bfloat16)
    patches = make_patches(normed, CZ)
    reduced = jnp.dot(patches, w_reduce, preferred_element_type=jnp.float32)
    key_input = layer_norm(reduced, gain_keys).astype(jnp.bfloat16)
    tok_cos, tok_sin = token_tables(slab_index * CZ, CZ, HEAD)
    queries = jnp.dot(normed, w_query, preferred_element_type=jnp.float32).reshape(
        tok_rows, heads_dev, HEAD
    )
    queries = rotate(queries, tok_cos, tok_sin).astype(jnp.bfloat16)
    initial = (
        jnp.full((heads_dev, tok_rows), -1e30, jnp.float32),
        jnp.zeros((heads_dev, tok_rows), jnp.float32),
        jnp.zeros((heads_dev, tok_rows, HEAD), jnp.float32),
    )
    state_tuple = initial
    local_rows = key_input.shape[0]
    own_cos, own_sin = key_tables(slab_index * local_rows, local_rows, HEAD)
    own_keys = jnp.dot(key_input, w_key, preferred_element_type=jnp.float32).reshape(
        local_rows, heads_dev, HEAD
    )
    own_keys = rotate(own_keys, own_cos, own_sin).astype(jnp.bfloat16)
    own_values = jnp.dot(key_input, w_value, preferred_element_type=jnp.float32).astype(
        jnp.bfloat16
    )
    key_width = heads_dev * HEAD
    pieces = jnp.concatenate([own_keys.reshape(local_rows, key_width), own_values], axis=1)
    pieces = slab_gather(pieces, lax.psum(1, SLAB), lax.psum(1, ("z", "xl")))
    row_count = pieces.shape[0]
    block_rows = math.gcd(row_count, 1024)
    block_count = row_count // block_rows
    blocks = pieces.reshape(block_count, block_rows, pieces.shape[1])

    def one_block(state_inner, rows_in):
        key_block = rows_in[:, :key_width].reshape(block_rows, heads_dev, HEAD)
        value_block = rows_in[:, key_width:].reshape(block_rows, heads_dev, HEAD)
        return (attend_piece(state_inner, queries, key_block, value_block), None)

    state_tuple, _ = lax.scan(one_block, state_tuple, blocks)
    row_max, row_sum, weighted = state_tuple
    heads_out = (
        (weighted / row_sum[:, :, None])
        .transpose(1, 0, 2)
        .reshape(tok_rows, heads_dev * HEAD)
        .astype(jnp.bfloat16)
    )
    partial_value = jnp.dot(heads_out, w_out, preferred_element_type=jnp.float32)
    head_total = head_sum(partial_value, lax.psum(1, FFN)).astype(jnp.float32)
    attended = head_total.astype(jnp.bfloat16)
    residual = tokens.astype(jnp.float32) + head_total
    normed_ffn = layer_norm(residual, gain_ffn).astype(jnp.bfloat16)
    channels = w_up.shape[1]
    pre = (
        jnp.dot(normed_ffn, w_up, preferred_element_type=jnp.float32)
        .astype(jnp.bfloat16)
        .reshape(CZ, GY, GX, channels)
    )
    pre_wide = padded_2(pre, ((SLAB, 0),), 1)
    pre_pad = jnp.pad(pre_wide, ((0, 0), (1, 1), (1, 1), (0, 0)))
    mixed = depth_conv(pre_pad, w_depth, CZ).reshape(tok_rows, channels)
    normal_cdf = 0.5 * (1.0 + lax.erf(mixed * ROOT_HALF))
    normal_pdf = jnp.exp(-0.5 * mixed * mixed) * NORMAL_SCALE
    activated = (mixed * normal_cdf).astype(jnp.bfloat16)
    grad_act = jnp.einsum("td,cd->tc", grad_out, w_down, preferred_element_type=jnp.float32)
    grad_mixed = (
        (grad_act * (normal_cdf + mixed * normal_pdf))
        .astype(jnp.bfloat16)
        .reshape(CZ, GY, GX, channels)
    )
    grad_wide = padded_2(grad_mixed, ((SLAB, 0),), 1)
    grad_pad = jnp.pad(grad_wide, ((0, 0), (1, 1), (1, 1), (0, 0)))
    grad_pre = (
        depth_conv(grad_pad, w_depth[::-1], CZ).astype(jnp.bfloat16).reshape(tok_rows, channels)
    )
    up_full = jnp.einsum("td,tc->dc", normed_ffn, grad_pre, preferred_element_type=jnp.float32)
    down_full = jnp.einsum("td,tc->dc", grad_out, activated, preferred_element_type=jnp.float32)
    grads = slab_scatter(jnp.concatenate([up_full, down_full], axis=1), lax.psum(1, SLAB))
    return (attended, grads[:, :channels], grads[:, channels:])


def solution(mesh):
    mesh = Mesh(mesh.devices.reshape(4, 8, 2, 2, 2), SLAB + FFN)
    in_specs = (
        P(SLAB, None),
        P(),
        P(),
        P(),
        P(None, FFN),
        P(None, FFN),
        P(None, FFN),
        P(FFN, None),
        P(),
        P(None, FFN),
        P(None, FFN),
        P(FFN, None),
        P(SLAB, None),
    )
    out_specs = (P(SLAB, None), P(SLAB, FFN), P(SLAB, FFN))
    return jax.shard_map(
        per_device, mesh=mesh, in_specs=in_specs, out_specs=out_specs, check_vma=False
    )
```

```python
import functools
import math

import jax
import jax.numpy as jnp
from jax import lax
from jax.experimental import pallas as pl
from jax.experimental.pallas import tpu as pltpu
from jax.sharding import Mesh
from jax.sharding import PartitionSpec as P

HEAD = 64
GX = 16
GY = 16
CZ = 2
SLAB = ("y", "z", "xl")
FFN = ("xh", "core")


EPSILON = 1e-05
ROPE_BASE = 100.0
ROOT_HALF = 0.7071067811865476
NORMAL_SCALE = 0.3989422804014327


MESH = pl.DeviceIdType.MESH


def peer_id(p):
    return (p // 16, p // 2 % 8, p % 2, lax.axis_index("xh"), lax.axis_index("core"))


def greet_all(count, me):
    barrier = pltpu.get_barrier_semaphore()

    def body(k, carry):
        peer = lax.rem(me + k, count)
        pl.semaphore_signal(barrier, inc=1, device_id=peer_id(peer), device_id_type=MESH)
        return carry

    lax.fori_loop(1, count, body, 0)
    pl.semaphore_wait(barrier, count - 1)


def gather_kernel(
    row_size, x_ref, out_ref, send_a, recv_a, send_b, recv_b, send_c, recv_c, local_sem
):
    me = lax.axis_index(SLAB)
    block = x_ref.shape[0]
    own_y, spot = me // row_size, me % row_size
    y_count = lax.psum(1, "y")
    barrier = pltpu.get_barrier_semaphore()

    def greet(k, carry):
        peer = own_y * row_size + lax.rem(spot + k, row_size)
        pl.semaphore_signal(barrier, inc=1, device_id=peer_id(peer), device_id_type=MESH)
        return carry

    lax.fori_loop(1, row_size, greet, 0)
    left_y = lax.rem(own_y + y_count - 1, y_count)
    right_y = lax.rem(own_y + 1, y_count)
    for other_y in (left_y, right_y):
        peer = other_y * row_size + spot
        pl.semaphore_signal(barrier, inc=1, device_id=peer_id(peer), device_id_type=MESH)
    pl.semaphore_wait(barrier, row_size + 1)

    def along_row(target, source):
        return pltpu.make_async_remote_copy(
            src_ref=x_ref,
            dst_ref=out_ref.at[pl.ds((own_y * row_size + source) * block, block)],
            send_sem=send_a.at[target],
            recv_sem=recv_a.at[source],
            device_id=peer_id(own_y * row_size + target),
            device_id_type=MESH,
        )

    def start_row(k, carry):
        along_row(lax.rem(spot + k, row_size), spot).start()
        return carry

    lax.fori_loop(1, row_size, start_row, 0)
    local = pltpu.make_async_copy(x_ref, out_ref.at[pl.ds(me * block, block)], local_sem)
    local.start()
    local.wait()

    def finish_row(k, carry):
        other = lax.rem(spot + k, row_size)
        along_row(other, spot).wait_send()
        along_row(other, other).wait_recv()
        return carry

    lax.fori_loop(1, row_size, finish_row, 0)
    row_rows = row_size * block

    def across(target_y, source_y):
        return pltpu.make_async_remote_copy(
            src_ref=out_ref.at[pl.ds(source_y * row_rows, row_rows)],
            dst_ref=out_ref.at[pl.ds(source_y * row_rows, row_rows)],
            send_sem=send_b.at[target_y],
            recv_sem=recv_b.at[source_y],
            device_id=peer_id(target_y * row_size + spot),
            device_id_type=MESH,
        )

    for other_y in (left_y, right_y):
        across(other_y, own_y).start()
    for other_y in (left_y, right_y):
        across(other_y, own_y).wait_send()
        across(other_y, other_y).wait_recv()
    half = row_rows // 2

    def forward(target_y, source_y, part):
        rows = pl.ds(source_y * row_rows + part * half, half)
        return pltpu.make_async_remote_copy(
            src_ref=out_ref.at[rows],
            dst_ref=out_ref.at[rows],
            send_sem=send_c.at[part],
            recv_sem=recv_c.at[part],
            device_id=peer_id(target_y * row_size + spot),
            device_id_type=MESH,
        )

    far_y = lax.rem(own_y + 2, y_count)
    forward(right_y, left_y, 0).start()
    forward(left_y, right_y, 1).start()
    forward(right_y, left_y, 0).wait_send()
    forward(left_y, right_y, 1).wait_send()
    forward(right_y, far_y, 0).wait_recv()
    forward(left_y, far_y, 1).wait_recv()


def slab_gather(x, count, row_size):
    rows, width = x.shape
    y_count = count // row_size
    assert y_count == 4
    return pl.pallas_call(
        functools.partial(gather_kernel, row_size),
        out_shape=jax.ShapeDtypeStruct((count * rows, width), x.dtype),
        in_specs=[pl.BlockSpec(memory_space=pltpu.VMEM)],
        out_specs=pl.BlockSpec(memory_space=pltpu.VMEM),
        scratch_shapes=[
            pltpu.SemaphoreType.DMA((row_size,)),
            pltpu.SemaphoreType.DMA((row_size,)),
            pltpu.SemaphoreType.DMA((y_count,)),
            pltpu.SemaphoreType.DMA((y_count,)),
            pltpu.SemaphoreType.DMA((2,)),
            pltpu.SemaphoreType.DMA((2,)),
            pltpu.SemaphoreType.DMA(()),
        ],
        compiler_params=pltpu.CompilerParams(collective_id=0, has_side_effects=True),
    )(x)


def head_peer(q):
    return (lax.axis_index("y"), lax.axis_index("z"), lax.axis_index("xl"), q // 2, q % 2)


def head_sum_kernel(count, part_ref, out_ref, slots, send_sem, recv_sem, send_back, recv_back):
    me = lax.axis_index(FFN)
    barrier = pltpu.get_barrier_semaphore()
    for k in range(1, count):
        pl.semaphore_signal(
            barrier, inc=1, device_id=head_peer(lax.rem(me + k, count)), device_id_type=MESH
        )
    pl.semaphore_wait(barrier, count - 1)

    def share(peer, source):
        return pltpu.make_async_remote_copy(
            src_ref=part_ref.at[peer],
            dst_ref=slots.at[source],
            send_sem=send_sem.at[peer],
            recv_sem=recv_sem.at[source],
            device_id=head_peer(peer),
            device_id_type=MESH,
        )

    def spread(peer, source):
        return pltpu.make_async_remote_copy(
            src_ref=out_ref.at[source],
            dst_ref=out_ref.at[source],
            send_sem=send_back.at[peer],
            recv_sem=recv_back.at[source],
            device_id=head_peer(peer),
            device_id_type=MESH,
        )

    peers = [lax.rem(me + k, count) for k in range(1, count)]
    for peer in peers:
        share(peer, me).start()
    total = part_ref[me].astype(jnp.float32)
    for peer in peers:
        share(peer, me).wait_send()
        share(peer, peer).wait_recv()
        total = total + slots[peer].astype(jnp.float32)
    out_ref[me] = total.astype(out_ref.dtype)
    for peer in peers:
        spread(peer, me).start()
    for peer in peers:
        spread(peer, me).wait_send()
        spread(peer, peer).wait_recv()


def head_sum(partial_value, count):
    rows, width = partial_value.shape
    parts = partial_value.astype(jnp.bfloat16).reshape(count, rows // count, width)
    summed = pl.pallas_call(
        functools.partial(head_sum_kernel, count),
        out_shape=jax.ShapeDtypeStruct(parts.shape, parts.dtype),
        in_specs=[pl.BlockSpec(memory_space=pltpu.VMEM)],
        out_specs=pl.BlockSpec(memory_space=pltpu.VMEM),
        scratch_shapes=[
            pltpu.VMEM(parts.shape, parts.dtype),
            pltpu.SemaphoreType.DMA((count,)),
            pltpu.SemaphoreType.DMA((count,)),
            pltpu.SemaphoreType.DMA((count,)),
            pltpu.SemaphoreType.DMA((count,)),
        ],
        compiler_params=pltpu.CompilerParams(collective_id=2, has_side_effects=True),
    )(parts)
    return summed.reshape(rows, width)


def scatter_kernel(count, g_ref, out_ref, slots, send_sem, recv_sem):
    me = lax.axis_index(SLAB)
    greet_all(count, me)

    def copy_to(peer, source):
        return pltpu.make_async_remote_copy(
            src_ref=g_ref.at[peer],
            dst_ref=slots.at[source],
            send_sem=send_sem.at[peer],
            recv_sem=recv_sem.at[source],
            device_id=peer_id(peer),
            device_id_type=MESH,
        )

    def start(k, carry):
        copy_to(lax.rem(me + k, count), me).start()
        return carry

    lax.fori_loop(1, count, start, 0)
    out_ref[...] = g_ref[me].astype(jnp.float32)

    def finish(k, carry):
        peer = lax.rem(me + k, count)
        copy_to(peer, me).wait_send()
        copy_to(peer, peer).wait_recv()
        out_ref[...] += slots[peer].astype(jnp.float32)
        return carry

    lax.fori_loop(1, count, finish, 0)


def slab_scatter(g, count):
    total_rows, width = g.shape
    rows = total_rows // count
    tile_rows = 16
    g = g.astype(jnp.bfloat16).reshape(count, tile_rows, rows * width // tile_rows)
    summed = pl.pallas_call(
        functools.partial(scatter_kernel, count),
        out_shape=jax.ShapeDtypeStruct(g.shape[1:], jnp.float32),
        in_specs=[pl.BlockSpec(memory_space=pltpu.VMEM)],
        out_specs=pl.BlockSpec(memory_space=pltpu.VMEM),
        scratch_shapes=[
            pltpu.VMEM(g.shape, g.dtype),
            pltpu.SemaphoreType.DMA((count,)),
            pltpu.SemaphoreType.DMA((count,)),
        ],
        compiler_params=pltpu.CompilerParams(collective_id=1, has_side_effects=True),
    )(g)
    return summed.reshape(rows, width)


def padded_2(cells, sides, width):
    for axis, dim in sides:
        count = lax.psum(1, axis)
        ends = count - 1
        head = lax.slice_in_dim(cells, 0, width, axis=dim)
        tail = lax.slice_in_dim(cells, cells.shape[dim] - width, cells.shape[dim], axis=dim)
        cells = jnp.concatenate(
            [
                lax.ppermute(tail, axis, [(i, (i + 1) % count) for i in range(ends)]),
                cells,
                lax.ppermute(head, axis, [((i + 1) % count, i) for i in range(ends)]),
            ],
            axis=dim,
        )
    return cells


def layer_norm(values, scale_gain):
    values = values.astype(jnp.float32)
    centered = values - jnp.mean(values, axis=-1, keepdims=True)
    variance = jnp.mean(centered * centered, axis=-1, keepdims=True)
    return centered * lax.rsqrt(variance + EPSILON) * scale_gain


def rope_tables(coord_x, coord_y, coord_z, head_size):
    pair_count = head_size // 2
    position = jnp.arange(pair_count, dtype=jnp.int32)
    axis_pick = position % 3
    per_axis = (pair_count + 2) // 3
    frequency = ROPE_BASE ** (-(position // 3).astype(jnp.float32) / per_axis)
    angles = (
        coord_x[:, None] * (axis_pick == 0)
        + coord_y[:, None] * (axis_pick == 1)
        + coord_z[:, None] * (axis_pick == 2)
    ) * frequency
    return (jnp.cos(angles)[:, None, :], jnp.sin(angles)[:, None, :])


def token_tables(first_plane, planes, head_size):
    position = jnp.arange(planes * GY * GX, dtype=jnp.int32)
    coord_x = (position % GX).astype(jnp.float32)
    coord_y = (position // GX % GY).astype(jnp.float32)
    coord_z = (first_plane + position // (GX * GY)).astype(jnp.float32)
    return rope_tables(coord_x, coord_y, coord_z, head_size)


def key_tables(first_row, row_count, head_size):
    position = first_row + jnp.arange(row_count, dtype=jnp.int32)
    half_x = GX // 2
    half_y = GY // 2
    coord_x = (position % half_x).astype(jnp.float32) * 2.0 + 0.5
    coord_y = (position // half_x % half_y).astype(jnp.float32) * 2.0 + 0.5
    coord_z = (position // (half_x * half_y)).astype(jnp.float32) * 2.0 + 0.5
    return rope_tables(coord_x, coord_y, coord_z, head_size)


def rotate(values, cosine, sine_table):
    half_size = values.shape[-1] // 2
    front_half = values[..., :half_size]
    back_half = values[..., half_size:]
    return jnp.concatenate(
        [
            front_half * cosine - back_half * sine_table,
            back_half * cosine + front_half * sine_table,
        ],
        axis=-1,
    )


def make_patches(normed, planes):
    width = normed.shape[-1]
    cell_grid = normed.reshape(planes // 2, 2, GY // 2, 2, GX // 2, 2, width)
    return cell_grid.transpose(0, 2, 4, 1, 3, 5, 6).reshape(-1, 8 * width)


def depth_conv(padded, weights, planes):
    height = padded.shape[1] - 2
    width_x = padded.shape[2] - 2
    result = jnp.zeros((planes, height, width_x, padded.shape[3]), jnp.float32)
    for offset in range(27):
        shift_z = offset // 9
        shift_y = offset // 3 % 3
        shift_x = offset % 3
        window = padded[
            shift_z : shift_z + planes, shift_y : shift_y + height, shift_x : shift_x + width_x
        ]
        result = result + window.astype(jnp.float32) * weights[offset]
    return result


def attend_piece(state_tuple, queries, key_rows, value_rows):
    row_max, row_sum, weighted = state_tuple
    score_scale = key_rows.shape[-1] ** (-0.5)
    scores = (
        jnp.einsum("qhd,khd->hqk", queries, key_rows, preferred_element_type=jnp.float32)
        * score_scale
    )
    new_max = jnp.maximum(row_max, jnp.max(scores, axis=2))
    rescale = jnp.exp(row_max - new_max)
    expo = jnp.exp(scores - new_max[:, :, None])
    row_sum = row_sum * rescale + jnp.sum(expo, axis=2)
    weighted = weighted * rescale[:, :, None] + jnp.einsum(
        "hqk,khd->hqd", expo.astype(jnp.bfloat16), value_rows, preferred_element_type=jnp.float32
    )
    return (new_max, row_sum, weighted)


def per_device(
    tokens,
    gain_attn,
    w_reduce,
    gain_keys,
    w_query,
    w_key,
    w_value,
    w_out,
    gain_ffn,
    w_up,
    w_depth,
    w_down,
    grad_out,
):
    slab_index = lax.axis_index(SLAB)
    tok_rows = tokens.shape[0]
    heads_dev = w_query.shape[1] // HEAD
    normed = layer_norm(tokens, gain_attn).astype(jnp.bfloat16)
    patches = make_patches(normed, CZ)
    reduced = jnp.dot(patches, w_reduce, preferred_element_type=jnp.float32)
    key_input = layer_norm(reduced, gain_keys).astype(jnp.bfloat16)
    tok_cos, tok_sin = token_tables(slab_index * CZ, CZ, HEAD)
    queries = jnp.dot(normed, w_query, preferred_element_type=jnp.float32).reshape(
        tok_rows, heads_dev, HEAD
    )
    queries = rotate(queries, tok_cos, tok_sin).astype(jnp.bfloat16)
    initial = (
        jnp.full((heads_dev, tok_rows), -1e30, jnp.float32),
        jnp.zeros((heads_dev, tok_rows), jnp.float32),
        jnp.zeros((heads_dev, tok_rows, HEAD), jnp.float32),
    )
    state_tuple = initial
    local_rows = key_input.shape[0]
    own_cos, own_sin = key_tables(slab_index * local_rows, local_rows, HEAD)
    own_keys = jnp.dot(key_input, w_key, preferred_element_type=jnp.float32).reshape(
        local_rows, heads_dev, HEAD
    )
    own_keys = rotate(own_keys, own_cos, own_sin).astype(jnp.bfloat16)
    own_values = jnp.dot(key_input, w_value, preferred_element_type=jnp.float32).astype(
        jnp.bfloat16
    )
    key_width = heads_dev * HEAD
    pieces = jnp.concatenate([own_keys.reshape(local_rows, key_width), own_values], axis=1)
    pieces = slab_gather(pieces, lax.psum(1, SLAB), lax.psum(1, ("z", "xl")))
    row_count = pieces.shape[0]
    block_rows = math.gcd(row_count, 1024)
    block_count = row_count // block_rows
    blocks = pieces.reshape(block_count, block_rows, pieces.shape[1])

    def one_block(state_inner, rows_in):
        key_block = rows_in[:, :key_width].reshape(block_rows, heads_dev, HEAD)
        value_block = rows_in[:, key_width:].reshape(block_rows, heads_dev, HEAD)
        return (attend_piece(state_inner, queries, key_block, value_block), None)

    state_tuple, _ = lax.scan(one_block, state_tuple, blocks)
    row_max, row_sum, weighted = state_tuple
    heads_out = (
        (weighted / row_sum[:, :, None])
        .transpose(1, 0, 2)
        .reshape(tok_rows, heads_dev * HEAD)
        .astype(jnp.bfloat16)
    )
    partial_value = jnp.dot(heads_out, w_out, preferred_element_type=jnp.float32)
    head_total = head_sum(partial_value, lax.psum(1, FFN)).astype(jnp.float32)
    attended = head_total.astype(jnp.bfloat16)
    residual = tokens.astype(jnp.float32) + head_total
    normed_ffn = layer_norm(residual, gain_ffn).astype(jnp.bfloat16)
    channels = w_up.shape[1]
    pre = (
        jnp.dot(normed_ffn, w_up, preferred_element_type=jnp.float32)
        .astype(jnp.bfloat16)
        .reshape(CZ, GY, GX, channels)
    )
    pre_wide = padded_2(pre, ((SLAB, 0),), 1)
    pre_pad = jnp.pad(pre_wide, ((0, 0), (1, 1), (1, 1), (0, 0)))
    mixed = depth_conv(pre_pad, w_depth, CZ).reshape(tok_rows, channels)
    normal_cdf = 0.5 * (1.0 + lax.erf(mixed * ROOT_HALF))
    normal_pdf = jnp.exp(-0.5 * mixed * mixed) * NORMAL_SCALE
    activated = (mixed * normal_cdf).astype(jnp.bfloat16)
    grad_act = jnp.einsum("td,cd->tc", grad_out, w_down, preferred_element_type=jnp.float32)
    grad_mixed = (
        (grad_act * (normal_cdf + mixed * normal_pdf))
        .astype(jnp.bfloat16)
        .reshape(CZ, GY, GX, channels)
    )
    grad_wide = padded_2(grad_mixed, ((SLAB, 0),), 1)
    grad_pad = jnp.pad(grad_wide, ((0, 0), (1, 1), (1, 1), (0, 0)))
    grad_pre = (
        depth_conv(grad_pad, w_depth[::-1], CZ).astype(jnp.bfloat16).reshape(tok_rows, channels)
    )
    up_full = jnp.einsum("td,tc->dc", normed_ffn, grad_pre, preferred_element_type=jnp.float32)
    down_full = jnp.einsum("td,tc->dc", grad_out, activated, preferred_element_type=jnp.float32)
    grads = slab_scatter(jnp.concatenate([up_full, down_full], axis=1), lax.psum(1, SLAB))
    return (attended, grads[:, :channels], grads[:, channels:])


def solution(mesh):
    mesh = Mesh(mesh.devices.reshape(4, 8, 2, 2, 2), SLAB + FFN)
    in_specs = (
        P(SLAB, None),
        P(),
        P(),
        P(),
        P(None, FFN),
        P(None, FFN),
        P(None, FFN),
        P(FFN, None),
        P(),
        P(None, FFN),
        P(None, FFN),
        P(FFN, None),
        P(SLAB, None),
    )
    out_specs = (P(SLAB, None), P(SLAB, FFN), P(SLAB, FFN))
    return jax.shard_map(
        per_device, mesh=mesh, in_specs=in_specs, out_specs=out_specs, check_vma=False
    )
```

```python
import functools
import math

import jax
import jax.numpy as jnp
from jax import lax
from jax.experimental import pallas as pl
from jax.experimental.pallas import tpu as pltpu
from jax.sharding import Mesh
from jax.sharding import PartitionSpec as P

HEAD = 64
GX = 16
GY = 16
CZ = 2
SLAB = ("y", "z", "xl")
FFN = ("xh", "core")


EPSILON = 1e-05
ROPE_BASE = 100.0
ROOT_HALF = 0.7071067811865476
NORMAL_SCALE = 0.3989422804014327


MESH = pl.DeviceIdType.MESH


def peer_id(p):
    return (p // 16, p // 2 % 8, p % 2, lax.axis_index("xh"), lax.axis_index("core"))


def gather_kernel(
    row_size, x_ref, out_ref, send_a, recv_a, send_b, recv_b, send_c, recv_c, local_sem
):
    me = lax.axis_index(SLAB)
    block = x_ref.shape[0]
    own_y, spot = me // row_size, me % row_size
    y_count = lax.psum(1, "y")
    barrier = pltpu.get_barrier_semaphore()

    def greet(k, carry):
        peer = own_y * row_size + lax.rem(spot + k, row_size)
        pl.semaphore_signal(barrier, inc=1, device_id=peer_id(peer), device_id_type=MESH)
        return carry

    lax.fori_loop(1, row_size, greet, 0)
    left_y = lax.rem(own_y + y_count - 1, y_count)
    right_y = lax.rem(own_y + 1, y_count)
    for other_y in (left_y, right_y):
        peer = other_y * row_size + spot
        pl.semaphore_signal(barrier, inc=1, device_id=peer_id(peer), device_id_type=MESH)
    pl.semaphore_wait(barrier, row_size + 1)

    def along_row(target, source):
        return pltpu.make_async_remote_copy(
            src_ref=x_ref,
            dst_ref=out_ref.at[pl.ds((own_y * row_size + source) * block, block)],
            send_sem=send_a.at[target],
            recv_sem=recv_a.at[source],
            device_id=peer_id(own_y * row_size + target),
            device_id_type=MESH,
        )

    def start_row(k, carry):
        along_row(lax.rem(spot + k, row_size), spot).start()
        return carry

    lax.fori_loop(1, row_size, start_row, 0)
    local = pltpu.make_async_copy(x_ref, out_ref.at[pl.ds(me * block, block)], local_sem)
    local.start()
    local.wait()

    def finish_row(k, carry):
        other = lax.rem(spot + k, row_size)
        along_row(other, spot).wait_send()
        along_row(other, other).wait_recv()
        return carry

    lax.fori_loop(1, row_size, finish_row, 0)
    row_rows = row_size * block

    def across(target_y, source_y):
        return pltpu.make_async_remote_copy(
            src_ref=out_ref.at[pl.ds(source_y * row_rows, row_rows)],
            dst_ref=out_ref.at[pl.ds(source_y * row_rows, row_rows)],
            send_sem=send_b.at[target_y],
            recv_sem=recv_b.at[source_y],
            device_id=peer_id(target_y * row_size + spot),
            device_id_type=MESH,
        )

    for other_y in (left_y, right_y):
        across(other_y, own_y).start()
    for other_y in (left_y, right_y):
        across(other_y, own_y).wait_send()
        across(other_y, other_y).wait_recv()
    half = row_rows // 2

    def forward(target_y, source_y, part):
        rows = pl.ds(source_y * row_rows + part * half, half)
        return pltpu.make_async_remote_copy(
            src_ref=out_ref.at[rows],
            dst_ref=out_ref.at[rows],
            send_sem=send_c.at[part],
            recv_sem=recv_c.at[part],
            device_id=peer_id(target_y * row_size + spot),
            device_id_type=MESH,
        )

    far_y = lax.rem(own_y + 2, y_count)
    forward(right_y, left_y, 0).start()
    forward(left_y, right_y, 1).start()
    forward(right_y, left_y, 0).wait_send()
    forward(left_y, right_y, 1).wait_send()
    forward(right_y, far_y, 0).wait_recv()
    forward(left_y, far_y, 1).wait_recv()


def slab_gather(x, count, row_size):
    rows, width = x.shape
    y_count = count // row_size
    assert y_count == 4
    return pl.pallas_call(
        functools.partial(gather_kernel, row_size),
        out_shape=jax.ShapeDtypeStruct((count * rows, width), x.dtype),
        in_specs=[pl.BlockSpec(memory_space=pltpu.VMEM)],
        out_specs=pl.BlockSpec(memory_space=pltpu.VMEM),
        scratch_shapes=[
            pltpu.SemaphoreType.DMA((row_size,)),
            pltpu.SemaphoreType.DMA((row_size,)),
            pltpu.SemaphoreType.DMA((y_count,)),
            pltpu.SemaphoreType.DMA((y_count,)),
            pltpu.SemaphoreType.DMA((2,)),
            pltpu.SemaphoreType.DMA((2,)),
            pltpu.SemaphoreType.DMA(()),
        ],
        compiler_params=pltpu.CompilerParams(collective_id=0, has_side_effects=True),
    )(x)


def head_peer(q):
    return (lax.axis_index("y"), lax.axis_index("z"), lax.axis_index("xl"), q // 2, q % 2)


def head_sum_kernel(count, part_ref, out_ref, slots, send_sem, recv_sem, send_back, recv_back):
    me = lax.axis_index(FFN)
    barrier = pltpu.get_barrier_semaphore()
    for k in range(1, count):
        pl.semaphore_signal(
            barrier, inc=1, device_id=head_peer(lax.rem(me + k, count)), device_id_type=MESH
        )
    pl.semaphore_wait(barrier, count - 1)

    def share(peer, source):
        return pltpu.make_async_remote_copy(
            src_ref=part_ref.at[peer],
            dst_ref=slots.at[source],
            send_sem=send_sem.at[peer],
            recv_sem=recv_sem.at[source],
            device_id=head_peer(peer),
            device_id_type=MESH,
        )

    def spread(peer, source):
        return pltpu.make_async_remote_copy(
            src_ref=out_ref.at[source],
            dst_ref=out_ref.at[source],
            send_sem=send_back.at[peer],
            recv_sem=recv_back.at[source],
            device_id=head_peer(peer),
            device_id_type=MESH,
        )

    peers = [lax.rem(me + k, count) for k in range(1, count)]
    for peer in peers:
        share(peer, me).start()
    total = part_ref[me].astype(jnp.float32)
    for peer in peers:
        share(peer, me).wait_send()
        share(peer, peer).wait_recv()
        total = total + slots[peer].astype(jnp.float32)
    out_ref[me] = total.astype(out_ref.dtype)
    for peer in peers:
        spread(peer, me).start()
    for peer in peers:
        spread(peer, me).wait_send()
        spread(peer, peer).wait_recv()


def head_sum(partial_value, count):
    rows, width = partial_value.shape
    parts = partial_value.astype(jnp.bfloat16).reshape(count, rows // count, width)
    summed = pl.pallas_call(
        functools.partial(head_sum_kernel, count),
        out_shape=jax.ShapeDtypeStruct(parts.shape, parts.dtype),
        in_specs=[pl.BlockSpec(memory_space=pltpu.VMEM)],
        out_specs=pl.BlockSpec(memory_space=pltpu.VMEM),
        scratch_shapes=[
            pltpu.VMEM(parts.shape, parts.dtype),
            pltpu.SemaphoreType.DMA((count,)),
            pltpu.SemaphoreType.DMA((count,)),
            pltpu.SemaphoreType.DMA((count,)),
            pltpu.SemaphoreType.DMA((count,)),
        ],
        compiler_params=pltpu.CompilerParams(collective_id=2, has_side_effects=True),
    )(parts)
    return summed.reshape(rows, width)


def scatter_kernel(
    row_size, g_ref, out_ref, slots_y, totals, sums, slots_row, send_a, recv_a, send_b, recv_b
):
    me = lax.axis_index(SLAB)
    own_y, spot = me // row_size, me % row_size
    y_count = lax.psum(1, "y")
    barrier = pltpu.get_barrier_semaphore()

    def greet(k, carry):
        peer = own_y * row_size + lax.rem(spot + k, row_size)
        pl.semaphore_signal(barrier, inc=1, device_id=peer_id(peer), device_id_type=MESH)
        return carry

    lax.fori_loop(1, row_size, greet, 0)
    others = [lax.rem(own_y + j, y_count) for j in range(1, y_count)]
    for other_y in others:
        pl.semaphore_signal(
            barrier, inc=1, device_id=peer_id(other_y * row_size + spot), device_id_type=MESH
        )
    pl.semaphore_wait(barrier, row_size + y_count - 2)

    def across(target_y, source_y):
        return pltpu.make_async_remote_copy(
            src_ref=g_ref.at[pl.ds(target_y * row_size, row_size)],
            dst_ref=slots_y.at[source_y],
            send_sem=send_a.at[target_y],
            recv_sem=recv_a.at[source_y],
            device_id=peer_id(target_y * row_size + spot),
            device_id_type=MESH,
        )

    for other_y in others:
        across(other_y, own_y).start()
    total = g_ref[pl.ds(own_y * row_size, row_size)].astype(jnp.float32)
    for other_y in others:
        across(other_y, own_y).wait_send()
        across(other_y, other_y).wait_recv()
        total = total + slots_y[other_y].astype(jnp.float32)
    totals[...] = total
    sums[...] = total.astype(sums.dtype)

    def along_row(target, source):
        return pltpu.make_async_remote_copy(
            src_ref=sums.at[target],
            dst_ref=slots_row.at[source],
            send_sem=send_b.at[target],
            recv_sem=recv_b.at[source],
            device_id=peer_id(own_y * row_size + target),
            device_id_type=MESH,
        )

    def start_row(k, carry):
        along_row(lax.rem(spot + k, row_size), spot).start()
        return carry

    lax.fori_loop(1, row_size, start_row, 0)
    out_ref[...] = totals[spot]

    def finish_row(k, carry):
        other = lax.rem(spot + k, row_size)
        along_row(other, spot).wait_send()
        along_row(other, other).wait_recv()
        out_ref[...] += slots_row[other].astype(jnp.float32)
        return carry

    lax.fori_loop(1, row_size, finish_row, 0)


def slab_scatter(g, count, row_size):
    total_rows, width = g.shape
    rows = total_rows // count
    y_count = count // row_size
    tile_rows = 16
    g = g.astype(jnp.bfloat16).reshape(count, tile_rows, rows * width // tile_rows)
    summed = pl.pallas_call(
        functools.partial(scatter_kernel, row_size),
        out_shape=jax.ShapeDtypeStruct(g.shape[1:], jnp.float32),
        in_specs=[pl.BlockSpec(memory_space=pltpu.VMEM)],
        out_specs=pl.BlockSpec(memory_space=pltpu.VMEM),
        scratch_shapes=[
            pltpu.VMEM((y_count, row_size) + g.shape[1:], g.dtype),
            pltpu.VMEM((row_size,) + g.shape[1:], jnp.float32),
            pltpu.VMEM((row_size,) + g.shape[1:], g.dtype),
            pltpu.VMEM((row_size,) + g.shape[1:], g.dtype),
            pltpu.SemaphoreType.DMA((y_count,)),
            pltpu.SemaphoreType.DMA((y_count,)),
            pltpu.SemaphoreType.DMA((row_size,)),
            pltpu.SemaphoreType.DMA((row_size,)),
        ],
        compiler_params=pltpu.CompilerParams(collective_id=1, has_side_effects=True),
    )(g)
    return summed.reshape(rows, width)


def padded_2(cells, sides, width):
    for axis, dim in sides:
        count = lax.psum(1, axis)
        ends = count - 1
        head = lax.slice_in_dim(cells, 0, width, axis=dim)
        tail = lax.slice_in_dim(cells, cells.shape[dim] - width, cells.shape[dim], axis=dim)
        cells = jnp.concatenate(
            [
                lax.ppermute(tail, axis, [(i, (i + 1) % count) for i in range(ends)]),
                cells,
                lax.ppermute(head, axis, [((i + 1) % count, i) for i in range(ends)]),
            ],
            axis=dim,
        )
    return cells


def layer_norm(values, scale_gain):
    values = values.astype(jnp.float32)
    centered = values - jnp.mean(values, axis=-1, keepdims=True)
    variance = jnp.mean(centered * centered, axis=-1, keepdims=True)
    return centered * lax.rsqrt(variance + EPSILON) * scale_gain


def rope_tables(coord_x, coord_y, coord_z, head_size):
    pair_count = head_size // 2
    position = jnp.arange(pair_count, dtype=jnp.int32)
    axis_pick = position % 3
    per_axis = (pair_count + 2) // 3
    frequency = ROPE_BASE ** (-(position // 3).astype(jnp.float32) / per_axis)
    angles = (
        coord_x[:, None] * (axis_pick == 0)
        + coord_y[:, None] * (axis_pick == 1)
        + coord_z[:, None] * (axis_pick == 2)
    ) * frequency
    return (jnp.cos(angles)[:, None, :], jnp.sin(angles)[:, None, :])


def token_tables(first_plane, planes, head_size):
    position = jnp.arange(planes * GY * GX, dtype=jnp.int32)
    coord_x = (position % GX).astype(jnp.float32)
    coord_y = (position // GX % GY).astype(jnp.float32)
    coord_z = (first_plane + position // (GX * GY)).astype(jnp.float32)
    return rope_tables(coord_x, coord_y, coord_z, head_size)


def key_tables(first_row, row_count, head_size):
    position = first_row + jnp.arange(row_count, dtype=jnp.int32)
    half_x = GX // 2
    half_y = GY // 2
    coord_x = (position % half_x).astype(jnp.float32) * 2.0 + 0.5
    coord_y = (position // half_x % half_y).astype(jnp.float32) * 2.0 + 0.5
    coord_z = (position // (half_x * half_y)).astype(jnp.float32) * 2.0 + 0.5
    return rope_tables(coord_x, coord_y, coord_z, head_size)


def rotate(values, cosine, sine_table):
    half_size = values.shape[-1] // 2
    front_half = values[..., :half_size]
    back_half = values[..., half_size:]
    return jnp.concatenate(
        [
            front_half * cosine - back_half * sine_table,
            back_half * cosine + front_half * sine_table,
        ],
        axis=-1,
    )


def make_patches(normed, planes):
    width = normed.shape[-1]
    cell_grid = normed.reshape(planes // 2, 2, GY // 2, 2, GX // 2, 2, width)
    return cell_grid.transpose(0, 2, 4, 1, 3, 5, 6).reshape(-1, 8 * width)


def depth_conv(padded, weights, planes):
    height = padded.shape[1] - 2
    width_x = padded.shape[2] - 2
    result = jnp.zeros((planes, height, width_x, padded.shape[3]), jnp.float32)
    for offset in range(27):
        shift_z = offset // 9
        shift_y = offset // 3 % 3
        shift_x = offset % 3
        window = padded[
            shift_z : shift_z + planes, shift_y : shift_y + height, shift_x : shift_x + width_x
        ]
        result = result + window.astype(jnp.float32) * weights[offset]
    return result


def attend_piece(state_tuple, queries, key_rows, value_rows):
    row_max, row_sum, weighted = state_tuple
    score_scale = key_rows.shape[-1] ** (-0.5)
    scores = (
        jnp.einsum("qhd,khd->hqk", queries, key_rows, preferred_element_type=jnp.float32)
        * score_scale
    )
    new_max = jnp.maximum(row_max, jnp.max(scores, axis=2))
    rescale = jnp.exp(row_max - new_max)
    expo = jnp.exp(scores - new_max[:, :, None])
    row_sum = row_sum * rescale + jnp.sum(expo, axis=2)
    weighted = weighted * rescale[:, :, None] + jnp.einsum(
        "hqk,khd->hqd", expo.astype(jnp.bfloat16), value_rows, preferred_element_type=jnp.float32
    )
    return (new_max, row_sum, weighted)


def per_device(
    tokens,
    gain_attn,
    w_reduce,
    gain_keys,
    w_query,
    w_key,
    w_value,
    w_out,
    gain_ffn,
    w_up,
    w_depth,
    w_down,
    grad_out,
):
    slab_index = lax.axis_index(SLAB)
    tok_rows = tokens.shape[0]
    heads_dev = w_query.shape[1] // HEAD
    normed = layer_norm(tokens, gain_attn).astype(jnp.bfloat16)
    patches = make_patches(normed, CZ)
    reduced = jnp.dot(patches, w_reduce, preferred_element_type=jnp.float32)
    key_input = layer_norm(reduced, gain_keys).astype(jnp.bfloat16)
    tok_cos, tok_sin = token_tables(slab_index * CZ, CZ, HEAD)
    queries = jnp.dot(normed, w_query, preferred_element_type=jnp.float32).reshape(
        tok_rows, heads_dev, HEAD
    )
    queries = rotate(queries, tok_cos, tok_sin).astype(jnp.bfloat16)
    initial = (
        jnp.full((heads_dev, tok_rows), -1e30, jnp.float32),
        jnp.zeros((heads_dev, tok_rows), jnp.float32),
        jnp.zeros((heads_dev, tok_rows, HEAD), jnp.float32),
    )
    state_tuple = initial
    local_rows = key_input.shape[0]
    own_cos, own_sin = key_tables(slab_index * local_rows, local_rows, HEAD)
    own_keys = jnp.dot(key_input, w_key, preferred_element_type=jnp.float32).reshape(
        local_rows, heads_dev, HEAD
    )
    own_keys = rotate(own_keys, own_cos, own_sin).astype(jnp.bfloat16)
    own_values = jnp.dot(key_input, w_value, preferred_element_type=jnp.float32).astype(
        jnp.bfloat16
    )
    key_width = heads_dev * HEAD
    pieces = jnp.concatenate([own_keys.reshape(local_rows, key_width), own_values], axis=1)
    pieces = slab_gather(pieces, lax.psum(1, SLAB), lax.psum(1, ("z", "xl")))
    row_count = pieces.shape[0]
    block_rows = math.gcd(row_count, 1024)
    block_count = row_count // block_rows
    blocks = pieces.reshape(block_count, block_rows, pieces.shape[1])

    def one_block(state_inner, rows_in):
        key_block = rows_in[:, :key_width].reshape(block_rows, heads_dev, HEAD)
        value_block = rows_in[:, key_width:].reshape(block_rows, heads_dev, HEAD)
        return (attend_piece(state_inner, queries, key_block, value_block), None)

    state_tuple, _ = lax.scan(one_block, state_tuple, blocks)
    row_max, row_sum, weighted = state_tuple
    heads_out = (
        (weighted / row_sum[:, :, None])
        .transpose(1, 0, 2)
        .reshape(tok_rows, heads_dev * HEAD)
        .astype(jnp.bfloat16)
    )
    partial_value = jnp.dot(heads_out, w_out, preferred_element_type=jnp.float32)
    head_total = head_sum(partial_value, lax.psum(1, FFN)).astype(jnp.float32)
    attended = head_total.astype(jnp.bfloat16)
    residual = tokens.astype(jnp.float32) + head_total
    normed_ffn = layer_norm(residual, gain_ffn).astype(jnp.bfloat16)
    channels = w_up.shape[1]
    pre = (
        jnp.dot(normed_ffn, w_up, preferred_element_type=jnp.float32)
        .astype(jnp.bfloat16)
        .reshape(CZ, GY, GX, channels)
    )
    pre_wide = padded_2(pre, ((SLAB, 0),), 1)
    pre_pad = jnp.pad(pre_wide, ((0, 0), (1, 1), (1, 1), (0, 0)))
    mixed = depth_conv(pre_pad, w_depth, CZ).reshape(tok_rows, channels)
    normal_cdf = 0.5 * (1.0 + lax.erf(mixed * ROOT_HALF))
    normal_pdf = jnp.exp(-0.5 * mixed * mixed) * NORMAL_SCALE
    activated = (mixed * normal_cdf).astype(jnp.bfloat16)
    grad_act = jnp.einsum("td,cd->tc", grad_out, w_down, preferred_element_type=jnp.float32)
    grad_mixed = (
        (grad_act * (normal_cdf + mixed * normal_pdf))
        .astype(jnp.bfloat16)
        .reshape(CZ, GY, GX, channels)
    )
    grad_wide = padded_2(grad_mixed, ((SLAB, 0),), 1)
    grad_pad = jnp.pad(grad_wide, ((0, 0), (1, 1), (1, 1), (0, 0)))
    grad_pre = (
        depth_conv(grad_pad, w_depth[::-1], CZ).astype(jnp.bfloat16).reshape(tok_rows, channels)
    )
    up_full = jnp.einsum("td,tc->dc", normed_ffn, grad_pre, preferred_element_type=jnp.float32)
    down_full = jnp.einsum("td,tc->dc", grad_out, activated, preferred_element_type=jnp.float32)
    grads = slab_scatter(
        jnp.concatenate([up_full, down_full], axis=1),
        lax.psum(1, SLAB),
        lax.psum(1, ("z", "xl")),
    )
    return (attended, grads[:, :channels], grads[:, channels:])


def solution(mesh):
    mesh = Mesh(mesh.devices.reshape(4, 8, 2, 2, 2), SLAB + FFN)
    in_specs = (
        P(SLAB, None),
        P(),
        P(),
        P(),
        P(None, FFN),
        P(None, FFN),
        P(None, FFN),
        P(FFN, None),
        P(),
        P(None, FFN),
        P(None, FFN),
        P(FFN, None),
        P(SLAB, None),
    )
    out_specs = (P(SLAB, None), P(SLAB, FFN), P(SLAB, FFN))
    return jax.shard_map(
        per_device, mesh=mesh, in_specs=in_specs, out_specs=out_specs, check_vma=False
    )
```

```python
import functools
import math

import jax
import jax.numpy as jnp
from jax import lax
from jax.experimental import pallas as pl
from jax.experimental.pallas import tpu as pltpu
from jax.sharding import Mesh
from jax.sharding import PartitionSpec as P

HEAD = 64
GX = 16
GY = 16
CZ = 2
SLAB = ("y", "z", "xl")
FFN = ("xh", "core")


EPSILON = 1e-05
ROPE_BASE = 100.0
ROOT_HALF = 0.7071067811865476
NORMAL_SCALE = 0.3989422804014327


MESH = pl.DeviceIdType.MESH


def peer_id(p):
    return (p // 16, p // 2 % 8, p % 2, lax.axis_index("xh"), lax.axis_index("core"))


def gather_kernel(
    row_size, x_ref, out_ref, send_a, recv_a, send_b, recv_b, send_c, recv_c, local_sem
):
    me = lax.axis_index(SLAB)
    block = x_ref.shape[0]
    own_y, spot = me // row_size, me % row_size
    y_count = lax.psum(1, "y")
    barrier = pltpu.get_barrier_semaphore()

    def greet(k, carry):
        peer = own_y * row_size + lax.rem(spot + k, row_size)
        pl.semaphore_signal(barrier, inc=1, device_id=peer_id(peer), device_id_type=MESH)
        return carry

    lax.fori_loop(1, row_size, greet, 0)
    left_y = lax.rem(own_y + y_count - 1, y_count)
    right_y = lax.rem(own_y + 1, y_count)
    for other_y in (left_y, right_y):
        peer = other_y * row_size + spot
        pl.semaphore_signal(barrier, inc=1, device_id=peer_id(peer), device_id_type=MESH)
    pl.semaphore_wait(barrier, row_size + 1)

    def along_row(target, source):
        return pltpu.make_async_remote_copy(
            src_ref=x_ref,
            dst_ref=out_ref.at[pl.ds((own_y * row_size + source) * block, block)],
            send_sem=send_a.at[target],
            recv_sem=recv_a.at[source],
            device_id=peer_id(own_y * row_size + target),
            device_id_type=MESH,
        )

    def start_row(k, carry):
        along_row(lax.rem(spot + k, row_size), spot).start()
        return carry

    lax.fori_loop(1, row_size, start_row, 0)
    local = pltpu.make_async_copy(x_ref, out_ref.at[pl.ds(me * block, block)], local_sem)
    local.start()
    local.wait()

    def finish_row(k, carry):
        other = lax.rem(spot + k, row_size)
        along_row(other, spot).wait_send()
        along_row(other, other).wait_recv()
        return carry

    lax.fori_loop(1, row_size, finish_row, 0)
    row_rows = row_size * block

    def across(target_y, source_y):
        return pltpu.make_async_remote_copy(
            src_ref=out_ref.at[pl.ds(source_y * row_rows, row_rows)],
            dst_ref=out_ref.at[pl.ds(source_y * row_rows, row_rows)],
            send_sem=send_b.at[target_y],
            recv_sem=recv_b.at[source_y],
            device_id=peer_id(target_y * row_size + spot),
            device_id_type=MESH,
        )

    for other_y in (left_y, right_y):
        across(other_y, own_y).start()
    for other_y in (left_y, right_y):
        across(other_y, own_y).wait_send()
        across(other_y, other_y).wait_recv()
    half = row_rows // 2

    def forward(target_y, source_y, part):
        rows = pl.ds(source_y * row_rows + part * half, half)
        return pltpu.make_async_remote_copy(
            src_ref=out_ref.at[rows],
            dst_ref=out_ref.at[rows],
            send_sem=send_c.at[part],
            recv_sem=recv_c.at[part],
            device_id=peer_id(target_y * row_size + spot),
            device_id_type=MESH,
        )

    far_y = lax.rem(own_y + 2, y_count)
    forward(right_y, left_y, 0).start()
    forward(left_y, right_y, 1).start()
    forward(right_y, left_y, 0).wait_send()
    forward(left_y, right_y, 1).wait_send()
    forward(right_y, far_y, 0).wait_recv()
    forward(left_y, far_y, 1).wait_recv()


def slab_gather(x, count, row_size):
    rows, width = x.shape
    y_count = count // row_size
    assert y_count == 4
    return pl.pallas_call(
        functools.partial(gather_kernel, row_size),
        out_shape=jax.ShapeDtypeStruct((count * rows, width), x.dtype),
        in_specs=[pl.BlockSpec(memory_space=pltpu.VMEM)],
        out_specs=pl.BlockSpec(memory_space=pltpu.VMEM),
        scratch_shapes=[
            pltpu.SemaphoreType.DMA((row_size,)),
            pltpu.SemaphoreType.DMA((row_size,)),
            pltpu.SemaphoreType.DMA((y_count,)),
            pltpu.SemaphoreType.DMA((y_count,)),
            pltpu.SemaphoreType.DMA((2,)),
            pltpu.SemaphoreType.DMA((2,)),
            pltpu.SemaphoreType.DMA(()),
        ],
        compiler_params=pltpu.CompilerParams(collective_id=0, has_side_effects=True),
    )(x)


def head_peer(q):
    return (lax.axis_index("y"), lax.axis_index("z"), lax.axis_index("xl"), q // 2, q % 2)


def head_sum_kernel(count, part_ref, out_ref, slots, send_sem, recv_sem, send_back, recv_back):
    me = lax.axis_index(FFN)
    barrier = pltpu.get_barrier_semaphore()
    for k in range(1, count):
        pl.semaphore_signal(
            barrier, inc=1, device_id=head_peer(lax.rem(me + k, count)), device_id_type=MESH
        )
    pl.semaphore_wait(barrier, count - 1)

    def share(peer, source):
        return pltpu.make_async_remote_copy(
            src_ref=part_ref.at[peer],
            dst_ref=slots.at[source],
            send_sem=send_sem.at[peer],
            recv_sem=recv_sem.at[source],
            device_id=head_peer(peer),
            device_id_type=MESH,
        )

    def spread(peer, source):
        return pltpu.make_async_remote_copy(
            src_ref=out_ref.at[source],
            dst_ref=out_ref.at[source],
            send_sem=send_back.at[peer],
            recv_sem=recv_back.at[source],
            device_id=head_peer(peer),
            device_id_type=MESH,
        )

    peers = [lax.rem(me + k, count) for k in range(1, count)]
    for peer in peers:
        share(peer, me).start()
    total = part_ref[me].astype(jnp.float32)
    for peer in peers:
        share(peer, me).wait_send()
        share(peer, peer).wait_recv()
        total = total + slots[peer].astype(jnp.float32)
    out_ref[me] = total.astype(out_ref.dtype)
    for peer in peers:
        spread(peer, me).start()
    for peer in peers:
        spread(peer, me).wait_send()
        spread(peer, peer).wait_recv()


def head_sum(partial_value, count):
    rows, width = partial_value.shape
    parts = partial_value.astype(jnp.bfloat16).reshape(count, rows // count, width)
    summed = pl.pallas_call(
        functools.partial(head_sum_kernel, count),
        out_shape=jax.ShapeDtypeStruct(parts.shape, parts.dtype),
        in_specs=[pl.BlockSpec(memory_space=pltpu.VMEM)],
        out_specs=pl.BlockSpec(memory_space=pltpu.VMEM),
        scratch_shapes=[
            pltpu.VMEM(parts.shape, parts.dtype),
            pltpu.SemaphoreType.DMA((count,)),
            pltpu.SemaphoreType.DMA((count,)),
            pltpu.SemaphoreType.DMA((count,)),
            pltpu.SemaphoreType.DMA((count,)),
        ],
        compiler_params=pltpu.CompilerParams(collective_id=2, has_side_effects=True),
    )(parts)
    return summed.reshape(rows, width)


def scatter_kernel(
    row_size, g_ref, out_ref, slots_y, totals, sums, slots_row, send_a, recv_a, send_b, recv_b
):
    me = lax.axis_index(SLAB)
    own_y, spot = me // row_size, me % row_size
    y_count = lax.psum(1, "y")
    barrier = pltpu.get_barrier_semaphore()

    def greet(k, carry):
        peer = own_y * row_size + lax.rem(spot + k, row_size)
        pl.semaphore_signal(barrier, inc=1, device_id=peer_id(peer), device_id_type=MESH)
        return carry

    lax.fori_loop(1, row_size, greet, 0)
    others = [lax.rem(own_y + j, y_count) for j in range(1, y_count)]
    for other_y in others:
        pl.semaphore_signal(
            barrier, inc=1, device_id=peer_id(other_y * row_size + spot), device_id_type=MESH
        )
    pl.semaphore_wait(barrier, row_size + y_count - 2)

    def across(target_y, source_y):
        return pltpu.make_async_remote_copy(
            src_ref=g_ref.at[pl.ds(target_y * row_size, row_size)],
            dst_ref=slots_y.at[source_y],
            send_sem=send_a.at[target_y],
            recv_sem=recv_a.at[source_y],
            device_id=peer_id(target_y * row_size + spot),
            device_id_type=MESH,
        )

    for other_y in others:
        across(other_y, own_y).start()
    total = g_ref[pl.ds(own_y * row_size, row_size)].astype(jnp.float32)
    for other_y in others:
        across(other_y, own_y).wait_send()
        across(other_y, other_y).wait_recv()
        total = total + slots_y[other_y].astype(jnp.float32)
    totals[...] = total
    sums[...] = total.astype(sums.dtype)

    def along_row(target, source):
        return pltpu.make_async_remote_copy(
            src_ref=sums.at[target],
            dst_ref=slots_row.at[source],
            send_sem=send_b.at[target],
            recv_sem=recv_b.at[source],
            device_id=peer_id(own_y * row_size + target),
            device_id_type=MESH,
        )

    def start_row(k, carry):
        along_row(lax.rem(spot + k, row_size), spot).start()
        return carry

    lax.fori_loop(1, row_size, start_row, 0)
    out_ref[...] = totals[spot]

    def finish_row(k, carry):
        other = lax.rem(spot + k, row_size)
        along_row(other, spot).wait_send()
        along_row(other, other).wait_recv()
        out_ref[...] += slots_row[other].astype(jnp.float32)
        return carry

    lax.fori_loop(1, row_size, finish_row, 0)


def slab_scatter(g, count, row_size):
    total_rows, width = g.shape
    rows = total_rows // count
    y_count = count // row_size
    tile_rows = 16
    g = g.astype(jnp.bfloat16).reshape(count, tile_rows, rows * width // tile_rows)
    summed = pl.pallas_call(
        functools.partial(scatter_kernel, row_size),
        out_shape=jax.ShapeDtypeStruct(g.shape[1:], jnp.float32),
        in_specs=[pl.BlockSpec(memory_space=pltpu.VMEM)],
        out_specs=pl.BlockSpec(memory_space=pltpu.VMEM),
        scratch_shapes=[
            pltpu.VMEM((y_count, row_size) + g.shape[1:], g.dtype),
            pltpu.VMEM((row_size,) + g.shape[1:], jnp.float32),
            pltpu.VMEM((row_size,) + g.shape[1:], g.dtype),
            pltpu.VMEM((row_size,) + g.shape[1:], g.dtype),
            pltpu.SemaphoreType.DMA((y_count,)),
            pltpu.SemaphoreType.DMA((y_count,)),
            pltpu.SemaphoreType.DMA((row_size,)),
            pltpu.SemaphoreType.DMA((row_size,)),
        ],
        compiler_params=pltpu.CompilerParams(collective_id=1, has_side_effects=True),
    )(g)
    return summed.reshape(rows, width)


def attention_kernel(heads, q_tile, q_ref, kv_ref, out_ref):
    key_width = heads * HEAD
    score_scale = HEAD ** (-0.5)
    for head in range(heads):
        keys = kv_ref[:, head * HEAD : (head + 1) * HEAD]
        values = kv_ref[:, key_width + head * HEAD : key_width + (head + 1) * HEAD]
        for first in range(0, q_ref.shape[0], q_tile):
            queries = q_ref[first : first + q_tile, head * HEAD : (head + 1) * HEAD]
            scores = lax.dot_general(
                queries, keys, (((1,), (1,)), ((), ())), preferred_element_type=jnp.float32
            ) * score_scale
            top = jnp.max(scores, axis=1, keepdims=True)
            weights = jnp.exp(scores - top)
            row_sum = jnp.sum(weights, axis=1, keepdims=True)
            mixed = jnp.dot(
                weights.astype(jnp.bfloat16), values, preferred_element_type=jnp.float32
            )
            out_ref[first : first + q_tile, head * HEAD : (head + 1) * HEAD] = (
                mixed / row_sum
            ).astype(out_ref.dtype)


def attention(queries, kv, heads, q_tile=256):
    return pl.pallas_call(
        functools.partial(attention_kernel, heads, q_tile),
        out_shape=jax.ShapeDtypeStruct(queries.shape, jnp.bfloat16),
        in_specs=[pl.BlockSpec(memory_space=pltpu.VMEM)] * 2,
        out_specs=pl.BlockSpec(memory_space=pltpu.VMEM),
    )(queries, kv)


def padded_2(cells, sides, width):
    for axis, dim in sides:
        count = lax.psum(1, axis)
        ends = count - 1
        head = lax.slice_in_dim(cells, 0, width, axis=dim)
        tail = lax.slice_in_dim(cells, cells.shape[dim] - width, cells.shape[dim], axis=dim)
        cells = jnp.concatenate(
            [
                lax.ppermute(tail, axis, [(i, (i + 1) % count) for i in range(ends)]),
                cells,
                lax.ppermute(head, axis, [((i + 1) % count, i) for i in range(ends)]),
            ],
            axis=dim,
        )
    return cells


def layer_norm(values, scale_gain):
    values = values.astype(jnp.float32)
    centered = values - jnp.mean(values, axis=-1, keepdims=True)
    variance = jnp.mean(centered * centered, axis=-1, keepdims=True)
    return centered * lax.rsqrt(variance + EPSILON) * scale_gain


def rope_tables(coord_x, coord_y, coord_z, head_size):
    pair_count = head_size // 2
    position = jnp.arange(pair_count, dtype=jnp.int32)
    axis_pick = position % 3
    per_axis = (pair_count + 2) // 3
    frequency = ROPE_BASE ** (-(position // 3).astype(jnp.float32) / per_axis)
    angles = (
        coord_x[:, None] * (axis_pick == 0)
        + coord_y[:, None] * (axis_pick == 1)
        + coord_z[:, None] * (axis_pick == 2)
    ) * frequency
    return (jnp.cos(angles)[:, None, :], jnp.sin(angles)[:, None, :])


def token_tables(first_plane, planes, head_size):
    position = jnp.arange(planes * GY * GX, dtype=jnp.int32)
    coord_x = (position % GX).astype(jnp.float32)
    coord_y = (position // GX % GY).astype(jnp.float32)
    coord_z = (first_plane + position // (GX * GY)).astype(jnp.float32)
    return rope_tables(coord_x, coord_y, coord_z, head_size)


def key_tables(first_row, row_count, head_size):
    position = first_row + jnp.arange(row_count, dtype=jnp.int32)
    half_x = GX // 2
    half_y = GY // 2
    coord_x = (position % half_x).astype(jnp.float32) * 2.0 + 0.5
    coord_y = (position // half_x % half_y).astype(jnp.float32) * 2.0 + 0.5
    coord_z = (position // (half_x * half_y)).astype(jnp.float32) * 2.0 + 0.5
    return rope_tables(coord_x, coord_y, coord_z, head_size)


def rotate(values, cosine, sine_table):
    half_size = values.shape[-1] // 2
    front_half = values[..., :half_size]
    back_half = values[..., half_size:]
    return jnp.concatenate(
        [
            front_half * cosine - back_half * sine_table,
            back_half * cosine + front_half * sine_table,
        ],
        axis=-1,
    )


def make_patches(normed, planes):
    width = normed.shape[-1]
    cell_grid = normed.reshape(planes // 2, 2, GY // 2, 2, GX // 2, 2, width)
    return cell_grid.transpose(0, 2, 4, 1, 3, 5, 6).reshape(-1, 8 * width)


def depth_conv(padded, weights, planes):
    height = padded.shape[1] - 2
    width_x = padded.shape[2] - 2
    result = jnp.zeros((planes, height, width_x, padded.shape[3]), jnp.float32)
    for offset in range(27):
        shift_z = offset // 9
        shift_y = offset // 3 % 3
        shift_x = offset % 3
        window = padded[
            shift_z : shift_z + planes, shift_y : shift_y + height, shift_x : shift_x + width_x
        ]
        result = result + window.astype(jnp.float32) * weights[offset]
    return result


def per_device(
    tokens,
    gain_attn,
    w_reduce,
    gain_keys,
    w_query,
    w_key,
    w_value,
    w_out,
    gain_ffn,
    w_up,
    w_depth,
    w_down,
    grad_out,
):
    slab_index = lax.axis_index(SLAB)
    tok_rows = tokens.shape[0]
    heads_dev = w_query.shape[1] // HEAD
    normed = layer_norm(tokens, gain_attn).astype(jnp.bfloat16)
    patches = make_patches(normed, CZ)
    reduced = jnp.dot(patches, w_reduce, preferred_element_type=jnp.float32)
    key_input = layer_norm(reduced, gain_keys).astype(jnp.bfloat16)
    tok_cos, tok_sin = token_tables(slab_index * CZ, CZ, HEAD)
    queries = jnp.dot(normed, w_query, preferred_element_type=jnp.float32).reshape(
        tok_rows, heads_dev, HEAD
    )
    queries = rotate(queries, tok_cos, tok_sin).astype(jnp.bfloat16)
    local_rows = key_input.shape[0]
    own_cos, own_sin = key_tables(slab_index * local_rows, local_rows, HEAD)
    own_keys = jnp.dot(key_input, w_key, preferred_element_type=jnp.float32).reshape(
        local_rows, heads_dev, HEAD
    )
    own_keys = rotate(own_keys, own_cos, own_sin).astype(jnp.bfloat16)
    own_values = jnp.dot(key_input, w_value, preferred_element_type=jnp.float32).astype(
        jnp.bfloat16
    )
    key_width = heads_dev * HEAD
    pieces = jnp.concatenate([own_keys.reshape(local_rows, key_width), own_values], axis=1)
    pieces = slab_gather(pieces, lax.psum(1, SLAB), lax.psum(1, ("z", "xl")))
    heads_out = attention(queries.reshape(tok_rows, key_width), pieces, heads_dev)
    partial_value = jnp.dot(heads_out, w_out, preferred_element_type=jnp.float32)
    head_total = head_sum(partial_value, lax.psum(1, FFN)).astype(jnp.float32)
    attended = head_total.astype(jnp.bfloat16)
    residual = tokens.astype(jnp.float32) + head_total
    normed_ffn = layer_norm(residual, gain_ffn).astype(jnp.bfloat16)
    channels = w_up.shape[1]
    pre = (
        jnp.dot(normed_ffn, w_up, preferred_element_type=jnp.float32)
        .astype(jnp.bfloat16)
        .reshape(CZ, GY, GX, channels)
    )
    pre_wide = padded_2(pre, ((SLAB, 0),), 1)
    pre_pad = jnp.pad(pre_wide, ((0, 0), (1, 1), (1, 1), (0, 0)))
    mixed = depth_conv(pre_pad, w_depth, CZ).reshape(tok_rows, channels)
    normal_cdf = 0.5 * (1.0 + lax.erf(mixed * ROOT_HALF))
    normal_pdf = jnp.exp(-0.5 * mixed * mixed) * NORMAL_SCALE
    activated = (mixed * normal_cdf).astype(jnp.bfloat16)
    grad_act = jnp.einsum("td,cd->tc", grad_out, w_down, preferred_element_type=jnp.float32)
    grad_mixed = (
        (grad_act * (normal_cdf + mixed * normal_pdf))
        .astype(jnp.bfloat16)
        .reshape(CZ, GY, GX, channels)
    )
    grad_wide = padded_2(grad_mixed, ((SLAB, 0),), 1)
    grad_pad = jnp.pad(grad_wide, ((0, 0), (1, 1), (1, 1), (0, 0)))
    grad_pre = (
        depth_conv(grad_pad, w_depth[::-1], CZ).astype(jnp.bfloat16).reshape(tok_rows, channels)
    )
    up_full = jnp.einsum("td,tc->dc", normed_ffn, grad_pre, preferred_element_type=jnp.float32)
    down_full = jnp.einsum("td,tc->dc", grad_out, activated, preferred_element_type=jnp.float32)
    grads = slab_scatter(
        jnp.concatenate([up_full, down_full], axis=1),
        lax.psum(1, SLAB),
        lax.psum(1, ("z", "xl")),
    )
    return (attended, grads[:, :channels], grads[:, channels:])


def solution(mesh):
    mesh = Mesh(mesh.devices.reshape(4, 8, 2, 2, 2), SLAB + FFN)
    in_specs = (
        P(SLAB, None),
        P(),
        P(),
        P(),
        P(None, FFN),
        P(None, FFN),
        P(None, FFN),
        P(FFN, None),
        P(),
        P(None, FFN),
        P(None, FFN),
        P(FFN, None),
        P(SLAB, None),
    )
    out_specs = (P(SLAB, None), P(SLAB, FFN), P(SLAB, FFN))
    return jax.shard_map(
        per_device, mesh=mesh, in_specs=in_specs, out_specs=out_specs, check_vma=False
    )
```

```python
import functools
import math

import jax
import jax.numpy as jnp
from jax import lax
from jax.experimental import pallas as pl
from jax.experimental.pallas import tpu as pltpu
from jax.sharding import Mesh
from jax.sharding import PartitionSpec as P

HEAD = 64
GX = 16
GY = 16
CZ = 2
SLAB = ("y", "z", "xl")
FFN = ("xh", "core")


EPSILON = 1e-05
ROPE_BASE = 100.0
ROOT_HALF = 0.7071067811865476
NORMAL_SCALE = 0.3989422804014327


MESH = pl.DeviceIdType.MESH


def peer_id(p):
    return (p // 16, p // 2 % 8, p % 2, lax.axis_index("xh"), lax.axis_index("core"))


def gather_kernel(
    row_size, x_ref, out_ref, send_a, recv_a, send_b, recv_b, send_c, recv_c, local_sem
):
    me = lax.axis_index(SLAB)
    block = x_ref.shape[0]
    own_y, spot = me // row_size, me % row_size
    y_count = lax.psum(1, "y")
    barrier = pltpu.get_barrier_semaphore()

    def greet(k, carry):
        peer = own_y * row_size + lax.rem(spot + k, row_size)
        pl.semaphore_signal(barrier, inc=1, device_id=peer_id(peer), device_id_type=MESH)
        return carry

    lax.fori_loop(1, row_size, greet, 0)
    left_y = lax.rem(own_y + y_count - 1, y_count)
    right_y = lax.rem(own_y + 1, y_count)
    for other_y in (left_y, right_y):
        peer = other_y * row_size + spot
        pl.semaphore_signal(barrier, inc=1, device_id=peer_id(peer), device_id_type=MESH)
    pl.semaphore_wait(barrier, row_size + 1)

    def along_row(target, source):
        return pltpu.make_async_remote_copy(
            src_ref=x_ref,
            dst_ref=out_ref.at[pl.ds((own_y * row_size + source) * block, block)],
            send_sem=send_a.at[target],
            recv_sem=recv_a.at[source],
            device_id=peer_id(own_y * row_size + target),
            device_id_type=MESH,
        )

    def start_row(k, carry):
        along_row(lax.rem(spot + k, row_size), spot).start()
        return carry

    lax.fori_loop(1, row_size, start_row, 0)
    local = pltpu.make_async_copy(x_ref, out_ref.at[pl.ds(me * block, block)], local_sem)
    local.start()
    local.wait()

    def finish_row(k, carry):
        other = lax.rem(spot + k, row_size)
        along_row(other, spot).wait_send()
        along_row(other, other).wait_recv()
        return carry

    lax.fori_loop(1, row_size, finish_row, 0)
    row_rows = row_size * block

    def across(target_y, source_y):
        return pltpu.make_async_remote_copy(
            src_ref=out_ref.at[pl.ds(source_y * row_rows, row_rows)],
            dst_ref=out_ref.at[pl.ds(source_y * row_rows, row_rows)],
            send_sem=send_b.at[target_y],
            recv_sem=recv_b.at[source_y],
            device_id=peer_id(target_y * row_size + spot),
            device_id_type=MESH,
        )

    for other_y in (left_y, right_y):
        across(other_y, own_y).start()
    for other_y in (left_y, right_y):
        across(other_y, own_y).wait_send()
        across(other_y, other_y).wait_recv()
    half = row_rows // 2

    def forward(target_y, source_y, part):
        rows = pl.ds(source_y * row_rows + part * half, half)
        return pltpu.make_async_remote_copy(
            src_ref=out_ref.at[rows],
            dst_ref=out_ref.at[rows],
            send_sem=send_c.at[part],
            recv_sem=recv_c.at[part],
            device_id=peer_id(target_y * row_size + spot),
            device_id_type=MESH,
        )

    far_y = lax.rem(own_y + 2, y_count)
    forward(right_y, left_y, 0).start()
    forward(left_y, right_y, 1).start()
    forward(right_y, left_y, 0).wait_send()
    forward(left_y, right_y, 1).wait_send()
    forward(right_y, far_y, 0).wait_recv()
    forward(left_y, far_y, 1).wait_recv()


def slab_gather(x, count, row_size):
    rows, width = x.shape
    y_count = count // row_size
    assert y_count == 4
    return pl.pallas_call(
        functools.partial(gather_kernel, row_size),
        out_shape=jax.ShapeDtypeStruct((count * rows, width), x.dtype),
        in_specs=[pl.BlockSpec(memory_space=pltpu.VMEM)],
        out_specs=pl.BlockSpec(memory_space=pltpu.VMEM),
        scratch_shapes=[
            pltpu.SemaphoreType.DMA((row_size,)),
            pltpu.SemaphoreType.DMA((row_size,)),
            pltpu.SemaphoreType.DMA((y_count,)),
            pltpu.SemaphoreType.DMA((y_count,)),
            pltpu.SemaphoreType.DMA((2,)),
            pltpu.SemaphoreType.DMA((2,)),
            pltpu.SemaphoreType.DMA(()),
        ],
        compiler_params=pltpu.CompilerParams(collective_id=0, has_side_effects=True),
    )(x)


def head_peer(q):
    return (lax.axis_index("y"), lax.axis_index("z"), lax.axis_index("xl"), q // 2, q % 2)


def head_sum_kernel(count, part_ref, out_ref, slots, send_sem, recv_sem, send_back, recv_back):
    me = lax.axis_index(FFN)
    barrier = pltpu.get_barrier_semaphore()
    for k in range(1, count):
        pl.semaphore_signal(
            barrier, inc=1, device_id=head_peer(lax.rem(me + k, count)), device_id_type=MESH
        )
    pl.semaphore_wait(barrier, count - 1)

    def share(peer, source):
        return pltpu.make_async_remote_copy(
            src_ref=part_ref.at[peer],
            dst_ref=slots.at[source],
            send_sem=send_sem.at[peer],
            recv_sem=recv_sem.at[source],
            device_id=head_peer(peer),
            device_id_type=MESH,
        )

    def spread(peer, source):
        return pltpu.make_async_remote_copy(
            src_ref=out_ref.at[source],
            dst_ref=out_ref.at[source],
            send_sem=send_back.at[peer],
            recv_sem=recv_back.at[source],
            device_id=head_peer(peer),
            device_id_type=MESH,
        )

    peers = [lax.rem(me + k, count) for k in range(1, count)]
    for peer in peers:
        share(peer, me).start()
    total = part_ref[me].astype(jnp.float32)
    for peer in peers:
        share(peer, me).wait_send()
        share(peer, peer).wait_recv()
        total = total + slots[peer].astype(jnp.float32)
    out_ref[me] = total.astype(out_ref.dtype)
    for peer in peers:
        spread(peer, me).start()
    for peer in peers:
        spread(peer, me).wait_send()
        spread(peer, peer).wait_recv()


def head_sum(partial_value, count):
    rows, width = partial_value.shape
    parts = partial_value.astype(jnp.bfloat16).reshape(count, rows // count, width)
    summed = pl.pallas_call(
        functools.partial(head_sum_kernel, count),
        out_shape=jax.ShapeDtypeStruct(parts.shape, parts.dtype),
        in_specs=[pl.BlockSpec(memory_space=pltpu.VMEM)],
        out_specs=pl.BlockSpec(memory_space=pltpu.VMEM),
        scratch_shapes=[
            pltpu.VMEM(parts.shape, parts.dtype),
            pltpu.SemaphoreType.DMA((count,)),
            pltpu.SemaphoreType.DMA((count,)),
            pltpu.SemaphoreType.DMA((count,)),
            pltpu.SemaphoreType.DMA((count,)),
        ],
        compiler_params=pltpu.CompilerParams(collective_id=2, has_side_effects=True),
    )(parts)
    return summed.reshape(rows, width)


def scatter_kernel(
    row_size, g_ref, out_ref, slots_y, totals, sums, slots_row, send_a, recv_a, send_b, recv_b
):
    me = lax.axis_index(SLAB)
    own_y, spot = me // row_size, me % row_size
    y_count = lax.psum(1, "y")
    barrier = pltpu.get_barrier_semaphore()

    def greet(k, carry):
        peer = own_y * row_size + lax.rem(spot + k, row_size)
        pl.semaphore_signal(barrier, inc=1, device_id=peer_id(peer), device_id_type=MESH)
        return carry

    lax.fori_loop(1, row_size, greet, 0)
    others = [lax.rem(own_y + j, y_count) for j in range(1, y_count)]
    for other_y in others:
        pl.semaphore_signal(
            barrier, inc=1, device_id=peer_id(other_y * row_size + spot), device_id_type=MESH
        )
    pl.semaphore_wait(barrier, row_size + y_count - 2)

    def across(target_y, source_y):
        return pltpu.make_async_remote_copy(
            src_ref=g_ref.at[pl.ds(target_y * row_size, row_size)],
            dst_ref=slots_y.at[source_y],
            send_sem=send_a.at[target_y],
            recv_sem=recv_a.at[source_y],
            device_id=peer_id(target_y * row_size + spot),
            device_id_type=MESH,
        )

    for other_y in others:
        across(other_y, own_y).start()
    total = g_ref[pl.ds(own_y * row_size, row_size)].astype(jnp.float32)
    for other_y in others:
        across(other_y, own_y).wait_send()
        across(other_y, other_y).wait_recv()
        total = total + slots_y[other_y].astype(jnp.float32)
    totals[...] = total
    sums[...] = total.astype(sums.dtype)

    def along_row(target, source):
        return pltpu.make_async_remote_copy(
            src_ref=sums.at[target],
            dst_ref=slots_row.at[source],
            send_sem=send_b.at[target],
            recv_sem=recv_b.at[source],
            device_id=peer_id(own_y * row_size + target),
            device_id_type=MESH,
        )

    def start_row(k, carry):
        along_row(lax.rem(spot + k, row_size), spot).start()
        return carry

    lax.fori_loop(1, row_size, start_row, 0)
    out_ref[...] = totals[spot]

    def finish_row(k, carry):
        other = lax.rem(spot + k, row_size)
        along_row(other, spot).wait_send()
        along_row(other, other).wait_recv()
        out_ref[...] += slots_row[other].astype(jnp.float32)
        return carry

    lax.fori_loop(1, row_size, finish_row, 0)


def slab_scatter(g, count, row_size):
    total_rows, width = g.shape
    rows = total_rows // count
    y_count = count // row_size
    tile_rows = 16
    g = g.astype(jnp.bfloat16).reshape(count, tile_rows, rows * width // tile_rows)
    summed = pl.pallas_call(
        functools.partial(scatter_kernel, row_size),
        out_shape=jax.ShapeDtypeStruct(g.shape[1:], jnp.float32),
        in_specs=[pl.BlockSpec(memory_space=pltpu.VMEM)],
        out_specs=pl.BlockSpec(memory_space=pltpu.VMEM),
        scratch_shapes=[
            pltpu.VMEM((y_count, row_size) + g.shape[1:], g.dtype),
            pltpu.VMEM((row_size,) + g.shape[1:], jnp.float32),
            pltpu.VMEM((row_size,) + g.shape[1:], g.dtype),
            pltpu.VMEM((row_size,) + g.shape[1:], g.dtype),
            pltpu.SemaphoreType.DMA((y_count,)),
            pltpu.SemaphoreType.DMA((y_count,)),
            pltpu.SemaphoreType.DMA((row_size,)),
            pltpu.SemaphoreType.DMA((row_size,)),
        ],
        compiler_params=pltpu.CompilerParams(collective_id=1, has_side_effects=True),
    )(g)
    return summed.reshape(rows, width)


def attention_kernel(heads, q_tile, q_ref, kv_ref, out_ref):
    key_width = heads * HEAD
    score_scale = HEAD ** (-0.5)
    for head in range(heads):
        keys = kv_ref[:, head * HEAD : (head + 1) * HEAD]
        values = kv_ref[:, key_width + head * HEAD : key_width + (head + 1) * HEAD]
        for first in range(0, q_ref.shape[0], q_tile):
            queries = q_ref[first : first + q_tile, head * HEAD : (head + 1) * HEAD]
            scores = lax.dot_general(
                queries, keys, (((1,), (1,)), ((), ())), preferred_element_type=jnp.float32
            ) * score_scale
            top = jnp.max(scores, axis=1, keepdims=True)
            weights = jnp.exp(scores - top)
            row_sum = jnp.sum(weights, axis=1, keepdims=True)
            mixed = jnp.dot(
                weights.astype(jnp.bfloat16), values, preferred_element_type=jnp.float32
            )
            out_ref[first : first + q_tile, head * HEAD : (head + 1) * HEAD] = (
                mixed / row_sum
            ).astype(out_ref.dtype)


def attention(queries, kv, heads, q_tile=256):
    return pl.pallas_call(
        functools.partial(attention_kernel, heads, q_tile),
        out_shape=jax.ShapeDtypeStruct(queries.shape, jnp.bfloat16),
        in_specs=[pl.BlockSpec(memory_space=pltpu.VMEM)] * 2,
        out_specs=pl.BlockSpec(memory_space=pltpu.VMEM),
    )(queries, kv)


def halo_kernel(count, cells_ref, below_ref, above_ref, send_sem, recv_sem):
    me = lax.axis_index(SLAB)
    plane = below_ref.shape[0]
    after = lax.rem(me + 1, count)
    before = lax.rem(me + count - 1, count)
    barrier = pltpu.get_barrier_semaphore()
    for peer in (before, after):
        pl.semaphore_signal(barrier, inc=1, device_id=peer_id(peer), device_id_type=MESH)
    pl.semaphore_wait(barrier, 2)
    up = pltpu.make_async_remote_copy(
        src_ref=cells_ref.at[pl.ds(cells_ref.shape[0] - plane, plane)],
        dst_ref=below_ref,
        send_sem=send_sem.at[0],
        recv_sem=recv_sem.at[0],
        device_id=peer_id(after),
        device_id_type=MESH,
    )
    down = pltpu.make_async_remote_copy(
        src_ref=cells_ref.at[pl.ds(0, plane)],
        dst_ref=above_ref,
        send_sem=send_sem.at[1],
        recv_sem=recv_sem.at[1],
        device_id=peer_id(before),
        device_id_type=MESH,
    )
    up.start()
    down.start()
    up.wait()
    down.wait()


def halo_planes(cells, collective):
    count = lax.psum(1, SLAB)
    me = lax.axis_index(SLAB)
    plane_shape = cells.shape[1:]
    flat = cells.reshape(cells.shape[0] * math.prod(plane_shape[:-1]), plane_shape[-1])
    plane = flat.shape[0] // cells.shape[0]
    below, above = pl.pallas_call(
        functools.partial(halo_kernel, count),
        out_shape=[jax.ShapeDtypeStruct((plane, flat.shape[1]), flat.dtype)] * 2,
        in_specs=[pl.BlockSpec(memory_space=pltpu.VMEM)],
        out_specs=[pl.BlockSpec(memory_space=pltpu.VMEM)] * 2,
        scratch_shapes=[pltpu.SemaphoreType.DMA((2,)), pltpu.SemaphoreType.DMA((2,))],
        compiler_params=pltpu.CompilerParams(collective_id=collective, has_side_effects=True),
    )(flat)
    below = jnp.where(me > 0, below, jnp.zeros_like(below)).reshape((1,) + plane_shape)
    above = jnp.where(me < count - 1, above, jnp.zeros_like(above)).reshape((1,) + plane_shape)
    return jnp.concatenate([below, cells, above], axis=0)


def layer_norm(values, scale_gain):
    values = values.astype(jnp.float32)
    centered = values - jnp.mean(values, axis=-1, keepdims=True)
    variance = jnp.mean(centered * centered, axis=-1, keepdims=True)
    return centered * lax.rsqrt(variance + EPSILON) * scale_gain


def rope_tables(coord_x, coord_y, coord_z, head_size):
    pair_count = head_size // 2
    position = jnp.arange(pair_count, dtype=jnp.int32)
    axis_pick = position % 3
    per_axis = (pair_count + 2) // 3
    frequency = ROPE_BASE ** (-(position // 3).astype(jnp.float32) / per_axis)
    angles = (
        coord_x[:, None] * (axis_pick == 0)
        + coord_y[:, None] * (axis_pick == 1)
        + coord_z[:, None] * (axis_pick == 2)
    ) * frequency
    return (jnp.cos(angles)[:, None, :], jnp.sin(angles)[:, None, :])


def token_tables(first_plane, planes, head_size):
    position = jnp.arange(planes * GY * GX, dtype=jnp.int32)
    coord_x = (position % GX).astype(jnp.float32)
    coord_y = (position // GX % GY).astype(jnp.float32)
    coord_z = (first_plane + position // (GX * GY)).astype(jnp.float32)
    return rope_tables(coord_x, coord_y, coord_z, head_size)


def key_tables(first_row, row_count, head_size):
    position = first_row + jnp.arange(row_count, dtype=jnp.int32)
    half_x = GX // 2
    half_y = GY // 2
    coord_x = (position % half_x).astype(jnp.float32) * 2.0 + 0.5
    coord_y = (position // half_x % half_y).astype(jnp.float32) * 2.0 + 0.5
    coord_z = (position // (half_x * half_y)).astype(jnp.float32) * 2.0 + 0.5
    return rope_tables(coord_x, coord_y, coord_z, head_size)


def rotate(values, cosine, sine_table):
    half_size = values.shape[-1] // 2
    front_half = values[..., :half_size]
    back_half = values[..., half_size:]
    return jnp.concatenate(
        [
            front_half * cosine - back_half * sine_table,
            back_half * cosine + front_half * sine_table,
        ],
        axis=-1,
    )


def make_patches(normed, planes):
    width = normed.shape[-1]
    cell_grid = normed.reshape(planes // 2, 2, GY // 2, 2, GX // 2, 2, width)
    return cell_grid.transpose(0, 2, 4, 1, 3, 5, 6).reshape(-1, 8 * width)


def depth_conv(padded, weights, planes):
    height = padded.shape[1] - 2
    width_x = padded.shape[2] - 2
    result = jnp.zeros((planes, height, width_x, padded.shape[3]), jnp.float32)
    for offset in range(27):
        shift_z = offset // 9
        shift_y = offset // 3 % 3
        shift_x = offset % 3
        window = padded[
            shift_z : shift_z + planes, shift_y : shift_y + height, shift_x : shift_x + width_x
        ]
        result = result + window.astype(jnp.float32) * weights[offset]
    return result


def per_device(
    tokens,
    gain_attn,
    w_reduce,
    gain_keys,
    w_query,
    w_key,
    w_value,
    w_out,
    gain_ffn,
    w_up,
    w_depth,
    w_down,
    grad_out,
):
    slab_index = lax.axis_index(SLAB)
    tok_rows = tokens.shape[0]
    heads_dev = w_query.shape[1] // HEAD
    normed = layer_norm(tokens, gain_attn).astype(jnp.bfloat16)
    patches = make_patches(normed, CZ)
    reduced = jnp.dot(patches, w_reduce, preferred_element_type=jnp.float32)
    key_input = layer_norm(reduced, gain_keys).astype(jnp.bfloat16)
    tok_cos, tok_sin = token_tables(slab_index * CZ, CZ, HEAD)
    queries = jnp.dot(normed, w_query, preferred_element_type=jnp.float32).reshape(
        tok_rows, heads_dev, HEAD
    )
    queries = rotate(queries, tok_cos, tok_sin).astype(jnp.bfloat16)
    local_rows = key_input.shape[0]
    own_cos, own_sin = key_tables(slab_index * local_rows, local_rows, HEAD)
    own_keys = jnp.dot(key_input, w_key, preferred_element_type=jnp.float32).reshape(
        local_rows, heads_dev, HEAD
    )
    own_keys = rotate(own_keys, own_cos, own_sin).astype(jnp.bfloat16)
    own_values = jnp.dot(key_input, w_value, preferred_element_type=jnp.float32).astype(
        jnp.bfloat16
    )
    key_width = heads_dev * HEAD
    pieces = jnp.concatenate([own_keys.reshape(local_rows, key_width), own_values], axis=1)
    pieces = slab_gather(pieces, lax.psum(1, SLAB), lax.psum(1, ("z", "xl")))
    heads_out = attention(queries.reshape(tok_rows, key_width), pieces, heads_dev)
    partial_value = jnp.dot(heads_out, w_out, preferred_element_type=jnp.float32)
    head_total = head_sum(partial_value, lax.psum(1, FFN)).astype(jnp.float32)
    attended = head_total.astype(jnp.bfloat16)
    residual = tokens.astype(jnp.float32) + head_total
    normed_ffn = layer_norm(residual, gain_ffn).astype(jnp.bfloat16)
    channels = w_up.shape[1]
    pre = (
        jnp.dot(normed_ffn, w_up, preferred_element_type=jnp.float32)
        .astype(jnp.bfloat16)
        .reshape(CZ, GY, GX, channels)
    )
    pre_wide = halo_planes(pre, 3)
    pre_pad = jnp.pad(pre_wide, ((0, 0), (1, 1), (1, 1), (0, 0)))
    mixed = depth_conv(pre_pad, w_depth, CZ).reshape(tok_rows, channels)
    normal_cdf = 0.5 * (1.0 + lax.erf(mixed * ROOT_HALF))
    normal_pdf = jnp.exp(-0.5 * mixed * mixed) * NORMAL_SCALE
    activated = (mixed * normal_cdf).astype(jnp.bfloat16)
    grad_act = jnp.einsum("td,cd->tc", grad_out, w_down, preferred_element_type=jnp.float32)
    grad_mixed = (
        (grad_act * (normal_cdf + mixed * normal_pdf))
        .astype(jnp.bfloat16)
        .reshape(CZ, GY, GX, channels)
    )
    grad_wide = halo_planes(grad_mixed, 4)
    grad_pad = jnp.pad(grad_wide, ((0, 0), (1, 1), (1, 1), (0, 0)))
    grad_pre = (
        depth_conv(grad_pad, w_depth[::-1], CZ).astype(jnp.bfloat16).reshape(tok_rows, channels)
    )
    up_full = jnp.einsum("td,tc->dc", normed_ffn, grad_pre, preferred_element_type=jnp.float32)
    down_full = jnp.einsum("td,tc->dc", grad_out, activated, preferred_element_type=jnp.float32)
    grads = slab_scatter(
        jnp.concatenate([up_full, down_full], axis=1),
        lax.psum(1, SLAB),
        lax.psum(1, ("z", "xl")),
    )
    return (attended, grads[:, :channels], grads[:, channels:])


def solution(mesh):
    mesh = Mesh(mesh.devices.reshape(4, 8, 2, 2, 2), SLAB + FFN)
    in_specs = (
        P(SLAB, None),
        P(),
        P(),
        P(),
        P(None, FFN),
        P(None, FFN),
        P(None, FFN),
        P(FFN, None),
        P(),
        P(None, FFN),
        P(None, FFN),
        P(FFN, None),
        P(SLAB, None),
    )
    out_specs = (P(SLAB, None), P(SLAB, FFN), P(SLAB, FFN))
    return jax.shard_map(
        per_device, mesh=mesh, in_specs=in_specs, out_specs=out_specs, check_vma=False
    )
```

```python
import functools
import math

import jax
import jax.numpy as jnp
from jax import lax
from jax.experimental import pallas as pl
from jax.experimental.pallas import tpu as pltpu
from jax.sharding import Mesh
from jax.sharding import PartitionSpec as P

HEAD = 64
GX = 16
GY = 16
CZ = 2
SLAB = ("y", "z", "xl")
FFN = ("xh", "core")


EPSILON = 1e-05
ROPE_BASE = 100.0
ROOT_HALF = 0.7071067811865476
NORMAL_SCALE = 0.3989422804014327


MESH = pl.DeviceIdType.MESH


def peer_id(p):
    return (p // 16, p // 2 % 8, p % 2, lax.axis_index("xh"), lax.axis_index("core"))


def gather_kernel(
    row_size, x_ref, out_ref, send_a, recv_a, send_b, recv_b, send_c, recv_c, local_sem
):
    me = lax.axis_index(SLAB)
    block = x_ref.shape[0]
    own_y, spot = me // row_size, me % row_size
    y_count = lax.psum(1, "y")
    barrier = pltpu.get_barrier_semaphore()

    def greet(k, carry):
        peer = own_y * row_size + lax.rem(spot + k, row_size)
        pl.semaphore_signal(barrier, inc=1, device_id=peer_id(peer), device_id_type=MESH)
        return carry

    lax.fori_loop(1, row_size, greet, 0)
    left_y = lax.rem(own_y + y_count - 1, y_count)
    right_y = lax.rem(own_y + 1, y_count)
    for other_y in (left_y, right_y):
        peer = other_y * row_size + spot
        pl.semaphore_signal(barrier, inc=1, device_id=peer_id(peer), device_id_type=MESH)
    pl.semaphore_wait(barrier, row_size + 1)

    def along_row(target, source):
        return pltpu.make_async_remote_copy(
            src_ref=x_ref,
            dst_ref=out_ref.at[pl.ds((own_y * row_size + source) * block, block)],
            send_sem=send_a.at[target],
            recv_sem=recv_a.at[source],
            device_id=peer_id(own_y * row_size + target),
            device_id_type=MESH,
        )

    def start_row(k, carry):
        along_row(lax.rem(spot + k, row_size), spot).start()
        return carry

    lax.fori_loop(1, row_size, start_row, 0)
    local = pltpu.make_async_copy(x_ref, out_ref.at[pl.ds(me * block, block)], local_sem)
    local.start()
    local.wait()

    def finish_row(k, carry):
        other = lax.rem(spot + k, row_size)
        along_row(other, spot).wait_send()
        along_row(other, other).wait_recv()
        return carry

    lax.fori_loop(1, row_size, finish_row, 0)
    row_rows = row_size * block

    def across(target_y, source_y):
        return pltpu.make_async_remote_copy(
            src_ref=out_ref.at[pl.ds(source_y * row_rows, row_rows)],
            dst_ref=out_ref.at[pl.ds(source_y * row_rows, row_rows)],
            send_sem=send_b.at[target_y],
            recv_sem=recv_b.at[source_y],
            device_id=peer_id(target_y * row_size + spot),
            device_id_type=MESH,
        )

    for other_y in (left_y, right_y):
        across(other_y, own_y).start()
    for other_y in (left_y, right_y):
        across(other_y, own_y).wait_send()
        across(other_y, other_y).wait_recv()
    half = row_rows // 2

    def forward(target_y, source_y, part):
        rows = pl.ds(source_y * row_rows + part * half, half)
        return pltpu.make_async_remote_copy(
            src_ref=out_ref.at[rows],
            dst_ref=out_ref.at[rows],
            send_sem=send_c.at[part],
            recv_sem=recv_c.at[part],
            device_id=peer_id(target_y * row_size + spot),
            device_id_type=MESH,
        )

    far_y = lax.rem(own_y + 2, y_count)
    forward(right_y, left_y, 0).start()
    forward(left_y, right_y, 1).start()
    forward(right_y, left_y, 0).wait_send()
    forward(left_y, right_y, 1).wait_send()
    forward(right_y, far_y, 0).wait_recv()
    forward(left_y, far_y, 1).wait_recv()


def slab_gather(x, count, row_size):
    rows, width = x.shape
    y_count = count // row_size
    assert y_count == 4
    return pl.pallas_call(
        functools.partial(gather_kernel, row_size),
        out_shape=jax.ShapeDtypeStruct((count * rows, width), x.dtype),
        in_specs=[pl.BlockSpec(memory_space=pltpu.VMEM)],
        out_specs=pl.BlockSpec(memory_space=pltpu.VMEM),
        scratch_shapes=[
            pltpu.SemaphoreType.DMA((row_size,)),
            pltpu.SemaphoreType.DMA((row_size,)),
            pltpu.SemaphoreType.DMA((y_count,)),
            pltpu.SemaphoreType.DMA((y_count,)),
            pltpu.SemaphoreType.DMA((2,)),
            pltpu.SemaphoreType.DMA((2,)),
            pltpu.SemaphoreType.DMA(()),
        ],
        compiler_params=pltpu.CompilerParams(collective_id=0, has_side_effects=True),
    )(x)


def head_peer(q):
    return (lax.axis_index("y"), lax.axis_index("z"), lax.axis_index("xl"), q // 2, q % 2)


def head_sum_kernel(count, part_ref, out_ref, slots, send_sem, recv_sem, send_back, recv_back):
    me = lax.axis_index(FFN)
    barrier = pltpu.get_barrier_semaphore()
    for k in range(1, count):
        pl.semaphore_signal(
            barrier, inc=1, device_id=head_peer(lax.rem(me + k, count)), device_id_type=MESH
        )
    pl.semaphore_wait(barrier, count - 1)

    def share(peer, source):
        return pltpu.make_async_remote_copy(
            src_ref=part_ref.at[peer],
            dst_ref=slots.at[source],
            send_sem=send_sem.at[peer],
            recv_sem=recv_sem.at[source],
            device_id=head_peer(peer),
            device_id_type=MESH,
        )

    def spread(peer, source):
        return pltpu.make_async_remote_copy(
            src_ref=out_ref.at[source],
            dst_ref=out_ref.at[source],
            send_sem=send_back.at[peer],
            recv_sem=recv_back.at[source],
            device_id=head_peer(peer),
            device_id_type=MESH,
        )

    peers = [lax.rem(me + k, count) for k in range(1, count)]
    for peer in peers:
        share(peer, me).start()
    total = part_ref[me].astype(jnp.float32)
    for peer in peers:
        share(peer, me).wait_send()
        share(peer, peer).wait_recv()
        total = total + slots[peer].astype(jnp.float32)
    out_ref[me] = total.astype(out_ref.dtype)
    for peer in peers:
        spread(peer, me).start()
    for peer in peers:
        spread(peer, me).wait_send()
        spread(peer, peer).wait_recv()


def head_sum(partial_value, count):
    rows, width = partial_value.shape
    parts = partial_value.astype(jnp.bfloat16).reshape(count, rows // count, width)
    summed = pl.pallas_call(
        functools.partial(head_sum_kernel, count),
        out_shape=jax.ShapeDtypeStruct(parts.shape, parts.dtype),
        in_specs=[pl.BlockSpec(memory_space=pltpu.VMEM)],
        out_specs=pl.BlockSpec(memory_space=pltpu.VMEM),
        scratch_shapes=[
            pltpu.VMEM(parts.shape, parts.dtype),
            pltpu.SemaphoreType.DMA((count,)),
            pltpu.SemaphoreType.DMA((count,)),
            pltpu.SemaphoreType.DMA((count,)),
            pltpu.SemaphoreType.DMA((count,)),
        ],
        compiler_params=pltpu.CompilerParams(collective_id=2, has_side_effects=True),
    )(parts)
    return summed.reshape(rows, width)


def scatter_kernel(
    row_size, g_ref, out_ref, slots_y, totals, sums, slots_row, send_a, recv_a, send_b, recv_b
):
    me = lax.axis_index(SLAB)
    own_y, spot = me // row_size, me % row_size
    y_count = lax.psum(1, "y")
    barrier = pltpu.get_barrier_semaphore()

    def greet(k, carry):
        peer = own_y * row_size + lax.rem(spot + k, row_size)
        pl.semaphore_signal(barrier, inc=1, device_id=peer_id(peer), device_id_type=MESH)
        return carry

    lax.fori_loop(1, row_size, greet, 0)
    others = [lax.rem(own_y + j, y_count) for j in range(1, y_count)]
    for other_y in others:
        pl.semaphore_signal(
            barrier, inc=1, device_id=peer_id(other_y * row_size + spot), device_id_type=MESH
        )
    pl.semaphore_wait(barrier, row_size + y_count - 2)

    def across(target_y, source_y):
        return pltpu.make_async_remote_copy(
            src_ref=g_ref.at[pl.ds(target_y * row_size, row_size)],
            dst_ref=slots_y.at[source_y],
            send_sem=send_a.at[target_y],
            recv_sem=recv_a.at[source_y],
            device_id=peer_id(target_y * row_size + spot),
            device_id_type=MESH,
        )

    for other_y in others:
        across(other_y, own_y).start()
    total = g_ref[pl.ds(own_y * row_size, row_size)].astype(jnp.float32)
    for other_y in others:
        across(other_y, own_y).wait_send()
        across(other_y, other_y).wait_recv()
        total = total + slots_y[other_y].astype(jnp.float32)
    totals[...] = total
    sums[...] = total.astype(sums.dtype)

    def along_row(target, source):
        return pltpu.make_async_remote_copy(
            src_ref=sums.at[target],
            dst_ref=slots_row.at[source],
            send_sem=send_b.at[target],
            recv_sem=recv_b.at[source],
            device_id=peer_id(own_y * row_size + target),
            device_id_type=MESH,
        )

    def start_row(k, carry):
        along_row(lax.rem(spot + k, row_size), spot).start()
        return carry

    lax.fori_loop(1, row_size, start_row, 0)
    out_ref[...] = totals[spot]

    def finish_row(k, carry):
        other = lax.rem(spot + k, row_size)
        along_row(other, spot).wait_send()
        along_row(other, other).wait_recv()
        out_ref[...] += slots_row[other].astype(jnp.float32)
        return carry

    lax.fori_loop(1, row_size, finish_row, 0)


def slab_scatter(g, count, row_size):
    total_rows, width = g.shape
    rows = total_rows // count
    y_count = count // row_size
    tile_rows = 16
    g = g.astype(jnp.bfloat16).reshape(count, tile_rows, rows * width // tile_rows)
    summed = pl.pallas_call(
        functools.partial(scatter_kernel, row_size),
        out_shape=jax.ShapeDtypeStruct(g.shape[1:], jnp.float32),
        in_specs=[pl.BlockSpec(memory_space=pltpu.VMEM)],
        out_specs=pl.BlockSpec(memory_space=pltpu.VMEM),
        scratch_shapes=[
            pltpu.VMEM((y_count, row_size) + g.shape[1:], g.dtype),
            pltpu.VMEM((row_size,) + g.shape[1:], jnp.float32),
            pltpu.VMEM((row_size,) + g.shape[1:], g.dtype),
            pltpu.VMEM((row_size,) + g.shape[1:], g.dtype),
            pltpu.SemaphoreType.DMA((y_count,)),
            pltpu.SemaphoreType.DMA((y_count,)),
            pltpu.SemaphoreType.DMA((row_size,)),
            pltpu.SemaphoreType.DMA((row_size,)),
        ],
        compiler_params=pltpu.CompilerParams(collective_id=1, has_side_effects=True),
    )(g)
    return summed.reshape(rows, width)


def attention_kernel(heads, q_tile, q_ref, kv_ref, out_ref):
    key_width = heads * HEAD
    score_scale = HEAD ** (-0.5)
    for head in range(heads):
        keys = kv_ref[:, head * HEAD : (head + 1) * HEAD]
        values = kv_ref[:, key_width + head * HEAD : key_width + (head + 1) * HEAD]
        for first in range(0, q_ref.shape[0], q_tile):
            queries = q_ref[first : first + q_tile, head * HEAD : (head + 1) * HEAD]
            scores = lax.dot_general(
                queries, keys, (((1,), (1,)), ((), ())), preferred_element_type=jnp.float32
            ) * score_scale
            top = jnp.max(scores, axis=1, keepdims=True)
            weights = jnp.exp(scores - top)
            row_sum = jnp.sum(weights, axis=1, keepdims=True)
            mixed = jnp.dot(
                weights.astype(jnp.bfloat16), values, preferred_element_type=jnp.float32
            )
            out_ref[first : first + q_tile, head * HEAD : (head + 1) * HEAD] = (
                mixed / row_sum
            ).astype(out_ref.dtype)


def attention(queries, kv, heads, q_tile=256):
    return pl.pallas_call(
        functools.partial(attention_kernel, heads, q_tile),
        out_shape=jax.ShapeDtypeStruct(queries.shape, jnp.bfloat16),
        in_specs=[pl.BlockSpec(memory_space=pltpu.VMEM)] * 2,
        out_specs=pl.BlockSpec(memory_space=pltpu.VMEM),
    )(queries, kv)


def padded_2(cells, sides, width):
    for axis, dim in sides:
        count = lax.psum(1, axis)
        ends = count - 1
        head = lax.slice_in_dim(cells, 0, width, axis=dim)
        tail = lax.slice_in_dim(cells, cells.shape[dim] - width, cells.shape[dim], axis=dim)
        cells = jnp.concatenate(
            [
                lax.ppermute(tail, axis, [(i, (i + 1) % count) for i in range(ends)]),
                cells,
                lax.ppermute(head, axis, [((i + 1) % count, i) for i in range(ends)]),
            ],
            axis=dim,
        )
    return cells


def layer_norm(values, scale_gain):
    values = values.astype(jnp.float32)
    centered = values - jnp.mean(values, axis=-1, keepdims=True)
    variance = jnp.mean(centered * centered, axis=-1, keepdims=True)
    return centered * lax.rsqrt(variance + EPSILON) * scale_gain


def rope_tables(coord_x, coord_y, coord_z, head_size):
    pair_count = head_size // 2
    position = jnp.arange(pair_count, dtype=jnp.int32)
    axis_pick = position % 3
    per_axis = (pair_count + 2) // 3
    frequency = ROPE_BASE ** (-(position // 3).astype(jnp.float32) / per_axis)
    angles = (
        coord_x[:, None] * (axis_pick == 0)
        + coord_y[:, None] * (axis_pick == 1)
        + coord_z[:, None] * (axis_pick == 2)
    ) * frequency
    return (jnp.cos(angles)[:, None, :], jnp.sin(angles)[:, None, :])


def token_tables(first_plane, planes, head_size):
    position = jnp.arange(planes * GY * GX, dtype=jnp.int32)
    coord_x = (position % GX).astype(jnp.float32)
    coord_y = (position // GX % GY).astype(jnp.float32)
    coord_z = (first_plane + position // (GX * GY)).astype(jnp.float32)
    return rope_tables(coord_x, coord_y, coord_z, head_size)


def key_tables(first_row, row_count, head_size):
    position = first_row + jnp.arange(row_count, dtype=jnp.int32)
    half_x = GX // 2
    half_y = GY // 2
    coord_x = (position % half_x).astype(jnp.float32) * 2.0 + 0.5
    coord_y = (position // half_x % half_y).astype(jnp.float32) * 2.0 + 0.5
    coord_z = (position // (half_x * half_y)).astype(jnp.float32) * 2.0 + 0.5
    return rope_tables(coord_x, coord_y, coord_z, head_size)


def rotate(values, cosine, sine_table):
    half_size = values.shape[-1] // 2
    front_half = values[..., :half_size]
    back_half = values[..., half_size:]
    return jnp.concatenate(
        [
            front_half * cosine - back_half * sine_table,
            back_half * cosine + front_half * sine_table,
        ],
        axis=-1,
    )


def make_patches(normed, planes):
    width = normed.shape[-1]
    cell_grid = normed.reshape(planes // 2, 2, GY // 2, 2, GX // 2, 2, width)
    return cell_grid.transpose(0, 2, 4, 1, 3, 5, 6).reshape(-1, 8 * width)


def depth_conv(padded, weights, planes):
    height = padded.shape[1] - 2
    width_x = padded.shape[2] - 2
    result = jnp.zeros((planes, height, width_x, padded.shape[3]), jnp.float32)
    for offset in range(27):
        shift_z = offset // 9
        shift_y = offset // 3 % 3
        shift_x = offset % 3
        window = padded[
            shift_z : shift_z + planes, shift_y : shift_y + height, shift_x : shift_x + width_x
        ]
        result = result + window.astype(jnp.float32) * weights[offset]
    return result


def per_device(
    tokens,
    gain_attn,
    w_reduce,
    gain_keys,
    w_query,
    w_key,
    w_value,
    w_out,
    gain_ffn,
    w_up,
    w_depth,
    w_down,
    grad_out,
):
    slab_index = lax.axis_index(SLAB)
    tok_rows = tokens.shape[0]
    heads_dev = w_query.shape[1] // HEAD
    normed = layer_norm(tokens, gain_attn).astype(jnp.bfloat16)
    patches = make_patches(normed, CZ)
    reduced = jnp.dot(patches, w_reduce, preferred_element_type=jnp.float32)
    key_input = layer_norm(reduced, gain_keys).astype(jnp.bfloat16)
    tok_cos, tok_sin = token_tables(slab_index * CZ, CZ, HEAD)
    queries = jnp.dot(normed, w_query, preferred_element_type=jnp.float32).reshape(
        tok_rows, heads_dev, HEAD
    )
    queries = rotate(queries, tok_cos, tok_sin).astype(jnp.bfloat16)
    local_rows = key_input.shape[0]
    own_cos, own_sin = key_tables(slab_index * local_rows, local_rows, HEAD)
    own_keys = jnp.dot(key_input, w_key, preferred_element_type=jnp.float32).reshape(
        local_rows, heads_dev, HEAD
    )
    own_keys = rotate(own_keys, own_cos, own_sin).astype(jnp.bfloat16)
    own_values = jnp.dot(key_input, w_value, preferred_element_type=jnp.float32).astype(
        jnp.bfloat16
    )
    key_width = heads_dev * HEAD
    pieces = jnp.concatenate([own_keys.reshape(local_rows, key_width), own_values], axis=1)
    pieces = slab_gather(pieces, lax.psum(1, SLAB), lax.psum(1, ("z", "xl")))
    heads_out = attention(queries.reshape(tok_rows, key_width), pieces, heads_dev)
    partial_value = jnp.dot(heads_out, w_out, preferred_element_type=jnp.float32)
    head_total = head_sum(partial_value, lax.psum(1, FFN)).astype(jnp.float32)
    attended = head_total.astype(jnp.bfloat16)
    residual = tokens.astype(jnp.float32) + head_total
    normed_ffn = layer_norm(residual, gain_ffn).astype(jnp.bfloat16)
    channels = w_up.shape[1]
    pre = (
        jnp.dot(normed_ffn, w_up, preferred_element_type=jnp.float32)
        .astype(jnp.bfloat16)
        .reshape(CZ, GY, GX, channels)
    )
    plane_rows = GY * GX
    pre_wide = padded_2(pre, ((SLAB, 0),), CZ)
    pre_pad = jnp.pad(pre_wide, ((0, 0), (1, 1), (1, 1), (0, 0)))
    mixed_wide = depth_conv(pre_pad, w_depth, CZ + 2).reshape(-1, channels)
    normal_cdf = 0.5 * (1.0 + lax.erf(mixed_wide * ROOT_HALF))
    normal_pdf = jnp.exp(-0.5 * mixed_wide * mixed_wide) * NORMAL_SCALE
    mixed = mixed_wide[plane_rows : plane_rows + tok_rows]
    activated = (mixed * normal_cdf[plane_rows : plane_rows + tok_rows]).astype(jnp.bfloat16)
    grad_out_wide = padded_2(grad_out, ((SLAB, 0),), plane_rows)
    grad_act = jnp.einsum(
        "td,cd->tc", grad_out_wide, w_down, preferred_element_type=jnp.float32
    )
    grad_mixed = (
        (grad_act * (normal_cdf + mixed_wide * normal_pdf))
        .astype(jnp.bfloat16)
        .reshape(CZ + 2, GY, GX, channels)
    )
    grad_pad = jnp.pad(grad_mixed, ((0, 0), (1, 1), (1, 1), (0, 0)))
    grad_pre = (
        depth_conv(grad_pad, w_depth[::-1], CZ).astype(jnp.bfloat16).reshape(tok_rows, channels)
    )
    up_full = jnp.einsum("td,tc->dc", normed_ffn, grad_pre, preferred_element_type=jnp.float32)
    down_full = jnp.einsum("td,tc->dc", grad_out, activated, preferred_element_type=jnp.float32)
    grads = slab_scatter(
        jnp.concatenate([up_full, down_full], axis=1),
        lax.psum(1, SLAB),
        lax.psum(1, ("z", "xl")),
    )
    return (attended, grads[:, :channels], grads[:, channels:])


def solution(mesh):
    mesh = Mesh(mesh.devices.reshape(4, 8, 2, 2, 2), SLAB + FFN)
    in_specs = (
        P(SLAB, None),
        P(),
        P(),
        P(),
        P(None, FFN),
        P(None, FFN),
        P(None, FFN),
        P(FFN, None),
        P(),
        P(None, FFN),
        P(None, FFN),
        P(FFN, None),
        P(SLAB, None),
    )
    out_specs = (P(SLAB, None), P(SLAB, FFN), P(SLAB, FFN))
    return jax.shard_map(
        per_device, mesh=mesh, in_specs=in_specs, out_specs=out_specs, check_vma=False
    )
```

```python
import functools
import math

import jax
import jax.numpy as jnp
from jax import lax
from jax.experimental import pallas as pl
from jax.experimental.pallas import tpu as pltpu
from jax.sharding import Mesh
from jax.sharding import PartitionSpec as P

HEAD = 64
GX = 16
GY = 16
CZ = 2
SLAB = ("y", "z", "xl")
FFN = ("xh", "core")


EPSILON = 1e-05
ROPE_BASE = 100.0
ROOT_HALF = 0.7071067811865476
NORMAL_SCALE = 0.3989422804014327


MESH = pl.DeviceIdType.MESH


def peer_id(p):
    return (p // 16, p // 2 % 8, p % 2, lax.axis_index("xh"), lax.axis_index("core"))


def gather_kernel(
    row_size, x_ref, out_ref, send_a, recv_a, send_l, recv_l, send_r, recv_r, send_f, recv_f,
    local_sem,
):
    me = lax.axis_index(SLAB)
    block = x_ref.shape[0]
    own_y, spot = me // row_size, me % row_size
    y_count = lax.psum(1, "y")
    half = row_size // 2
    left_y = lax.rem(own_y + y_count - 1, y_count)
    right_y = lax.rem(own_y + 1, y_count)
    far_y = lax.rem(own_y + 2, y_count)
    barrier = pltpu.get_barrier_semaphore()

    def greet(k, carry):
        peer = own_y * row_size + lax.rem(spot + k, row_size)
        pl.semaphore_signal(barrier, inc=1, device_id=peer_id(peer), device_id_type=MESH)
        return carry

    lax.fori_loop(1, row_size, greet, 0)
    for other_y in (left_y, right_y):
        peer = other_y * row_size + spot
        pl.semaphore_signal(barrier, inc=1, device_id=peer_id(peer), device_id_type=MESH)
    pl.semaphore_wait(barrier, row_size + 1)

    def piece(row_y, index):
        return out_ref.at[pl.ds((row_y * row_size + index) * block, block)]

    def along_row(target, source):
        return pltpu.make_async_remote_copy(
            src_ref=x_ref,
            dst_ref=piece(own_y, source),
            send_sem=send_a.at[target],
            recv_sem=recv_a.at[source],
            device_id=peer_id(own_y * row_size + target),
            device_id_type=MESH,
        )

    def sideways(target_y, row_y, index, send_sem, recv_sem):
        return pltpu.make_async_remote_copy(
            src_ref=piece(row_y, index),
            dst_ref=piece(row_y, index),
            send_sem=send_sem.at[index],
            recv_sem=recv_sem.at[index],
            device_id=peer_id(target_y * row_size + spot),
            device_id_type=MESH,
        )

    def to_left(row_y, index):
        return sideways(left_y, row_y, index, send_l, recv_r)

    def to_right(row_y, index):
        return sideways(right_y, row_y, index, send_r, recv_l)

    def start_row(k, carry):
        along_row(lax.rem(spot + k, row_size), spot).start()
        return carry

    lax.fori_loop(1, row_size, start_row, 0)
    local = pltpu.make_async_copy(x_ref, piece(own_y, spot), local_sem)
    local.start()
    local.wait()
    to_left(own_y, spot).start()
    to_right(own_y, spot).start()

    def pass_row(k, carry):
        other = lax.rem(spot + k, row_size)
        along_row(other, other).wait_recv()
        to_left(own_y, other).start()
        to_right(own_y, other).start()
        return carry

    lax.fori_loop(1, row_size, pass_row, 0)

    def from_left(index):
        return sideways(right_y, left_y, index, send_f, recv_f)

    def from_right(index):
        return sideways(left_y, right_y, index, send_f, recv_f)

    def pass_low(index, carry):
        to_right(left_y, index).wait_recv()
        from_left(index).start()
        to_left(right_y, index).wait_recv()
        return carry

    def pass_high(index, carry):
        to_left(right_y, index).wait_recv()
        from_right(index).start()
        to_right(left_y, index).wait_recv()
        return carry

    lax.fori_loop(0, half, pass_low, 0)
    lax.fori_loop(half, row_size, pass_high, 0)

    def finish(index, carry):
        sideways(left_y, far_y, index, send_f, recv_f).wait_recv()
        to_left(own_y, index).wait_send()
        to_right(own_y, index).wait_send()
        return carry

    lax.fori_loop(0, row_size, finish, 0)

    def finish_row(k, carry):
        along_row(lax.rem(spot + k, row_size), spot).wait_send()
        return carry

    lax.fori_loop(1, row_size, finish_row, 0)

    def finish_low(index, carry):
        from_left(index).wait_send()
        return carry

    def finish_high(index, carry):
        from_right(index).wait_send()
        return carry

    lax.fori_loop(0, half, finish_low, 0)
    lax.fori_loop(half, row_size, finish_high, 0)


def slab_gather(x, count, row_size):
    rows, width = x.shape
    y_count = count // row_size
    assert y_count == 4
    return pl.pallas_call(
        functools.partial(gather_kernel, row_size),
        out_shape=jax.ShapeDtypeStruct((count * rows, width), x.dtype),
        in_specs=[pl.BlockSpec(memory_space=pltpu.VMEM)],
        out_specs=pl.BlockSpec(memory_space=pltpu.VMEM),
        scratch_shapes=[pltpu.SemaphoreType.DMA((row_size,))] * 8
        + [pltpu.SemaphoreType.DMA(())],
        compiler_params=pltpu.CompilerParams(collective_id=0, has_side_effects=True),
    )(x)


def head_peer(q):
    return (lax.axis_index("y"), lax.axis_index("z"), lax.axis_index("xl"), q // 2, q % 2)


def head_sum_kernel(count, part_ref, out_ref, slots, send_sem, recv_sem, send_back, recv_back):
    me = lax.axis_index(FFN)
    barrier = pltpu.get_barrier_semaphore()
    for k in range(1, count):
        pl.semaphore_signal(
            barrier, inc=1, device_id=head_peer(lax.rem(me + k, count)), device_id_type=MESH
        )
    pl.semaphore_wait(barrier, count - 1)

    def share(peer, source):
        return pltpu.make_async_remote_copy(
            src_ref=part_ref.at[peer],
            dst_ref=slots.at[source],
            send_sem=send_sem.at[peer],
            recv_sem=recv_sem.at[source],
            device_id=head_peer(peer),
            device_id_type=MESH,
        )

    def spread(peer, source):
        return pltpu.make_async_remote_copy(
            src_ref=out_ref.at[source],
            dst_ref=out_ref.at[source],
            send_sem=send_back.at[peer],
            recv_sem=recv_back.at[source],
            device_id=head_peer(peer),
            device_id_type=MESH,
        )

    peers = [lax.rem(me + k, count) for k in range(1, count)]
    for peer in peers:
        share(peer, me).start()
    total = part_ref[me].astype(jnp.float32)
    for peer in peers:
        share(peer, me).wait_send()
        share(peer, peer).wait_recv()
        total = total + slots[peer].astype(jnp.float32)
    out_ref[me] = total.astype(out_ref.dtype)
    for peer in peers:
        spread(peer, me).start()
    for peer in peers:
        spread(peer, me).wait_send()
        spread(peer, peer).wait_recv()


def head_sum(partial_value, count):
    rows, width = partial_value.shape
    parts = partial_value.astype(jnp.bfloat16).reshape(count, rows // count, width)
    summed = pl.pallas_call(
        functools.partial(head_sum_kernel, count),
        out_shape=jax.ShapeDtypeStruct(parts.shape, parts.dtype),
        in_specs=[pl.BlockSpec(memory_space=pltpu.VMEM)],
        out_specs=pl.BlockSpec(memory_space=pltpu.VMEM),
        scratch_shapes=[
            pltpu.VMEM(parts.shape, parts.dtype),
            pltpu.SemaphoreType.DMA((count,)),
            pltpu.SemaphoreType.DMA((count,)),
            pltpu.SemaphoreType.DMA((count,)),
            pltpu.SemaphoreType.DMA((count,)),
        ],
        compiler_params=pltpu.CompilerParams(collective_id=2, has_side_effects=True),
    )(parts)
    return summed.reshape(rows, width)


def scatter_kernel(
    row_size, g_ref, out_ref, slots_y, totals, sums, slots_row, send_a, recv_a, send_b, recv_b
):
    me = lax.axis_index(SLAB)
    own_y, spot = me // row_size, me % row_size
    y_count = lax.psum(1, "y")
    barrier = pltpu.get_barrier_semaphore()

    def greet(k, carry):
        peer = own_y * row_size + lax.rem(spot + k, row_size)
        pl.semaphore_signal(barrier, inc=1, device_id=peer_id(peer), device_id_type=MESH)
        return carry

    lax.fori_loop(1, row_size, greet, 0)
    others = [lax.rem(own_y + j, y_count) for j in range(1, y_count)]
    for other_y in others:
        pl.semaphore_signal(
            barrier, inc=1, device_id=peer_id(other_y * row_size + spot), device_id_type=MESH
        )
    pl.semaphore_wait(barrier, row_size + y_count - 2)

    def across(target_y, source_y):
        return pltpu.make_async_remote_copy(
            src_ref=g_ref.at[pl.ds(target_y * row_size, row_size)],
            dst_ref=slots_y.at[source_y],
            send_sem=send_a.at[target_y],
            recv_sem=recv_a.at[source_y],
            device_id=peer_id(target_y * row_size + spot),
            device_id_type=MESH,
        )

    for other_y in others:
        across(other_y, own_y).start()
    total = g_ref[pl.ds(own_y * row_size, row_size)].astype(jnp.float32)
    for other_y in others:
        across(other_y, own_y).wait_send()
        across(other_y, other_y).wait_recv()
        total = total + slots_y[other_y].astype(jnp.float32)
    totals[...] = total
    sums[...] = total.astype(sums.dtype)

    def along_row(target, source):
        return pltpu.make_async_remote_copy(
            src_ref=sums.at[target],
            dst_ref=slots_row.at[source],
            send_sem=send_b.at[target],
            recv_sem=recv_b.at[source],
            device_id=peer_id(own_y * row_size + target),
            device_id_type=MESH,
        )

    def start_row(k, carry):
        along_row(lax.rem(spot + k, row_size), spot).start()
        return carry

    lax.fori_loop(1, row_size, start_row, 0)
    out_ref[...] = totals[spot]

    def finish_row(k, carry):
        other = lax.rem(spot + k, row_size)
        along_row(other, spot).wait_send()
        along_row(other, other).wait_recv()
        out_ref[...] += slots_row[other].astype(jnp.float32)
        return carry

    lax.fori_loop(1, row_size, finish_row, 0)


def slab_scatter(g, count, row_size):
    total_rows, width = g.shape
    rows = total_rows // count
    y_count = count // row_size
    tile_rows = 16
    g = g.astype(jnp.bfloat16).reshape(count, tile_rows, rows * width // tile_rows)
    summed = pl.pallas_call(
        functools.partial(scatter_kernel, row_size),
        out_shape=jax.ShapeDtypeStruct(g.shape[1:], jnp.float32),
        in_specs=[pl.BlockSpec(memory_space=pltpu.VMEM)],
        out_specs=pl.BlockSpec(memory_space=pltpu.VMEM),
        scratch_shapes=[
            pltpu.VMEM((y_count, row_size) + g.shape[1:], g.dtype),
            pltpu.VMEM((row_size,) + g.shape[1:], jnp.float32),
            pltpu.VMEM((row_size,) + g.shape[1:], g.dtype),
            pltpu.VMEM((row_size,) + g.shape[1:], g.dtype),
            pltpu.SemaphoreType.DMA((y_count,)),
            pltpu.SemaphoreType.DMA((y_count,)),
            pltpu.SemaphoreType.DMA((row_size,)),
            pltpu.SemaphoreType.DMA((row_size,)),
        ],
        compiler_params=pltpu.CompilerParams(collective_id=1, has_side_effects=True),
    )(g)
    return summed.reshape(rows, width)


def attention_kernel(heads, q_tile, q_ref, kv_ref, out_ref):
    key_width = heads * HEAD
    score_scale = HEAD ** (-0.5)
    for head in range(heads):
        keys = kv_ref[:, head * HEAD : (head + 1) * HEAD]
        values = kv_ref[:, key_width + head * HEAD : key_width + (head + 1) * HEAD]
        for first in range(0, q_ref.shape[0], q_tile):
            queries = q_ref[first : first + q_tile, head * HEAD : (head + 1) * HEAD]
            scores = lax.dot_general(
                queries, keys, (((1,), (1,)), ((), ())), preferred_element_type=jnp.float32
            ) * score_scale
            top = jnp.max(scores, axis=1, keepdims=True)
            weights = jnp.exp(scores - top)
            row_sum = jnp.sum(weights, axis=1, keepdims=True)
            mixed = jnp.dot(
                weights.astype(jnp.bfloat16), values, preferred_element_type=jnp.float32
            )
            out_ref[first : first + q_tile, head * HEAD : (head + 1) * HEAD] = (
                mixed / row_sum
            ).astype(out_ref.dtype)


def attention(queries, kv, heads, q_tile=256):
    return pl.pallas_call(
        functools.partial(attention_kernel, heads, q_tile),
        out_shape=jax.ShapeDtypeStruct(queries.shape, jnp.bfloat16),
        in_specs=[pl.BlockSpec(memory_space=pltpu.VMEM)] * 2,
        out_specs=pl.BlockSpec(memory_space=pltpu.VMEM),
    )(queries, kv)


def padded_2(cells, sides, width):
    for axis, dim in sides:
        count = lax.psum(1, axis)
        ends = count - 1
        head = lax.slice_in_dim(cells, 0, width, axis=dim)
        tail = lax.slice_in_dim(cells, cells.shape[dim] - width, cells.shape[dim], axis=dim)
        cells = jnp.concatenate(
            [
                lax.ppermute(tail, axis, [(i, (i + 1) % count) for i in range(ends)]),
                cells,
                lax.ppermute(head, axis, [((i + 1) % count, i) for i in range(ends)]),
            ],
            axis=dim,
        )
    return cells


def layer_norm(values, scale_gain):
    values = values.astype(jnp.float32)
    centered = values - jnp.mean(values, axis=-1, keepdims=True)
    variance = jnp.mean(centered * centered, axis=-1, keepdims=True)
    return centered * lax.rsqrt(variance + EPSILON) * scale_gain


def rope_tables(coord_x, coord_y, coord_z, head_size):
    pair_count = head_size // 2
    position = jnp.arange(pair_count, dtype=jnp.int32)
    axis_pick = position % 3
    per_axis = (pair_count + 2) // 3
    frequency = ROPE_BASE ** (-(position // 3).astype(jnp.float32) / per_axis)
    angles = (
        coord_x[:, None] * (axis_pick == 0)
        + coord_y[:, None] * (axis_pick == 1)
        + coord_z[:, None] * (axis_pick == 2)
    ) * frequency
    return (jnp.cos(angles)[:, None, :], jnp.sin(angles)[:, None, :])


def token_tables(first_plane, planes, head_size):
    position = jnp.arange(planes * GY * GX, dtype=jnp.int32)
    coord_x = (position % GX).astype(jnp.float32)
    coord_y = (position // GX % GY).astype(jnp.float32)
    coord_z = (first_plane + position // (GX * GY)).astype(jnp.float32)
    return rope_tables(coord_x, coord_y, coord_z, head_size)


def key_tables(first_row, row_count, head_size):
    position = first_row + jnp.arange(row_count, dtype=jnp.int32)
    half_x = GX // 2
    half_y = GY // 2
    coord_x = (position % half_x).astype(jnp.float32) * 2.0 + 0.5
    coord_y = (position // half_x % half_y).astype(jnp.float32) * 2.0 + 0.5
    coord_z = (position // (half_x * half_y)).astype(jnp.float32) * 2.0 + 0.5
    return rope_tables(coord_x, coord_y, coord_z, head_size)


def rotate(values, cosine, sine_table):
    half_size = values.shape[-1] // 2
    front_half = values[..., :half_size]
    back_half = values[..., half_size:]
    return jnp.concatenate(
        [
            front_half * cosine - back_half * sine_table,
            back_half * cosine + front_half * sine_table,
        ],
        axis=-1,
    )


def make_patches(normed, planes):
    width = normed.shape[-1]
    cell_grid = normed.reshape(planes // 2, 2, GY // 2, 2, GX // 2, 2, width)
    return cell_grid.transpose(0, 2, 4, 1, 3, 5, 6).reshape(-1, 8 * width)


def depth_conv(padded, weights, planes):
    height = padded.shape[1] - 2
    width_x = padded.shape[2] - 2
    result = jnp.zeros((planes, height, width_x, padded.shape[3]), jnp.float32)
    for offset in range(27):
        shift_z = offset // 9
        shift_y = offset // 3 % 3
        shift_x = offset % 3
        window = padded[
            shift_z : shift_z + planes, shift_y : shift_y + height, shift_x : shift_x + width_x
        ]
        result = result + window.astype(jnp.float32) * weights[offset]
    return result


def per_device(
    tokens,
    gain_attn,
    w_reduce,
    gain_keys,
    w_query,
    w_key,
    w_value,
    w_out,
    gain_ffn,
    w_up,
    w_depth,
    w_down,
    grad_out,
):
    slab_index = lax.axis_index(SLAB)
    tok_rows = tokens.shape[0]
    heads_dev = w_query.shape[1] // HEAD
    normed = layer_norm(tokens, gain_attn).astype(jnp.bfloat16)
    patches = make_patches(normed, CZ)
    reduced = jnp.dot(patches, w_reduce, preferred_element_type=jnp.float32)
    key_input = layer_norm(reduced, gain_keys).astype(jnp.bfloat16)
    tok_cos, tok_sin = token_tables(slab_index * CZ, CZ, HEAD)
    queries = jnp.dot(normed, w_query, preferred_element_type=jnp.float32).reshape(
        tok_rows, heads_dev, HEAD
    )
    queries = rotate(queries, tok_cos, tok_sin).astype(jnp.bfloat16)
    local_rows = key_input.shape[0]
    own_cos, own_sin = key_tables(slab_index * local_rows, local_rows, HEAD)
    own_keys = jnp.dot(key_input, w_key, preferred_element_type=jnp.float32).reshape(
        local_rows, heads_dev, HEAD
    )
    own_keys = rotate(own_keys, own_cos, own_sin).astype(jnp.bfloat16)
    own_values = jnp.dot(key_input, w_value, preferred_element_type=jnp.float32).astype(
        jnp.bfloat16
    )
    key_width = heads_dev * HEAD
    pieces = jnp.concatenate([own_keys.reshape(local_rows, key_width), own_values], axis=1)
    pieces = slab_gather(pieces, lax.psum(1, SLAB), lax.psum(1, ("z", "xl")))
    heads_out = attention(queries.reshape(tok_rows, key_width), pieces, heads_dev)
    partial_value = jnp.dot(heads_out, w_out, preferred_element_type=jnp.float32)
    head_total = head_sum(partial_value, lax.psum(1, FFN)).astype(jnp.float32)
    attended = head_total.astype(jnp.bfloat16)
    residual = tokens.astype(jnp.float32) + head_total
    normed_ffn = layer_norm(residual, gain_ffn).astype(jnp.bfloat16)
    channels = w_up.shape[1]
    pre = (
        jnp.dot(normed_ffn, w_up, preferred_element_type=jnp.float32)
        .astype(jnp.bfloat16)
        .reshape(CZ, GY, GX, channels)
    )
    pre_wide = padded_2(pre, ((SLAB, 0),), 1)
    pre_pad = jnp.pad(pre_wide, ((0, 0), (1, 1), (1, 1), (0, 0)))
    mixed = depth_conv(pre_pad, w_depth, CZ).reshape(tok_rows, channels)
    normal_cdf = 0.5 * (1.0 + lax.erf(mixed * ROOT_HALF))
    normal_pdf = jnp.exp(-0.5 * mixed * mixed) * NORMAL_SCALE
    activated = (mixed * normal_cdf).astype(jnp.bfloat16)
    grad_act = jnp.einsum("td,cd->tc", grad_out, w_down, preferred_element_type=jnp.float32)
    grad_mixed = (
        (grad_act * (normal_cdf + mixed * normal_pdf))
        .astype(jnp.bfloat16)
        .reshape(CZ, GY, GX, channels)
    )
    grad_wide = padded_2(grad_mixed, ((SLAB, 0),), 1)
    grad_pad = jnp.pad(grad_wide, ((0, 0), (1, 1), (1, 1), (0, 0)))
    grad_pre = (
        depth_conv(grad_pad, w_depth[::-1], CZ).astype(jnp.bfloat16).reshape(tok_rows, channels)
    )
    up_full = jnp.einsum("td,tc->dc", normed_ffn, grad_pre, preferred_element_type=jnp.float32)
    down_full = jnp.einsum("td,tc->dc", grad_out, activated, preferred_element_type=jnp.float32)
    grads = slab_scatter(
        jnp.concatenate([up_full, down_full], axis=1),
        lax.psum(1, SLAB),
        lax.psum(1, ("z", "xl")),
    )
    return (attended, grads[:, :channels], grads[:, channels:])


def solution(mesh):
    mesh = Mesh(mesh.devices.reshape(4, 8, 2, 2, 2), SLAB + FFN)
    in_specs = (
        P(SLAB, None),
        P(),
        P(),
        P(),
        P(None, FFN),
        P(None, FFN),
        P(None, FFN),
        P(FFN, None),
        P(),
        P(None, FFN),
        P(None, FFN),
        P(FFN, None),
        P(SLAB, None),
    )
    out_specs = (P(SLAB, None), P(SLAB, FFN), P(SLAB, FFN))
    return jax.shard_map(
        per_device, mesh=mesh, in_specs=in_specs, out_specs=out_specs, check_vma=False
    )
```

```python
import functools
import math

import jax
import jax.numpy as jnp
from jax import lax
from jax.experimental import pallas as pl
from jax.experimental.pallas import tpu as pltpu
from jax.sharding import Mesh
from jax.sharding import PartitionSpec as P

HEAD = 64
GX = 16
GY = 16
CZ = 2
SLAB = ("y", "z", "xl")
FFN = ("xh", "core")


EPSILON = 1e-05
ROPE_BASE = 100.0
ROOT_HALF = 0.7071067811865476
NORMAL_SCALE = 0.3989422804014327


MESH = pl.DeviceIdType.MESH


def peer_id(p):
    return (p // 16, p // 2 % 8, p % 2, lax.axis_index("xh"), lax.axis_index("core"))


def attend_rows(kv_ref, q_ref, top_ref, total_ref, acc_ref, first_row, row_rows, first):
    heads, q_rows, _ = top_ref.shape
    q_tile = q_rows // 2
    key_width = heads * HEAD
    score_scale = HEAD ** (-0.5)
    rows = pl.ds(pl.multiple_of(first_row, row_rows), row_rows)
    for head in range(heads):
        keys = kv_ref[rows, head * HEAD : (head + 1) * HEAD]
        values = kv_ref[rows, key_width + head * HEAD : key_width + (head + 1) * HEAD]
        for start in range(0, q_rows, q_tile):
            tile = slice(start, start + q_tile)
            columns = slice(head * HEAD, (head + 1) * HEAD)
            scores = lax.dot_general(
                q_ref[tile, columns], keys, (((1,), (1,)), ((), ())),
                preferred_element_type=jnp.float32,
            ) * score_scale
            top = jnp.max(scores, axis=1, keepdims=True)
            if not first:
                old_top = top_ref[head, tile]
                top = jnp.maximum(top, old_top)
                rescale = jnp.exp(old_top - top)
            weights = jnp.exp(scores - top)
            row_sum = jnp.sum(weights, axis=1, keepdims=True)
            mixed = jnp.dot(
                weights.astype(jnp.bfloat16), values, preferred_element_type=jnp.float32
            )
            if not first:
                row_sum = row_sum + rescale * total_ref[head, tile]
                mixed = mixed + rescale * acc_ref[tile, columns]
            top_ref[head, tile] = top
            total_ref[head, tile] = row_sum
            acc_ref[tile, columns] = mixed


def gather_kernel(
    row_size, x_ref, q_ref, heads_ref, out_ref, top_ref, total_ref, acc_ref,
    send_a, recv_a, send_b, recv_b, send_c, recv_c, local_sem,
):
    me = lax.axis_index(SLAB)
    block = x_ref.shape[0]
    own_y, spot = me // row_size, me % row_size
    y_count = lax.psum(1, "y")
    barrier = pltpu.get_barrier_semaphore()

    def greet(k, carry):
        peer = own_y * row_size + lax.rem(spot + k, row_size)
        pl.semaphore_signal(barrier, inc=1, device_id=peer_id(peer), device_id_type=MESH)
        return carry

    lax.fori_loop(1, row_size, greet, 0)
    left_y = lax.rem(own_y + y_count - 1, y_count)
    right_y = lax.rem(own_y + 1, y_count)
    for other_y in (left_y, right_y):
        peer = other_y * row_size + spot
        pl.semaphore_signal(barrier, inc=1, device_id=peer_id(peer), device_id_type=MESH)
    pl.semaphore_wait(barrier, row_size + 1)

    def along_row(target, source):
        return pltpu.make_async_remote_copy(
            src_ref=x_ref,
            dst_ref=out_ref.at[pl.ds((own_y * row_size + source) * block, block)],
            send_sem=send_a.at[target],
            recv_sem=recv_a.at[source],
            device_id=peer_id(own_y * row_size + target),
            device_id_type=MESH,
        )

    def start_row(k, carry):
        along_row(lax.rem(spot + k, row_size), spot).start()
        return carry

    lax.fori_loop(1, row_size, start_row, 0)
    local = pltpu.make_async_copy(x_ref, out_ref.at[pl.ds(me * block, block)], local_sem)
    local.start()
    local.wait()

    def finish_row(k, carry):
        other = lax.rem(spot + k, row_size)
        along_row(other, spot).wait_send()
        along_row(other, other).wait_recv()
        return carry

    lax.fori_loop(1, row_size, finish_row, 0)
    row_rows = row_size * block

    def across(target_y, source_y):
        return pltpu.make_async_remote_copy(
            src_ref=out_ref.at[pl.ds(source_y * row_rows, row_rows)],
            dst_ref=out_ref.at[pl.ds(source_y * row_rows, row_rows)],
            send_sem=send_b.at[target_y],
            recv_sem=recv_b.at[source_y],
            device_id=peer_id(target_y * row_size + spot),
            device_id_type=MESH,
        )

    for other_y in (left_y, right_y):
        across(other_y, own_y).start()
    attend = functools.partial(
        attend_rows, out_ref, q_ref, top_ref, total_ref, acc_ref, row_rows=row_rows
    )
    attend(own_y * row_rows, first=True)
    for other_y in (left_y, right_y):
        across(other_y, own_y).wait_send()
        across(other_y, other_y).wait_recv()
    half = row_rows // 2

    def forward(target_y, source_y, part):
        rows = pl.ds(source_y * row_rows + part * half, half)
        return pltpu.make_async_remote_copy(
            src_ref=out_ref.at[rows],
            dst_ref=out_ref.at[rows],
            send_sem=send_c.at[part],
            recv_sem=recv_c.at[part],
            device_id=peer_id(target_y * row_size + spot),
            device_id_type=MESH,
        )

    far_y = lax.rem(own_y + 2, y_count)
    forward(right_y, left_y, 0).start()
    forward(left_y, right_y, 1).start()
    attend(left_y * row_rows, first=False)
    attend(right_y * row_rows, first=False)
    forward(right_y, left_y, 0).wait_send()
    forward(left_y, right_y, 1).wait_send()
    forward(right_y, far_y, 0).wait_recv()
    forward(left_y, far_y, 1).wait_recv()
    attend(far_y * row_rows, first=False)
    heads = top_ref.shape[0]
    for head in range(heads):
        columns = slice(head * HEAD, (head + 1) * HEAD)
        heads_ref[:, columns] = (acc_ref[:, columns] / total_ref[head]).astype(heads_ref.dtype)


def gather_attend(x, queries, count, row_size, heads):
    rows, width = x.shape
    q_rows = queries.shape[0]
    y_count = count // row_size
    assert y_count == 4
    return pl.pallas_call(
        functools.partial(gather_kernel, row_size),
        out_shape=jax.ShapeDtypeStruct(queries.shape, jnp.bfloat16),
        in_specs=[pl.BlockSpec(memory_space=pltpu.VMEM)] * 2,
        out_specs=pl.BlockSpec(memory_space=pltpu.VMEM),
        scratch_shapes=[
            pltpu.VMEM((count * rows, width), x.dtype),
            pltpu.VMEM((heads, q_rows, 1), jnp.float32),
            pltpu.VMEM((heads, q_rows, 1), jnp.float32),
            pltpu.VMEM(queries.shape, jnp.float32),
            pltpu.SemaphoreType.DMA((row_size,)),
            pltpu.SemaphoreType.DMA((row_size,)),
            pltpu.SemaphoreType.DMA((y_count,)),
            pltpu.SemaphoreType.DMA((y_count,)),
            pltpu.SemaphoreType.DMA((2,)),
            pltpu.SemaphoreType.DMA((2,)),
            pltpu.SemaphoreType.DMA(()),
        ],
        compiler_params=pltpu.CompilerParams(collective_id=0, has_side_effects=True),
    )(x, queries)


def head_peer(q):
    return (lax.axis_index("y"), lax.axis_index("z"), lax.axis_index("xl"), q // 2, q % 2)


def head_sum_kernel(count, part_ref, out_ref, slots, send_sem, recv_sem, send_back, recv_back):
    me = lax.axis_index(FFN)
    barrier = pltpu.get_barrier_semaphore()
    for k in range(1, count):
        pl.semaphore_signal(
            barrier, inc=1, device_id=head_peer(lax.rem(me + k, count)), device_id_type=MESH
        )
    pl.semaphore_wait(barrier, count - 1)

    def share(peer, source):
        return pltpu.make_async_remote_copy(
            src_ref=part_ref.at[peer],
            dst_ref=slots.at[source],
            send_sem=send_sem.at[peer],
            recv_sem=recv_sem.at[source],
            device_id=head_peer(peer),
            device_id_type=MESH,
        )

    def spread(peer, source):
        return pltpu.make_async_remote_copy(
            src_ref=out_ref.at[source],
            dst_ref=out_ref.at[source],
            send_sem=send_back.at[peer],
            recv_sem=recv_back.at[source],
            device_id=head_peer(peer),
            device_id_type=MESH,
        )

    peers = [lax.rem(me + k, count) for k in range(1, count)]
    for peer in peers:
        share(peer, me).start()
    total = part_ref[me].astype(jnp.float32)
    for peer in peers:
        share(peer, me).wait_send()
        share(peer, peer).wait_recv()
        total = total + slots[peer].astype(jnp.float32)
    out_ref[me] = total.astype(out_ref.dtype)
    for peer in peers:
        spread(peer, me).start()
    for peer in peers:
        spread(peer, me).wait_send()
        spread(peer, peer).wait_recv()


def head_sum(partial_value, count):
    rows, width = partial_value.shape
    parts = partial_value.astype(jnp.bfloat16).reshape(count, rows // count, width)
    summed = pl.pallas_call(
        functools.partial(head_sum_kernel, count),
        out_shape=jax.ShapeDtypeStruct(parts.shape, parts.dtype),
        in_specs=[pl.BlockSpec(memory_space=pltpu.VMEM)],
        out_specs=pl.BlockSpec(memory_space=pltpu.VMEM),
        scratch_shapes=[
            pltpu.VMEM(parts.shape, parts.dtype),
            pltpu.SemaphoreType.DMA((count,)),
            pltpu.SemaphoreType.DMA((count,)),
            pltpu.SemaphoreType.DMA((count,)),
            pltpu.SemaphoreType.DMA((count,)),
        ],
        compiler_params=pltpu.CompilerParams(collective_id=2, has_side_effects=True),
    )(parts)
    return summed.reshape(rows, width)


def scatter_kernel(
    row_size, g_ref, out_ref, slots_y, totals, sums, slots_row, send_a, recv_a, send_b, recv_b
):
    me = lax.axis_index(SLAB)
    own_y, spot = me // row_size, me % row_size
    y_count = lax.psum(1, "y")
    barrier = pltpu.get_barrier_semaphore()

    def greet(k, carry):
        peer = own_y * row_size + lax.rem(spot + k, row_size)
        pl.semaphore_signal(barrier, inc=1, device_id=peer_id(peer), device_id_type=MESH)
        return carry

    lax.fori_loop(1, row_size, greet, 0)
    others = [lax.rem(own_y + j, y_count) for j in range(1, y_count)]
    for other_y in others:
        pl.semaphore_signal(
            barrier, inc=1, device_id=peer_id(other_y * row_size + spot), device_id_type=MESH
        )
    pl.semaphore_wait(barrier, row_size + y_count - 2)

    def across(target_y, source_y):
        return pltpu.make_async_remote_copy(
            src_ref=g_ref.at[pl.ds(target_y * row_size, row_size)],
            dst_ref=slots_y.at[source_y],
            send_sem=send_a.at[target_y],
            recv_sem=recv_a.at[source_y],
            device_id=peer_id(target_y * row_size + spot),
            device_id_type=MESH,
        )

    for other_y in others:
        across(other_y, own_y).start()
    total = g_ref[pl.ds(own_y * row_size, row_size)].astype(jnp.float32)
    for other_y in others:
        across(other_y, own_y).wait_send()
        across(other_y, other_y).wait_recv()
        total = total + slots_y[other_y].astype(jnp.float32)
    totals[...] = total
    sums[...] = total.astype(sums.dtype)

    def along_row(target, source):
        return pltpu.make_async_remote_copy(
            src_ref=sums.at[target],
            dst_ref=slots_row.at[source],
            send_sem=send_b.at[target],
            recv_sem=recv_b.at[source],
            device_id=peer_id(own_y * row_size + target),
            device_id_type=MESH,
        )

    def start_row(k, carry):
        along_row(lax.rem(spot + k, row_size), spot).start()
        return carry

    lax.fori_loop(1, row_size, start_row, 0)
    out_ref[...] = totals[spot]

    def finish_row(k, carry):
        other = lax.rem(spot + k, row_size)
        along_row(other, spot).wait_send()
        along_row(other, other).wait_recv()
        out_ref[...] += slots_row[other].astype(jnp.float32)
        return carry

    lax.fori_loop(1, row_size, finish_row, 0)


def slab_scatter(g, count, row_size):
    total_rows, width = g.shape
    rows = total_rows // count
    y_count = count // row_size
    tile_rows = 16
    g = g.astype(jnp.bfloat16).reshape(count, tile_rows, rows * width // tile_rows)
    summed = pl.pallas_call(
        functools.partial(scatter_kernel, row_size),
        out_shape=jax.ShapeDtypeStruct(g.shape[1:], jnp.float32),
        in_specs=[pl.BlockSpec(memory_space=pltpu.VMEM)],
        out_specs=pl.BlockSpec(memory_space=pltpu.VMEM),
        scratch_shapes=[
            pltpu.VMEM((y_count, row_size) + g.shape[1:], g.dtype),
            pltpu.VMEM((row_size,) + g.shape[1:], jnp.float32),
            pltpu.VMEM((row_size,) + g.shape[1:], g.dtype),
            pltpu.VMEM((row_size,) + g.shape[1:], g.dtype),
            pltpu.SemaphoreType.DMA((y_count,)),
            pltpu.SemaphoreType.DMA((y_count,)),
            pltpu.SemaphoreType.DMA((row_size,)),
            pltpu.SemaphoreType.DMA((row_size,)),
        ],
        compiler_params=pltpu.CompilerParams(collective_id=1, has_side_effects=True),
    )(g)
    return summed.reshape(rows, width)


def padded_2(cells, sides, width):
    for axis, dim in sides:
        count = lax.psum(1, axis)
        ends = count - 1
        head = lax.slice_in_dim(cells, 0, width, axis=dim)
        tail = lax.slice_in_dim(cells, cells.shape[dim] - width, cells.shape[dim], axis=dim)
        cells = jnp.concatenate(
            [
                lax.ppermute(tail, axis, [(i, (i + 1) % count) for i in range(ends)]),
                cells,
                lax.ppermute(head, axis, [((i + 1) % count, i) for i in range(ends)]),
            ],
            axis=dim,
        )
    return cells


def layer_norm(values, scale_gain):
    values = values.astype(jnp.float32)
    centered = values - jnp.mean(values, axis=-1, keepdims=True)
    variance = jnp.mean(centered * centered, axis=-1, keepdims=True)
    return centered * lax.rsqrt(variance + EPSILON) * scale_gain


def rope_tables(coord_x, coord_y, coord_z, head_size):
    pair_count = head_size // 2
    position = jnp.arange(pair_count, dtype=jnp.int32)
    axis_pick = position % 3
    per_axis = (pair_count + 2) // 3
    frequency = ROPE_BASE ** (-(position // 3).astype(jnp.float32) / per_axis)
    angles = (
        coord_x[:, None] * (axis_pick == 0)
        + coord_y[:, None] * (axis_pick == 1)
        + coord_z[:, None] * (axis_pick == 2)
    ) * frequency
    return (jnp.cos(angles)[:, None, :], jnp.sin(angles)[:, None, :])


def token_tables(first_plane, planes, head_size):
    position = jnp.arange(planes * GY * GX, dtype=jnp.int32)
    coord_x = (position % GX).astype(jnp.float32)
    coord_y = (position // GX % GY).astype(jnp.float32)
    coord_z = (first_plane + position // (GX * GY)).astype(jnp.float32)
    return rope_tables(coord_x, coord_y, coord_z, head_size)


def key_tables(first_row, row_count, head_size):
    position = first_row + jnp.arange(row_count, dtype=jnp.int32)
    half_x = GX // 2
    half_y = GY // 2
    coord_x = (position % half_x).astype(jnp.float32) * 2.0 + 0.5
    coord_y = (position // half_x % half_y).astype(jnp.float32) * 2.0 + 0.5
    coord_z = (position // (half_x * half_y)).astype(jnp.float32) * 2.0 + 0.5
    return rope_tables(coord_x, coord_y, coord_z, head_size)


def rotate(values, cosine, sine_table):
    half_size = values.shape[-1] // 2
    front_half = values[..., :half_size]
    back_half = values[..., half_size:]
    return jnp.concatenate(
        [
            front_half * cosine - back_half * sine_table,
            back_half * cosine + front_half * sine_table,
        ],
        axis=-1,
    )


def make_patches(normed, planes):
    width = normed.shape[-1]
    cell_grid = normed.reshape(planes // 2, 2, GY // 2, 2, GX // 2, 2, width)
    return cell_grid.transpose(0, 2, 4, 1, 3, 5, 6).reshape(-1, 8 * width)


def depth_conv(padded, weights, planes):
    height = padded.shape[1] - 2
    width_x = padded.shape[2] - 2
    result = jnp.zeros((planes, height, width_x, padded.shape[3]), jnp.float32)
    for offset in range(27):
        shift_z = offset // 9
        shift_y = offset // 3 % 3
        shift_x = offset % 3
        window = padded[
            shift_z : shift_z + planes, shift_y : shift_y + height, shift_x : shift_x + width_x
        ]
        result = result + window.astype(jnp.float32) * weights[offset]
    return result


def per_device(
    tokens,
    gain_attn,
    w_reduce,
    gain_keys,
    w_query,
    w_key,
    w_value,
    w_out,
    gain_ffn,
    w_up,
    w_depth,
    w_down,
    grad_out,
):
    slab_index = lax.axis_index(SLAB)
    tok_rows = tokens.shape[0]
    heads_dev = w_query.shape[1] // HEAD
    normed = layer_norm(tokens, gain_attn).astype(jnp.bfloat16)
    patches = make_patches(normed, CZ)
    reduced = jnp.dot(patches, w_reduce, preferred_element_type=jnp.float32)
    key_input = layer_norm(reduced, gain_keys).astype(jnp.bfloat16)
    tok_cos, tok_sin = token_tables(slab_index * CZ, CZ, HEAD)
    queries = jnp.dot(normed, w_query, preferred_element_type=jnp.float32).reshape(
        tok_rows, heads_dev, HEAD
    )
    queries = rotate(queries, tok_cos, tok_sin).astype(jnp.bfloat16)
    local_rows = key_input.shape[0]
    own_cos, own_sin = key_tables(slab_index * local_rows, local_rows, HEAD)
    own_keys = jnp.dot(key_input, w_key, preferred_element_type=jnp.float32).reshape(
        local_rows, heads_dev, HEAD
    )
    own_keys = rotate(own_keys, own_cos, own_sin).astype(jnp.bfloat16)
    own_values = jnp.dot(key_input, w_value, preferred_element_type=jnp.float32).astype(
        jnp.bfloat16
    )
    key_width = heads_dev * HEAD
    pieces = jnp.concatenate([own_keys.reshape(local_rows, key_width), own_values], axis=1)
    heads_out = gather_attend(
        pieces,
        queries.reshape(tok_rows, key_width),
        lax.psum(1, SLAB),
        lax.psum(1, ("z", "xl")),
        heads_dev,
    )
    partial_value = jnp.dot(heads_out, w_out, preferred_element_type=jnp.float32)
    head_total = head_sum(partial_value, lax.psum(1, FFN)).astype(jnp.float32)
    attended = head_total.astype(jnp.bfloat16)
    residual = tokens.astype(jnp.float32) + head_total
    normed_ffn = layer_norm(residual, gain_ffn).astype(jnp.bfloat16)
    channels = w_up.shape[1]
    pre = (
        jnp.dot(normed_ffn, w_up, preferred_element_type=jnp.float32)
        .astype(jnp.bfloat16)
        .reshape(CZ, GY, GX, channels)
    )
    pre_wide = padded_2(pre, ((SLAB, 0),), 1)
    pre_pad = jnp.pad(pre_wide, ((0, 0), (1, 1), (1, 1), (0, 0)))
    mixed = depth_conv(pre_pad, w_depth, CZ).reshape(tok_rows, channels)
    normal_cdf = 0.5 * (1.0 + lax.erf(mixed * ROOT_HALF))
    normal_pdf = jnp.exp(-0.5 * mixed * mixed) * NORMAL_SCALE
    activated = (mixed * normal_cdf).astype(jnp.bfloat16)
    grad_act = jnp.einsum("td,cd->tc", grad_out, w_down, preferred_element_type=jnp.float32)
    grad_mixed = (
        (grad_act * (normal_cdf + mixed * normal_pdf))
        .astype(jnp.bfloat16)
        .reshape(CZ, GY, GX, channels)
    )
    grad_wide = padded_2(grad_mixed, ((SLAB, 0),), 1)
    grad_pad = jnp.pad(grad_wide, ((0, 0), (1, 1), (1, 1), (0, 0)))
    grad_pre = (
        depth_conv(grad_pad, w_depth[::-1], CZ).astype(jnp.bfloat16).reshape(tok_rows, channels)
    )
    up_full = jnp.einsum("td,tc->dc", normed_ffn, grad_pre, preferred_element_type=jnp.float32)
    down_full = jnp.einsum("td,tc->dc", grad_out, activated, preferred_element_type=jnp.float32)
    grads = slab_scatter(
        jnp.concatenate([up_full, down_full], axis=1),
        lax.psum(1, SLAB),
        lax.psum(1, ("z", "xl")),
    )
    return (attended, grads[:, :channels], grads[:, channels:])


def solution(mesh):
    mesh = Mesh(mesh.devices.reshape(4, 8, 2, 2, 2), SLAB + FFN)
    in_specs = (
        P(SLAB, None),
        P(),
        P(),
        P(),
        P(None, FFN),
        P(None, FFN),
        P(None, FFN),
        P(FFN, None),
        P(),
        P(None, FFN),
        P(None, FFN),
        P(FFN, None),
        P(SLAB, None),
    )
    out_specs = (P(SLAB, None), P(SLAB, FFN), P(SLAB, FFN))
    return jax.shard_map(
        per_device, mesh=mesh, in_specs=in_specs, out_specs=out_specs, check_vma=False
    )
```

```python
import functools
import math

import jax
import jax.numpy as jnp
from jax import lax
from jax.experimental import pallas as pl
from jax.experimental.pallas import tpu as pltpu
from jax.sharding import Mesh
from jax.sharding import PartitionSpec as P

HEAD = 64
GX = 16
GY = 16
CZ = 2
SLAB = ("y", "z", "xl")
FFN = ("xh", "core")


EPSILON = 1e-05
ROPE_BASE = 100.0
ROOT_HALF = 0.7071067811865476
NORMAL_SCALE = 0.3989422804014327


MESH = pl.DeviceIdType.MESH


def peer_id(p):
    return (p // 16, p // 2 % 8, p % 2, lax.axis_index("xh"), lax.axis_index("core"))


def attend_rows(kv_ref, q_ref, top_ref, total_ref, acc_ref, first_row, row_rows, first):
    heads, q_rows, _ = top_ref.shape
    q_tile = q_rows // 2
    key_width = heads * HEAD
    score_scale = HEAD ** (-0.5)
    rows = pl.ds(pl.multiple_of(first_row, row_rows), row_rows)
    for head in range(heads):
        keys = kv_ref[rows, head * HEAD : (head + 1) * HEAD]
        values = kv_ref[rows, key_width + head * HEAD : key_width + (head + 1) * HEAD]
        for start in range(0, q_rows, q_tile):
            tile = slice(start, start + q_tile)
            columns = slice(head * HEAD, (head + 1) * HEAD)
            scores = lax.dot_general(
                q_ref[tile, columns], keys, (((1,), (1,)), ((), ())),
                preferred_element_type=jnp.float32,
            ) * score_scale
            top = jnp.max(scores, axis=1, keepdims=True)
            if not first:
                old_top = top_ref[head, tile]
                top = jnp.maximum(top, old_top)
                rescale = jnp.exp(old_top - top)
            weights = jnp.exp(scores - top)
            row_sum = jnp.sum(weights, axis=1, keepdims=True)
            mixed = jnp.dot(
                weights.astype(jnp.bfloat16), values, preferred_element_type=jnp.float32
            )
            if not first:
                row_sum = row_sum + rescale * total_ref[head, tile]
                mixed = mixed + rescale * acc_ref[tile, columns]
            top_ref[head, tile] = top
            total_ref[head, tile] = row_sum
            acc_ref[tile, columns] = mixed


def gather_kernel(
    row_size, x_ref, q_ref, heads_ref, out_ref, top_ref, total_ref, acc_ref,
    send_a, recv_a, send_b, recv_b, send_c, recv_c, local_sem,
):
    me = lax.axis_index(SLAB)
    block = x_ref.shape[0]
    own_y, spot = me // row_size, me % row_size
    y_count = lax.psum(1, "y")
    barrier = pltpu.get_barrier_semaphore()

    def greet(k, carry):
        peer = own_y * row_size + lax.rem(spot + k, row_size)
        pl.semaphore_signal(barrier, inc=1, device_id=peer_id(peer), device_id_type=MESH)
        return carry

    lax.fori_loop(1, row_size, greet, 0)
    left_y = lax.rem(own_y + y_count - 1, y_count)
    right_y = lax.rem(own_y + 1, y_count)
    for other_y in (left_y, right_y):
        peer = other_y * row_size + spot
        pl.semaphore_signal(barrier, inc=1, device_id=peer_id(peer), device_id_type=MESH)
    pl.semaphore_wait(barrier, row_size + 1)

    def along_row(target, source):
        return pltpu.make_async_remote_copy(
            src_ref=x_ref,
            dst_ref=out_ref.at[pl.ds((own_y * row_size + source) * block, block)],
            send_sem=send_a.at[target],
            recv_sem=recv_a.at[source],
            device_id=peer_id(own_y * row_size + target),
            device_id_type=MESH,
        )

    def start_row(k, carry):
        along_row(lax.rem(spot + k, row_size), spot).start()
        return carry

    lax.fori_loop(1, row_size, start_row, 0)
    local = pltpu.make_async_copy(x_ref, out_ref.at[pl.ds(me * block, block)], local_sem)
    local.start()
    local.wait()

    def finish_row(k, carry):
        other = lax.rem(spot + k, row_size)
        along_row(other, spot).wait_send()
        along_row(other, other).wait_recv()
        return carry

    lax.fori_loop(1, row_size, finish_row, 0)
    row_rows = row_size * block

    def across(target_y, source_y):
        return pltpu.make_async_remote_copy(
            src_ref=out_ref.at[pl.ds(source_y * row_rows, row_rows)],
            dst_ref=out_ref.at[pl.ds(source_y * row_rows, row_rows)],
            send_sem=send_b.at[target_y],
            recv_sem=recv_b.at[source_y],
            device_id=peer_id(target_y * row_size + spot),
            device_id_type=MESH,
        )

    for other_y in (left_y, right_y):
        across(other_y, own_y).start()
    attend = functools.partial(
        attend_rows, out_ref, q_ref, top_ref, total_ref, acc_ref, row_rows=row_rows
    )
    attend(own_y * row_rows, first=True)
    for other_y in (left_y, right_y):
        across(other_y, own_y).wait_send()
        across(other_y, other_y).wait_recv()
    half = row_rows // 2

    def forward(target_y, source_y, part):
        rows = pl.ds(source_y * row_rows + part * half, half)
        return pltpu.make_async_remote_copy(
            src_ref=out_ref.at[rows],
            dst_ref=out_ref.at[rows],
            send_sem=send_c.at[part],
            recv_sem=recv_c.at[part],
            device_id=peer_id(target_y * row_size + spot),
            device_id_type=MESH,
        )

    far_y = lax.rem(own_y + 2, y_count)
    forward(right_y, left_y, 0).start()
    forward(left_y, right_y, 1).start()
    attend(left_y * row_rows, first=False)
    attend(right_y * row_rows, first=False)
    forward(right_y, left_y, 0).wait_send()
    forward(left_y, right_y, 1).wait_send()
    forward(right_y, far_y, 0).wait_recv()
    forward(left_y, far_y, 1).wait_recv()
    attend(far_y * row_rows, first=False)
    heads = top_ref.shape[0]
    for head in range(heads):
        columns = slice(head * HEAD, (head + 1) * HEAD)
        heads_ref[:, columns] = (acc_ref[:, columns] / total_ref[head]).astype(heads_ref.dtype)


def gather_attend(x, queries, count, row_size, heads):
    rows, width = x.shape
    q_rows = queries.shape[0]
    y_count = count // row_size
    assert y_count == 4
    return pl.pallas_call(
        functools.partial(gather_kernel, row_size),
        out_shape=jax.ShapeDtypeStruct(queries.shape, jnp.bfloat16),
        in_specs=[pl.BlockSpec(memory_space=pltpu.VMEM)] * 2,
        out_specs=pl.BlockSpec(memory_space=pltpu.VMEM),
        scratch_shapes=[
            pltpu.VMEM((count * rows, width), x.dtype),
            pltpu.VMEM((heads, q_rows, 1), jnp.float32),
            pltpu.VMEM((heads, q_rows, 1), jnp.float32),
            pltpu.VMEM(queries.shape, jnp.float32),
            pltpu.SemaphoreType.DMA((row_size,)),
            pltpu.SemaphoreType.DMA((row_size,)),
            pltpu.SemaphoreType.DMA((y_count,)),
            pltpu.SemaphoreType.DMA((y_count,)),
            pltpu.SemaphoreType.DMA((2,)),
            pltpu.SemaphoreType.DMA((2,)),
            pltpu.SemaphoreType.DMA(()),
        ],
        compiler_params=pltpu.CompilerParams(collective_id=0, has_side_effects=True),
    )(x, queries)


def head_peer(q):
    return (lax.axis_index("y"), lax.axis_index("z"), lax.axis_index("xl"), q // 2, q % 2)


def head_sum_kernel(count, part_ref, out_ref, slots, send_sem, recv_sem, send_back, recv_back):
    me = lax.axis_index(FFN)
    barrier = pltpu.get_barrier_semaphore()
    for k in range(1, count):
        pl.semaphore_signal(
            barrier, inc=1, device_id=head_peer(lax.rem(me + k, count)), device_id_type=MESH
        )
    pl.semaphore_wait(barrier, count - 1)

    def share(peer, source):
        return pltpu.make_async_remote_copy(
            src_ref=part_ref.at[peer],
            dst_ref=slots.at[source],
            send_sem=send_sem.at[peer],
            recv_sem=recv_sem.at[source],
            device_id=head_peer(peer),
            device_id_type=MESH,
        )

    def spread(peer, source):
        return pltpu.make_async_remote_copy(
            src_ref=out_ref.at[source],
            dst_ref=out_ref.at[source],
            send_sem=send_back.at[peer],
            recv_sem=recv_back.at[source],
            device_id=head_peer(peer),
            device_id_type=MESH,
        )

    peers = [lax.rem(me + k, count) for k in range(1, count)]
    for peer in peers:
        share(peer, me).start()
    total = part_ref[me].astype(jnp.float32)
    for peer in peers:
        share(peer, me).wait_send()
        share(peer, peer).wait_recv()
        total = total + slots[peer].astype(jnp.float32)
    out_ref[me] = total.astype(out_ref.dtype)
    for peer in peers:
        spread(peer, me).start()
    for peer in peers:
        spread(peer, me).wait_send()
        spread(peer, peer).wait_recv()


def head_sum(partial_value, count):
    rows, width = partial_value.shape
    parts = partial_value.astype(jnp.bfloat16).reshape(count, rows // count, width)
    summed = pl.pallas_call(
        functools.partial(head_sum_kernel, count),
        out_shape=jax.ShapeDtypeStruct(parts.shape, parts.dtype),
        in_specs=[pl.BlockSpec(memory_space=pltpu.VMEM)],
        out_specs=pl.BlockSpec(memory_space=pltpu.VMEM),
        scratch_shapes=[
            pltpu.VMEM(parts.shape, parts.dtype),
            pltpu.SemaphoreType.DMA((count,)),
            pltpu.SemaphoreType.DMA((count,)),
            pltpu.SemaphoreType.DMA((count,)),
            pltpu.SemaphoreType.DMA((count,)),
        ],
        compiler_params=pltpu.CompilerParams(collective_id=2, has_side_effects=True),
    )(parts)
    return summed.reshape(rows, width)


def scatter_kernel(
    row_size, g_ref, out_ref, slots_y, totals, sums, slots_row, send_a, recv_a, send_b, recv_b
):
    me = lax.axis_index(SLAB)
    own_y, spot = me // row_size, me % row_size
    y_count = lax.psum(1, "y")
    barrier = pltpu.get_barrier_semaphore()

    def greet(k, carry):
        peer = own_y * row_size + lax.rem(spot + k, row_size)
        pl.semaphore_signal(barrier, inc=1, device_id=peer_id(peer), device_id_type=MESH)
        return carry

    lax.fori_loop(1, row_size, greet, 0)
    others = [lax.rem(own_y + j, y_count) for j in range(1, y_count)]
    for other_y in others:
        pl.semaphore_signal(
            barrier, inc=1, device_id=peer_id(other_y * row_size + spot), device_id_type=MESH
        )
    pl.semaphore_wait(barrier, row_size + y_count - 2)

    def across(target_y, source_y):
        return pltpu.make_async_remote_copy(
            src_ref=g_ref.at[pl.ds(target_y * row_size, row_size)],
            dst_ref=slots_y.at[source_y],
            send_sem=send_a.at[target_y],
            recv_sem=recv_a.at[source_y],
            device_id=peer_id(target_y * row_size + spot),
            device_id_type=MESH,
        )

    for other_y in others:
        across(other_y, own_y).start()
    total = g_ref[pl.ds(own_y * row_size, row_size)].astype(jnp.float32)
    for other_y in others:
        across(other_y, own_y).wait_send()
        across(other_y, other_y).wait_recv()
        total = total + slots_y[other_y].astype(jnp.float32)
    totals[...] = total
    sums[...] = total.astype(sums.dtype)

    def along_row(target, source):
        return pltpu.make_async_remote_copy(
            src_ref=sums.at[target],
            dst_ref=slots_row.at[source],
            send_sem=send_b.at[target],
            recv_sem=recv_b.at[source],
            device_id=peer_id(own_y * row_size + target),
            device_id_type=MESH,
        )

    def start_row(k, carry):
        along_row(lax.rem(spot + k, row_size), spot).start()
        return carry

    lax.fori_loop(1, row_size, start_row, 0)
    out_ref[...] = totals[spot]

    def finish_row(k, carry):
        other = lax.rem(spot + k, row_size)
        along_row(other, spot).wait_send()
        along_row(other, other).wait_recv()
        out_ref[...] += slots_row[other].astype(jnp.float32)
        return carry

    lax.fori_loop(1, row_size, finish_row, 0)


def slab_scatter(g, count, row_size):
    total_rows, width = g.shape
    rows = total_rows // count
    y_count = count // row_size
    tile_rows = 16
    g = g.astype(jnp.bfloat16).reshape(count, tile_rows, rows * width // tile_rows)
    summed = pl.pallas_call(
        functools.partial(scatter_kernel, row_size),
        out_shape=jax.ShapeDtypeStruct(g.shape[1:], jnp.float32),
        in_specs=[pl.BlockSpec(memory_space=pltpu.VMEM)],
        out_specs=pl.BlockSpec(memory_space=pltpu.VMEM),
        scratch_shapes=[
            pltpu.VMEM((y_count, row_size) + g.shape[1:], g.dtype),
            pltpu.VMEM((row_size,) + g.shape[1:], jnp.float32),
            pltpu.VMEM((row_size,) + g.shape[1:], g.dtype),
            pltpu.VMEM((row_size,) + g.shape[1:], g.dtype),
            pltpu.SemaphoreType.DMA((y_count,)),
            pltpu.SemaphoreType.DMA((y_count,)),
            pltpu.SemaphoreType.DMA((row_size,)),
            pltpu.SemaphoreType.DMA((row_size,)),
        ],
        compiler_params=pltpu.CompilerParams(collective_id=1, has_side_effects=True),
    )(g)
    return summed.reshape(rows, width)


def layer_norm(values, scale_gain):
    values = values.astype(jnp.float32)
    centered = values - jnp.mean(values, axis=-1, keepdims=True)
    variance = jnp.mean(centered * centered, axis=-1, keepdims=True)
    return centered * lax.rsqrt(variance + EPSILON) * scale_gain


def rope_tables(coord_x, coord_y, coord_z, head_size):
    pair_count = head_size // 2
    position = jnp.arange(pair_count, dtype=jnp.int32)
    axis_pick = position % 3
    per_axis = (pair_count + 2) // 3
    frequency = ROPE_BASE ** (-(position // 3).astype(jnp.float32) / per_axis)
    angles = (
        coord_x[:, None] * (axis_pick == 0)
        + coord_y[:, None] * (axis_pick == 1)
        + coord_z[:, None] * (axis_pick == 2)
    ) * frequency
    return (jnp.cos(angles)[:, None, :], jnp.sin(angles)[:, None, :])


def token_tables(first_plane, planes, head_size):
    position = jnp.arange(planes * GY * GX, dtype=jnp.int32)
    coord_x = (position % GX).astype(jnp.float32)
    coord_y = (position // GX % GY).astype(jnp.float32)
    coord_z = (first_plane + position // (GX * GY)).astype(jnp.float32)
    return rope_tables(coord_x, coord_y, coord_z, head_size)


def key_tables(first_row, row_count, head_size):
    position = first_row + jnp.arange(row_count, dtype=jnp.int32)
    half_x = GX // 2
    half_y = GY // 2
    coord_x = (position % half_x).astype(jnp.float32) * 2.0 + 0.5
    coord_y = (position // half_x % half_y).astype(jnp.float32) * 2.0 + 0.5
    coord_z = (position // (half_x * half_y)).astype(jnp.float32) * 2.0 + 0.5
    return rope_tables(coord_x, coord_y, coord_z, head_size)


def rotate(values, cosine, sine_table):
    half_size = values.shape[-1] // 2
    front_half = values[..., :half_size]
    back_half = values[..., half_size:]
    return jnp.concatenate(
        [
            front_half * cosine - back_half * sine_table,
            back_half * cosine + front_half * sine_table,
        ],
        axis=-1,
    )


def make_patches(normed, planes):
    width = normed.shape[-1]
    cell_grid = normed.reshape(planes // 2, 2, GY // 2, 2, GX // 2, 2, width)
    return cell_grid.transpose(0, 2, 4, 1, 3, 5, 6).reshape(-1, 8 * width)


def depth_conv(padded, weights, planes):
    height = padded.shape[1] - 2
    width_x = padded.shape[2] - 2
    result = jnp.zeros((planes, height, width_x, padded.shape[3]), jnp.float32)
    for offset in range(27):
        shift_z = offset // 9
        shift_y = offset // 3 % 3
        shift_x = offset % 3
        window = padded[
            shift_z : shift_z + planes, shift_y : shift_y + height, shift_x : shift_x + width_x
        ]
        result = result + window.astype(jnp.float32) * weights[offset]
    return result


def conv_with_halos(cells, weights):
    count = lax.psum(1, SLAB)
    ends = count - 1
    planes = cells.shape[0]
    below = lax.ppermute(cells[planes - 1], SLAB, [(i, i + 1) for i in range(ends)])
    above = lax.ppermute(cells[0], SLAB, [(i + 1, i) for i in range(ends)])
    own = depth_conv(jnp.pad(cells, ((1, 1), (1, 1), (1, 1), (0, 0))), weights, planes)
    height, width_x = cells.shape[1], cells.shape[2]

    def plane_terms(plane, first):
        padded = jnp.pad(plane, ((1, 1), (1, 1), (0, 0))).astype(jnp.float32)
        total = jnp.zeros(plane.shape, jnp.float32)
        for offset in range(9):
            shift_y, shift_x = offset // 3, offset % 3
            window = padded[shift_y : shift_y + height, shift_x : shift_x + width_x]
            total = total + window * weights[first + offset]
        return total

    own = own.at[0].add(plane_terms(below, 0))
    return own.at[planes - 1].add(plane_terms(above, 18))


def per_device(
    tokens,
    gain_attn,
    w_reduce,
    gain_keys,
    w_query,
    w_key,
    w_value,
    w_out,
    gain_ffn,
    w_up,
    w_depth,
    w_down,
    grad_out,
):
    slab_index = lax.axis_index(SLAB)
    tok_rows = tokens.shape[0]
    heads_dev = w_query.shape[1] // HEAD
    normed = layer_norm(tokens, gain_attn).astype(jnp.bfloat16)
    patches = make_patches(normed, CZ)
    reduced = jnp.dot(patches, w_reduce, preferred_element_type=jnp.float32)
    key_input = layer_norm(reduced, gain_keys).astype(jnp.bfloat16)
    tok_cos, tok_sin = token_tables(slab_index * CZ, CZ, HEAD)
    queries = jnp.dot(normed, w_query, preferred_element_type=jnp.float32).reshape(
        tok_rows, heads_dev, HEAD
    )
    queries = rotate(queries, tok_cos, tok_sin).astype(jnp.bfloat16)
    local_rows = key_input.shape[0]
    own_cos, own_sin = key_tables(slab_index * local_rows, local_rows, HEAD)
    own_keys = jnp.dot(key_input, w_key, preferred_element_type=jnp.float32).reshape(
        local_rows, heads_dev, HEAD
    )
    own_keys = rotate(own_keys, own_cos, own_sin).astype(jnp.bfloat16)
    own_values = jnp.dot(key_input, w_value, preferred_element_type=jnp.float32).astype(
        jnp.bfloat16
    )
    key_width = heads_dev * HEAD
    pieces = jnp.concatenate([own_keys.reshape(local_rows, key_width), own_values], axis=1)
    heads_out = gather_attend(
        pieces,
        queries.reshape(tok_rows, key_width),
        lax.psum(1, SLAB),
        lax.psum(1, ("z", "xl")),
        heads_dev,
    )
    partial_value = jnp.dot(heads_out, w_out, preferred_element_type=jnp.float32)
    head_total = head_sum(partial_value, lax.psum(1, FFN)).astype(jnp.float32)
    attended = head_total.astype(jnp.bfloat16)
    residual = tokens.astype(jnp.float32) + head_total
    normed_ffn = layer_norm(residual, gain_ffn).astype(jnp.bfloat16)
    channels = w_up.shape[1]
    pre = (
        jnp.dot(normed_ffn, w_up, preferred_element_type=jnp.float32)
        .astype(jnp.bfloat16)
        .reshape(CZ, GY, GX, channels)
    )
    mixed = conv_with_halos(pre, w_depth).reshape(tok_rows, channels)
    normal_cdf = 0.5 * (1.0 + lax.erf(mixed * ROOT_HALF))
    normal_pdf = jnp.exp(-0.5 * mixed * mixed) * NORMAL_SCALE
    activated = (mixed * normal_cdf).astype(jnp.bfloat16)
    grad_act = jnp.einsum("td,cd->tc", grad_out, w_down, preferred_element_type=jnp.float32)
    grad_mixed = (
        (grad_act * (normal_cdf + mixed * normal_pdf))
        .astype(jnp.bfloat16)
        .reshape(CZ, GY, GX, channels)
    )
    grad_pre = (
        conv_with_halos(grad_mixed, w_depth[::-1])
        .astype(jnp.bfloat16)
        .reshape(tok_rows, channels)
    )
    up_full = jnp.einsum("td,tc->dc", normed_ffn, grad_pre, preferred_element_type=jnp.float32)
    down_full = jnp.einsum("td,tc->dc", grad_out, activated, preferred_element_type=jnp.float32)
    grads = slab_scatter(
        jnp.concatenate([up_full, down_full], axis=1),
        lax.psum(1, SLAB),
        lax.psum(1, ("z", "xl")),
    )
    return (attended, grads[:, :channels], grads[:, channels:])


def solution(mesh):
    mesh = Mesh(mesh.devices.reshape(4, 8, 2, 2, 2), SLAB + FFN)
    in_specs = (
        P(SLAB, None),
        P(),
        P(),
        P(),
        P(None, FFN),
        P(None, FFN),
        P(None, FFN),
        P(FFN, None),
        P(),
        P(None, FFN),
        P(None, FFN),
        P(FFN, None),
        P(SLAB, None),
    )
    out_specs = (P(SLAB, None), P(SLAB, FFN), P(SLAB, FFN))
    return jax.shard_map(
        per_device, mesh=mesh, in_specs=in_specs, out_specs=out_specs, check_vma=False
    )
```

```python
import functools
import math

import jax
import jax.numpy as jnp
from jax import lax
from jax.experimental import pallas as pl
from jax.experimental.pallas import tpu as pltpu
from jax.sharding import Mesh
from jax.sharding import PartitionSpec as P

HEAD = 64
GX = 16
GY = 16
CZ = 2
SLAB = ("y", "z", "xl")
FFN = ("xh", "core")


EPSILON = 1e-05
ROPE_BASE = 100.0
ROOT_HALF = 0.7071067811865476
NORMAL_SCALE = 0.3989422804014327


MESH = pl.DeviceIdType.MESH


def peer_id(p):
    return (p // 16, p // 2 % 8, p % 2, lax.axis_index("xh"), lax.axis_index("core"))


def attend_rows(kv_ref, q_ref, top_ref, total_ref, acc_ref, first_row, row_rows, first):
    heads, q_rows, _ = top_ref.shape
    q_tile = q_rows // 2
    key_width = heads * HEAD
    score_scale = HEAD ** (-0.5)
    rows = pl.ds(pl.multiple_of(first_row, row_rows), row_rows)
    for head in range(heads):
        keys = kv_ref[rows, head * HEAD : (head + 1) * HEAD]
        values = kv_ref[rows, key_width + head * HEAD : key_width + (head + 1) * HEAD]
        for start in range(0, q_rows, q_tile):
            tile = slice(start, start + q_tile)
            columns = slice(head * HEAD, (head + 1) * HEAD)
            scores = lax.dot_general(
                q_ref[tile, columns], keys, (((1,), (1,)), ((), ())),
                preferred_element_type=jnp.float32,
            ) * score_scale
            top = jnp.max(scores, axis=1, keepdims=True)
            if not first:
                old_top = top_ref[head, tile]
                top = jnp.maximum(top, old_top)
                rescale = jnp.exp(old_top - top)
            weights = jnp.exp(scores - top)
            row_sum = jnp.sum(weights, axis=1, keepdims=True)
            mixed = jnp.dot(
                weights.astype(jnp.bfloat16), values, preferred_element_type=jnp.float32
            )
            if not first:
                row_sum = row_sum + rescale * total_ref[head, tile]
                mixed = mixed + rescale * acc_ref[tile, columns]
            top_ref[head, tile] = top
            total_ref[head, tile] = row_sum
            acc_ref[tile, columns] = mixed


def gather_kernel(
    row_size, x_ref, q_ref, heads_ref, out_ref, top_ref, total_ref, acc_ref,
    send_a, recv_a, send_b, recv_b, send_c, recv_c, local_sem,
):
    me = lax.axis_index(SLAB)
    block = x_ref.shape[0]
    own_y, spot = me // row_size, me % row_size
    y_count = lax.psum(1, "y")
    barrier = pltpu.get_barrier_semaphore()

    def greet(k, carry):
        peer = own_y * row_size + lax.rem(spot + k, row_size)
        pl.semaphore_signal(barrier, inc=1, device_id=peer_id(peer), device_id_type=MESH)
        return carry

    lax.fori_loop(1, row_size, greet, 0)
    left_y = lax.rem(own_y + y_count - 1, y_count)
    right_y = lax.rem(own_y + 1, y_count)
    for other_y in (left_y, right_y):
        peer = other_y * row_size + spot
        pl.semaphore_signal(barrier, inc=1, device_id=peer_id(peer), device_id_type=MESH)
    pl.semaphore_wait(barrier, row_size + 1)

    def along_row(target, source):
        return pltpu.make_async_remote_copy(
            src_ref=x_ref,
            dst_ref=out_ref.at[pl.ds((own_y * row_size + source) * block, block)],
            send_sem=send_a.at[target],
            recv_sem=recv_a.at[source],
            device_id=peer_id(own_y * row_size + target),
            device_id_type=MESH,
        )

    def start_row(k, carry):
        along_row(lax.rem(spot + k, row_size), spot).start()
        return carry

    lax.fori_loop(1, row_size, start_row, 0)
    local = pltpu.make_async_copy(x_ref, out_ref.at[pl.ds(me * block, block)], local_sem)
    local.start()
    local.wait()

    def finish_row(k, carry):
        other = lax.rem(spot + k, row_size)
        along_row(other, spot).wait_send()
        along_row(other, other).wait_recv()
        return carry

    lax.fori_loop(1, row_size, finish_row, 0)
    row_rows = row_size * block

    def across(target_y, source_y):
        return pltpu.make_async_remote_copy(
            src_ref=out_ref.at[pl.ds(source_y * row_rows, row_rows)],
            dst_ref=out_ref.at[pl.ds(source_y * row_rows, row_rows)],
            send_sem=send_b.at[target_y],
            recv_sem=recv_b.at[source_y],
            device_id=peer_id(target_y * row_size + spot),
            device_id_type=MESH,
        )

    for other_y in (left_y, right_y):
        across(other_y, own_y).start()
    attend = functools.partial(
        attend_rows, out_ref, q_ref, top_ref, total_ref, acc_ref, row_rows=row_rows
    )
    attend(own_y * row_rows, first=True)
    for other_y in (left_y, right_y):
        across(other_y, own_y).wait_send()
        across(other_y, other_y).wait_recv()
    half = row_rows // 2

    def forward(target_y, source_y, part):
        rows = pl.ds(source_y * row_rows + part * half, half)
        return pltpu.make_async_remote_copy(
            src_ref=out_ref.at[rows],
            dst_ref=out_ref.at[rows],
            send_sem=send_c.at[part],
            recv_sem=recv_c.at[part],
            device_id=peer_id(target_y * row_size + spot),
            device_id_type=MESH,
        )

    far_y = lax.rem(own_y + 2, y_count)
    forward(right_y, left_y, 0).start()
    forward(left_y, right_y, 1).start()
    attend(left_y * row_rows, first=False)
    attend(right_y * row_rows, first=False)
    forward(right_y, left_y, 0).wait_send()
    forward(left_y, right_y, 1).wait_send()
    forward(right_y, far_y, 0).wait_recv()
    forward(left_y, far_y, 1).wait_recv()
    attend(far_y * row_rows, first=False)
    heads = top_ref.shape[0]
    for head in range(heads):
        columns = slice(head * HEAD, (head + 1) * HEAD)
        heads_ref[:, columns] = (acc_ref[:, columns] / total_ref[head]).astype(heads_ref.dtype)


def gather_attend(x, queries, count, row_size, heads):
    rows, width = x.shape
    q_rows = queries.shape[0]
    y_count = count // row_size
    assert y_count == 4
    return pl.pallas_call(
        functools.partial(gather_kernel, row_size),
        out_shape=jax.ShapeDtypeStruct(queries.shape, jnp.bfloat16),
        in_specs=[pl.BlockSpec(memory_space=pltpu.VMEM)] * 2,
        out_specs=pl.BlockSpec(memory_space=pltpu.VMEM),
        scratch_shapes=[
            pltpu.VMEM((count * rows, width), x.dtype),
            pltpu.VMEM((heads, q_rows, 1), jnp.float32),
            pltpu.VMEM((heads, q_rows, 1), jnp.float32),
            pltpu.VMEM(queries.shape, jnp.float32),
            pltpu.SemaphoreType.DMA((row_size,)),
            pltpu.SemaphoreType.DMA((row_size,)),
            pltpu.SemaphoreType.DMA((y_count,)),
            pltpu.SemaphoreType.DMA((y_count,)),
            pltpu.SemaphoreType.DMA((2,)),
            pltpu.SemaphoreType.DMA((2,)),
            pltpu.SemaphoreType.DMA(()),
        ],
        compiler_params=pltpu.CompilerParams(collective_id=0, has_side_effects=True),
    )(x, queries)


def head_peer(q):
    return (lax.axis_index("y"), lax.axis_index("z"), lax.axis_index("xl"), q // 2, q % 2)


def head_sum_kernel(count, part_ref, out_ref, slots, send_sem, recv_sem, send_back, recv_back):
    me = lax.axis_index(FFN)
    barrier = pltpu.get_barrier_semaphore()
    for k in range(1, count):
        pl.semaphore_signal(
            barrier, inc=1, device_id=head_peer(lax.rem(me + k, count)), device_id_type=MESH
        )
    pl.semaphore_wait(barrier, count - 1)

    def share(peer, source):
        return pltpu.make_async_remote_copy(
            src_ref=part_ref.at[peer],
            dst_ref=slots.at[source],
            send_sem=send_sem.at[peer],
            recv_sem=recv_sem.at[source],
            device_id=head_peer(peer),
            device_id_type=MESH,
        )

    def spread(peer, source):
        return pltpu.make_async_remote_copy(
            src_ref=out_ref.at[source],
            dst_ref=out_ref.at[source],
            send_sem=send_back.at[peer],
            recv_sem=recv_back.at[source],
            device_id=head_peer(peer),
            device_id_type=MESH,
        )

    peers = [lax.rem(me + k, count) for k in range(1, count)]
    for peer in peers:
        share(peer, me).start()
    total = part_ref[me].astype(jnp.float32)
    for peer in peers:
        share(peer, me).wait_send()
        share(peer, peer).wait_recv()
        total = total + slots[peer].astype(jnp.float32)
    out_ref[me] = total.astype(out_ref.dtype)
    for peer in peers:
        spread(peer, me).start()
    for peer in peers:
        spread(peer, me).wait_send()
        spread(peer, peer).wait_recv()


def head_sum(partial_value, count):
    rows, width = partial_value.shape
    parts = partial_value.astype(jnp.bfloat16).reshape(count, rows // count, width)
    summed = pl.pallas_call(
        functools.partial(head_sum_kernel, count),
        out_shape=jax.ShapeDtypeStruct(parts.shape, parts.dtype),
        in_specs=[pl.BlockSpec(memory_space=pltpu.VMEM)],
        out_specs=pl.BlockSpec(memory_space=pltpu.VMEM),
        scratch_shapes=[
            pltpu.VMEM(parts.shape, parts.dtype),
            pltpu.SemaphoreType.DMA((count,)),
            pltpu.SemaphoreType.DMA((count,)),
            pltpu.SemaphoreType.DMA((count,)),
            pltpu.SemaphoreType.DMA((count,)),
        ],
        compiler_params=pltpu.CompilerParams(collective_id=2, has_side_effects=True),
    )(parts)
    return summed.reshape(rows, width)


def scatter_kernel(
    row_size, g_ref, out_ref, slots_y, totals, sums, slots_row, send_a, recv_a, send_b, recv_b
):
    me = lax.axis_index(SLAB)
    own_y, spot = me // row_size, me % row_size
    y_count = lax.psum(1, "y")
    barrier = pltpu.get_barrier_semaphore()

    def greet(k, carry):
        peer = own_y * row_size + lax.rem(spot + k, row_size)
        pl.semaphore_signal(barrier, inc=1, device_id=peer_id(peer), device_id_type=MESH)
        return carry

    lax.fori_loop(1, row_size, greet, 0)
    others = [lax.rem(own_y + j, y_count) for j in range(1, y_count)]
    for other_y in others:
        pl.semaphore_signal(
            barrier, inc=1, device_id=peer_id(other_y * row_size + spot), device_id_type=MESH
        )
    pl.semaphore_wait(barrier, row_size + y_count - 2)

    def across(target_y, source_y):
        return pltpu.make_async_remote_copy(
            src_ref=g_ref.at[pl.ds(target_y * row_size, row_size)],
            dst_ref=slots_y.at[source_y],
            send_sem=send_a.at[target_y],
            recv_sem=recv_a.at[source_y],
            device_id=peer_id(target_y * row_size + spot),
            device_id_type=MESH,
        )

    for other_y in others:
        across(other_y, own_y).start()
    total = g_ref[pl.ds(own_y * row_size, row_size)].astype(jnp.float32)
    for other_y in others:
        across(other_y, own_y).wait_send()
        across(other_y, other_y).wait_recv()
        total = total + slots_y[other_y].astype(jnp.float32)
    totals[...] = total
    sums[...] = total.astype(sums.dtype)

    def along_row(target, source):
        return pltpu.make_async_remote_copy(
            src_ref=sums.at[target],
            dst_ref=slots_row.at[source],
            send_sem=send_b.at[target],
            recv_sem=recv_b.at[source],
            device_id=peer_id(own_y * row_size + target),
            device_id_type=MESH,
        )

    def start_row(k, carry):
        along_row(lax.rem(spot + k, row_size), spot).start()
        return carry

    lax.fori_loop(1, row_size, start_row, 0)
    out_ref[...] = totals[spot]

    def finish_row(k, carry):
        other = lax.rem(spot + k, row_size)
        along_row(other, spot).wait_send()
        along_row(other, other).wait_recv()
        out_ref[...] += slots_row[other].astype(jnp.float32)
        return carry

    lax.fori_loop(1, row_size, finish_row, 0)


def slab_scatter(g, count, row_size, collective):
    total_rows, width = g.shape
    rows = total_rows // count
    y_count = count // row_size
    tile_rows = 16
    g = g.astype(jnp.bfloat16).reshape(count, tile_rows, rows * width // tile_rows)
    summed = pl.pallas_call(
        functools.partial(scatter_kernel, row_size),
        out_shape=jax.ShapeDtypeStruct(g.shape[1:], jnp.float32),
        in_specs=[pl.BlockSpec(memory_space=pltpu.VMEM)],
        out_specs=pl.BlockSpec(memory_space=pltpu.VMEM),
        scratch_shapes=[
            pltpu.VMEM((y_count, row_size) + g.shape[1:], g.dtype),
            pltpu.VMEM((row_size,) + g.shape[1:], jnp.float32),
            pltpu.VMEM((row_size,) + g.shape[1:], g.dtype),
            pltpu.VMEM((row_size,) + g.shape[1:], g.dtype),
            pltpu.SemaphoreType.DMA((y_count,)),
            pltpu.SemaphoreType.DMA((y_count,)),
            pltpu.SemaphoreType.DMA((row_size,)),
            pltpu.SemaphoreType.DMA((row_size,)),
        ],
        compiler_params=pltpu.CompilerParams(collective_id=collective, has_side_effects=True),
    )(g)
    return summed.reshape(rows, width)


def layer_norm(values, scale_gain):
    values = values.astype(jnp.float32)
    centered = values - jnp.mean(values, axis=-1, keepdims=True)
    variance = jnp.mean(centered * centered, axis=-1, keepdims=True)
    return centered * lax.rsqrt(variance + EPSILON) * scale_gain


def rope_tables(coord_x, coord_y, coord_z, head_size):
    pair_count = head_size // 2
    position = jnp.arange(pair_count, dtype=jnp.int32)
    axis_pick = position % 3
    per_axis = (pair_count + 2) // 3
    frequency = ROPE_BASE ** (-(position // 3).astype(jnp.float32) / per_axis)
    angles = (
        coord_x[:, None] * (axis_pick == 0)
        + coord_y[:, None] * (axis_pick == 1)
        + coord_z[:, None] * (axis_pick == 2)
    ) * frequency
    return (jnp.cos(angles)[:, None, :], jnp.sin(angles)[:, None, :])


def token_tables(first_plane, planes, head_size):
    position = jnp.arange(planes * GY * GX, dtype=jnp.int32)
    coord_x = (position % GX).astype(jnp.float32)
    coord_y = (position // GX % GY).astype(jnp.float32)
    coord_z = (first_plane + position // (GX * GY)).astype(jnp.float32)
    return rope_tables(coord_x, coord_y, coord_z, head_size)


def key_tables(first_row, row_count, head_size):
    position = first_row + jnp.arange(row_count, dtype=jnp.int32)
    half_x = GX // 2
    half_y = GY // 2
    coord_x = (position % half_x).astype(jnp.float32) * 2.0 + 0.5
    coord_y = (position // half_x % half_y).astype(jnp.float32) * 2.0 + 0.5
    coord_z = (position // (half_x * half_y)).astype(jnp.float32) * 2.0 + 0.5
    return rope_tables(coord_x, coord_y, coord_z, head_size)


def rotate(values, cosine, sine_table):
    half_size = values.shape[-1] // 2
    front_half = values[..., :half_size]
    back_half = values[..., half_size:]
    return jnp.concatenate(
        [
            front_half * cosine - back_half * sine_table,
            back_half * cosine + front_half * sine_table,
        ],
        axis=-1,
    )


def make_patches(normed, planes):
    width = normed.shape[-1]
    cell_grid = normed.reshape(planes // 2, 2, GY // 2, 2, GX // 2, 2, width)
    return cell_grid.transpose(0, 2, 4, 1, 3, 5, 6).reshape(-1, 8 * width)


def depth_conv(padded, weights, planes):
    height = padded.shape[1] - 2
    width_x = padded.shape[2] - 2
    result = jnp.zeros((planes, height, width_x, padded.shape[3]), jnp.float32)
    for offset in range(27):
        shift_z = offset // 9
        shift_y = offset // 3 % 3
        shift_x = offset % 3
        window = padded[
            shift_z : shift_z + planes, shift_y : shift_y + height, shift_x : shift_x + width_x
        ]
        result = result + window.astype(jnp.float32) * weights[offset]
    return result


def conv_with_halos(cells, weights):
    count = lax.psum(1, SLAB)
    ends = count - 1
    planes = cells.shape[0]
    below = lax.ppermute(cells[planes - 1], SLAB, [(i, i + 1) for i in range(ends)])
    above = lax.ppermute(cells[0], SLAB, [(i + 1, i) for i in range(ends)])
    own = depth_conv(jnp.pad(cells, ((1, 1), (1, 1), (1, 1), (0, 0))), weights, planes)
    height, width_x = cells.shape[1], cells.shape[2]

    def plane_terms(plane, first):
        padded = jnp.pad(plane, ((1, 1), (1, 1), (0, 0))).astype(jnp.float32)
        total = jnp.zeros(plane.shape, jnp.float32)
        for offset in range(9):
            shift_y, shift_x = offset // 3, offset % 3
            window = padded[shift_y : shift_y + height, shift_x : shift_x + width_x]
            total = total + window * weights[first + offset]
        return total

    own = own.at[0].add(plane_terms(below, 0))
    return own.at[planes - 1].add(plane_terms(above, 18))


def per_device(
    tokens,
    gain_attn,
    w_reduce,
    gain_keys,
    w_query,
    w_key,
    w_value,
    w_out,
    gain_ffn,
    w_up,
    w_depth,
    w_down,
    grad_out,
):
    slab_index = lax.axis_index(SLAB)
    tok_rows = tokens.shape[0]
    heads_dev = w_query.shape[1] // HEAD
    normed = layer_norm(tokens, gain_attn).astype(jnp.bfloat16)
    patches = make_patches(normed, CZ)
    reduced = jnp.dot(patches, w_reduce, preferred_element_type=jnp.float32)
    key_input = layer_norm(reduced, gain_keys).astype(jnp.bfloat16)
    tok_cos, tok_sin = token_tables(slab_index * CZ, CZ, HEAD)
    queries = jnp.dot(normed, w_query, preferred_element_type=jnp.float32).reshape(
        tok_rows, heads_dev, HEAD
    )
    queries = rotate(queries, tok_cos, tok_sin).astype(jnp.bfloat16)
    local_rows = key_input.shape[0]
    own_cos, own_sin = key_tables(slab_index * local_rows, local_rows, HEAD)
    own_keys = jnp.dot(key_input, w_key, preferred_element_type=jnp.float32).reshape(
        local_rows, heads_dev, HEAD
    )
    own_keys = rotate(own_keys, own_cos, own_sin).astype(jnp.bfloat16)
    own_values = jnp.dot(key_input, w_value, preferred_element_type=jnp.float32).astype(
        jnp.bfloat16
    )
    key_width = heads_dev * HEAD
    pieces = jnp.concatenate([own_keys.reshape(local_rows, key_width), own_values], axis=1)
    heads_out = gather_attend(
        pieces,
        queries.reshape(tok_rows, key_width),
        lax.psum(1, SLAB),
        lax.psum(1, ("z", "xl")),
        heads_dev,
    )
    partial_value = jnp.dot(heads_out, w_out, preferred_element_type=jnp.float32)
    head_total = head_sum(partial_value, lax.psum(1, FFN)).astype(jnp.float32)
    attended = head_total.astype(jnp.bfloat16)
    residual = tokens.astype(jnp.float32) + head_total
    normed_ffn = layer_norm(residual, gain_ffn).astype(jnp.bfloat16)
    channels = w_up.shape[1]
    pre = (
        jnp.dot(normed_ffn, w_up, preferred_element_type=jnp.float32)
        .astype(jnp.bfloat16)
        .reshape(CZ, GY, GX, channels)
    )
    mixed = conv_with_halos(pre, w_depth).reshape(tok_rows, channels)
    normal_cdf = 0.5 * (1.0 + lax.erf(mixed * ROOT_HALF))
    normal_pdf = jnp.exp(-0.5 * mixed * mixed) * NORMAL_SCALE
    activated = (mixed * normal_cdf).astype(jnp.bfloat16)
    down_full = jnp.einsum("td,tc->dc", grad_out, activated, preferred_element_type=jnp.float32)
    grad_act = jnp.einsum("td,cd->tc", grad_out, w_down, preferred_element_type=jnp.float32)
    grad_mixed = (
        (grad_act * (normal_cdf + mixed * normal_pdf))
        .astype(jnp.bfloat16)
        .reshape(CZ, GY, GX, channels)
    )
    grad_pre = (
        conv_with_halos(grad_mixed, w_depth[::-1])
        .astype(jnp.bfloat16)
        .reshape(tok_rows, channels)
    )
    up_full = jnp.einsum("td,tc->dc", normed_ffn, grad_pre, preferred_element_type=jnp.float32)
    slab_count = lax.psum(1, SLAB)
    row_size = lax.psum(1, ("z", "xl"))
    grad_down = slab_scatter(down_full, slab_count, row_size, 1)
    grad_up = slab_scatter(up_full, slab_count, row_size, 5)
    return (attended, grad_up, grad_down)


def solution(mesh):
    mesh = Mesh(mesh.devices.reshape(4, 8, 2, 2, 2), SLAB + FFN)
    in_specs = (
        P(SLAB, None),
        P(),
        P(),
        P(),
        P(None, FFN),
        P(None, FFN),
        P(None, FFN),
        P(FFN, None),
        P(),
        P(None, FFN),
        P(None, FFN),
        P(FFN, None),
        P(SLAB, None),
    )
    out_specs = (P(SLAB, None), P(SLAB, FFN), P(SLAB, FFN))
    return jax.shard_map(
        per_device, mesh=mesh, in_specs=in_specs, out_specs=out_specs, check_vma=False
    )
```

```python
import functools
import math

import jax
import jax.numpy as jnp
from jax import lax
from jax.experimental import pallas as pl
from jax.experimental.pallas import tpu as pltpu
from jax.sharding import Mesh
from jax.sharding import PartitionSpec as P

HEAD = 64
GX = 16
GY = 16
CZ = 2
SLAB = ("y", "z", "xl")
FFN = ("xh", "core")


EPSILON = 1e-05
ROPE_BASE = 100.0
ROOT_HALF = 0.7071067811865476
NORMAL_SCALE = 0.3989422804014327


MESH = pl.DeviceIdType.MESH


def peer_id(p):
    return (p // 16, p // 2 % 8, p % 2, lax.axis_index("xh"), lax.axis_index("core"))


def attend_rows(kv_ref, q_ref, top_ref, total_ref, acc_ref, first_row, row_rows, first):
    heads, q_rows, _ = top_ref.shape
    q_tile = q_rows // 2
    key_width = heads * HEAD
    score_scale = HEAD ** (-0.5)
    rows = pl.ds(pl.multiple_of(first_row, row_rows), row_rows)
    for head in range(heads):
        keys = kv_ref[rows, head * HEAD : (head + 1) * HEAD]
        values = kv_ref[rows, key_width + head * HEAD : key_width + (head + 1) * HEAD]
        for start in range(0, q_rows, q_tile):
            tile = slice(start, start + q_tile)
            columns = slice(head * HEAD, (head + 1) * HEAD)
            scores = lax.dot_general(
                q_ref[tile, columns], keys, (((1,), (1,)), ((), ())),
                preferred_element_type=jnp.float32,
            ) * score_scale
            top = jnp.max(scores, axis=1, keepdims=True)
            if not first:
                old_top = top_ref[head, tile]
                top = jnp.maximum(top, old_top)
                rescale = jnp.exp(old_top - top)
            weights = jnp.exp(scores - top)
            row_sum = jnp.sum(weights, axis=1, keepdims=True)
            mixed = jnp.dot(
                weights.astype(jnp.bfloat16), values, preferred_element_type=jnp.float32
            )
            if not first:
                row_sum = row_sum + rescale * total_ref[head, tile]
                mixed = mixed + rescale * acc_ref[tile, columns]
            top_ref[head, tile] = top
            total_ref[head, tile] = row_sum
            acc_ref[tile, columns] = mixed


def gather_kernel(
    row_size, x_ref, q_ref, heads_ref, out_ref, top_ref, total_ref, acc_ref,
    send_a, recv_a, send_b, recv_b, send_c, recv_c, local_sem,
):
    me = lax.axis_index(SLAB)
    block = x_ref.shape[0]
    own_y, spot = me // row_size, me % row_size
    y_count = lax.psum(1, "y")
    barrier = pltpu.get_barrier_semaphore()

    def greet(k, carry):
        peer = own_y * row_size + lax.rem(spot + k, row_size)
        pl.semaphore_signal(barrier, inc=1, device_id=peer_id(peer), device_id_type=MESH)
        return carry

    lax.fori_loop(1, row_size, greet, 0)
    left_y = lax.rem(own_y + y_count - 1, y_count)
    right_y = lax.rem(own_y + 1, y_count)
    for other_y in (left_y, right_y):
        peer = other_y * row_size + spot
        pl.semaphore_signal(barrier, inc=1, device_id=peer_id(peer), device_id_type=MESH)
    pl.semaphore_wait(barrier, row_size + 1)

    def along_row(target, source):
        return pltpu.make_async_remote_copy(
            src_ref=x_ref,
            dst_ref=out_ref.at[pl.ds((own_y * row_size + source) * block, block)],
            send_sem=send_a.at[target],
            recv_sem=recv_a.at[source],
            device_id=peer_id(own_y * row_size + target),
            device_id_type=MESH,
        )

    def start_row(k, carry):
        along_row(lax.rem(spot + k, row_size), spot).start()
        return carry

    lax.fori_loop(1, row_size, start_row, 0)
    local = pltpu.make_async_copy(x_ref, out_ref.at[pl.ds(me * block, block)], local_sem)
    local.start()
    local.wait()

    def finish_row(k, carry):
        other = lax.rem(spot + k, row_size)
        along_row(other, spot).wait_send()
        along_row(other, other).wait_recv()
        return carry

    lax.fori_loop(1, row_size, finish_row, 0)
    row_rows = row_size * block

    def across(target_y, source_y):
        return pltpu.make_async_remote_copy(
            src_ref=out_ref.at[pl.ds(source_y * row_rows, row_rows)],
            dst_ref=out_ref.at[pl.ds(source_y * row_rows, row_rows)],
            send_sem=send_b.at[target_y],
            recv_sem=recv_b.at[source_y],
            device_id=peer_id(target_y * row_size + spot),
            device_id_type=MESH,
        )

    for other_y in (left_y, right_y):
        across(other_y, own_y).start()
    attend = functools.partial(
        attend_rows, out_ref, q_ref, top_ref, total_ref, acc_ref, row_rows=row_rows
    )
    attend(own_y * row_rows, first=True)
    for other_y in (left_y, right_y):
        across(other_y, own_y).wait_send()
        across(other_y, other_y).wait_recv()
    half = row_rows // 2

    def forward(target_y, source_y, part):
        rows = pl.ds(source_y * row_rows + part * half, half)
        return pltpu.make_async_remote_copy(
            src_ref=out_ref.at[rows],
            dst_ref=out_ref.at[rows],
            send_sem=send_c.at[part],
            recv_sem=recv_c.at[part],
            device_id=peer_id(target_y * row_size + spot),
            device_id_type=MESH,
        )

    far_y = lax.rem(own_y + 2, y_count)
    forward(right_y, left_y, 0).start()
    forward(left_y, right_y, 1).start()
    attend(left_y * row_rows, first=False)
    attend(right_y * row_rows, first=False)
    forward(right_y, left_y, 0).wait_send()
    forward(left_y, right_y, 1).wait_send()
    forward(right_y, far_y, 0).wait_recv()
    forward(left_y, far_y, 1).wait_recv()
    attend(far_y * row_rows, first=False)
    heads = top_ref.shape[0]
    for head in range(heads):
        columns = slice(head * HEAD, (head + 1) * HEAD)
        heads_ref[:, columns] = (acc_ref[:, columns] / total_ref[head]).astype(heads_ref.dtype)


def gather_attend(x, queries, count, row_size, heads):
    rows, width = x.shape
    q_rows = queries.shape[0]
    y_count = count // row_size
    assert y_count == 4
    return pl.pallas_call(
        functools.partial(gather_kernel, row_size),
        out_shape=jax.ShapeDtypeStruct(queries.shape, jnp.bfloat16),
        in_specs=[pl.BlockSpec(memory_space=pltpu.VMEM)] * 2,
        out_specs=pl.BlockSpec(memory_space=pltpu.VMEM),
        scratch_shapes=[
            pltpu.VMEM((count * rows, width), x.dtype),
            pltpu.VMEM((heads, q_rows, 1), jnp.float32),
            pltpu.VMEM((heads, q_rows, 1), jnp.float32),
            pltpu.VMEM(queries.shape, jnp.float32),
            pltpu.SemaphoreType.DMA((row_size,)),
            pltpu.SemaphoreType.DMA((row_size,)),
            pltpu.SemaphoreType.DMA((y_count,)),
            pltpu.SemaphoreType.DMA((y_count,)),
            pltpu.SemaphoreType.DMA((2,)),
            pltpu.SemaphoreType.DMA((2,)),
            pltpu.SemaphoreType.DMA(()),
        ],
        compiler_params=pltpu.CompilerParams(collective_id=0, has_side_effects=True),
    )(x, queries)


def head_peer(q):
    return (lax.axis_index("y"), lax.axis_index("z"), lax.axis_index("xl"), q // 2, q % 2)


def head_sum_kernel(count, part_ref, out_ref, slots, send_sem, recv_sem, send_back, recv_back):
    me = lax.axis_index(FFN)
    barrier = pltpu.get_barrier_semaphore()
    for k in range(1, count):
        pl.semaphore_signal(
            barrier, inc=1, device_id=head_peer(lax.rem(me + k, count)), device_id_type=MESH
        )
    pl.semaphore_wait(barrier, count - 1)

    def share(peer, source):
        return pltpu.make_async_remote_copy(
            src_ref=part_ref.at[peer],
            dst_ref=slots.at[source],
            send_sem=send_sem.at[peer],
            recv_sem=recv_sem.at[source],
            device_id=head_peer(peer),
            device_id_type=MESH,
        )

    def spread(peer, source):
        return pltpu.make_async_remote_copy(
            src_ref=out_ref.at[source],
            dst_ref=out_ref.at[source],
            send_sem=send_back.at[peer],
            recv_sem=recv_back.at[source],
            device_id=head_peer(peer),
            device_id_type=MESH,
        )

    peers = [lax.rem(me + k, count) for k in range(1, count)]
    for peer in peers:
        share(peer, me).start()
    total = part_ref[me].astype(jnp.float32)
    for peer in peers:
        share(peer, me).wait_send()
        share(peer, peer).wait_recv()
        total = total + slots[peer].astype(jnp.float32)
    out_ref[me] = total.astype(out_ref.dtype)
    for peer in peers:
        spread(peer, me).start()
    for peer in peers:
        spread(peer, me).wait_send()
        spread(peer, peer).wait_recv()


def head_sum(partial_value, count):
    rows, width = partial_value.shape
    parts = partial_value.astype(jnp.bfloat16).reshape(count, rows // count, width)
    summed = pl.pallas_call(
        functools.partial(head_sum_kernel, count),
        out_shape=jax.ShapeDtypeStruct(parts.shape, parts.dtype),
        in_specs=[pl.BlockSpec(memory_space=pltpu.VMEM)],
        out_specs=pl.BlockSpec(memory_space=pltpu.VMEM),
        scratch_shapes=[
            pltpu.VMEM(parts.shape, parts.dtype),
            pltpu.SemaphoreType.DMA((count,)),
            pltpu.SemaphoreType.DMA((count,)),
            pltpu.SemaphoreType.DMA((count,)),
            pltpu.SemaphoreType.DMA((count,)),
        ],
        compiler_params=pltpu.CompilerParams(collective_id=2, has_side_effects=True),
    )(parts)
    return summed.reshape(rows, width)


def scatter_kernel(
    row_size, g_ref, out_ref, slots_y, totals, sums, slots_row, send_a, recv_a, send_b, recv_b
):
    me = lax.axis_index(SLAB)
    own_y, spot = me // row_size, me % row_size
    y_count = lax.psum(1, "y")
    barrier = pltpu.get_barrier_semaphore()

    def greet(k, carry):
        peer = own_y * row_size + lax.rem(spot + k, row_size)
        pl.semaphore_signal(barrier, inc=1, device_id=peer_id(peer), device_id_type=MESH)
        return carry

    lax.fori_loop(1, row_size, greet, 0)
    others = [lax.rem(own_y + j, y_count) for j in range(1, y_count)]
    for other_y in others:
        pl.semaphore_signal(
            barrier, inc=1, device_id=peer_id(other_y * row_size + spot), device_id_type=MESH
        )
    pl.semaphore_wait(barrier, row_size + y_count - 2)

    def across(target_y, source_y):
        return pltpu.make_async_remote_copy(
            src_ref=g_ref.at[pl.ds(target_y * row_size, row_size)],
            dst_ref=slots_y.at[source_y],
            send_sem=send_a.at[target_y],
            recv_sem=recv_a.at[source_y],
            device_id=peer_id(target_y * row_size + spot),
            device_id_type=MESH,
        )

    for other_y in others:
        across(other_y, own_y).start()
    total = g_ref[pl.ds(own_y * row_size, row_size)].astype(jnp.float32)
    for other_y in others:
        across(other_y, own_y).wait_send()
        across(other_y, other_y).wait_recv()
        total = total + slots_y[other_y].astype(jnp.float32)
    totals[...] = total
    sums[...] = total.astype(sums.dtype)

    def along_row(target, source):
        return pltpu.make_async_remote_copy(
            src_ref=sums.at[target],
            dst_ref=slots_row.at[source],
            send_sem=send_b.at[target],
            recv_sem=recv_b.at[source],
            device_id=peer_id(own_y * row_size + target),
            device_id_type=MESH,
        )

    def start_row(k, carry):
        along_row(lax.rem(spot + k, row_size), spot).start()
        return carry

    lax.fori_loop(1, row_size, start_row, 0)
    out_ref[...] = totals[spot]

    def finish_row(k, carry):
        other = lax.rem(spot + k, row_size)
        along_row(other, spot).wait_send()
        along_row(other, other).wait_recv()
        out_ref[...] += slots_row[other].astype(jnp.float32)
        return carry

    lax.fori_loop(1, row_size, finish_row, 0)


def slab_scatter(g, count, row_size):
    total_rows, width = g.shape
    rows = total_rows // count
    y_count = count // row_size
    tile_rows = 16
    g = g.astype(jnp.bfloat16).reshape(count, tile_rows, rows * width // tile_rows)
    summed = pl.pallas_call(
        functools.partial(scatter_kernel, row_size),
        out_shape=jax.ShapeDtypeStruct(g.shape[1:], jnp.float32),
        in_specs=[pl.BlockSpec(memory_space=pltpu.VMEM)],
        out_specs=pl.BlockSpec(memory_space=pltpu.VMEM),
        scratch_shapes=[
            pltpu.VMEM((y_count, row_size) + g.shape[1:], g.dtype),
            pltpu.VMEM((row_size,) + g.shape[1:], jnp.float32),
            pltpu.VMEM((row_size,) + g.shape[1:], g.dtype),
            pltpu.VMEM((row_size,) + g.shape[1:], g.dtype),
            pltpu.SemaphoreType.DMA((y_count,)),
            pltpu.SemaphoreType.DMA((y_count,)),
            pltpu.SemaphoreType.DMA((row_size,)),
            pltpu.SemaphoreType.DMA((row_size,)),
        ],
        compiler_params=pltpu.CompilerParams(collective_id=1, has_side_effects=True),
    )(g)
    return summed.reshape(rows, width)


def layer_norm(values, scale_gain):
    values = values.astype(jnp.float32)
    centered = values - jnp.mean(values, axis=-1, keepdims=True)
    variance = jnp.mean(centered * centered, axis=-1, keepdims=True)
    return centered * lax.rsqrt(variance + EPSILON) * scale_gain


def rope_tables(coord_x, coord_y, coord_z, head_size):
    pair_count = head_size // 2
    position = jnp.arange(pair_count, dtype=jnp.int32)
    axis_pick = position % 3
    per_axis = (pair_count + 2) // 3
    frequency = ROPE_BASE ** (-(position // 3).astype(jnp.float32) / per_axis)
    angles = (
        coord_x[:, None] * (axis_pick == 0)
        + coord_y[:, None] * (axis_pick == 1)
        + coord_z[:, None] * (axis_pick == 2)
    ) * frequency
    return (jnp.cos(angles)[:, None, :], jnp.sin(angles)[:, None, :])


def token_tables(first_plane, planes, head_size):
    position = jnp.arange(planes * GY * GX, dtype=jnp.int32)
    coord_x = (position % GX).astype(jnp.float32)
    coord_y = (position // GX % GY).astype(jnp.float32)
    coord_z = (first_plane + position // (GX * GY)).astype(jnp.float32)
    return rope_tables(coord_x, coord_y, coord_z, head_size)


def key_tables(first_row, row_count, head_size):
    position = first_row + jnp.arange(row_count, dtype=jnp.int32)
    half_x = GX // 2
    half_y = GY // 2
    coord_x = (position % half_x).astype(jnp.float32) * 2.0 + 0.5
    coord_y = (position // half_x % half_y).astype(jnp.float32) * 2.0 + 0.5
    coord_z = (position // (half_x * half_y)).astype(jnp.float32) * 2.0 + 0.5
    return rope_tables(coord_x, coord_y, coord_z, head_size)


def rotate(values, cosine, sine_table):
    half_size = values.shape[-1] // 2
    front_half = values[..., :half_size]
    back_half = values[..., half_size:]
    return jnp.concatenate(
        [
            front_half * cosine - back_half * sine_table,
            back_half * cosine + front_half * sine_table,
        ],
        axis=-1,
    )


def make_patches(normed, planes):
    width = normed.shape[-1]
    cell_grid = normed.reshape(planes // 2, 2, GY // 2, 2, GX // 2, 2, width)
    return cell_grid.transpose(0, 2, 4, 1, 3, 5, 6).reshape(-1, 8 * width)


def depth_conv(padded, weights, planes):
    height = padded.shape[1] - 2
    width_x = padded.shape[2] - 2
    result = jnp.zeros((planes, height, width_x, padded.shape[3]), jnp.float32)
    for offset in range(27):
        shift_z = offset // 9
        shift_y = offset // 3 % 3
        shift_x = offset % 3
        window = padded[
            shift_z : shift_z + planes, shift_y : shift_y + height, shift_x : shift_x + width_x
        ]
        result = result + window.astype(jnp.float32) * weights[offset]
    return result


def conv_with_halos(cells, weights):
    count = lax.psum(1, SLAB)
    ends = count - 1
    planes = cells.shape[0]
    below = lax.ppermute(cells[planes - 1], SLAB, [(i, i + 1) for i in range(ends)])
    above = lax.ppermute(cells[0], SLAB, [(i + 1, i) for i in range(ends)])
    own = depth_conv(jnp.pad(cells, ((1, 1), (1, 1), (1, 1), (0, 0))), weights, planes)
    height, width_x = cells.shape[1], cells.shape[2]

    def plane_terms(plane, first):
        padded = jnp.pad(plane, ((1, 1), (1, 1), (0, 0))).astype(jnp.float32)
        total = jnp.zeros(plane.shape, jnp.float32)
        for offset in range(9):
            shift_y, shift_x = offset // 3, offset % 3
            window = padded[shift_y : shift_y + height, shift_x : shift_x + width_x]
            total = total + window * weights[first + offset]
        return total

    own = own.at[0].add(plane_terms(below, 0))
    return own.at[planes - 1].add(plane_terms(above, 18))


def per_device(
    tokens,
    gain_attn,
    w_reduce,
    gain_keys,
    w_query,
    w_key,
    w_value,
    w_out,
    gain_ffn,
    w_up,
    w_depth,
    w_down,
    grad_out,
):
    slab_index = lax.axis_index(SLAB)
    tok_rows = tokens.shape[0]
    heads_dev = w_query.shape[1] // HEAD
    normed = layer_norm(tokens, gain_attn).astype(jnp.bfloat16)
    patches = make_patches(normed, CZ)
    reduced = jnp.dot(patches, w_reduce, preferred_element_type=jnp.float32)
    key_input = layer_norm(reduced, gain_keys).astype(jnp.bfloat16)
    tok_cos, tok_sin = token_tables(slab_index * CZ, CZ, HEAD)
    queries = jnp.dot(normed, w_query, preferred_element_type=jnp.float32).reshape(
        tok_rows, heads_dev, HEAD
    )
    queries = rotate(queries, tok_cos, tok_sin).astype(jnp.bfloat16)
    local_rows = key_input.shape[0]
    own_cos, own_sin = key_tables(slab_index * local_rows, local_rows, HEAD)
    own_keys = jnp.dot(key_input, w_key, preferred_element_type=jnp.float32).reshape(
        local_rows, heads_dev, HEAD
    )
    own_keys = rotate(own_keys, own_cos, own_sin).astype(jnp.bfloat16)
    own_values = jnp.dot(key_input, w_value, preferred_element_type=jnp.float32).astype(
        jnp.bfloat16
    )
    key_width = heads_dev * HEAD
    pieces = jnp.concatenate([own_keys.reshape(local_rows, key_width), own_values], axis=1)
    heads_out = gather_attend(
        pieces,
        queries.reshape(tok_rows, key_width),
        lax.psum(1, SLAB),
        lax.psum(1, ("z", "xl")),
        heads_dev,
    )
    partial_value = jnp.dot(heads_out, w_out, preferred_element_type=jnp.float32)
    head_total = head_sum(partial_value, lax.psum(1, FFN)).astype(jnp.float32)
    attended = head_total.astype(jnp.bfloat16)
    residual = tokens.astype(jnp.float32) + head_total
    normed_ffn = layer_norm(residual, gain_ffn).astype(jnp.bfloat16)
    channels = w_up.shape[1]
    pre = (
        jnp.dot(normed_ffn, w_up, preferred_element_type=jnp.float32)
        .astype(jnp.bfloat16)
        .reshape(CZ, GY, GX, channels)
    )
    mixed = conv_with_halos(pre, w_depth).reshape(tok_rows, channels)
    normal_cdf = 0.5 * (1.0 + lax.erf(mixed * ROOT_HALF))
    normal_pdf = jnp.exp(-0.5 * mixed * mixed) * NORMAL_SCALE
    activated = (mixed * normal_cdf).astype(jnp.bfloat16)
    grad_act = lax.optimization_barrier(
        jnp.einsum("td,cd->tc", grad_out, w_down, preferred_element_type=jnp.float32)
    )
    grad_mixed = (
        (grad_act * (normal_cdf + mixed * normal_pdf))
        .astype(jnp.bfloat16)
        .reshape(CZ, GY, GX, channels)
    )
    grad_pre = (
        conv_with_halos(grad_mixed, w_depth[::-1])
        .astype(jnp.bfloat16)
        .reshape(tok_rows, channels)
    )
    up_full = jnp.einsum("td,tc->dc", normed_ffn, grad_pre, preferred_element_type=jnp.float32)
    down_full = jnp.einsum("td,tc->dc", grad_out, activated, preferred_element_type=jnp.float32)
    grads = slab_scatter(
        jnp.concatenate([up_full, down_full], axis=1),
        lax.psum(1, SLAB),
        lax.psum(1, ("z", "xl")),
    )
    return (attended, grads[:, :channels], grads[:, channels:])


def solution(mesh):
    mesh = Mesh(mesh.devices.reshape(4, 8, 2, 2, 2), SLAB + FFN)
    in_specs = (
        P(SLAB, None),
        P(),
        P(),
        P(),
        P(None, FFN),
        P(None, FFN),
        P(None, FFN),
        P(FFN, None),
        P(),
        P(None, FFN),
        P(None, FFN),
        P(FFN, None),
        P(SLAB, None),
    )
    out_specs = (P(SLAB, None), P(SLAB, FFN), P(SLAB, FFN))
    return jax.shard_map(
        per_device, mesh=mesh, in_specs=in_specs, out_specs=out_specs, check_vma=False
    )
```

```python
import functools
import math

import jax
import jax.numpy as jnp
from jax import lax
from jax.experimental import pallas as pl
from jax.experimental.pallas import tpu as pltpu
from jax.sharding import Mesh
from jax.sharding import PartitionSpec as P

HEAD = 64
GX = 16
GY = 16
CZ = 2
SLAB = ("y", "z", "xl")
FFN = ("xh", "core")


EPSILON = 1e-05
ROPE_BASE = 100.0
ROOT_HALF = 0.7071067811865476
NORMAL_SCALE = 0.3989422804014327


MESH = pl.DeviceIdType.MESH


def peer_id(p):
    return (p // 16, p // 2 % 8, p % 2, lax.axis_index("xh"), lax.axis_index("core"))


def attend_rows(kv_ref, q_ref, top_ref, total_ref, acc_ref, first_row, row_rows, first):
    heads, q_rows, _ = top_ref.shape
    q_tile = q_rows // 2
    key_width = heads * HEAD
    score_scale = HEAD ** (-0.5)
    rows = pl.ds(pl.multiple_of(first_row, row_rows), row_rows)
    for head in range(heads):
        keys = kv_ref[rows, head * HEAD : (head + 1) * HEAD]
        values = kv_ref[rows, key_width + head * HEAD : key_width + (head + 1) * HEAD]
        for start in range(0, q_rows, q_tile):
            tile = slice(start, start + q_tile)
            columns = slice(head * HEAD, (head + 1) * HEAD)
            scores = lax.dot_general(
                q_ref[tile, columns], keys, (((1,), (1,)), ((), ())),
                preferred_element_type=jnp.float32,
            ) * score_scale
            top = jnp.max(scores, axis=1, keepdims=True)
            if not first:
                old_top = top_ref[head, tile]
                top = jnp.maximum(top, old_top)
                rescale = jnp.exp(old_top - top)
            weights = jnp.exp(scores - top)
            row_sum = jnp.sum(weights, axis=1, keepdims=True)
            mixed = jnp.dot(
                weights.astype(jnp.bfloat16), values, preferred_element_type=jnp.float32
            )
            if not first:
                row_sum = row_sum + rescale * total_ref[head, tile]
                mixed = mixed + rescale * acc_ref[tile, columns]
            top_ref[head, tile] = top
            total_ref[head, tile] = row_sum
            acc_ref[tile, columns] = mixed


def gather_kernel(
    row_size, x_ref, q_ref, heads_ref, out_ref, top_ref, total_ref, acc_ref,
    send_a, recv_a, send_b, recv_b, send_c, recv_c, local_sem,
):
    me = lax.axis_index(SLAB)
    block = x_ref.shape[0]
    own_y, spot = me // row_size, me % row_size
    y_count = lax.psum(1, "y")
    barrier = pltpu.get_barrier_semaphore()

    def greet(k, carry):
        peer = own_y * row_size + lax.rem(spot + k, row_size)
        pl.semaphore_signal(barrier, inc=1, device_id=peer_id(peer), device_id_type=MESH)
        return carry

    lax.fori_loop(1, row_size, greet, 0)
    left_y = lax.rem(own_y + y_count - 1, y_count)
    right_y = lax.rem(own_y + 1, y_count)
    for other_y in (left_y, right_y):
        peer = other_y * row_size + spot
        pl.semaphore_signal(barrier, inc=1, device_id=peer_id(peer), device_id_type=MESH)
    pl.semaphore_wait(barrier, row_size + 1)

    def along_row(target, source):
        return pltpu.make_async_remote_copy(
            src_ref=x_ref,
            dst_ref=out_ref.at[pl.ds((own_y * row_size + source) * block, block)],
            send_sem=send_a.at[target],
            recv_sem=recv_a.at[source],
            device_id=peer_id(own_y * row_size + target),
            device_id_type=MESH,
        )

    def start_row(k, carry):
        along_row(lax.rem(spot + k, row_size), spot).start()
        return carry

    lax.fori_loop(1, row_size, start_row, 0)
    local = pltpu.make_async_copy(x_ref, out_ref.at[pl.ds(me * block, block)], local_sem)
    local.start()
    local.wait()

    def finish_row(k, carry):
        other = lax.rem(spot + k, row_size)
        along_row(other, spot).wait_send()
        along_row(other, other).wait_recv()
        return carry

    lax.fori_loop(1, row_size, finish_row, 0)
    row_rows = row_size * block

    def across(target_y, source_y):
        return pltpu.make_async_remote_copy(
            src_ref=out_ref.at[pl.ds(source_y * row_rows, row_rows)],
            dst_ref=out_ref.at[pl.ds(source_y * row_rows, row_rows)],
            send_sem=send_b.at[target_y],
            recv_sem=recv_b.at[source_y],
            device_id=peer_id(target_y * row_size + spot),
            device_id_type=MESH,
        )

    for other_y in (left_y, right_y):
        across(other_y, own_y).start()
    attend = functools.partial(
        attend_rows, out_ref, q_ref, top_ref, total_ref, acc_ref, row_rows=row_rows
    )
    attend(own_y * row_rows, first=True)
    for other_y in (left_y, right_y):
        across(other_y, own_y).wait_send()
        across(other_y, other_y).wait_recv()
    half = row_rows // 2

    def forward(target_y, source_y, part):
        rows = pl.ds(source_y * row_rows + part * half, half)
        return pltpu.make_async_remote_copy(
            src_ref=out_ref.at[rows],
            dst_ref=out_ref.at[rows],
            send_sem=send_c.at[part],
            recv_sem=recv_c.at[part],
            device_id=peer_id(target_y * row_size + spot),
            device_id_type=MESH,
        )

    far_y = lax.rem(own_y + 2, y_count)
    forward(right_y, left_y, 0).start()
    forward(left_y, right_y, 1).start()
    attend(left_y * row_rows, first=False)
    attend(right_y * row_rows, first=False)
    forward(right_y, left_y, 0).wait_send()
    forward(left_y, right_y, 1).wait_send()
    forward(right_y, far_y, 0).wait_recv()
    forward(left_y, far_y, 1).wait_recv()
    attend(far_y * row_rows, first=False)
    heads = top_ref.shape[0]
    for head in range(heads):
        columns = slice(head * HEAD, (head + 1) * HEAD)
        heads_ref[:, columns] = (acc_ref[:, columns] / total_ref[head]).astype(heads_ref.dtype)


def gather_attend(x, queries, count, row_size, heads):
    rows, width = x.shape
    q_rows = queries.shape[0]
    y_count = count // row_size
    assert y_count == 4
    return pl.pallas_call(
        functools.partial(gather_kernel, row_size),
        out_shape=jax.ShapeDtypeStruct(queries.shape, jnp.bfloat16),
        in_specs=[pl.BlockSpec(memory_space=pltpu.VMEM)] * 2,
        out_specs=pl.BlockSpec(memory_space=pltpu.VMEM),
        scratch_shapes=[
            pltpu.VMEM((count * rows, width), x.dtype),
            pltpu.VMEM((heads, q_rows, 1), jnp.float32),
            pltpu.VMEM((heads, q_rows, 1), jnp.float32),
            pltpu.VMEM(queries.shape, jnp.float32),
            pltpu.SemaphoreType.DMA((row_size,)),
            pltpu.SemaphoreType.DMA((row_size,)),
            pltpu.SemaphoreType.DMA((y_count,)),
            pltpu.SemaphoreType.DMA((y_count,)),
            pltpu.SemaphoreType.DMA((2,)),
            pltpu.SemaphoreType.DMA((2,)),
            pltpu.SemaphoreType.DMA(()),
        ],
        compiler_params=pltpu.CompilerParams(collective_id=0, has_side_effects=True),
    )(x, queries)


def head_peer(q):
    return (lax.axis_index("y"), lax.axis_index("z"), lax.axis_index("xl"), q // 2, q % 2)


def head_sum_kernel(count, part_ref, out_ref, slots, send_sem, recv_sem, send_back, recv_back):
    me = lax.axis_index(FFN)
    barrier = pltpu.get_barrier_semaphore()
    for k in range(1, count):
        pl.semaphore_signal(
            barrier, inc=1, device_id=head_peer(lax.rem(me + k, count)), device_id_type=MESH
        )
    pl.semaphore_wait(barrier, count - 1)

    def share(peer, source):
        return pltpu.make_async_remote_copy(
            src_ref=part_ref.at[peer],
            dst_ref=slots.at[source],
            send_sem=send_sem.at[peer],
            recv_sem=recv_sem.at[source],
            device_id=head_peer(peer),
            device_id_type=MESH,
        )

    def spread(peer, source):
        return pltpu.make_async_remote_copy(
            src_ref=out_ref.at[source],
            dst_ref=out_ref.at[source],
            send_sem=send_back.at[peer],
            recv_sem=recv_back.at[source],
            device_id=head_peer(peer),
            device_id_type=MESH,
        )

    peers = [lax.rem(me + k, count) for k in range(1, count)]
    for peer in peers:
        share(peer, me).start()
    total = part_ref[me].astype(jnp.float32)
    for peer in peers:
        share(peer, me).wait_send()
        share(peer, peer).wait_recv()
        total = total + slots[peer].astype(jnp.float32)
    out_ref[me] = total.astype(out_ref.dtype)
    for peer in peers:
        spread(peer, me).start()
    for peer in peers:
        spread(peer, me).wait_send()
        spread(peer, peer).wait_recv()


def head_sum(partial_value, count):
    rows, width = partial_value.shape
    parts = partial_value.astype(jnp.bfloat16).reshape(count, rows // count, width)
    summed = pl.pallas_call(
        functools.partial(head_sum_kernel, count),
        out_shape=jax.ShapeDtypeStruct(parts.shape, parts.dtype),
        in_specs=[pl.BlockSpec(memory_space=pltpu.VMEM)],
        out_specs=pl.BlockSpec(memory_space=pltpu.VMEM),
        scratch_shapes=[
            pltpu.VMEM(parts.shape, parts.dtype),
            pltpu.SemaphoreType.DMA((count,)),
            pltpu.SemaphoreType.DMA((count,)),
            pltpu.SemaphoreType.DMA((count,)),
            pltpu.SemaphoreType.DMA((count,)),
        ],
        compiler_params=pltpu.CompilerParams(collective_id=2, has_side_effects=True),
    )(parts)
    return summed.reshape(rows, width)


def scatter_kernel(
    row_size, g_ref, out_ref, slots_y, totals, sums, slots_row, send_a, recv_a, send_b, recv_b
):
    me = lax.axis_index(SLAB)
    own_y, spot = me // row_size, me % row_size
    y_count = lax.psum(1, "y")
    barrier = pltpu.get_barrier_semaphore()

    def greet(k, carry):
        peer = own_y * row_size + lax.rem(spot + k, row_size)
        pl.semaphore_signal(barrier, inc=1, device_id=peer_id(peer), device_id_type=MESH)
        return carry

    lax.fori_loop(1, row_size, greet, 0)
    left_y = lax.rem(own_y + y_count - 1, y_count)
    right_y = lax.rem(own_y + 1, y_count)
    far_y = lax.rem(own_y + 2, y_count)
    for other_y in (left_y, right_y):
        pl.semaphore_signal(
            barrier, inc=1, device_id=peer_id(other_y * row_size + spot), device_id_type=MESH
        )
    pl.semaphore_wait(barrier, row_size + 1)
    half = row_size // 2

    def hop(src, dst, index, target_y):
        return pltpu.make_async_remote_copy(
            src_ref=src,
            dst_ref=dst,
            send_sem=send_a.at[index],
            recv_sem=recv_a.at[index],
            device_id=peer_id(target_y * row_size + spot),
            device_id_type=MESH,
        )

    def rows_of(row_y, first, count):
        return g_ref.at[pl.ds(row_y * row_size + first, count)]

    near_right = hop(rows_of(right_y, 0, row_size), slots_y.at[0], 0, right_y)
    near_left = hop(rows_of(left_y, 0, row_size), slots_y.at[1], 1, left_y)
    low, high = pl.ds(0, half), pl.ds(half, half)
    pass_right = hop(rows_of(far_y, 0, half), slots_y.at[2, low], 2, right_y)
    pass_left = hop(rows_of(far_y, half, half), slots_y.at[2, high], 3, left_y)
    for copy in (pass_right, pass_left, near_right, near_left):
        copy.start()
    pass_right.wait_recv()
    on_right = hop(slots_y.at[2, low], slots_y.at[3, low], 4, right_y)
    on_right.start()
    pass_left.wait_recv()
    on_left = hop(slots_y.at[2, high], slots_y.at[3, high], 5, left_y)
    on_left.start()
    total = g_ref[pl.ds(own_y * row_size, row_size)].astype(jnp.float32)
    for copy in (near_right, near_left):
        copy.wait_recv()
    total = total + slots_y[0].astype(jnp.float32) + slots_y[1].astype(jnp.float32)
    for copy in (on_right, on_left):
        copy.wait_recv()
    total = total + slots_y[3].astype(jnp.float32)
    for copy in (pass_right, pass_left, near_right, near_left, on_right, on_left):
        copy.wait_send()
    totals[...] = total
    sums[...] = total.astype(sums.dtype)

    def along_row(target, source):
        return pltpu.make_async_remote_copy(
            src_ref=sums.at[target],
            dst_ref=slots_row.at[source],
            send_sem=send_b.at[target],
            recv_sem=recv_b.at[source],
            device_id=peer_id(own_y * row_size + target),
            device_id_type=MESH,
        )

    def start_row(k, carry):
        along_row(lax.rem(spot + k, row_size), spot).start()
        return carry

    lax.fori_loop(1, row_size, start_row, 0)
    out_ref[...] = totals[spot]

    def finish_row(k, carry):
        other = lax.rem(spot + k, row_size)
        along_row(other, spot).wait_send()
        along_row(other, other).wait_recv()
        out_ref[...] += slots_row[other].astype(jnp.float32)
        return carry

    lax.fori_loop(1, row_size, finish_row, 0)


def slab_scatter(g, count, row_size):
    total_rows, width = g.shape
    rows = total_rows // count
    y_count = count // row_size
    assert y_count == 4
    tile_rows = 16
    g = g.astype(jnp.bfloat16).reshape(count, tile_rows, rows * width // tile_rows)
    summed = pl.pallas_call(
        functools.partial(scatter_kernel, row_size),
        out_shape=jax.ShapeDtypeStruct(g.shape[1:], jnp.float32),
        in_specs=[pl.BlockSpec(memory_space=pltpu.VMEM)],
        out_specs=pl.BlockSpec(memory_space=pltpu.VMEM),
        scratch_shapes=[
            pltpu.VMEM((y_count, row_size) + g.shape[1:], g.dtype),
            pltpu.VMEM((row_size,) + g.shape[1:], jnp.float32),
            pltpu.VMEM((row_size,) + g.shape[1:], g.dtype),
            pltpu.VMEM((row_size,) + g.shape[1:], g.dtype),
            pltpu.SemaphoreType.DMA((6,)),
            pltpu.SemaphoreType.DMA((6,)),
            pltpu.SemaphoreType.DMA((row_size,)),
            pltpu.SemaphoreType.DMA((row_size,)),
        ],
        compiler_params=pltpu.CompilerParams(collective_id=1, has_side_effects=True),
    )(g)
    return summed.reshape(rows, width)


def layer_norm(values, scale_gain):
    values = values.astype(jnp.float32)
    centered = values - jnp.mean(values, axis=-1, keepdims=True)
    variance = jnp.mean(centered * centered, axis=-1, keepdims=True)
    return centered * lax.rsqrt(variance + EPSILON) * scale_gain


def rope_tables(coord_x, coord_y, coord_z, head_size):
    pair_count = head_size // 2
    position = jnp.arange(pair_count, dtype=jnp.int32)
    axis_pick = position % 3
    per_axis = (pair_count + 2) // 3
    frequency = ROPE_BASE ** (-(position // 3).astype(jnp.float32) / per_axis)
    angles = (
        coord_x[:, None] * (axis_pick == 0)
        + coord_y[:, None] * (axis_pick == 1)
        + coord_z[:, None] * (axis_pick == 2)
    ) * frequency
    return (jnp.cos(angles)[:, None, :], jnp.sin(angles)[:, None, :])


def token_tables(first_plane, planes, head_size):
    position = jnp.arange(planes * GY * GX, dtype=jnp.int32)
    coord_x = (position % GX).astype(jnp.float32)
    coord_y = (position // GX % GY).astype(jnp.float32)
    coord_z = (first_plane + position // (GX * GY)).astype(jnp.float32)
    return rope_tables(coord_x, coord_y, coord_z, head_size)


def key_tables(first_row, row_count, head_size):
    position = first_row + jnp.arange(row_count, dtype=jnp.int32)
    half_x = GX // 2
    half_y = GY // 2
    coord_x = (position % half_x).astype(jnp.float32) * 2.0 + 0.5
    coord_y = (position // half_x % half_y).astype(jnp.float32) * 2.0 + 0.5
    coord_z = (position // (half_x * half_y)).astype(jnp.float32) * 2.0 + 0.5
    return rope_tables(coord_x, coord_y, coord_z, head_size)


def rotate(values, cosine, sine_table):
    half_size = values.shape[-1] // 2
    front_half = values[..., :half_size]
    back_half = values[..., half_size:]
    return jnp.concatenate(
        [
            front_half * cosine - back_half * sine_table,
            back_half * cosine + front_half * sine_table,
        ],
        axis=-1,
    )


def make_patches(normed, planes):
    width = normed.shape[-1]
    cell_grid = normed.reshape(planes // 2, 2, GY // 2, 2, GX // 2, 2, width)
    return cell_grid.transpose(0, 2, 4, 1, 3, 5, 6).reshape(-1, 8 * width)


def depth_conv(padded, weights, planes):
    height = padded.shape[1] - 2
    width_x = padded.shape[2] - 2
    result = jnp.zeros((planes, height, width_x, padded.shape[3]), jnp.float32)
    for offset in range(27):
        shift_z = offset // 9
        shift_y = offset // 3 % 3
        shift_x = offset % 3
        window = padded[
            shift_z : shift_z + planes, shift_y : shift_y + height, shift_x : shift_x + width_x
        ]
        result = result + window.astype(jnp.float32) * weights[offset]
    return result


def conv_with_halos(cells, weights):
    count = lax.psum(1, SLAB)
    ends = count - 1
    planes = cells.shape[0]
    below = lax.ppermute(cells[planes - 1], SLAB, [(i, i + 1) for i in range(ends)])
    above = lax.ppermute(cells[0], SLAB, [(i + 1, i) for i in range(ends)])
    own = depth_conv(jnp.pad(cells, ((1, 1), (1, 1), (1, 1), (0, 0))), weights, planes)
    height, width_x = cells.shape[1], cells.shape[2]

    def plane_terms(plane, first):
        padded = jnp.pad(plane, ((1, 1), (1, 1), (0, 0))).astype(jnp.float32)
        total = jnp.zeros(plane.shape, jnp.float32)
        for offset in range(9):
            shift_y, shift_x = offset // 3, offset % 3
            window = padded[shift_y : shift_y + height, shift_x : shift_x + width_x]
            total = total + window * weights[first + offset]
        return total

    own = own.at[0].add(plane_terms(below, 0))
    return own.at[planes - 1].add(plane_terms(above, 18))


def per_device(
    tokens,
    gain_attn,
    w_reduce,
    gain_keys,
    w_query,
    w_key,
    w_value,
    w_out,
    gain_ffn,
    w_up,
    w_depth,
    w_down,
    grad_out,
):
    slab_index = lax.axis_index(SLAB)
    tok_rows = tokens.shape[0]
    heads_dev = w_query.shape[1] // HEAD
    normed = layer_norm(tokens, gain_attn).astype(jnp.bfloat16)
    patches = make_patches(normed, CZ)
    reduced = jnp.dot(patches, w_reduce, preferred_element_type=jnp.float32)
    key_input = layer_norm(reduced, gain_keys).astype(jnp.bfloat16)
    tok_cos, tok_sin = token_tables(slab_index * CZ, CZ, HEAD)
    queries = jnp.dot(normed, w_query, preferred_element_type=jnp.float32).reshape(
        tok_rows, heads_dev, HEAD
    )
    queries = rotate(queries, tok_cos, tok_sin).astype(jnp.bfloat16)
    local_rows = key_input.shape[0]
    own_cos, own_sin = key_tables(slab_index * local_rows, local_rows, HEAD)
    own_keys = jnp.dot(key_input, w_key, preferred_element_type=jnp.float32).reshape(
        local_rows, heads_dev, HEAD
    )
    own_keys = rotate(own_keys, own_cos, own_sin).astype(jnp.bfloat16)
    own_values = jnp.dot(key_input, w_value, preferred_element_type=jnp.float32).astype(
        jnp.bfloat16
    )
    key_width = heads_dev * HEAD
    pieces = jnp.concatenate([own_keys.reshape(local_rows, key_width), own_values], axis=1)
    heads_out = gather_attend(
        pieces,
        queries.reshape(tok_rows, key_width),
        lax.psum(1, SLAB),
        lax.psum(1, ("z", "xl")),
        heads_dev,
    )
    partial_value = jnp.dot(heads_out, w_out, preferred_element_type=jnp.float32)
    head_total = head_sum(partial_value, lax.psum(1, FFN)).astype(jnp.float32)
    attended = head_total.astype(jnp.bfloat16)
    residual = tokens.astype(jnp.float32) + head_total
    normed_ffn = layer_norm(residual, gain_ffn).astype(jnp.bfloat16)
    channels = w_up.shape[1]
    pre = (
        jnp.dot(normed_ffn, w_up, preferred_element_type=jnp.float32)
        .astype(jnp.bfloat16)
        .reshape(CZ, GY, GX, channels)
    )
    mixed = conv_with_halos(pre, w_depth).reshape(tok_rows, channels)
    normal_cdf = 0.5 * (1.0 + lax.erf(mixed * ROOT_HALF))
    normal_pdf = jnp.exp(-0.5 * mixed * mixed) * NORMAL_SCALE
    activated = (mixed * normal_cdf).astype(jnp.bfloat16)
    grad_act = lax.optimization_barrier(
        jnp.einsum("td,cd->tc", grad_out, w_down, preferred_element_type=jnp.float32)
    )
    grad_mixed = (
        (grad_act * (normal_cdf + mixed * normal_pdf))
        .astype(jnp.bfloat16)
        .reshape(CZ, GY, GX, channels)
    )
    grad_pre = (
        conv_with_halos(grad_mixed, w_depth[::-1])
        .astype(jnp.bfloat16)
        .reshape(tok_rows, channels)
    )
    up_full = jnp.einsum("td,tc->dc", normed_ffn, grad_pre, preferred_element_type=jnp.float32)
    down_full = jnp.einsum("td,tc->dc", grad_out, activated, preferred_element_type=jnp.float32)
    grads = slab_scatter(
        jnp.concatenate([up_full, down_full], axis=1),
        lax.psum(1, SLAB),
        lax.psum(1, ("z", "xl")),
    )
    return (attended, grads[:, :channels], grads[:, channels:])


def solution(mesh):
    mesh = Mesh(mesh.devices.reshape(4, 8, 2, 2, 2), SLAB + FFN)
    in_specs = (
        P(SLAB, None),
        P(),
        P(),
        P(),
        P(None, FFN),
        P(None, FFN),
        P(None, FFN),
        P(FFN, None),
        P(),
        P(None, FFN),
        P(None, FFN),
        P(FFN, None),
        P(SLAB, None),
    )
    out_specs = (P(SLAB, None), P(SLAB, FFN), P(SLAB, FFN))
    return jax.shard_map(
        per_device, mesh=mesh, in_specs=in_specs, out_specs=out_specs, check_vma=False
    )
```

```python
import functools
import math

import jax
import jax.numpy as jnp
from jax import lax
from jax.experimental import pallas as pl
from jax.experimental.pallas import tpu as pltpu
from jax.sharding import Mesh
from jax.sharding import PartitionSpec as P

HEAD = 64
GX = 16
GY = 16
CZ = 2
SLAB = ("y", "z", "xl")
FFN = ("xh", "core")


EPSILON = 1e-05
ROPE_BASE = 100.0
ROOT_HALF = 0.7071067811865476
NORMAL_SCALE = 0.3989422804014327


MESH = pl.DeviceIdType.MESH


def peer_id(p):
    return (p // 16, p // 2 % 8, p % 2, lax.axis_index("xh"), lax.axis_index("core"))


def attend_rows(kv_ref, q_ref, top_ref, total_ref, acc_ref, first_row, row_rows, first):
    heads, q_rows, _ = top_ref.shape
    q_tile = q_rows // 2
    key_width = heads * HEAD
    score_scale = HEAD ** (-0.5)
    rows = pl.ds(pl.multiple_of(first_row, row_rows), row_rows)
    for head in range(heads):
        keys = kv_ref[rows, head * HEAD : (head + 1) * HEAD]
        values = kv_ref[rows, key_width + head * HEAD : key_width + (head + 1) * HEAD]
        for start in range(0, q_rows, q_tile):
            tile = slice(start, start + q_tile)
            columns = slice(head * HEAD, (head + 1) * HEAD)
            scores = lax.dot_general(
                q_ref[tile, columns], keys, (((1,), (1,)), ((), ())),
                preferred_element_type=jnp.float32,
            ) * score_scale
            top = jnp.max(scores, axis=1, keepdims=True)
            if not first:
                old_top = top_ref[head, tile]
                top = jnp.maximum(top, old_top)
                rescale = jnp.exp(old_top - top)
            weights = jnp.exp(scores - top)
            row_sum = jnp.sum(weights, axis=1, keepdims=True)
            mixed = jnp.dot(
                weights.astype(jnp.bfloat16), values, preferred_element_type=jnp.float32
            )
            if not first:
                row_sum = row_sum + rescale * total_ref[head, tile]
                mixed = mixed + rescale * acc_ref[tile, columns]
            top_ref[head, tile] = top
            total_ref[head, tile] = row_sum
            acc_ref[tile, columns] = mixed


def gather_kernel(
    row_size, x_ref, q_ref, heads_ref, out_ref, top_ref, total_ref, acc_ref,
    send_a, recv_a, send_b, recv_b, send_c, recv_c, local_sem,
):
    me = lax.axis_index(SLAB)
    block = x_ref.shape[0]
    own_y, spot = me // row_size, me % row_size
    y_count = lax.psum(1, "y")
    barrier = pltpu.get_barrier_semaphore()

    def greet(k, carry):
        peer = own_y * row_size + lax.rem(spot + k, row_size)
        pl.semaphore_signal(barrier, inc=1, device_id=peer_id(peer), device_id_type=MESH)
        return carry

    lax.fori_loop(1, row_size, greet, 0)
    left_y = lax.rem(own_y + y_count - 1, y_count)
    right_y = lax.rem(own_y + 1, y_count)
    for other_y in (left_y, right_y):
        peer = other_y * row_size + spot
        pl.semaphore_signal(barrier, inc=1, device_id=peer_id(peer), device_id_type=MESH)
    pl.semaphore_wait(barrier, row_size + 1)

    def along_row(target, source):
        return pltpu.make_async_remote_copy(
            src_ref=x_ref,
            dst_ref=out_ref.at[pl.ds((own_y * row_size + source) * block, block)],
            send_sem=send_a.at[target],
            recv_sem=recv_a.at[source],
            device_id=peer_id(own_y * row_size + target),
            device_id_type=MESH,
        )

    def start_row(k, carry):
        along_row(lax.rem(spot + k, row_size), spot).start()
        return carry

    lax.fori_loop(1, row_size, start_row, 0)
    local = pltpu.make_async_copy(x_ref, out_ref.at[pl.ds(me * block, block)], local_sem)
    local.start()
    local.wait()

    def finish_row(k, carry):
        other = lax.rem(spot + k, row_size)
        along_row(other, spot).wait_send()
        along_row(other, other).wait_recv()
        return carry

    lax.fori_loop(1, row_size, finish_row, 0)
    row_rows = row_size * block

    def across(target_y, source_y):
        return pltpu.make_async_remote_copy(
            src_ref=out_ref.at[pl.ds(source_y * row_rows, row_rows)],
            dst_ref=out_ref.at[pl.ds(source_y * row_rows, row_rows)],
            send_sem=send_b.at[target_y],
            recv_sem=recv_b.at[source_y],
            device_id=peer_id(target_y * row_size + spot),
            device_id_type=MESH,
        )

    for other_y in (left_y, right_y):
        across(other_y, own_y).start()
    attend = functools.partial(
        attend_rows, out_ref, q_ref, top_ref, total_ref, acc_ref, row_rows=row_rows
    )
    attend(own_y * row_rows, first=True)
    for other_y in (left_y, right_y):
        across(other_y, own_y).wait_send()
        across(other_y, other_y).wait_recv()
    half = row_rows // 2

    def forward(target_y, source_y, part):
        rows = pl.ds(source_y * row_rows + part * half, half)
        return pltpu.make_async_remote_copy(
            src_ref=out_ref.at[rows],
            dst_ref=out_ref.at[rows],
            send_sem=send_c.at[part],
            recv_sem=recv_c.at[part],
            device_id=peer_id(target_y * row_size + spot),
            device_id_type=MESH,
        )

    far_y = lax.rem(own_y + 2, y_count)
    forward(right_y, left_y, 0).start()
    forward(left_y, right_y, 1).start()
    attend(left_y * row_rows, first=False)
    attend(right_y * row_rows, first=False)
    forward(right_y, left_y, 0).wait_send()
    forward(left_y, right_y, 1).wait_send()
    forward(right_y, far_y, 0).wait_recv()
    forward(left_y, far_y, 1).wait_recv()
    attend(far_y * row_rows, first=False)
    heads = top_ref.shape[0]
    for head in range(heads):
        columns = slice(head * HEAD, (head + 1) * HEAD)
        heads_ref[:, columns] = (acc_ref[:, columns] / total_ref[head]).astype(heads_ref.dtype)


def gather_attend(x, queries, count, row_size, heads):
    rows, width = x.shape
    q_rows = queries.shape[0]
    y_count = count // row_size
    assert y_count == 4
    return pl.pallas_call(
        functools.partial(gather_kernel, row_size),
        out_shape=jax.ShapeDtypeStruct(queries.shape, jnp.bfloat16),
        in_specs=[pl.BlockSpec(memory_space=pltpu.VMEM)] * 2,
        out_specs=pl.BlockSpec(memory_space=pltpu.VMEM),
        scratch_shapes=[
            pltpu.VMEM((count * rows, width), x.dtype),
            pltpu.VMEM((heads, q_rows, 1), jnp.float32),
            pltpu.VMEM((heads, q_rows, 1), jnp.float32),
            pltpu.VMEM(queries.shape, jnp.float32),
            pltpu.SemaphoreType.DMA((row_size,)),
            pltpu.SemaphoreType.DMA((row_size,)),
            pltpu.SemaphoreType.DMA((y_count,)),
            pltpu.SemaphoreType.DMA((y_count,)),
            pltpu.SemaphoreType.DMA((2,)),
            pltpu.SemaphoreType.DMA((2,)),
            pltpu.SemaphoreType.DMA(()),
        ],
        compiler_params=pltpu.CompilerParams(collective_id=0, has_side_effects=True),
    )(x, queries)


def head_peer(q):
    return (lax.axis_index("y"), lax.axis_index("z"), lax.axis_index("xl"), q // 2, q % 2)


def head_sum_kernel(count, part_ref, out_ref, slots, send_sem, recv_sem, send_back, recv_back):
    me = lax.axis_index(FFN)
    barrier = pltpu.get_barrier_semaphore()
    for k in range(1, count):
        pl.semaphore_signal(
            barrier, inc=1, device_id=head_peer(lax.rem(me + k, count)), device_id_type=MESH
        )
    pl.semaphore_wait(barrier, count - 1)

    def share(peer, source):
        return pltpu.make_async_remote_copy(
            src_ref=part_ref.at[peer],
            dst_ref=slots.at[source],
            send_sem=send_sem.at[peer],
            recv_sem=recv_sem.at[source],
            device_id=head_peer(peer),
            device_id_type=MESH,
        )

    def spread(peer, source):
        return pltpu.make_async_remote_copy(
            src_ref=out_ref.at[source],
            dst_ref=out_ref.at[source],
            send_sem=send_back.at[peer],
            recv_sem=recv_back.at[source],
            device_id=head_peer(peer),
            device_id_type=MESH,
        )

    peers = [lax.rem(me + k, count) for k in range(1, count)]
    for peer in peers:
        share(peer, me).start()
    total = part_ref[me].astype(jnp.float32)
    for peer in peers:
        share(peer, me).wait_send()
        share(peer, peer).wait_recv()
        total = total + slots[peer].astype(jnp.float32)
    out_ref[me] = total.astype(out_ref.dtype)
    for peer in peers:
        spread(peer, me).start()
    for peer in peers:
        spread(peer, me).wait_send()
        spread(peer, peer).wait_recv()


def head_sum(partial_value, count):
    rows, width = partial_value.shape
    parts = partial_value.astype(jnp.bfloat16).reshape(count, rows // count, width)
    summed = pl.pallas_call(
        functools.partial(head_sum_kernel, count),
        out_shape=jax.ShapeDtypeStruct(parts.shape, parts.dtype),
        in_specs=[pl.BlockSpec(memory_space=pltpu.VMEM)],
        out_specs=pl.BlockSpec(memory_space=pltpu.VMEM),
        scratch_shapes=[
            pltpu.VMEM(parts.shape, parts.dtype),
            pltpu.SemaphoreType.DMA((count,)),
            pltpu.SemaphoreType.DMA((count,)),
            pltpu.SemaphoreType.DMA((count,)),
            pltpu.SemaphoreType.DMA((count,)),
        ],
        compiler_params=pltpu.CompilerParams(collective_id=2, has_side_effects=True),
    )(parts)
    return summed.reshape(rows, width)


def scatter_kernel(
    row_size, g_ref, out_ref, slots_y, totals, sums, slots_row, send_a, recv_a, send_b, recv_b
):
    me = lax.axis_index(SLAB)
    own_y, spot = me // row_size, me % row_size
    y_count = lax.psum(1, "y")
    barrier = pltpu.get_barrier_semaphore()

    def greet(k, carry):
        peer = own_y * row_size + lax.rem(spot + k, row_size)
        pl.semaphore_signal(barrier, inc=1, device_id=peer_id(peer), device_id_type=MESH)
        return carry

    lax.fori_loop(1, row_size, greet, 0)
    others = [lax.rem(own_y + j, y_count) for j in range(1, y_count)]
    for other_y in others:
        pl.semaphore_signal(
            barrier, inc=1, device_id=peer_id(other_y * row_size + spot), device_id_type=MESH
        )
    pl.semaphore_wait(barrier, row_size + y_count - 2)

    def across(target_y, source_y):
        return pltpu.make_async_remote_copy(
            src_ref=g_ref.at[pl.ds(target_y * row_size, row_size)],
            dst_ref=slots_y.at[source_y],
            send_sem=send_a.at[target_y],
            recv_sem=recv_a.at[source_y],
            device_id=peer_id(target_y * row_size + spot),
            device_id_type=MESH,
        )

    for other_y in others:
        across(other_y, own_y).start()
    total = g_ref[pl.ds(own_y * row_size, row_size)].astype(jnp.float32)
    for other_y in others:
        across(other_y, own_y).wait_send()
        across(other_y, other_y).wait_recv()
        total = total + slots_y[other_y].astype(jnp.float32)
    totals[...] = total
    sums[...] = total.astype(sums.dtype)

    def along_row(target, source):
        return pltpu.make_async_remote_copy(
            src_ref=sums.at[target],
            dst_ref=slots_row.at[source],
            send_sem=send_b.at[target],
            recv_sem=recv_b.at[source],
            device_id=peer_id(own_y * row_size + target),
            device_id_type=MESH,
        )

    def start_row(k, carry):
        along_row(lax.rem(spot + k, row_size), spot).start()
        return carry

    lax.fori_loop(1, row_size, start_row, 0)
    out_ref[...] = totals[spot]

    def finish_row(k, carry):
        other = lax.rem(spot + k, row_size)
        along_row(other, spot).wait_send()
        along_row(other, other).wait_recv()
        out_ref[...] += slots_row[other].astype(jnp.float32)
        return carry

    lax.fori_loop(1, row_size, finish_row, 0)


def slab_scatter(blocks, count, row_size):
    total_rows, width = blocks[0].shape
    rows = total_rows // count
    y_count = count // row_size
    g = jnp.concatenate(
        [block.astype(jnp.bfloat16).reshape(count, rows, width) for block in blocks], axis=1
    )
    summed = pl.pallas_call(
        functools.partial(scatter_kernel, row_size),
        out_shape=jax.ShapeDtypeStruct(g.shape[1:], jnp.float32),
        in_specs=[pl.BlockSpec(memory_space=pltpu.VMEM)],
        out_specs=pl.BlockSpec(memory_space=pltpu.VMEM),
        scratch_shapes=[
            pltpu.VMEM((y_count, row_size) + g.shape[1:], g.dtype),
            pltpu.VMEM((row_size,) + g.shape[1:], jnp.float32),
            pltpu.VMEM((row_size,) + g.shape[1:], g.dtype),
            pltpu.VMEM((row_size,) + g.shape[1:], g.dtype),
            pltpu.SemaphoreType.DMA((y_count,)),
            pltpu.SemaphoreType.DMA((y_count,)),
            pltpu.SemaphoreType.DMA((row_size,)),
            pltpu.SemaphoreType.DMA((row_size,)),
        ],
        compiler_params=pltpu.CompilerParams(collective_id=1, has_side_effects=True),
    )(g)
    return [summed[i * rows : (i + 1) * rows] for i in range(len(blocks))]


def layer_norm(values, scale_gain):
    values = values.astype(jnp.float32)
    centered = values - jnp.mean(values, axis=-1, keepdims=True)
    variance = jnp.mean(centered * centered, axis=-1, keepdims=True)
    return centered * lax.rsqrt(variance + EPSILON) * scale_gain


def rope_tables(coord_x, coord_y, coord_z, head_size):
    pair_count = head_size // 2
    position = jnp.arange(pair_count, dtype=jnp.int32)
    axis_pick = position % 3
    per_axis = (pair_count + 2) // 3
    frequency = ROPE_BASE ** (-(position // 3).astype(jnp.float32) / per_axis)
    angles = (
        coord_x[:, None] * (axis_pick == 0)
        + coord_y[:, None] * (axis_pick == 1)
        + coord_z[:, None] * (axis_pick == 2)
    ) * frequency
    return (jnp.cos(angles)[:, None, :], jnp.sin(angles)[:, None, :])


def token_tables(first_plane, planes, head_size):
    position = jnp.arange(planes * GY * GX, dtype=jnp.int32)
    coord_x = (position % GX).astype(jnp.float32)
    coord_y = (position // GX % GY).astype(jnp.float32)
    coord_z = (first_plane + position // (GX * GY)).astype(jnp.float32)
    return rope_tables(coord_x, coord_y, coord_z, head_size)


def key_tables(first_row, row_count, head_size):
    position = first_row + jnp.arange(row_count, dtype=jnp.int32)
    half_x = GX // 2
    half_y = GY // 2
    coord_x = (position % half_x).astype(jnp.float32) * 2.0 + 0.5
    coord_y = (position // half_x % half_y).astype(jnp.float32) * 2.0 + 0.5
    coord_z = (position // (half_x * half_y)).astype(jnp.float32) * 2.0 + 0.5
    return rope_tables(coord_x, coord_y, coord_z, head_size)


def rotate(values, cosine, sine_table):
    half_size = values.shape[-1] // 2
    front_half = values[..., :half_size]
    back_half = values[..., half_size:]
    return jnp.concatenate(
        [
            front_half * cosine - back_half * sine_table,
            back_half * cosine + front_half * sine_table,
        ],
        axis=-1,
    )


def make_patches(normed, planes):
    width = normed.shape[-1]
    cell_grid = normed.reshape(planes // 2, 2, GY // 2, 2, GX // 2, 2, width)
    return cell_grid.transpose(0, 2, 4, 1, 3, 5, 6).reshape(-1, 8 * width)


def depth_conv(padded, weights, planes):
    height = padded.shape[1] - 2
    width_x = padded.shape[2] - 2
    result = jnp.zeros((planes, height, width_x, padded.shape[3]), jnp.float32)
    for offset in range(27):
        shift_z = offset // 9
        shift_y = offset // 3 % 3
        shift_x = offset % 3
        window = padded[
            shift_z : shift_z + planes, shift_y : shift_y + height, shift_x : shift_x + width_x
        ]
        result = result + window.astype(jnp.float32) * weights[offset]
    return result


def conv_with_halos(cells, weights):
    count = lax.psum(1, SLAB)
    ends = count - 1
    planes = cells.shape[0]
    below = lax.ppermute(cells[planes - 1], SLAB, [(i, i + 1) for i in range(ends)])
    above = lax.ppermute(cells[0], SLAB, [(i + 1, i) for i in range(ends)])
    own = depth_conv(jnp.pad(cells, ((1, 1), (1, 1), (1, 1), (0, 0))), weights, planes)
    height, width_x = cells.shape[1], cells.shape[2]

    def plane_terms(plane, first):
        padded = jnp.pad(plane, ((1, 1), (1, 1), (0, 0))).astype(jnp.float32)
        total = jnp.zeros(plane.shape, jnp.float32)
        for offset in range(9):
            shift_y, shift_x = offset // 3, offset % 3
            window = padded[shift_y : shift_y + height, shift_x : shift_x + width_x]
            total = total + window * weights[first + offset]
        return total

    own = own.at[0].add(plane_terms(below, 0))
    return own.at[planes - 1].add(plane_terms(above, 18))


def per_device(
    tokens,
    gain_attn,
    w_reduce,
    gain_keys,
    w_query,
    w_key,
    w_value,
    w_out,
    gain_ffn,
    w_up,
    w_depth,
    w_down,
    grad_out,
):
    slab_index = lax.axis_index(SLAB)
    tok_rows = tokens.shape[0]
    heads_dev = w_query.shape[1] // HEAD
    normed = layer_norm(tokens, gain_attn).astype(jnp.bfloat16)
    patches = make_patches(normed, CZ)
    reduced = jnp.dot(patches, w_reduce, preferred_element_type=jnp.float32)
    key_input = layer_norm(reduced, gain_keys).astype(jnp.bfloat16)
    tok_cos, tok_sin = token_tables(slab_index * CZ, CZ, HEAD)
    queries = jnp.dot(normed, w_query, preferred_element_type=jnp.float32).reshape(
        tok_rows, heads_dev, HEAD
    )
    queries = rotate(queries, tok_cos, tok_sin).astype(jnp.bfloat16)
    local_rows = key_input.shape[0]
    own_cos, own_sin = key_tables(slab_index * local_rows, local_rows, HEAD)
    own_keys = jnp.dot(key_input, w_key, preferred_element_type=jnp.float32).reshape(
        local_rows, heads_dev, HEAD
    )
    own_keys = rotate(own_keys, own_cos, own_sin).astype(jnp.bfloat16)
    own_values = jnp.dot(key_input, w_value, preferred_element_type=jnp.float32).astype(
        jnp.bfloat16
    )
    key_width = heads_dev * HEAD
    pieces = jnp.concatenate([own_keys.reshape(local_rows, key_width), own_values], axis=1)
    heads_out = gather_attend(
        pieces,
        queries.reshape(tok_rows, key_width),
        lax.psum(1, SLAB),
        lax.psum(1, ("z", "xl")),
        heads_dev,
    )
    partial_value = jnp.dot(heads_out, w_out, preferred_element_type=jnp.float32)
    head_total = head_sum(partial_value, lax.psum(1, FFN)).astype(jnp.float32)
    attended = head_total.astype(jnp.bfloat16)
    residual = tokens.astype(jnp.float32) + head_total
    normed_ffn = layer_norm(residual, gain_ffn).astype(jnp.bfloat16)
    channels = w_up.shape[1]
    pre = (
        jnp.dot(normed_ffn, w_up, preferred_element_type=jnp.float32)
        .astype(jnp.bfloat16)
        .reshape(CZ, GY, GX, channels)
    )
    mixed = conv_with_halos(pre, w_depth).reshape(tok_rows, channels)
    normal_cdf = 0.5 * (1.0 + lax.erf(mixed * ROOT_HALF))
    normal_pdf = jnp.exp(-0.5 * mixed * mixed) * NORMAL_SCALE
    activated = (mixed * normal_cdf).astype(jnp.bfloat16)
    grad_act = lax.optimization_barrier(
        jnp.einsum("td,cd->tc", grad_out, w_down, preferred_element_type=jnp.float32)
    )
    grad_mixed = (
        (grad_act * (normal_cdf + mixed * normal_pdf))
        .astype(jnp.bfloat16)
        .reshape(CZ, GY, GX, channels)
    )
    grad_pre = (
        conv_with_halos(grad_mixed, w_depth[::-1])
        .astype(jnp.bfloat16)
        .reshape(tok_rows, channels)
    )
    up_full = jnp.einsum("td,tc->dc", normed_ffn, grad_pre, preferred_element_type=jnp.float32)
    down_full = jnp.einsum("td,tc->dc", grad_out, activated, preferred_element_type=jnp.float32)
    grad_up, grad_down = slab_scatter(
        [up_full, down_full], lax.psum(1, SLAB), lax.psum(1, ("z", "xl"))
    )
    return (attended, grad_up, grad_down)


def solution(mesh):
    mesh = Mesh(mesh.devices.reshape(4, 8, 2, 2, 2), SLAB + FFN)
    in_specs = (
        P(SLAB, None),
        P(),
        P(),
        P(),
        P(None, FFN),
        P(None, FFN),
        P(None, FFN),
        P(FFN, None),
        P(),
        P(None, FFN),
        P(None, FFN),
        P(FFN, None),
        P(SLAB, None),
    )
    out_specs = (P(SLAB, None), P(SLAB, FFN), P(SLAB, FFN))
    return jax.shard_map(
        per_device, mesh=mesh, in_specs=in_specs, out_specs=out_specs, check_vma=False
    )
```

```python
import functools
import math

import jax
import jax.numpy as jnp
from jax import lax
from jax.experimental import pallas as pl
from jax.experimental.pallas import tpu as pltpu
from jax.sharding import Mesh
from jax.sharding import PartitionSpec as P

HEAD = 64
GX = 16
GY = 16
CZ = 2
SLAB = ("y", "z", "xl")
FFN = ("xh", "core")


EPSILON = 1e-05
ROPE_BASE = 100.0
ROOT_HALF = 0.7071067811865476
NORMAL_SCALE = 0.3989422804014327


MESH = pl.DeviceIdType.MESH


def peer_id(p):
    return (p // 16, p // 2 % 8, p % 2, lax.axis_index("xh"), lax.axis_index("core"))


def attend_rows(kv_ref, q_ref, top_ref, total_ref, acc_ref, first_row, row_rows, first):
    heads, q_rows, _ = top_ref.shape
    q_tile = q_rows // 2
    key_width = heads * HEAD
    score_scale = HEAD ** (-0.5)
    rows = pl.ds(pl.multiple_of(first_row, row_rows), row_rows)
    for head in range(heads):
        keys = kv_ref[rows, head * HEAD : (head + 1) * HEAD]
        values = kv_ref[rows, key_width + head * HEAD : key_width + (head + 1) * HEAD]
        for start in range(0, q_rows, q_tile):
            tile = slice(start, start + q_tile)
            columns = slice(head * HEAD, (head + 1) * HEAD)
            scores = lax.dot_general(
                q_ref[tile, columns], keys, (((1,), (1,)), ((), ())),
                preferred_element_type=jnp.float32,
            ) * score_scale
            top = jnp.max(scores, axis=1, keepdims=True)
            if not first:
                old_top = top_ref[head, tile]
                top = jnp.maximum(top, old_top)
                rescale = jnp.exp(old_top - top)
            weights = jnp.exp(scores - top)
            row_sum = jnp.sum(weights, axis=1, keepdims=True)
            mixed = jnp.dot(
                weights.astype(jnp.bfloat16), values, preferred_element_type=jnp.float32
            )
            if not first:
                row_sum = row_sum + rescale * total_ref[head, tile]
                mixed = mixed + rescale * acc_ref[tile, columns]
            top_ref[head, tile] = top
            total_ref[head, tile] = row_sum
            acc_ref[tile, columns] = mixed


def gather_kernel(
    row_size, x_ref, q_ref, heads_ref, out_ref, top_ref, total_ref, acc_ref,
    send_a, recv_a, send_b, recv_b, send_c, recv_c, local_sem,
):
    me = lax.axis_index(SLAB)
    block = x_ref.shape[0]
    own_y, spot = me // row_size, me % row_size
    y_count = lax.psum(1, "y")
    barrier = pltpu.get_barrier_semaphore()

    def greet(k, carry):
        peer = own_y * row_size + lax.rem(spot + k, row_size)
        pl.semaphore_signal(barrier, inc=1, device_id=peer_id(peer), device_id_type=MESH)
        return carry

    lax.fori_loop(1, row_size, greet, 0)
    left_y = lax.rem(own_y + y_count - 1, y_count)
    right_y = lax.rem(own_y + 1, y_count)
    for other_y in (left_y, right_y):
        peer = other_y * row_size + spot
        pl.semaphore_signal(barrier, inc=1, device_id=peer_id(peer), device_id_type=MESH)
    pl.semaphore_wait(barrier, row_size + 1)

    def along_row(target, source):
        return pltpu.make_async_remote_copy(
            src_ref=x_ref,
            dst_ref=out_ref.at[pl.ds((own_y * row_size + source) * block, block)],
            send_sem=send_a.at[target],
            recv_sem=recv_a.at[source],
            device_id=peer_id(own_y * row_size + target),
            device_id_type=MESH,
        )

    def start_row(k, carry):
        along_row(lax.rem(spot + k, row_size), spot).start()
        return carry

    lax.fori_loop(1, row_size, start_row, 0)
    local = pltpu.make_async_copy(x_ref, out_ref.at[pl.ds(me * block, block)], local_sem)
    local.start()
    local.wait()

    def finish_row(k, carry):
        other = lax.rem(spot + k, row_size)
        along_row(other, spot).wait_send()
        along_row(other, other).wait_recv()
        return carry

    lax.fori_loop(1, row_size, finish_row, 0)
    row_rows = row_size * block

    def across(target_y, source_y):
        return pltpu.make_async_remote_copy(
            src_ref=out_ref.at[pl.ds(source_y * row_rows, row_rows)],
            dst_ref=out_ref.at[pl.ds(source_y * row_rows, row_rows)],
            send_sem=send_b.at[target_y],
            recv_sem=recv_b.at[source_y],
            device_id=peer_id(target_y * row_size + spot),
            device_id_type=MESH,
        )

    for other_y in (left_y, right_y):
        across(other_y, own_y).start()
    attend = functools.partial(
        attend_rows, out_ref, q_ref, top_ref, total_ref, acc_ref, row_rows=row_rows
    )
    attend(own_y * row_rows, first=True)
    for other_y in (left_y, right_y):
        across(other_y, own_y).wait_send()
        across(other_y, other_y).wait_recv()
    half = row_rows // 2

    def forward(target_y, source_y, part):
        rows = pl.ds(source_y * row_rows + part * half, half)
        return pltpu.make_async_remote_copy(
            src_ref=out_ref.at[rows],
            dst_ref=out_ref.at[rows],
            send_sem=send_c.at[part],
            recv_sem=recv_c.at[part],
            device_id=peer_id(target_y * row_size + spot),
            device_id_type=MESH,
        )

    far_y = lax.rem(own_y + 2, y_count)
    forward(right_y, left_y, 0).start()
    forward(left_y, right_y, 1).start()
    attend(left_y * row_rows, first=False)
    attend(right_y * row_rows, first=False)
    forward(right_y, left_y, 0).wait_send()
    forward(left_y, right_y, 1).wait_send()
    forward(right_y, far_y, 0).wait_recv()
    forward(left_y, far_y, 1).wait_recv()
    attend(far_y * row_rows, first=False)
    heads = top_ref.shape[0]
    for head in range(heads):
        columns = slice(head * HEAD, (head + 1) * HEAD)
        heads_ref[:, columns] = (acc_ref[:, columns] / total_ref[head]).astype(heads_ref.dtype)


def gather_attend(x, queries, count, row_size, heads):
    rows, width = x.shape
    q_rows = queries.shape[0]
    y_count = count // row_size
    assert y_count == 4
    return pl.pallas_call(
        functools.partial(gather_kernel, row_size),
        out_shape=jax.ShapeDtypeStruct(queries.shape, jnp.bfloat16),
        in_specs=[pl.BlockSpec(memory_space=pltpu.VMEM)] * 2,
        out_specs=pl.BlockSpec(memory_space=pltpu.VMEM),
        scratch_shapes=[
            pltpu.VMEM((count * rows, width), x.dtype),
            pltpu.VMEM((heads, q_rows, 1), jnp.float32),
            pltpu.VMEM((heads, q_rows, 1), jnp.float32),
            pltpu.VMEM(queries.shape, jnp.float32),
            pltpu.SemaphoreType.DMA((row_size,)),
            pltpu.SemaphoreType.DMA((row_size,)),
            pltpu.SemaphoreType.DMA((y_count,)),
            pltpu.SemaphoreType.DMA((y_count,)),
            pltpu.SemaphoreType.DMA((2,)),
            pltpu.SemaphoreType.DMA((2,)),
            pltpu.SemaphoreType.DMA(()),
        ],
        compiler_params=pltpu.CompilerParams(collective_id=0, has_side_effects=True),
    )(x, queries)


def head_peer(q):
    return (lax.axis_index("y"), lax.axis_index("z"), lax.axis_index("xl"), q // 2, q % 2)


def head_sum_kernel(count, part_ref, out_ref, slots, send_sem, recv_sem, send_back, recv_back):
    me = lax.axis_index(FFN)
    barrier = pltpu.get_barrier_semaphore()
    for k in range(1, count):
        pl.semaphore_signal(
            barrier, inc=1, device_id=head_peer(lax.rem(me + k, count)), device_id_type=MESH
        )
    pl.semaphore_wait(barrier, count - 1)

    def share(peer, source):
        return pltpu.make_async_remote_copy(
            src_ref=part_ref.at[peer],
            dst_ref=slots.at[source],
            send_sem=send_sem.at[peer],
            recv_sem=recv_sem.at[source],
            device_id=head_peer(peer),
            device_id_type=MESH,
        )

    def spread(peer, source):
        return pltpu.make_async_remote_copy(
            src_ref=out_ref.at[source],
            dst_ref=out_ref.at[source],
            send_sem=send_back.at[peer],
            recv_sem=recv_back.at[source],
            device_id=head_peer(peer),
            device_id_type=MESH,
        )

    peers = [lax.rem(me + k, count) for k in range(1, count)]
    for peer in peers:
        share(peer, me).start()
    total = part_ref[me].astype(jnp.float32)
    for peer in peers:
        share(peer, me).wait_send()
        share(peer, peer).wait_recv()
        total = total + slots[peer].astype(jnp.float32)
    out_ref[me] = total.astype(out_ref.dtype)
    for peer in peers:
        spread(peer, me).start()
    for peer in peers:
        spread(peer, me).wait_send()
        spread(peer, peer).wait_recv()


def head_sum(partial_value, count):
    rows, width = partial_value.shape
    parts = partial_value.astype(jnp.bfloat16).reshape(count, rows // count, width)
    summed = pl.pallas_call(
        functools.partial(head_sum_kernel, count),
        out_shape=jax.ShapeDtypeStruct(parts.shape, parts.dtype),
        in_specs=[pl.BlockSpec(memory_space=pltpu.VMEM)],
        out_specs=pl.BlockSpec(memory_space=pltpu.VMEM),
        scratch_shapes=[
            pltpu.VMEM(parts.shape, parts.dtype),
            pltpu.SemaphoreType.DMA((count,)),
            pltpu.SemaphoreType.DMA((count,)),
            pltpu.SemaphoreType.DMA((count,)),
            pltpu.SemaphoreType.DMA((count,)),
        ],
        compiler_params=pltpu.CompilerParams(collective_id=2, has_side_effects=True),
    )(parts)
    return summed.reshape(rows, width)


def scatter_kernel(
    row_size, g_ref, up_ref, down_ref, slots_y, totals, sums, slots_row,
    send_a, recv_a, send_b, recv_b,
):
    me = lax.axis_index(SLAB)
    own_y, spot = me // row_size, me % row_size
    y_count = lax.psum(1, "y")
    barrier = pltpu.get_barrier_semaphore()

    def greet(k, carry):
        peer = own_y * row_size + lax.rem(spot + k, row_size)
        pl.semaphore_signal(barrier, inc=1, device_id=peer_id(peer), device_id_type=MESH)
        return carry

    lax.fori_loop(1, row_size, greet, 0)
    others = [lax.rem(own_y + j, y_count) for j in range(1, y_count)]
    for other_y in others:
        pl.semaphore_signal(
            barrier, inc=1, device_id=peer_id(other_y * row_size + spot), device_id_type=MESH
        )
    pl.semaphore_wait(barrier, row_size + y_count - 2)

    def across(target_y, source_y):
        return pltpu.make_async_remote_copy(
            src_ref=g_ref.at[pl.ds(target_y * row_size, row_size)],
            dst_ref=slots_y.at[source_y],
            send_sem=send_a.at[target_y],
            recv_sem=recv_a.at[source_y],
            device_id=peer_id(target_y * row_size + spot),
            device_id_type=MESH,
        )

    for other_y in others:
        across(other_y, own_y).start()
    total = g_ref[pl.ds(own_y * row_size, row_size)].astype(jnp.float32)
    for other_y in others:
        across(other_y, own_y).wait_send()
        across(other_y, other_y).wait_recv()
        total = total + slots_y[other_y].astype(jnp.float32)
    totals[...] = total
    sums[...] = total.astype(sums.dtype)

    def along_row(target, source):
        return pltpu.make_async_remote_copy(
            src_ref=sums.at[target],
            dst_ref=slots_row.at[source],
            send_sem=send_b.at[target],
            recv_sem=recv_b.at[source],
            device_id=peer_id(own_y * row_size + target),
            device_id_type=MESH,
        )

    def start_row(k, carry):
        along_row(lax.rem(spot + k, row_size), spot).start()
        return carry

    lax.fori_loop(1, row_size, start_row, 0)
    rows = up_ref.shape[0]
    up_ref[...] = totals[spot, :rows]
    down_ref[...] = totals[spot, rows:]

    def finish_row(k, carry):
        other = lax.rem(spot + k, row_size)
        along_row(other, spot).wait_send()
        along_row(other, other).wait_recv()
        arrived = slots_row[other].astype(jnp.float32)
        up_ref[...] += arrived[:rows]
        down_ref[...] += arrived[rows:]
        return carry

    lax.fori_loop(1, row_size, finish_row, 0)


def slab_scatter(blocks, count, row_size):
    total_rows, width = blocks[0].shape
    rows = total_rows // count
    y_count = count // row_size
    g = jnp.concatenate(
        [block.astype(jnp.bfloat16).reshape(count, rows, width) for block in blocks], axis=1
    )
    summed = pl.pallas_call(
        functools.partial(scatter_kernel, row_size),
        out_shape=[jax.ShapeDtypeStruct((rows, width), jnp.float32)] * len(blocks),
        in_specs=[pl.BlockSpec(memory_space=pltpu.VMEM)],
        out_specs=[pl.BlockSpec(memory_space=pltpu.VMEM)] * len(blocks),
        scratch_shapes=[
            pltpu.VMEM((y_count, row_size) + g.shape[1:], g.dtype),
            pltpu.VMEM((row_size,) + g.shape[1:], jnp.float32),
            pltpu.VMEM((row_size,) + g.shape[1:], g.dtype),
            pltpu.VMEM((row_size,) + g.shape[1:], g.dtype),
            pltpu.SemaphoreType.DMA((y_count,)),
            pltpu.SemaphoreType.DMA((y_count,)),
            pltpu.SemaphoreType.DMA((row_size,)),
            pltpu.SemaphoreType.DMA((row_size,)),
        ],
        compiler_params=pltpu.CompilerParams(collective_id=1, has_side_effects=True),
    )(g)
    return summed


def layer_norm(values, scale_gain):
    values = values.astype(jnp.float32)
    centered = values - jnp.mean(values, axis=-1, keepdims=True)
    variance = jnp.mean(centered * centered, axis=-1, keepdims=True)
    return centered * lax.rsqrt(variance + EPSILON) * scale_gain


def rope_tables(coord_x, coord_y, coord_z, head_size):
    pair_count = head_size // 2
    position = jnp.arange(pair_count, dtype=jnp.int32)
    axis_pick = position % 3
    per_axis = (pair_count + 2) // 3
    frequency = ROPE_BASE ** (-(position // 3).astype(jnp.float32) / per_axis)
    angles = (
        coord_x[:, None] * (axis_pick == 0)
        + coord_y[:, None] * (axis_pick == 1)
        + coord_z[:, None] * (axis_pick == 2)
    ) * frequency
    return (jnp.cos(angles)[:, None, :], jnp.sin(angles)[:, None, :])


def token_tables(first_plane, planes, head_size):
    position = jnp.arange(planes * GY * GX, dtype=jnp.int32)
    coord_x = (position % GX).astype(jnp.float32)
    coord_y = (position // GX % GY).astype(jnp.float32)
    coord_z = (first_plane + position // (GX * GY)).astype(jnp.float32)
    return rope_tables(coord_x, coord_y, coord_z, head_size)


def key_tables(first_row, row_count, head_size):
    position = first_row + jnp.arange(row_count, dtype=jnp.int32)
    half_x = GX // 2
    half_y = GY // 2
    coord_x = (position % half_x).astype(jnp.float32) * 2.0 + 0.5
    coord_y = (position // half_x % half_y).astype(jnp.float32) * 2.0 + 0.5
    coord_z = (position // (half_x * half_y)).astype(jnp.float32) * 2.0 + 0.5
    return rope_tables(coord_x, coord_y, coord_z, head_size)


def rotate(values, cosine, sine_table):
    half_size = values.shape[-1] // 2
    front_half = values[..., :half_size]
    back_half = values[..., half_size:]
    return jnp.concatenate(
        [
            front_half * cosine - back_half * sine_table,
            back_half * cosine + front_half * sine_table,
        ],
        axis=-1,
    )


def make_patches(normed, planes):
    width = normed.shape[-1]
    cell_grid = normed.reshape(planes // 2, 2, GY // 2, 2, GX // 2, 2, width)
    return cell_grid.transpose(0, 2, 4, 1, 3, 5, 6).reshape(-1, 8 * width)


def depth_conv(padded, weights, planes):
    height = padded.shape[1] - 2
    width_x = padded.shape[2] - 2
    result = jnp.zeros((planes, height, width_x, padded.shape[3]), jnp.float32)
    for offset in range(27):
        shift_z = offset // 9
        shift_y = offset // 3 % 3
        shift_x = offset % 3
        window = padded[
            shift_z : shift_z + planes, shift_y : shift_y + height, shift_x : shift_x + width_x
        ]
        result = result + window.astype(jnp.float32) * weights[offset]
    return result


def conv_with_halos(cells, weights):
    count = lax.psum(1, SLAB)
    ends = count - 1
    planes = cells.shape[0]
    below = lax.ppermute(cells[planes - 1], SLAB, [(i, i + 1) for i in range(ends)])
    above = lax.ppermute(cells[0], SLAB, [(i + 1, i) for i in range(ends)])
    own = depth_conv(jnp.pad(cells, ((1, 1), (1, 1), (1, 1), (0, 0))), weights, planes)
    height, width_x = cells.shape[1], cells.shape[2]

    def plane_terms(plane, first):
        padded = jnp.pad(plane, ((1, 1), (1, 1), (0, 0))).astype(jnp.float32)
        total = jnp.zeros(plane.shape, jnp.float32)
        for offset in range(9):
            shift_y, shift_x = offset // 3, offset % 3
            window = padded[shift_y : shift_y + height, shift_x : shift_x + width_x]
            total = total + window * weights[first + offset]
        return total

    own = own.at[0].add(plane_terms(below, 0))
    return own.at[planes - 1].add(plane_terms(above, 18))


def per_device(
    tokens,
    gain_attn,
    w_reduce,
    gain_keys,
    w_query,
    w_key,
    w_value,
    w_out,
    gain_ffn,
    w_up,
    w_depth,
    w_down,
    grad_out,
):
    slab_index = lax.axis_index(SLAB)
    tok_rows = tokens.shape[0]
    heads_dev = w_query.shape[1] // HEAD
    normed = layer_norm(tokens, gain_attn).astype(jnp.bfloat16)
    patches = make_patches(normed, CZ)
    reduced = jnp.dot(patches, w_reduce, preferred_element_type=jnp.float32)
    key_input = layer_norm(reduced, gain_keys).astype(jnp.bfloat16)
    tok_cos, tok_sin = token_tables(slab_index * CZ, CZ, HEAD)
    queries = jnp.dot(normed, w_query, preferred_element_type=jnp.float32).reshape(
        tok_rows, heads_dev, HEAD
    )
    queries = rotate(queries, tok_cos, tok_sin).astype(jnp.bfloat16)
    local_rows = key_input.shape[0]
    own_cos, own_sin = key_tables(slab_index * local_rows, local_rows, HEAD)
    own_keys = jnp.dot(key_input, w_key, preferred_element_type=jnp.float32).reshape(
        local_rows, heads_dev, HEAD
    )
    own_keys = rotate(own_keys, own_cos, own_sin).astype(jnp.bfloat16)
    own_values = jnp.dot(key_input, w_value, preferred_element_type=jnp.float32).astype(
        jnp.bfloat16
    )
    key_width = heads_dev * HEAD
    pieces = jnp.concatenate([own_keys.reshape(local_rows, key_width), own_values], axis=1)
    heads_out = gather_attend(
        pieces,
        queries.reshape(tok_rows, key_width),
        lax.psum(1, SLAB),
        lax.psum(1, ("z", "xl")),
        heads_dev,
    )
    partial_value = jnp.dot(heads_out, w_out, preferred_element_type=jnp.float32)
    head_total = head_sum(partial_value, lax.psum(1, FFN)).astype(jnp.float32)
    attended = head_total.astype(jnp.bfloat16)
    residual = tokens.astype(jnp.float32) + head_total
    normed_ffn = layer_norm(residual, gain_ffn).astype(jnp.bfloat16)
    channels = w_up.shape[1]
    pre = (
        jnp.dot(normed_ffn, w_up, preferred_element_type=jnp.float32)
        .astype(jnp.bfloat16)
        .reshape(CZ, GY, GX, channels)
    )
    mixed = conv_with_halos(pre, w_depth).reshape(tok_rows, channels)
    normal_cdf = 0.5 * (1.0 + lax.erf(mixed * ROOT_HALF))
    normal_pdf = jnp.exp(-0.5 * mixed * mixed) * NORMAL_SCALE
    activated = (mixed * normal_cdf).astype(jnp.bfloat16)
    grad_act = lax.optimization_barrier(
        jnp.einsum("td,cd->tc", grad_out, w_down, preferred_element_type=jnp.float32)
    )
    grad_mixed = (
        (grad_act * (normal_cdf + mixed * normal_pdf))
        .astype(jnp.bfloat16)
        .reshape(CZ, GY, GX, channels)
    )
    grad_pre = (
        conv_with_halos(grad_mixed, w_depth[::-1])
        .astype(jnp.bfloat16)
        .reshape(tok_rows, channels)
    )
    up_full = jnp.einsum("td,tc->dc", normed_ffn, grad_pre, preferred_element_type=jnp.float32)
    down_full = jnp.einsum("td,tc->dc", grad_out, activated, preferred_element_type=jnp.float32)
    grad_up, grad_down = slab_scatter(
        [up_full, down_full], lax.psum(1, SLAB), lax.psum(1, ("z", "xl"))
    )
    return (attended, grad_up, grad_down)


def solution(mesh):
    mesh = Mesh(mesh.devices.reshape(4, 8, 2, 2, 2), SLAB + FFN)
    in_specs = (
        P(SLAB, None),
        P(),
        P(),
        P(),
        P(None, FFN),
        P(None, FFN),
        P(None, FFN),
        P(FFN, None),
        P(),
        P(None, FFN),
        P(None, FFN),
        P(FFN, None),
        P(SLAB, None),
    )
    out_specs = (P(SLAB, None), P(SLAB, FFN), P(SLAB, FFN))
    return jax.shard_map(
        per_device, mesh=mesh, in_specs=in_specs, out_specs=out_specs, check_vma=False
    )
```

```python
import functools
import math

import jax
import jax.numpy as jnp
from jax import lax
from jax.experimental import pallas as pl
from jax.experimental.pallas import tpu as pltpu
from jax.sharding import Mesh
from jax.sharding import PartitionSpec as P

HEAD = 64
GX = 16
GY = 16
CZ = 2
SLAB = ("y", "z", "xl")
FFN = ("xh", "core")


EPSILON = 1e-05
ROPE_BASE = 100.0
ROOT_HALF = 0.7071067811865476
NORMAL_SCALE = 0.3989422804014327


MESH = pl.DeviceIdType.MESH


def peer_id(p):
    return (p // 16, p // 2 % 8, p % 2, lax.axis_index("xh"), lax.axis_index("core"))


def attend_rows(kv_ref, q_ref, top_ref, total_ref, acc_ref, first_row, row_rows, first):
    heads, q_rows, _ = top_ref.shape
    q_tile = q_rows // 2
    key_width = heads * HEAD
    score_scale = HEAD ** (-0.5)
    rows = pl.ds(pl.multiple_of(first_row, row_rows), row_rows)
    for head in range(heads):
        keys = kv_ref[rows, head * HEAD : (head + 1) * HEAD]
        values = kv_ref[rows, key_width + head * HEAD : key_width + (head + 1) * HEAD]
        for start in range(0, q_rows, q_tile):
            tile = slice(start, start + q_tile)
            columns = slice(head * HEAD, (head + 1) * HEAD)
            scores = lax.dot_general(
                q_ref[tile, columns], keys, (((1,), (1,)), ((), ())),
                preferred_element_type=jnp.float32,
            ) * score_scale
            top = jnp.max(scores, axis=1, keepdims=True)
            if not first:
                old_top = top_ref[head, tile]
                top = jnp.maximum(top, old_top)
                rescale = jnp.exp(old_top - top)
            weights = jnp.exp(scores - top)
            row_sum = jnp.sum(weights, axis=1, keepdims=True)
            mixed = jnp.dot(
                weights.astype(jnp.bfloat16), values, preferred_element_type=jnp.float32
            )
            if not first:
                row_sum = row_sum + rescale * total_ref[head, tile]
                mixed = mixed + rescale * acc_ref[tile, columns]
            top_ref[head, tile] = top
            total_ref[head, tile] = row_sum
            acc_ref[tile, columns] = mixed


def gather_kernel(
    row_size, x_ref, q_ref, heads_ref, out_ref, top_ref, total_ref, acc_ref,
    send_a, recv_a, send_b, recv_b, send_c, recv_c, local_sem,
):
    me = lax.axis_index(SLAB)
    block = x_ref.shape[0]
    own_y, spot = me // row_size, me % row_size
    y_count = lax.psum(1, "y")
    barrier = pltpu.get_barrier_semaphore()

    def greet(k, carry):
        peer = own_y * row_size + lax.rem(spot + k, row_size)
        pl.semaphore_signal(barrier, inc=1, device_id=peer_id(peer), device_id_type=MESH)
        return carry

    lax.fori_loop(1, row_size, greet, 0)
    left_y = lax.rem(own_y + y_count - 1, y_count)
    right_y = lax.rem(own_y + 1, y_count)
    for other_y in (left_y, right_y):
        peer = other_y * row_size + spot
        pl.semaphore_signal(barrier, inc=1, device_id=peer_id(peer), device_id_type=MESH)
    pl.semaphore_wait(barrier, row_size + 1)

    def along_row(target, source):
        return pltpu.make_async_remote_copy(
            src_ref=x_ref,
            dst_ref=out_ref.at[pl.ds((own_y * row_size + source) * block, block)],
            send_sem=send_a.at[target],
            recv_sem=recv_a.at[source],
            device_id=peer_id(own_y * row_size + target),
            device_id_type=MESH,
        )

    def start_row(k, carry):
        along_row(lax.rem(spot + k, row_size), spot).start()
        return carry

    lax.fori_loop(1, row_size, start_row, 0)
    local = pltpu.make_async_copy(x_ref, out_ref.at[pl.ds(me * block, block)], local_sem)
    local.start()
    local.wait()

    def finish_row(k, carry):
        other = lax.rem(spot + k, row_size)
        along_row(other, spot).wait_send()
        along_row(other, other).wait_recv()
        return carry

    lax.fori_loop(1, row_size, finish_row, 0)
    row_rows = row_size * block

    def across(target_y, source_y):
        return pltpu.make_async_remote_copy(
            src_ref=out_ref.at[pl.ds(source_y * row_rows, row_rows)],
            dst_ref=out_ref.at[pl.ds(source_y * row_rows, row_rows)],
            send_sem=send_b.at[target_y],
            recv_sem=recv_b.at[source_y],
            device_id=peer_id(target_y * row_size + spot),
            device_id_type=MESH,
        )

    for other_y in (left_y, right_y):
        across(other_y, own_y).start()
    attend = functools.partial(
        attend_rows, out_ref, q_ref, top_ref, total_ref, acc_ref, row_rows=row_rows
    )
    attend(own_y * row_rows, first=True)
    for other_y in (left_y, right_y):
        across(other_y, own_y).wait_send()
        across(other_y, other_y).wait_recv()
    half = row_rows // 2

    def forward(target_y, source_y, part):
        rows = pl.ds(source_y * row_rows + part * half, half)
        return pltpu.make_async_remote_copy(
            src_ref=out_ref.at[rows],
            dst_ref=out_ref.at[rows],
            send_sem=send_c.at[part],
            recv_sem=recv_c.at[part],
            device_id=peer_id(target_y * row_size + spot),
            device_id_type=MESH,
        )

    far_y = lax.rem(own_y + 2, y_count)
    forward(right_y, left_y, 0).start()
    forward(left_y, right_y, 1).start()
    attend(left_y * row_rows, first=False)
    attend(right_y * row_rows, first=False)
    forward(right_y, left_y, 0).wait_send()
    forward(left_y, right_y, 1).wait_send()
    forward(right_y, far_y, 0).wait_recv()
    forward(left_y, far_y, 1).wait_recv()
    attend(far_y * row_rows, first=False)
    heads = top_ref.shape[0]
    for head in range(heads):
        columns = slice(head * HEAD, (head + 1) * HEAD)
        heads_ref[:, columns] = (acc_ref[:, columns] / total_ref[head]).astype(heads_ref.dtype)


def gather_attend(x, queries, count, row_size, heads):
    rows, width = x.shape
    q_rows = queries.shape[0]
    y_count = count // row_size
    assert y_count == 4
    return pl.pallas_call(
        functools.partial(gather_kernel, row_size),
        out_shape=jax.ShapeDtypeStruct(queries.shape, jnp.bfloat16),
        in_specs=[pl.BlockSpec(memory_space=pltpu.VMEM)] * 2,
        out_specs=pl.BlockSpec(memory_space=pltpu.VMEM),
        scratch_shapes=[
            pltpu.VMEM((count * rows, width), x.dtype),
            pltpu.VMEM((heads, q_rows, 1), jnp.float32),
            pltpu.VMEM((heads, q_rows, 1), jnp.float32),
            pltpu.VMEM(queries.shape, jnp.float32),
            pltpu.SemaphoreType.DMA((row_size,)),
            pltpu.SemaphoreType.DMA((row_size,)),
            pltpu.SemaphoreType.DMA((y_count,)),
            pltpu.SemaphoreType.DMA((y_count,)),
            pltpu.SemaphoreType.DMA((2,)),
            pltpu.SemaphoreType.DMA((2,)),
            pltpu.SemaphoreType.DMA(()),
        ],
        compiler_params=pltpu.CompilerParams(collective_id=0, has_side_effects=True),
    )(x, queries)


def head_peer(q):
    return (lax.axis_index("y"), lax.axis_index("z"), lax.axis_index("xl"), q // 2, q % 2)


def head_sum_kernel(count, part_ref, out_ref, slots, send_sem, recv_sem, send_back, recv_back):
    me = lax.axis_index(FFN)
    barrier = pltpu.get_barrier_semaphore()
    for k in range(1, count):
        pl.semaphore_signal(
            barrier, inc=1, device_id=head_peer(lax.rem(me + k, count)), device_id_type=MESH
        )
    pl.semaphore_wait(barrier, count - 1)

    def share(peer, source):
        return pltpu.make_async_remote_copy(
            src_ref=part_ref.at[peer],
            dst_ref=slots.at[source],
            send_sem=send_sem.at[peer],
            recv_sem=recv_sem.at[source],
            device_id=head_peer(peer),
            device_id_type=MESH,
        )

    def spread(peer, source):
        return pltpu.make_async_remote_copy(
            src_ref=out_ref.at[source],
            dst_ref=out_ref.at[source],
            send_sem=send_back.at[peer],
            recv_sem=recv_back.at[source],
            device_id=head_peer(peer),
            device_id_type=MESH,
        )

    peers = [lax.rem(me + k, count) for k in range(1, count)]
    for peer in peers:
        share(peer, me).start()
    total = part_ref[me].astype(jnp.float32)
    for peer in peers:
        share(peer, me).wait_send()
        share(peer, peer).wait_recv()
        total = total + slots[peer].astype(jnp.float32)
    out_ref[me] = total.astype(out_ref.dtype)
    for peer in peers:
        spread(peer, me).start()
    for peer in peers:
        spread(peer, me).wait_send()
        spread(peer, peer).wait_recv()


def head_sum(partial_value, count):
    rows, width = partial_value.shape
    parts = partial_value.astype(jnp.bfloat16).reshape(count, rows // count, width)
    summed = pl.pallas_call(
        functools.partial(head_sum_kernel, count),
        out_shape=jax.ShapeDtypeStruct(parts.shape, parts.dtype),
        in_specs=[pl.BlockSpec(memory_space=pltpu.VMEM)],
        out_specs=pl.BlockSpec(memory_space=pltpu.VMEM),
        scratch_shapes=[
            pltpu.VMEM(parts.shape, parts.dtype),
            pltpu.SemaphoreType.DMA((count,)),
            pltpu.SemaphoreType.DMA((count,)),
            pltpu.SemaphoreType.DMA((count,)),
            pltpu.SemaphoreType.DMA((count,)),
        ],
        compiler_params=pltpu.CompilerParams(collective_id=2, has_side_effects=True),
    )(parts)
    return summed.reshape(rows, width)


def scatter_kernel(
    row_size, g_ref, out_ref, slots_y, totals, sums, slots_row, send_a, recv_a, send_b, recv_b
):
    me = lax.axis_index(SLAB)
    own_y, spot = me // row_size, me % row_size
    y_count = lax.psum(1, "y")
    barrier = pltpu.get_barrier_semaphore()

    def greet(k, carry):
        peer = own_y * row_size + lax.rem(spot + k, row_size)
        pl.semaphore_signal(barrier, inc=1, device_id=peer_id(peer), device_id_type=MESH)
        return carry

    lax.fori_loop(1, row_size, greet, 0)
    others = [lax.rem(own_y + j, y_count) for j in range(1, y_count)]
    for other_y in others:
        pl.semaphore_signal(
            barrier, inc=1, device_id=peer_id(other_y * row_size + spot), device_id_type=MESH
        )
    pl.semaphore_wait(barrier, row_size + y_count - 2)

    def across(target_y, source_y):
        return pltpu.make_async_remote_copy(
            src_ref=g_ref.at[pl.ds(target_y * row_size, row_size)],
            dst_ref=slots_y.at[source_y],
            send_sem=send_a.at[target_y],
            recv_sem=recv_a.at[source_y],
            device_id=peer_id(target_y * row_size + spot),
            device_id_type=MESH,
        )

    for other_y in others:
        across(other_y, own_y).start()
    total = g_ref[pl.ds(own_y * row_size, row_size)].astype(jnp.float32)
    for other_y in others:
        across(other_y, own_y).wait_send()
        across(other_y, other_y).wait_recv()
        total = total + slots_y[other_y].astype(jnp.float32)
    totals[...] = total
    sums[...] = total.astype(sums.dtype)

    def along_row(target, source):
        return pltpu.make_async_remote_copy(
            src_ref=sums.at[target],
            dst_ref=slots_row.at[source],
            send_sem=send_b.at[target],
            recv_sem=recv_b.at[source],
            device_id=peer_id(own_y * row_size + target),
            device_id_type=MESH,
        )

    def start_row(k, carry):
        along_row(lax.rem(spot + k, row_size), spot).start()
        return carry

    lax.fori_loop(1, row_size, start_row, 0)
    out_ref[...] = totals[spot]

    def finish_row(k, carry):
        other = lax.rem(spot + k, row_size)
        along_row(other, spot).wait_send()
        along_row(other, other).wait_recv()
        out_ref[...] += slots_row[other].astype(jnp.float32)
        return carry

    lax.fori_loop(1, row_size, finish_row, 0)


def slab_scatter(blocks, count, row_size):
    total_rows, width = blocks[0].shape
    rows = total_rows // count
    y_count = count // row_size
    g = jnp.concatenate(
        [block.astype(jnp.bfloat16).reshape(count, rows, width) for block in blocks], axis=1
    )
    summed = pl.pallas_call(
        functools.partial(scatter_kernel, row_size),
        out_shape=jax.ShapeDtypeStruct(g.shape[1:], jnp.float32),
        in_specs=[pl.BlockSpec(memory_space=pltpu.VMEM)],
        out_specs=pl.BlockSpec(memory_space=pltpu.VMEM),
        scratch_shapes=[
            pltpu.VMEM((y_count, row_size) + g.shape[1:], g.dtype),
            pltpu.VMEM((row_size,) + g.shape[1:], jnp.float32),
            pltpu.VMEM((row_size,) + g.shape[1:], g.dtype),
            pltpu.VMEM((row_size,) + g.shape[1:], g.dtype),
            pltpu.SemaphoreType.DMA((y_count,)),
            pltpu.SemaphoreType.DMA((y_count,)),
            pltpu.SemaphoreType.DMA((row_size,)),
            pltpu.SemaphoreType.DMA((row_size,)),
        ],
        compiler_params=pltpu.CompilerParams(collective_id=1, has_side_effects=True),
    )(g)
    return [summed[i * rows : (i + 1) * rows] for i in range(len(blocks))]


def layer_norm(values, scale_gain):
    values = values.astype(jnp.float32)
    centered = values - jnp.mean(values, axis=-1, keepdims=True)
    variance = jnp.mean(centered * centered, axis=-1, keepdims=True)
    return centered * lax.rsqrt(variance + EPSILON) * scale_gain


def rope_tables(coord_x, coord_y, coord_z, head_size):
    pair_count = head_size // 2
    position = jnp.arange(pair_count, dtype=jnp.int32)
    axis_pick = position % 3
    per_axis = (pair_count + 2) // 3
    frequency = ROPE_BASE ** (-(position // 3).astype(jnp.float32) / per_axis)
    angles = (
        coord_x[:, None] * (axis_pick == 0)
        + coord_y[:, None] * (axis_pick == 1)
        + coord_z[:, None] * (axis_pick == 2)
    ) * frequency
    return (jnp.cos(angles)[:, None, :], jnp.sin(angles)[:, None, :])


def token_tables(first_plane, planes, head_size):
    position = jnp.arange(planes * GY * GX, dtype=jnp.int32)
    coord_x = (position % GX).astype(jnp.float32)
    coord_y = (position // GX % GY).astype(jnp.float32)
    coord_z = (first_plane + position // (GX * GY)).astype(jnp.float32)
    return rope_tables(coord_x, coord_y, coord_z, head_size)


def key_tables(first_row, row_count, head_size):
    position = first_row + jnp.arange(row_count, dtype=jnp.int32)
    half_x = GX // 2
    half_y = GY // 2
    coord_x = (position % half_x).astype(jnp.float32) * 2.0 + 0.5
    coord_y = (position // half_x % half_y).astype(jnp.float32) * 2.0 + 0.5
    coord_z = (position // (half_x * half_y)).astype(jnp.float32) * 2.0 + 0.5
    return rope_tables(coord_x, coord_y, coord_z, head_size)


def rotate(values, cosine, sine_table):
    half_size = values.shape[-1] // 2
    front_half = values[..., :half_size]
    back_half = values[..., half_size:]
    return jnp.concatenate(
        [
            front_half * cosine - back_half * sine_table,
            back_half * cosine + front_half * sine_table,
        ],
        axis=-1,
    )


def make_patches(normed, planes):
    width = normed.shape[-1]
    cell_grid = normed.reshape(planes // 2, 2, GY // 2, 2, GX // 2, 2, width)
    return cell_grid.transpose(0, 2, 4, 1, 3, 5, 6).reshape(-1, 8 * width)


def depth_conv(padded, weights, planes):
    height = padded.shape[1] - 2
    width_x = padded.shape[2] - 2
    result = jnp.zeros((planes, height, width_x, padded.shape[3]), jnp.float32)
    for offset in range(27):
        shift_z = offset // 9
        shift_y = offset // 3 % 3
        shift_x = offset % 3
        window = padded[
            shift_z : shift_z + planes, shift_y : shift_y + height, shift_x : shift_x + width_x
        ]
        result = result + window.astype(jnp.float32) * weights[offset]
    return result


def conv_with_halos(cells, weights):
    count = lax.psum(1, SLAB)
    ends = count - 1
    planes = cells.shape[0]
    below = lax.ppermute(cells[planes - 1], SLAB, [(i, i + 1) for i in range(ends)])
    above = lax.ppermute(cells[0], SLAB, [(i + 1, i) for i in range(ends)])
    own = depth_conv(jnp.pad(cells, ((1, 1), (1, 1), (1, 1), (0, 0))), weights, planes)
    height, width_x = cells.shape[1], cells.shape[2]

    def plane_terms(plane, first):
        padded = jnp.pad(plane, ((1, 1), (1, 1), (0, 0))).astype(jnp.float32)
        total = jnp.zeros(plane.shape, jnp.float32)
        for offset in range(9):
            shift_y, shift_x = offset // 3, offset % 3
            window = padded[shift_y : shift_y + height, shift_x : shift_x + width_x]
            total = total + window * weights[first + offset]
        return total

    own = own.at[0].add(plane_terms(below, 0))
    return own.at[planes - 1].add(plane_terms(above, 18))


def per_device(
    tokens,
    gain_attn,
    w_reduce,
    gain_keys,
    w_query,
    w_key,
    w_value,
    w_out,
    gain_ffn,
    w_up,
    w_depth,
    w_down,
    grad_out,
):
    slab_index = lax.axis_index(SLAB)
    tok_rows = tokens.shape[0]
    heads_dev = w_query.shape[1] // HEAD
    normed = layer_norm(tokens, gain_attn).astype(jnp.bfloat16)
    patches = make_patches(normed, CZ)
    reduced = jnp.dot(patches, w_reduce, preferred_element_type=jnp.float32)
    key_input = layer_norm(reduced, gain_keys).astype(jnp.bfloat16)
    tok_cos, tok_sin = token_tables(slab_index * CZ, CZ, HEAD)
    queries = jnp.dot(normed, w_query, preferred_element_type=jnp.float32)
    queries = jnp.concatenate(
        [
            rotate(queries[:, head * HEAD : (head + 1) * HEAD], tok_cos[:, 0], tok_sin[:, 0])
            for head in range(heads_dev)
        ],
        axis=1,
    ).astype(jnp.bfloat16)
    local_rows = key_input.shape[0]
    own_cos, own_sin = key_tables(slab_index * local_rows, local_rows, HEAD)
    own_keys = jnp.dot(key_input, w_key, preferred_element_type=jnp.float32).reshape(
        local_rows, heads_dev, HEAD
    )
    own_keys = rotate(own_keys, own_cos, own_sin).astype(jnp.bfloat16)
    own_values = jnp.dot(key_input, w_value, preferred_element_type=jnp.float32).astype(
        jnp.bfloat16
    )
    key_width = heads_dev * HEAD
    pieces = jnp.concatenate([own_keys.reshape(local_rows, key_width), own_values], axis=1)
    heads_out = gather_attend(
        pieces,
        queries,
        lax.psum(1, SLAB),
        lax.psum(1, ("z", "xl")),
        heads_dev,
    )
    partial_value = jnp.dot(heads_out, w_out, preferred_element_type=jnp.float32)
    head_total = head_sum(partial_value, lax.psum(1, FFN)).astype(jnp.float32)
    attended = head_total.astype(jnp.bfloat16)
    residual = tokens.astype(jnp.float32) + head_total
    normed_ffn = layer_norm(residual, gain_ffn).astype(jnp.bfloat16)
    channels = w_up.shape[1]
    pre = (
        jnp.dot(normed_ffn, w_up, preferred_element_type=jnp.float32)
        .astype(jnp.bfloat16)
        .reshape(CZ, GY, GX, channels)
    )
    mixed = conv_with_halos(pre, w_depth).reshape(tok_rows, channels)
    normal_cdf = 0.5 * (1.0 + lax.erf(mixed * ROOT_HALF))
    normal_pdf = jnp.exp(-0.5 * mixed * mixed) * NORMAL_SCALE
    activated = (mixed * normal_cdf).astype(jnp.bfloat16)
    grad_act = lax.optimization_barrier(
        jnp.einsum("td,cd->tc", grad_out, w_down, preferred_element_type=jnp.float32)
    )
    grad_mixed = (
        (grad_act * (normal_cdf + mixed * normal_pdf))
        .astype(jnp.bfloat16)
        .reshape(CZ, GY, GX, channels)
    )
    grad_pre = (
        conv_with_halos(grad_mixed, w_depth[::-1])
        .astype(jnp.bfloat16)
        .reshape(tok_rows, channels)
    )
    up_full = jnp.einsum("td,tc->dc", normed_ffn, grad_pre, preferred_element_type=jnp.float32)
    down_full = jnp.einsum("td,tc->dc", grad_out, activated, preferred_element_type=jnp.float32)
    grad_up, grad_down = slab_scatter(
        [up_full, down_full], lax.psum(1, SLAB), lax.psum(1, ("z", "xl"))
    )
    return (attended, grad_up, grad_down)


def solution(mesh):
    mesh = Mesh(mesh.devices.reshape(4, 8, 2, 2, 2), SLAB + FFN)
    in_specs = (
        P(SLAB, None),
        P(),
        P(),
        P(),
        P(None, FFN),
        P(None, FFN),
        P(None, FFN),
        P(FFN, None),
        P(),
        P(None, FFN),
        P(None, FFN),
        P(FFN, None),
        P(SLAB, None),
    )
    out_specs = (P(SLAB, None), P(SLAB, FFN), P(SLAB, FFN))
    return jax.shard_map(
        per_device, mesh=mesh, in_specs=in_specs, out_specs=out_specs, check_vma=False
    )
```

```python
import functools
import math

import jax
import jax.numpy as jnp
from jax import lax
from jax.experimental import pallas as pl
from jax.experimental.pallas import tpu as pltpu
from jax.sharding import Mesh
from jax.sharding import PartitionSpec as P

HEAD = 64
GX = 16
GY = 16
CZ = 2
SLAB = ("y", "z", "xl")
FFN = ("xh", "core")


EPSILON = 1e-05
ROPE_BASE = 100.0
ROOT_HALF = 0.7071067811865476
NORMAL_SCALE = 0.3989422804014327


MESH = pl.DeviceIdType.MESH


def peer_id(p):
    return (p // 16, p // 2 % 8, p % 2, lax.axis_index("xh"), lax.axis_index("core"))


def attend_rows(kv_ref, q_ref, top_ref, total_ref, acc_ref, first_row, row_rows, first):
    heads, q_rows, _ = top_ref.shape
    q_tile = q_rows
    key_width = heads * HEAD
    score_scale = HEAD ** (-0.5)
    rows = pl.ds(pl.multiple_of(first_row, row_rows), row_rows)
    for head in range(heads):
        keys = kv_ref[rows, head * HEAD : (head + 1) * HEAD]
        values = kv_ref[rows, key_width + head * HEAD : key_width + (head + 1) * HEAD]
        for start in range(0, q_rows, q_tile):
            tile = slice(start, start + q_tile)
            columns = slice(head * HEAD, (head + 1) * HEAD)
            scores = lax.dot_general(
                q_ref[tile, columns], keys, (((1,), (1,)), ((), ())),
                preferred_element_type=jnp.float32,
            ) * score_scale
            top = jnp.max(scores, axis=1, keepdims=True)
            if not first:
                old_top = top_ref[head, tile]
                top = jnp.maximum(top, old_top)
                rescale = jnp.exp(old_top - top)
            weights = jnp.exp(scores - top)
            row_sum = jnp.sum(weights, axis=1, keepdims=True)
            mixed = jnp.dot(
                weights.astype(jnp.bfloat16), values, preferred_element_type=jnp.float32
            )
            if not first:
                row_sum = row_sum + rescale * total_ref[head, tile]
                mixed = mixed + rescale * acc_ref[tile, columns]
            top_ref[head, tile] = top
            total_ref[head, tile] = row_sum
            acc_ref[tile, columns] = mixed


def gather_kernel(
    row_size, x_ref, q_ref, heads_ref, out_ref, top_ref, total_ref, acc_ref,
    send_a, recv_a, send_b, recv_b, send_c, recv_c, local_sem,
):
    me = lax.axis_index(SLAB)
    block = x_ref.shape[0]
    own_y, spot = me // row_size, me % row_size
    y_count = lax.psum(1, "y")
    barrier = pltpu.get_barrier_semaphore()

    def greet(k, carry):
        peer = own_y * row_size + lax.rem(spot + k, row_size)
        pl.semaphore_signal(barrier, inc=1, device_id=peer_id(peer), device_id_type=MESH)
        return carry

    lax.fori_loop(1, row_size, greet, 0)
    left_y = lax.rem(own_y + y_count - 1, y_count)
    right_y = lax.rem(own_y + 1, y_count)
    for other_y in (left_y, right_y):
        peer = other_y * row_size + spot
        pl.semaphore_signal(barrier, inc=1, device_id=peer_id(peer), device_id_type=MESH)
    pl.semaphore_wait(barrier, row_size + 1)

    def along_row(target, source):
        return pltpu.make_async_remote_copy(
            src_ref=x_ref,
            dst_ref=out_ref.at[pl.ds((own_y * row_size + source) * block, block)],
            send_sem=send_a.at[target],
            recv_sem=recv_a.at[source],
            device_id=peer_id(own_y * row_size + target),
            device_id_type=MESH,
        )

    def start_row(k, carry):
        along_row(lax.rem(spot + k, row_size), spot).start()
        return carry

    lax.fori_loop(1, row_size, start_row, 0)
    local = pltpu.make_async_copy(x_ref, out_ref.at[pl.ds(me * block, block)], local_sem)
    local.start()
    local.wait()

    def finish_row(k, carry):
        other = lax.rem(spot + k, row_size)
        along_row(other, spot).wait_send()
        along_row(other, other).wait_recv()
        return carry

    lax.fori_loop(1, row_size, finish_row, 0)
    row_rows = row_size * block

    def across(target_y, source_y):
        return pltpu.make_async_remote_copy(
            src_ref=out_ref.at[pl.ds(source_y * row_rows, row_rows)],
            dst_ref=out_ref.at[pl.ds(source_y * row_rows, row_rows)],
            send_sem=send_b.at[target_y],
            recv_sem=recv_b.at[source_y],
            device_id=peer_id(target_y * row_size + spot),
            device_id_type=MESH,
        )

    for other_y in (left_y, right_y):
        across(other_y, own_y).start()
    attend = functools.partial(
        attend_rows, out_ref, q_ref, top_ref, total_ref, acc_ref, row_rows=row_rows
    )
    attend(own_y * row_rows, first=True)
    for other_y in (left_y, right_y):
        across(other_y, own_y).wait_send()
        across(other_y, other_y).wait_recv()
    half = row_rows // 2

    def forward(target_y, source_y, part):
        rows = pl.ds(source_y * row_rows + part * half, half)
        return pltpu.make_async_remote_copy(
            src_ref=out_ref.at[rows],
            dst_ref=out_ref.at[rows],
            send_sem=send_c.at[part],
            recv_sem=recv_c.at[part],
            device_id=peer_id(target_y * row_size + spot),
            device_id_type=MESH,
        )

    far_y = lax.rem(own_y + 2, y_count)
    forward(right_y, left_y, 0).start()
    forward(left_y, right_y, 1).start()
    attend(left_y * row_rows, first=False)
    attend(right_y * row_rows, first=False)
    forward(right_y, left_y, 0).wait_send()
    forward(left_y, right_y, 1).wait_send()
    forward(right_y, far_y, 0).wait_recv()
    forward(left_y, far_y, 1).wait_recv()
    attend(far_y * row_rows, first=False)
    heads = top_ref.shape[0]
    for head in range(heads):
        columns = slice(head * HEAD, (head + 1) * HEAD)
        heads_ref[:, columns] = (acc_ref[:, columns] / total_ref[head]).astype(heads_ref.dtype)


def gather_attend(x, queries, count, row_size, heads):
    rows, width = x.shape
    q_rows = queries.shape[0]
    y_count = count // row_size
    assert y_count == 4
    return pl.pallas_call(
        functools.partial(gather_kernel, row_size),
        out_shape=jax.ShapeDtypeStruct(queries.shape, jnp.bfloat16),
        in_specs=[pl.BlockSpec(memory_space=pltpu.VMEM)] * 2,
        out_specs=pl.BlockSpec(memory_space=pltpu.VMEM),
        scratch_shapes=[
            pltpu.VMEM((count * rows, width), x.dtype),
            pltpu.VMEM((heads, q_rows, 1), jnp.float32),
            pltpu.VMEM((heads, q_rows, 1), jnp.float32),
            pltpu.VMEM(queries.shape, jnp.float32),
            pltpu.SemaphoreType.DMA((row_size,)),
            pltpu.SemaphoreType.DMA((row_size,)),
            pltpu.SemaphoreType.DMA((y_count,)),
            pltpu.SemaphoreType.DMA((y_count,)),
            pltpu.SemaphoreType.DMA((2,)),
            pltpu.SemaphoreType.DMA((2,)),
            pltpu.SemaphoreType.DMA(()),
        ],
        compiler_params=pltpu.CompilerParams(collective_id=0, has_side_effects=True),
    )(x, queries)


def head_peer(q):
    return (lax.axis_index("y"), lax.axis_index("z"), lax.axis_index("xl"), q // 2, q % 2)


def head_sum_kernel(count, part_ref, out_ref, slots, send_sem, recv_sem, send_back, recv_back):
    me = lax.axis_index(FFN)
    barrier = pltpu.get_barrier_semaphore()
    for k in range(1, count):
        pl.semaphore_signal(
            barrier, inc=1, device_id=head_peer(lax.rem(me + k, count)), device_id_type=MESH
        )
    pl.semaphore_wait(barrier, count - 1)

    def share(peer, source):
        return pltpu.make_async_remote_copy(
            src_ref=part_ref.at[peer],
            dst_ref=slots.at[source],
            send_sem=send_sem.at[peer],
            recv_sem=recv_sem.at[source],
            device_id=head_peer(peer),
            device_id_type=MESH,
        )

    def spread(peer, source):
        return pltpu.make_async_remote_copy(
            src_ref=out_ref.at[source],
            dst_ref=out_ref.at[source],
            send_sem=send_back.at[peer],
            recv_sem=recv_back.at[source],
            device_id=head_peer(peer),
            device_id_type=MESH,
        )

    peers = [lax.rem(me + k, count) for k in range(1, count)]
    for peer in peers:
        share(peer, me).start()
    total = part_ref[me].astype(jnp.float32)
    for peer in peers:
        share(peer, me).wait_send()
        share(peer, peer).wait_recv()
        total = total + slots[peer].astype(jnp.float32)
    out_ref[me] = total.astype(out_ref.dtype)
    for peer in peers:
        spread(peer, me).start()
    for peer in peers:
        spread(peer, me).wait_send()
        spread(peer, peer).wait_recv()


def head_sum(partial_value, count):
    rows, width = partial_value.shape
    parts = partial_value.astype(jnp.bfloat16).reshape(count, rows // count, width)
    summed = pl.pallas_call(
        functools.partial(head_sum_kernel, count),
        out_shape=jax.ShapeDtypeStruct(parts.shape, parts.dtype),
        in_specs=[pl.BlockSpec(memory_space=pltpu.VMEM)],
        out_specs=pl.BlockSpec(memory_space=pltpu.VMEM),
        scratch_shapes=[
            pltpu.VMEM(parts.shape, parts.dtype),
            pltpu.SemaphoreType.DMA((count,)),
            pltpu.SemaphoreType.DMA((count,)),
            pltpu.SemaphoreType.DMA((count,)),
            pltpu.SemaphoreType.DMA((count,)),
        ],
        compiler_params=pltpu.CompilerParams(collective_id=2, has_side_effects=True),
    )(parts)
    return summed.reshape(rows, width)


def scatter_kernel(
    row_size, g_ref, out_ref, slots_y, totals, sums, slots_row, send_a, recv_a, send_b, recv_b
):
    me = lax.axis_index(SLAB)
    own_y, spot = me // row_size, me % row_size
    y_count = lax.psum(1, "y")
    barrier = pltpu.get_barrier_semaphore()

    def greet(k, carry):
        peer = own_y * row_size + lax.rem(spot + k, row_size)
        pl.semaphore_signal(barrier, inc=1, device_id=peer_id(peer), device_id_type=MESH)
        return carry

    lax.fori_loop(1, row_size, greet, 0)
    others = [lax.rem(own_y + j, y_count) for j in range(1, y_count)]
    for other_y in others:
        pl.semaphore_signal(
            barrier, inc=1, device_id=peer_id(other_y * row_size + spot), device_id_type=MESH
        )
    pl.semaphore_wait(barrier, row_size + y_count - 2)

    def across(target_y, source_y):
        return pltpu.make_async_remote_copy(
            src_ref=g_ref.at[pl.ds(target_y * row_size, row_size)],
            dst_ref=slots_y.at[source_y],
            send_sem=send_a.at[target_y],
            recv_sem=recv_a.at[source_y],
            device_id=peer_id(target_y * row_size + spot),
            device_id_type=MESH,
        )

    for other_y in others:
        across(other_y, own_y).start()
    total = g_ref[pl.ds(own_y * row_size, row_size)].astype(jnp.float32)
    for other_y in others:
        across(other_y, own_y).wait_send()
        across(other_y, other_y).wait_recv()
        total = total + slots_y[other_y].astype(jnp.float32)
    totals[...] = total
    sums[...] = total.astype(sums.dtype)

    def along_row(target, source):
        return pltpu.make_async_remote_copy(
            src_ref=sums.at[target],
            dst_ref=slots_row.at[source],
            send_sem=send_b.at[target],
            recv_sem=recv_b.at[source],
            device_id=peer_id(own_y * row_size + target),
            device_id_type=MESH,
        )

    def start_row(k, carry):
        along_row(lax.rem(spot + k, row_size), spot).start()
        return carry

    lax.fori_loop(1, row_size, start_row, 0)
    out_ref[...] = totals[spot]

    def finish_row(k, carry):
        other = lax.rem(spot + k, row_size)
        along_row(other, spot).wait_send()
        along_row(other, other).wait_recv()
        out_ref[...] += slots_row[other].astype(jnp.float32)
        return carry

    lax.fori_loop(1, row_size, finish_row, 0)


def slab_scatter(blocks, count, row_size):
    total_rows, width = blocks[0].shape
    rows = total_rows // count
    y_count = count // row_size
    g = jnp.concatenate(
        [block.astype(jnp.bfloat16).reshape(count, rows, width) for block in blocks], axis=1
    )
    summed = pl.pallas_call(
        functools.partial(scatter_kernel, row_size),
        out_shape=jax.ShapeDtypeStruct(g.shape[1:], jnp.float32),
        in_specs=[pl.BlockSpec(memory_space=pltpu.VMEM)],
        out_specs=pl.BlockSpec(memory_space=pltpu.VMEM),
        scratch_shapes=[
            pltpu.VMEM((y_count, row_size) + g.shape[1:], g.dtype),
            pltpu.VMEM((row_size,) + g.shape[1:], jnp.float32),
            pltpu.VMEM((row_size,) + g.shape[1:], g.dtype),
            pltpu.VMEM((row_size,) + g.shape[1:], g.dtype),
            pltpu.SemaphoreType.DMA((y_count,)),
            pltpu.SemaphoreType.DMA((y_count,)),
            pltpu.SemaphoreType.DMA((row_size,)),
            pltpu.SemaphoreType.DMA((row_size,)),
        ],
        compiler_params=pltpu.CompilerParams(collective_id=1, has_side_effects=True),
    )(g)
    return [summed[i * rows : (i + 1) * rows] for i in range(len(blocks))]


def layer_norm(values, scale_gain):
    values = values.astype(jnp.float32)
    centered = values - jnp.mean(values, axis=-1, keepdims=True)
    variance = jnp.mean(centered * centered, axis=-1, keepdims=True)
    return centered * lax.rsqrt(variance + EPSILON) * scale_gain


def rope_tables(coord_x, coord_y, coord_z, head_size):
    pair_count = head_size // 2
    position = jnp.arange(pair_count, dtype=jnp.int32)
    axis_pick = position % 3
    per_axis = (pair_count + 2) // 3
    frequency = ROPE_BASE ** (-(position // 3).astype(jnp.float32) / per_axis)
    angles = (
        coord_x[:, None] * (axis_pick == 0)
        + coord_y[:, None] * (axis_pick == 1)
        + coord_z[:, None] * (axis_pick == 2)
    ) * frequency
    return (jnp.cos(angles)[:, None, :], jnp.sin(angles)[:, None, :])


def token_tables(first_plane, planes, head_size):
    position = jnp.arange(planes * GY * GX, dtype=jnp.int32)
    coord_x = (position % GX).astype(jnp.float32)
    coord_y = (position // GX % GY).astype(jnp.float32)
    coord_z = (first_plane + position // (GX * GY)).astype(jnp.float32)
    return rope_tables(coord_x, coord_y, coord_z, head_size)


def key_tables(first_row, row_count, head_size):
    position = first_row + jnp.arange(row_count, dtype=jnp.int32)
    half_x = GX // 2
    half_y = GY // 2
    coord_x = (position % half_x).astype(jnp.float32) * 2.0 + 0.5
    coord_y = (position // half_x % half_y).astype(jnp.float32) * 2.0 + 0.5
    coord_z = (position // (half_x * half_y)).astype(jnp.float32) * 2.0 + 0.5
    return rope_tables(coord_x, coord_y, coord_z, head_size)


def rotate(values, cosine, sine_table):
    half_size = values.shape[-1] // 2
    front_half = values[..., :half_size]
    back_half = values[..., half_size:]
    return jnp.concatenate(
        [
            front_half * cosine - back_half * sine_table,
            back_half * cosine + front_half * sine_table,
        ],
        axis=-1,
    )


def make_patches(normed, planes):
    width = normed.shape[-1]
    cell_grid = normed.reshape(planes // 2, 2, GY // 2, 2, GX // 2, 2, width)
    return cell_grid.transpose(0, 2, 4, 1, 3, 5, 6).reshape(-1, 8 * width)


def depth_conv(padded, weights, planes):
    height = padded.shape[1] - 2
    width_x = padded.shape[2] - 2
    result = jnp.zeros((planes, height, width_x, padded.shape[3]), jnp.float32)
    for offset in range(27):
        shift_z = offset // 9
        shift_y = offset // 3 % 3
        shift_x = offset % 3
        window = padded[
            shift_z : shift_z + planes, shift_y : shift_y + height, shift_x : shift_x + width_x
        ]
        result = result + window.astype(jnp.float32) * weights[offset]
    return result


def conv_with_halos(cells, weights):
    count = lax.psum(1, SLAB)
    ends = count - 1
    planes = cells.shape[0]
    below = lax.ppermute(cells[planes - 1], SLAB, [(i, i + 1) for i in range(ends)])
    above = lax.ppermute(cells[0], SLAB, [(i + 1, i) for i in range(ends)])
    own = depth_conv(jnp.pad(cells, ((1, 1), (1, 1), (1, 1), (0, 0))), weights, planes)
    height, width_x = cells.shape[1], cells.shape[2]

    def plane_terms(plane, first):
        padded = jnp.pad(plane, ((1, 1), (1, 1), (0, 0))).astype(jnp.float32)
        total = jnp.zeros(plane.shape, jnp.float32)
        for offset in range(9):
            shift_y, shift_x = offset // 3, offset % 3
            window = padded[shift_y : shift_y + height, shift_x : shift_x + width_x]
            total = total + window * weights[first + offset]
        return total

    own = own.at[0].add(plane_terms(below, 0))
    return own.at[planes - 1].add(plane_terms(above, 18))


def per_device(
    tokens,
    gain_attn,
    w_reduce,
    gain_keys,
    w_query,
    w_key,
    w_value,
    w_out,
    gain_ffn,
    w_up,
    w_depth,
    w_down,
    grad_out,
):
    slab_index = lax.axis_index(SLAB)
    tok_rows = tokens.shape[0]
    heads_dev = w_query.shape[1] // HEAD
    normed = layer_norm(tokens, gain_attn).astype(jnp.bfloat16)
    patches = make_patches(normed, CZ)
    reduced = jnp.dot(patches, w_reduce, preferred_element_type=jnp.float32)
    key_input = layer_norm(reduced, gain_keys).astype(jnp.bfloat16)
    tok_cos, tok_sin = token_tables(slab_index * CZ, CZ, HEAD)
    queries = jnp.dot(normed, w_query, preferred_element_type=jnp.float32).reshape(
        tok_rows, heads_dev, HEAD
    )
    queries = rotate(queries, tok_cos, tok_sin).astype(jnp.bfloat16)
    local_rows = key_input.shape[0]
    own_cos, own_sin = key_tables(slab_index * local_rows, local_rows, HEAD)
    own_keys = jnp.dot(key_input, w_key, preferred_element_type=jnp.float32).reshape(
        local_rows, heads_dev, HEAD
    )
    own_keys = rotate(own_keys, own_cos, own_sin).astype(jnp.bfloat16)
    own_values = jnp.dot(key_input, w_value, preferred_element_type=jnp.float32).astype(
        jnp.bfloat16
    )
    key_width = heads_dev * HEAD
    pieces = jnp.concatenate([own_keys.reshape(local_rows, key_width), own_values], axis=1)
    heads_out = gather_attend(
        pieces,
        queries.reshape(tok_rows, key_width),
        lax.psum(1, SLAB),
        lax.psum(1, ("z", "xl")),
        heads_dev,
    )
    partial_value = jnp.dot(heads_out, w_out, preferred_element_type=jnp.float32)
    head_total = head_sum(partial_value, lax.psum(1, FFN)).astype(jnp.float32)
    attended = head_total.astype(jnp.bfloat16)
    residual = tokens.astype(jnp.float32) + head_total
    normed_ffn = layer_norm(residual, gain_ffn).astype(jnp.bfloat16)
    channels = w_up.shape[1]
    pre = (
        jnp.dot(normed_ffn, w_up, preferred_element_type=jnp.float32)
        .astype(jnp.bfloat16)
        .reshape(CZ, GY, GX, channels)
    )
    mixed = conv_with_halos(pre, w_depth).reshape(tok_rows, channels)
    normal_cdf = 0.5 * (1.0 + lax.erf(mixed * ROOT_HALF))
    normal_pdf = jnp.exp(-0.5 * mixed * mixed) * NORMAL_SCALE
    activated = (mixed * normal_cdf).astype(jnp.bfloat16)
    grad_act = lax.optimization_barrier(
        jnp.einsum("td,cd->tc", grad_out, w_down, preferred_element_type=jnp.float32)
    )
    grad_mixed = (
        (grad_act * (normal_cdf + mixed * normal_pdf))
        .astype(jnp.bfloat16)
        .reshape(CZ, GY, GX, channels)
    )
    grad_pre = (
        conv_with_halos(grad_mixed, w_depth[::-1])
        .astype(jnp.bfloat16)
        .reshape(tok_rows, channels)
    )
    up_full = jnp.einsum("td,tc->dc", normed_ffn, grad_pre, preferred_element_type=jnp.float32)
    down_full = jnp.einsum("td,tc->dc", grad_out, activated, preferred_element_type=jnp.float32)
    grad_up, grad_down = slab_scatter(
        [up_full, down_full], lax.psum(1, SLAB), lax.psum(1, ("z", "xl"))
    )
    return (attended, grad_up, grad_down)


def solution(mesh):
    mesh = Mesh(mesh.devices.reshape(4, 8, 2, 2, 2), SLAB + FFN)
    in_specs = (
        P(SLAB, None),
        P(),
        P(),
        P(),
        P(None, FFN),
        P(None, FFN),
        P(None, FFN),
        P(FFN, None),
        P(),
        P(None, FFN),
        P(None, FFN),
        P(FFN, None),
        P(SLAB, None),
    )
    out_specs = (P(SLAB, None), P(SLAB, FFN), P(SLAB, FFN))
    return jax.shard_map(
        per_device, mesh=mesh, in_specs=in_specs, out_specs=out_specs, check_vma=False
    )
```

```python
import functools
import math

import jax
import jax.numpy as jnp
from jax import lax
from jax.experimental import pallas as pl
from jax.experimental.pallas import tpu as pltpu
from jax.sharding import Mesh
from jax.sharding import PartitionSpec as P

HEAD = 64
GX = 16
GY = 16
CZ = 2
SLAB = ("y", "z", "xl")
FFN = ("xh", "core")


EPSILON = 1e-05
ROPE_BASE = 100.0
ROOT_HALF = 0.7071067811865476
NORMAL_SCALE = 0.3989422804014327


MESH = pl.DeviceIdType.MESH


def peer_id(p):
    return (p // 16, p // 2 % 8, p % 2, lax.axis_index("xh"), lax.axis_index("core"))


def attend_rows(kv_ref, q_ref, top_ref, total_ref, acc_ref, first_row, row_rows, first):
    heads, q_rows, _ = top_ref.shape
    q_tile = q_rows
    key_width = heads * HEAD
    score_scale = HEAD ** (-0.5)
    rows = pl.ds(pl.multiple_of(first_row, row_rows), row_rows)
    for head in range(heads):
        keys = kv_ref[rows, head * HEAD : (head + 1) * HEAD]
        values = kv_ref[rows, key_width + head * HEAD : key_width + (head + 1) * HEAD]
        for start in range(0, q_rows, q_tile):
            tile = slice(start, start + q_tile)
            columns = slice(head * HEAD, (head + 1) * HEAD)
            scores = lax.dot_general(
                q_ref[tile, columns], keys, (((1,), (1,)), ((), ())),
                preferred_element_type=jnp.float32,
            ) * score_scale
            top = jnp.max(scores, axis=1, keepdims=True)
            if not first:
                old_top = top_ref[head, tile]
                top = jnp.maximum(top, old_top)
                rescale = jnp.exp(old_top - top)
            weights = jnp.exp(scores - top)
            row_sum = jnp.sum(weights, axis=1, keepdims=True)
            mixed = jnp.dot(
                weights.astype(jnp.bfloat16), values, preferred_element_type=jnp.float32
            )
            if not first:
                row_sum = row_sum + rescale * total_ref[head, tile]
                mixed = mixed + rescale * acc_ref[tile, columns]
            top_ref[head, tile] = top
            total_ref[head, tile] = row_sum
            acc_ref[tile, columns] = mixed


def gather_kernel(
    row_size, x_ref, q_ref, heads_ref, out_ref, top_ref, total_ref, acc_ref,
    send_a, recv_a, send_b, recv_b, send_c, recv_c, local_sem,
):
    me = lax.axis_index(SLAB)
    block = x_ref.shape[0]
    own_y, spot = me // row_size, me % row_size
    y_count = lax.psum(1, "y")
    barrier = pltpu.get_barrier_semaphore()

    def greet(k, carry):
        peer = own_y * row_size + lax.rem(spot + k, row_size)
        pl.semaphore_signal(barrier, inc=1, device_id=peer_id(peer), device_id_type=MESH)
        return carry

    lax.fori_loop(1, row_size, greet, 0)
    left_y = lax.rem(own_y + y_count - 1, y_count)
    right_y = lax.rem(own_y + 1, y_count)
    for other_y in (left_y, right_y):
        peer = other_y * row_size + spot
        pl.semaphore_signal(barrier, inc=1, device_id=peer_id(peer), device_id_type=MESH)
    pl.semaphore_wait(barrier, row_size + 1)

    def along_row(target, source):
        return pltpu.make_async_remote_copy(
            src_ref=x_ref,
            dst_ref=out_ref.at[pl.ds((own_y * row_size + source) * block, block)],
            send_sem=send_a.at[target],
            recv_sem=recv_a.at[source],
            device_id=peer_id(own_y * row_size + target),
            device_id_type=MESH,
        )

    def start_row(k, carry):
        along_row(lax.rem(spot + k, row_size), spot).start()
        return carry

    lax.fori_loop(1, row_size, start_row, 0)
    local = pltpu.make_async_copy(x_ref, out_ref.at[pl.ds(me * block, block)], local_sem)
    local.start()
    local.wait()

    def finish_row(k, carry):
        other = lax.rem(spot + k, row_size)
        along_row(other, spot).wait_send()
        along_row(other, other).wait_recv()
        return carry

    lax.fori_loop(1, row_size, finish_row, 0)
    row_rows = row_size * block

    def across(target_y, source_y):
        return pltpu.make_async_remote_copy(
            src_ref=out_ref.at[pl.ds(source_y * row_rows, row_rows)],
            dst_ref=out_ref.at[pl.ds(source_y * row_rows, row_rows)],
            send_sem=send_b.at[target_y],
            recv_sem=recv_b.at[source_y],
            device_id=peer_id(target_y * row_size + spot),
            device_id_type=MESH,
        )

    for other_y in (left_y, right_y):
        across(other_y, own_y).start()
    attend = functools.partial(
        attend_rows, out_ref, q_ref, top_ref, total_ref, acc_ref, row_rows=row_rows
    )
    attend(own_y * row_rows, first=True)
    for other_y in (left_y, right_y):
        across(other_y, own_y).wait_send()
        across(other_y, other_y).wait_recv()
    half = row_rows // 2

    def forward(target_y, source_y, part):
        rows = pl.ds(source_y * row_rows + part * half, half)
        return pltpu.make_async_remote_copy(
            src_ref=out_ref.at[rows],
            dst_ref=out_ref.at[rows],
            send_sem=send_c.at[part],
            recv_sem=recv_c.at[part],
            device_id=peer_id(target_y * row_size + spot),
            device_id_type=MESH,
        )

    far_y = lax.rem(own_y + 2, y_count)
    forward(right_y, left_y, 0).start()
    forward(left_y, right_y, 1).start()
    attend(left_y * row_rows, first=False)
    attend(right_y * row_rows, first=False)
    forward(right_y, left_y, 0).wait_send()
    forward(left_y, right_y, 1).wait_send()
    forward(right_y, far_y, 0).wait_recv()
    forward(left_y, far_y, 1).wait_recv()
    attend(far_y * row_rows, first=False)
    heads = top_ref.shape[0]
    for head in range(heads):
        columns = slice(head * HEAD, (head + 1) * HEAD)
        heads_ref[:, columns] = (acc_ref[:, columns] / total_ref[head]).astype(heads_ref.dtype)


def gather_attend(x, queries, count, row_size, heads):
    rows, width = x.shape
    q_rows = queries.shape[0]
    y_count = count // row_size
    assert y_count == 4
    return pl.pallas_call(
        functools.partial(gather_kernel, row_size),
        out_shape=jax.ShapeDtypeStruct(queries.shape, jnp.bfloat16),
        in_specs=[pl.BlockSpec(memory_space=pltpu.VMEM)] * 2,
        out_specs=pl.BlockSpec(memory_space=pltpu.VMEM),
        scratch_shapes=[
            pltpu.VMEM((count * rows, width), x.dtype),
            pltpu.VMEM((heads, q_rows, 1), jnp.float32),
            pltpu.VMEM((heads, q_rows, 1), jnp.float32),
            pltpu.VMEM(queries.shape, jnp.float32),
            pltpu.SemaphoreType.DMA((row_size,)),
            pltpu.SemaphoreType.DMA((row_size,)),
            pltpu.SemaphoreType.DMA((y_count,)),
            pltpu.SemaphoreType.DMA((y_count,)),
            pltpu.SemaphoreType.DMA((2,)),
            pltpu.SemaphoreType.DMA((2,)),
            pltpu.SemaphoreType.DMA(()),
        ],
        compiler_params=pltpu.CompilerParams(collective_id=0, has_side_effects=True),
    )(x, queries)


def head_peer(q):
    return (lax.axis_index("y"), lax.axis_index("z"), lax.axis_index("xl"), q // 2, q % 2)


def head_sum_kernel(count, part_ref, out_ref, slots, send_sem, recv_sem, send_back, recv_back):
    me = lax.axis_index(FFN)
    barrier = pltpu.get_barrier_semaphore()
    for k in range(1, count):
        pl.semaphore_signal(
            barrier, inc=1, device_id=head_peer(lax.rem(me + k, count)), device_id_type=MESH
        )
    pl.semaphore_wait(barrier, count - 1)

    def share(peer, source):
        return pltpu.make_async_remote_copy(
            src_ref=part_ref.at[peer],
            dst_ref=slots.at[source],
            send_sem=send_sem.at[peer],
            recv_sem=recv_sem.at[source],
            device_id=head_peer(peer),
            device_id_type=MESH,
        )

    def spread(peer, source):
        return pltpu.make_async_remote_copy(
            src_ref=out_ref.at[source],
            dst_ref=out_ref.at[source],
            send_sem=send_back.at[peer],
            recv_sem=recv_back.at[source],
            device_id=head_peer(peer),
            device_id_type=MESH,
        )

    peers = [lax.rem(me + k, count) for k in range(1, count)]
    for peer in peers:
        share(peer, me).start()
    total = part_ref[me].astype(jnp.float32)
    for peer in peers:
        share(peer, me).wait_send()
        share(peer, peer).wait_recv()
        total = total + slots[peer].astype(jnp.float32)
    out_ref[me] = total.astype(out_ref.dtype)
    for peer in peers:
        spread(peer, me).start()
    for peer in peers:
        spread(peer, me).wait_send()
        spread(peer, peer).wait_recv()


def head_sum(partial_value, count):
    rows, width = partial_value.shape
    parts = partial_value.astype(jnp.bfloat16).reshape(count, rows // count, width)
    summed = pl.pallas_call(
        functools.partial(head_sum_kernel, count),
        out_shape=jax.ShapeDtypeStruct(parts.shape, parts.dtype),
        in_specs=[pl.BlockSpec(memory_space=pltpu.VMEM)],
        out_specs=pl.BlockSpec(memory_space=pltpu.VMEM),
        scratch_shapes=[
            pltpu.VMEM(parts.shape, parts.dtype),
            pltpu.SemaphoreType.DMA((count,)),
            pltpu.SemaphoreType.DMA((count,)),
            pltpu.SemaphoreType.DMA((count,)),
            pltpu.SemaphoreType.DMA((count,)),
        ],
        compiler_params=pltpu.CompilerParams(collective_id=2, has_side_effects=True),
    )(parts)
    return summed.reshape(rows, width)


def scatter_kernel(
    row_size, g_ref, out_ref, slots_y, totals, sums, slots_row, send_a, recv_a, send_b, recv_b
):
    me = lax.axis_index(SLAB)
    own_y, spot = me // row_size, me % row_size
    y_count = lax.psum(1, "y")
    barrier = pltpu.get_barrier_semaphore()

    def greet(k, carry):
        peer = own_y * row_size + lax.rem(spot + k, row_size)
        pl.semaphore_signal(barrier, inc=1, device_id=peer_id(peer), device_id_type=MESH)
        return carry

    lax.fori_loop(1, row_size, greet, 0)
    others = [lax.rem(own_y + j, y_count) for j in range(1, y_count)]
    for other_y in others:
        pl.semaphore_signal(
            barrier, inc=1, device_id=peer_id(other_y * row_size + spot), device_id_type=MESH
        )
    pl.semaphore_wait(barrier, row_size + y_count - 2)

    def across(target_y, source_y):
        return pltpu.make_async_remote_copy(
            src_ref=g_ref.at[pl.ds(target_y * row_size, row_size)],
            dst_ref=slots_y.at[source_y],
            send_sem=send_a.at[target_y],
            recv_sem=recv_a.at[source_y],
            device_id=peer_id(target_y * row_size + spot),
            device_id_type=MESH,
        )

    for other_y in others:
        across(other_y, own_y).start()
    total = g_ref[pl.ds(own_y * row_size, row_size)].astype(jnp.float32)
    for other_y in others:
        across(other_y, own_y).wait_send()
        across(other_y, other_y).wait_recv()
        total = total + slots_y[other_y].astype(jnp.float32)
    totals[...] = total
    sums[...] = total.astype(sums.dtype)

    def along_row(target, source):
        return pltpu.make_async_remote_copy(
            src_ref=sums.at[target],
            dst_ref=slots_row.at[source],
            send_sem=send_b.at[target],
            recv_sem=recv_b.at[source],
            device_id=peer_id(own_y * row_size + target),
            device_id_type=MESH,
        )

    def start_row(k, carry):
        along_row(lax.rem(spot + k, row_size), spot).start()
        return carry

    lax.fori_loop(1, row_size, start_row, 0)
    out_ref[...] = totals[spot]

    def finish_row(k, carry):
        other = lax.rem(spot + k, row_size)
        along_row(other, spot).wait_send()
        along_row(other, other).wait_recv()
        out_ref[...] += slots_row[other].astype(jnp.float32)
        return carry

    lax.fori_loop(1, row_size, finish_row, 0)


def slab_scatter(blocks, count, row_size):
    total_rows, width = blocks[0].shape
    rows = total_rows // count
    y_count = count // row_size
    g = jnp.concatenate(
        [block.astype(jnp.bfloat16).reshape(count, rows, width) for block in blocks], axis=1
    )
    summed = pl.pallas_call(
        functools.partial(scatter_kernel, row_size),
        out_shape=jax.ShapeDtypeStruct(g.shape[1:], jnp.float32),
        in_specs=[pl.BlockSpec(memory_space=pltpu.VMEM)],
        out_specs=pl.BlockSpec(memory_space=pltpu.VMEM),
        scratch_shapes=[
            pltpu.VMEM((y_count, row_size) + g.shape[1:], g.dtype),
            pltpu.VMEM((row_size,) + g.shape[1:], jnp.float32),
            pltpu.VMEM((row_size,) + g.shape[1:], g.dtype),
            pltpu.VMEM((row_size,) + g.shape[1:], g.dtype),
            pltpu.SemaphoreType.DMA((y_count,)),
            pltpu.SemaphoreType.DMA((y_count,)),
            pltpu.SemaphoreType.DMA((row_size,)),
            pltpu.SemaphoreType.DMA((row_size,)),
        ],
        compiler_params=pltpu.CompilerParams(collective_id=1, has_side_effects=True),
    )(g)
    return [summed[i * rows : (i + 1) * rows] for i in range(len(blocks))]


def layer_norm(values, scale_gain):
    values = values.astype(jnp.float32)
    centered = values - jnp.mean(values, axis=-1, keepdims=True)
    variance = jnp.mean(centered * centered, axis=-1, keepdims=True)
    return centered * lax.rsqrt(variance + EPSILON) * scale_gain


def rope_tables(coord_x, coord_y, coord_z, head_size):
    pair_count = head_size // 2
    position = jnp.arange(pair_count, dtype=jnp.int32)
    axis_pick = position % 3
    per_axis = (pair_count + 2) // 3
    frequency = ROPE_BASE ** (-(position // 3).astype(jnp.float32) / per_axis)
    angles = (
        coord_x[:, None] * (axis_pick == 0)
        + coord_y[:, None] * (axis_pick == 1)
        + coord_z[:, None] * (axis_pick == 2)
    ) * frequency
    return (jnp.cos(angles)[:, None, :], jnp.sin(angles)[:, None, :])


def token_tables(first_plane, planes, head_size):
    position = jnp.arange(planes * GY * GX, dtype=jnp.int32)
    coord_x = (position % GX).astype(jnp.float32)
    coord_y = (position // GX % GY).astype(jnp.float32)
    coord_z = (first_plane + position // (GX * GY)).astype(jnp.float32)
    return rope_tables(coord_x, coord_y, coord_z, head_size)


def key_tables(first_row, row_count, head_size):
    position = first_row + jnp.arange(row_count, dtype=jnp.int32)
    half_x = GX // 2
    half_y = GY // 2
    coord_x = (position % half_x).astype(jnp.float32) * 2.0 + 0.5
    coord_y = (position // half_x % half_y).astype(jnp.float32) * 2.0 + 0.5
    coord_z = (position // (half_x * half_y)).astype(jnp.float32) * 2.0 + 0.5
    return rope_tables(coord_x, coord_y, coord_z, head_size)


def rotate(values, cosine, sine_table):
    half_size = values.shape[-1] // 2
    front_half = values[..., :half_size]
    back_half = values[..., half_size:]
    return jnp.concatenate(
        [
            front_half * cosine - back_half * sine_table,
            back_half * cosine + front_half * sine_table,
        ],
        axis=-1,
    )


def make_patches(normed, planes):
    width = normed.shape[-1]
    cell_grid = normed.reshape(planes // 2, 2, GY // 2, 2, GX // 2, 2, width)
    return cell_grid.transpose(0, 2, 4, 1, 3, 5, 6).reshape(-1, 8 * width)


def depth_conv(padded, weights, planes):
    height = padded.shape[1] - 2
    width_x = padded.shape[2] - 2
    result = jnp.zeros((planes, height, width_x, padded.shape[3]), jnp.float32)
    for offset in range(27):
        shift_z = offset // 9
        shift_y = offset // 3 % 3
        shift_x = offset % 3
        window = padded[
            shift_z : shift_z + planes, shift_y : shift_y + height, shift_x : shift_x + width_x
        ]
        result = result + window.astype(jnp.float32) * weights[offset]
    return result


def conv_with_halos(cells, weights):
    count = lax.psum(1, SLAB)
    ends = count - 1
    planes = cells.shape[0]
    below = lax.ppermute(cells[planes - 1], SLAB, [(i, i + 1) for i in range(ends)])
    above = lax.ppermute(cells[0], SLAB, [(i + 1, i) for i in range(ends)])
    own = depth_conv(jnp.pad(cells, ((1, 1), (1, 1), (1, 1), (0, 0))), weights, planes)
    height, width_x = cells.shape[1], cells.shape[2]

    def plane_terms(plane, first):
        padded = jnp.pad(plane, ((1, 1), (1, 1), (0, 0))).astype(jnp.float32)
        total = jnp.zeros(plane.shape, jnp.float32)
        for offset in range(9):
            shift_y, shift_x = offset // 3, offset % 3
            window = padded[shift_y : shift_y + height, shift_x : shift_x + width_x]
            total = total + window * weights[first + offset]
        return total

    own = own.at[0].add(plane_terms(below, 0))
    return own.at[planes - 1].add(plane_terms(above, 18))


def per_device(
    tokens,
    gain_attn,
    w_reduce,
    gain_keys,
    w_query,
    w_key,
    w_value,
    w_out,
    gain_ffn,
    w_up,
    w_depth,
    w_down,
    grad_out,
):
    slab_index = lax.axis_index(SLAB)
    tok_rows = tokens.shape[0]
    heads_dev = w_query.shape[1] // HEAD
    normed = layer_norm(tokens, gain_attn).astype(jnp.bfloat16)
    patches = make_patches(normed, CZ)
    reduced = jnp.dot(patches, w_reduce, preferred_element_type=jnp.float32)
    key_input = layer_norm(reduced, gain_keys).astype(jnp.bfloat16)
    tok_cos, tok_sin = token_tables(slab_index * CZ, CZ, HEAD)
    queries = jnp.dot(normed, w_query, preferred_element_type=jnp.float32)
    queries = jnp.concatenate(
        [
            rotate(queries[:, head * HEAD : (head + 1) * HEAD], tok_cos[:, 0], tok_sin[:, 0])
            for head in range(heads_dev)
        ],
        axis=1,
    ).astype(jnp.bfloat16)
    local_rows = key_input.shape[0]
    own_cos, own_sin = key_tables(slab_index * local_rows, local_rows, HEAD)
    own_keys = jnp.dot(key_input, w_key, preferred_element_type=jnp.float32).reshape(
        local_rows, heads_dev, HEAD
    )
    own_keys = rotate(own_keys, own_cos, own_sin).astype(jnp.bfloat16)
    own_values = jnp.dot(key_input, w_value, preferred_element_type=jnp.float32).astype(
        jnp.bfloat16
    )
    key_width = heads_dev * HEAD
    pieces = jnp.concatenate([own_keys.reshape(local_rows, key_width), own_values], axis=1)
    heads_out = gather_attend(
        pieces,
        queries,
        lax.psum(1, SLAB),
        lax.psum(1, ("z", "xl")),
        heads_dev,
    )
    partial_value = jnp.dot(heads_out, w_out, preferred_element_type=jnp.float32)
    head_total = head_sum(partial_value, lax.psum(1, FFN)).astype(jnp.float32)
    attended = head_total.astype(jnp.bfloat16)
    residual = tokens.astype(jnp.float32) + head_total
    normed_ffn = layer_norm(residual, gain_ffn).astype(jnp.bfloat16)
    channels = w_up.shape[1]
    pre = (
        jnp.dot(normed_ffn, w_up, preferred_element_type=jnp.float32)
        .astype(jnp.bfloat16)
        .reshape(CZ, GY, GX, channels)
    )
    mixed = conv_with_halos(pre, w_depth).reshape(tok_rows, channels)
    normal_cdf = 0.5 * (1.0 + lax.erf(mixed * ROOT_HALF))
    normal_pdf = jnp.exp(-0.5 * mixed * mixed) * NORMAL_SCALE
    activated = (mixed * normal_cdf).astype(jnp.bfloat16)
    grad_act = lax.optimization_barrier(
        jnp.einsum("td,cd->tc", grad_out, w_down, preferred_element_type=jnp.float32)
    )
    grad_mixed = (
        (grad_act * (normal_cdf + mixed * normal_pdf))
        .astype(jnp.bfloat16)
        .reshape(CZ, GY, GX, channels)
    )
    grad_pre = (
        conv_with_halos(grad_mixed, w_depth[::-1])
        .astype(jnp.bfloat16)
        .reshape(tok_rows, channels)
    )
    up_full = jnp.einsum("td,tc->dc", normed_ffn, grad_pre, preferred_element_type=jnp.float32)
    down_full = jnp.einsum("td,tc->dc", grad_out, activated, preferred_element_type=jnp.float32)
    grad_up, grad_down = slab_scatter(
        [up_full, down_full], lax.psum(1, SLAB), lax.psum(1, ("z", "xl"))
    )
    return (attended, grad_up, grad_down)


def solution(mesh):
    mesh = Mesh(mesh.devices.reshape(4, 8, 2, 2, 2), SLAB + FFN)
    in_specs = (
        P(SLAB, None),
        P(),
        P(),
        P(),
        P(None, FFN),
        P(None, FFN),
        P(None, FFN),
        P(FFN, None),
        P(),
        P(None, FFN),
        P(None, FFN),
        P(FFN, None),
        P(SLAB, None),
    )
    out_specs = (P(SLAB, None), P(SLAB, FFN), P(SLAB, FFN))
    return jax.shard_map(
        per_device, mesh=mesh, in_specs=in_specs, out_specs=out_specs, check_vma=False
    )
```
